32 devices in a mesh: dp: 8 (over z, core), tensor: 4 (over y, x).
Axes of the slice: x: 2, y: 2, z: 4, core: 2. Of those that a mesh axis runs over, the one named last changes fastest.
Arguments:
- latents: bfloat16 [8, 1024, 1536], P('dp'), may hold values from -6 to 6
- context: bfloat16 [8, 130, 768], P('dp'), may hold values from -6 to 6
- cotangent: bfloat16 [8, 1024, 1536], P('dp'), may hold values from -6 to 6
- self_gain: float32 [1536], replicated, may hold values from 0.5 to 1.5
- self_query: bfloat16 [1536, 1536], P(None, 'tensor'), may hold values from -0.15625 to 0.15625
- self_key: bfloat16 [1536, 1536], P(None, 'tensor'), may hold values from -0.15625 to 0.15625
- self_value: bfloat16 [1536, 1536], P(None, 'tensor'), may hold values from -0.15625 to 0.15625
- self_output: bfloat16 [1536, 1536], P('tensor'), may hold values from -2.5 to 2.5
- cross_gain: float32 [1536], replicated, may hold values from 0.5 to 1.5
- cross_query: bfloat16 [1536, 1536], P(None, 'tensor'), may hold values from -0.15625 to 0.15625
- cross_key: bfloat16 [768, 1536], P(None, 'tensor'), may hold values from -0.21875 to 0.21875
- cross_value: bfloat16 [768, 1536], P(None, 'tensor'), may hold values from -0.21875 to 0.21875
- cross_output: bfloat16 [1536, 1536], P('tensor'), may hold values from -0.875 to 0.875
- feed_gain: float32 [1536], replicated, may hold values from 0.5 to 1.5
- feed_gate: bfloat16 [1536, 6144], P(None, 'tensor'), may hold values from -0.15625 to 0.15625
- feed_up: bfloat16 [1536, 6144], P(None, 'tensor'), may hold values from -0.15625 to 0.15625
- feed_down: bfloat16 [6144, 1536], P('tensor'), may hold values from -0.078125 to 0.078125
Outputs:
- block_out: bfloat16 [8, 1024, 1536], P('dp')
- latent_grad: float32 [8, 1024, 1536], P('dp')
- self_gain_grad: float32 [1536], P('dp')
- self_query_grad: float32 [1536, 1536], P('dp', 'tensor')
- self_key_grad: float32 [1536, 1536], P('dp', 'tensor')
- self_value_grad: float32 [1536, 1536], P('dp', 'tensor')
- self_output_grad: float32 [1536, 1536], P('tensor', 'dp')
- cross_gain_grad: float32 [1536], P('dp')
- cross_query_grad: float32 [1536, 1536], P('dp', 'tensor')
- cross_key_grad: float32 [768, 1536], P('dp', 'tensor')
- cross_value_grad: float32 [768, 1536], P('dp', 'tensor')
- cross_output_grad: float32 [1536, 1536], P('tensor', 'dp')
- feed_gain_grad: float32 [1536], P('dp')
- feed_gate_grad: float32 [1536, 6144], P('dp', 'tensor')
- feed_up_grad: float32 [1536, 6144], P('dp', 'tensor')
- feed_down_grad: float32 [6144, 1536], P('tensor', 'dp')
The draws below stay inside these ranges and needn't reach their ends.
All inputs are finite; a program needn't handle non-finite values.
Results may differ from the reference program's by a relative error of at most 0.034.
Values may be sent and summed in bfloat16 or wider, within the bound.
A program may use at most 256 MiB of HBM per device.

```python
import jax
import jax.numpy as jnp
from jax import lax

D = 1536
HEADS = 24
HEAD_DIM = 64
FF = 6144
CDIM = 768
CTX = 130
LEN = 1024
SEQS = 8
HD = 1536
N_TENSOR = 4


def spiked(result, key, source, target, blocks, factor):
    def block_of(position):
        return (jnp.arange(result.shape[position]) // (result.shape[position] // blocks)).reshape((-1,) + (1,) * (result.ndim - 1 - position))

    one_side = jax.random.permutation(key, blocks)[block_of(target)]
    other_side = (block_of(target) + blocks // 2) % blocks
    return jnp.where((block_of(source) == one_side) | (block_of(source) == other_side), factor * result, result)


def level_of(stream_key, extent, split, smallest, top_value):
    def one(axis_at, shards_of):
        draws = jax.random.uniform(jax.random.fold_in(jax.random.fold_in(stream_key, 6), axis_at), (shards_of,), jnp.float32, smallest / len(split), top_value / len(split))
        return jnp.repeat(jnp.exp(draws), extent[axis_at] // shards_of).reshape((-1,) + (1,) * (len(extent) - axis_at - 1))

    factor_of = one(*split[0])
    for cut in split[1:]:
        factor_of = factor_of * one(*cut)
    return factor_of


def gaussian(key, dims, scale, reach, shards=(), kind=jnp.bfloat16):
    gain = level_of(key, dims, shards, -0.22, 0.18) if shards else 1.0
    drawn = jax.random.normal(key, dims, jnp.float32) * scale * gain
    return jnp.minimum(jnp.maximum(drawn, -reach), reach).astype(kind)


def heavy_noise(key, dims, deviation, reach, pieces, heavy, kind=jnp.bfloat16):
    values = deviation * jax.random.normal(key, dims, jnp.float32)
    if pieces:
        values = values * level_of(key, dims, pieces, -0.22, 0.18)
    return jnp.clip(spiked(values, jax.random.fold_in(key, 3), *heavy), -reach, reach).astype(kind)


def setup_inputs(seed: int = 0) -> dict:
    keys = jax.random.split(jax.random.key(seed), 18)
    return {
        "latents": gaussian(keys[0], (SEQS, LEN, D), 1.0, 6.0, ((0, 8),)),
        "context": gaussian(keys[1], (SEQS, CTX, CDIM), 1.0, 6.0, ((0, 8),)),
        "cotangent": heavy_noise(keys[2], (SEQS, LEN, D), 1.0, 6.0, ((0, 8),), (0, 2, 8, 2.0)),
        "self_gain": jnp.clip(1.0 + 0.1 * jax.random.normal(keys[3], (D,), jnp.float32), 0.5, 1.5),
        "self_query": gaussian(keys[4], (D, HD), D ** -0.5, 0.15625, ((1, 4),)),
        "self_key": gaussian(keys[5], (D, HD), D ** -0.5, 0.15625, ((1, 4),)),
        "self_value": gaussian(keys[6], (D, HD), D ** -0.5, 0.15625, ((1, 4),)),
        "self_output": gaussian(keys[7], (HD, D), (max(HD * 4 // LEN, 1)) ** -0.5, 2.5, ((0, 4),)),
        "cross_gain": jnp.clip(1.0 + 0.1 * jax.random.normal(keys[8], (D,), jnp.float32), 0.5, 1.5),
        "cross_query": gaussian(keys[9], (D, HD), D ** -0.5, 0.15625, ((1, 4),)),
        "cross_key": gaussian(keys[10], (CDIM, HD), CDIM ** -0.5, 0.21875, ((1, 4),)),
        "cross_value": gaussian(keys[11], (CDIM, HD), CDIM ** -0.5, 0.21875, ((1, 4),)),
        "cross_output": gaussian(keys[12], (HD, D), (max(HD * 4 // CTX, 1)) ** -0.5, 0.875, ((0, 4),)),
        "feed_gain": jnp.clip(1.0 + 0.1 * jax.random.normal(keys[13], (D,), jnp.float32), 0.5, 1.5),
        "feed_gate": gaussian(keys[14], (D, FF), D ** -0.5, 0.15625, ((1, 4),)),
        "feed_up": gaussian(keys[15], (D, FF), D ** -0.5, 0.15625, ((1, 4),)),
        "feed_down": gaussian(keys[16], (FF, D), FF ** -0.5, 0.078125, ((0, 4),)),
    }


@jax.custom_vjp
def low(v):
    return lax.optimization_barrier(v.astype(jnp.bfloat16)).astype(jnp.float32)

@jax.custom_vjp
def low_back(v):
    return v

def low_keep(v):
    return (low(v), None)

def low_pass(kept, grad):
    return (grad,)

def back_keep(v):
    return (v, None)

def back_low(kept, grad):
    return (low(grad),)
low.defvjp(low_keep, low_pass)
low_back.defvjp(back_keep, back_low)
norm_epsilon = 1e-05
highest = lax.Precision.HIGHEST

def product(left_rows, right_rows):
    return jnp.dot(left_rows, right_rows, precision=highest, preferred_element_type=jnp.float32)

def normalize(values, gain_vec):
    center = values - lax.optimization_barrier(jnp.mean(values, axis=-1, keepdims=True))
    variance = lax.optimization_barrier(jnp.mean(center * center, axis=-1, keepdims=True))
    return center * lax.rsqrt(variance + norm_epsilon) * gain_vec

def rotary_tables(length):
    half_dim = HEAD_DIM // 2
    frequency = 10000.0 ** (-jnp.arange(half_dim, dtype=jnp.float32) / half_dim)
    angles = jnp.arange(length, dtype=jnp.float32)[:, None] * frequency[None, :]
    return (jnp.cos(angles)[:, None, :], jnp.sin(angles)[:, None, :])

def rotate(values, cosine_table, sine_table):
    half_dim = values.shape[-1] // 2
    front_half = values[..., :half_dim]
    back_half = values[..., half_dim:]
    return jnp.concatenate([front_half * cosine_table - back_half * sine_table, back_half * cosine_table + front_half * sine_table], axis=-1)

def attend(queries, keys_in, values_in):
    length, heads, head_width = queries.shape
    block_rows = 512 if length % 512 == 0 else length
    score_scale = HEAD_DIM ** (-0.5)

    def one_block(query_blk):
        scores = low_back(score_scale * jnp.einsum('qhd,khd->hqk', query_blk, keys_in, precision=highest))
        attn_weights = jax.nn.softmax(scores, axis=-1)
        return jnp.einsum('hqk,khd->qhd', low(attn_weights), values_in, precision=highest)
    outputs = lax.map(jax.checkpoint(one_block), queries.reshape(length // block_rows, block_rows, heads, head_width))
    return outputs.reshape(length, heads * head_width)

def branch_sum(inputs, weight):
    length = inputs.shape[0]
    grouped = inputs.reshape(length, N_TENSOR, -1)
    blocks = weight.reshape(N_TENSOR, -1, weight.shape[1])
    parts = low(jnp.einsum('lgk,gkd->gld', grouped, blocks, precision=highest))
    return lax.optimization_barrier(jnp.sum(parts, axis=0))

def block_forward(latent_seq, context_seq, self_gain, self_query, self_key, self_value, self_output, cross_gain, cross_query, cross_key, cross_value, cross_output, feed_gain, feed_gate, feed_up, feed_down):
    length = latent_seq.shape[0]
    ctx_len = context_seq.shape[0]
    cosine_table, sine_table = rotary_tables(length)
    normed1 = low(normalize(latent_seq, self_gain))
    queries = low(rotate(low_back(product(normed1, self_query)).reshape(length, HEADS, HEAD_DIM), cosine_table, sine_table))
    keys_rot = low(rotate(low_back(product(normed1, self_key)).reshape(length, HEADS, HEAD_DIM), cosine_table, sine_table))
    value_rows = low(low_back(product(normed1, self_value))).reshape(length, HEADS, HEAD_DIM)
    self_attn = low(low_back(attend(queries, keys_rot, value_rows)))
    after1 = latent_seq + low_back(branch_sum(self_attn, self_output))
    normed2 = low(normalize(after1, cross_gain))
    cross_q = low(low_back(product(normed2, cross_query))).reshape(length, HEADS, HEAD_DIM)
    cross_k = low(low_back(product(context_seq, cross_key))).reshape(ctx_len, HEADS, HEAD_DIM)
    cross_v = low(low_back(product(context_seq, cross_value))).reshape(ctx_len, HEADS, HEAD_DIM)
    cross_attn = low(low_back(attend(cross_q, cross_k, cross_v)))
    after2 = after1 + low_back(branch_sum(cross_attn, cross_output))
    normed3 = low(normalize(after2, feed_gain))
    gate_rows = low_back(product(normed3, feed_gate))
    up_rows = low_back(product(normed3, feed_up))
    hidden = low(jax.nn.silu(gate_rows) * up_rows)
    return after2 + low_back(branch_sum(hidden, feed_down))

def reference(latents, context, cotangent, self_gain, self_query, self_key, self_value, self_output, cross_gain, cross_query, cross_key, cross_value, cross_output, feed_gain, feed_gate, feed_up, feed_down):
    weights = tuple((array.astype(jnp.float32) for array in (self_gain, self_query, self_key, self_value, self_output, cross_gain, cross_query, cross_key, cross_value, cross_output, feed_gain, feed_gate, feed_up, feed_down)))

    def one_sequence(carry, seq_item):
        latent_seq, context_seq, grad_seq = seq_item

        def forward(latent_in, *weight_in):
            return block_forward(latent_in, context_seq, *weight_in)
        output, pullback = jax.vjp(forward, latent_seq, *weights)
        pulled = pullback(grad_seq)
        summed = tuple((running + fresh_term for running, fresh_term in zip(carry, pulled[1:])))
        return (summed, (output.astype(jnp.bfloat16), pulled[0]))
    start_sums = tuple((jnp.zeros(array.shape, jnp.float32) for array in weights))
    totals, (block_out, latent_grad) = lax.scan(one_sequence, start_sums, (latents.astype(jnp.float32), context.astype(jnp.float32), cotangent.astype(jnp.float32)))
    return (block_out, latent_grad, totals[0], totals[1], totals[2], totals[3], totals[4], totals[5], totals[6], totals[7], totals[8], totals[9], totals[10], totals[11], totals[12], totals[13])
```

```python
import functools

import jax
import jax.numpy as jnp
from jax import lax
from jax.experimental import pallas as pl
from jax.experimental.pallas import tpu as pltpu
from jax.sharding import PartitionSpec as P

HEAD_DIM = 64
HALF = HEAD_DIM // 2
EPS = 1e-05
BF = jnp.bfloat16
F32 = jnp.float32
LOG2E = 1.4426950408889634
SCALE = HEAD_DIM**-0.5
VMEM_BYTES = 60 << 20
MESH_ID = pl.DeviceIdType.MESH
VSPEC = pl.BlockSpec(memory_space=pltpu.VMEM)
ANYSPEC = pl.BlockSpec(memory_space=pl.ANY)


def nn(a, b):
    return lax.dot_general(a, b, (((1,), (0,)), ((), ())), preferred_element_type=F32)


def nt(a, b):
    return lax.dot_general(a, b, (((1,), (1,)), ((), ())), preferred_element_type=F32)


def tn(a, b):
    return lax.dot_general(a, b, (((0,), (0,)), ((), ())), preferred_element_type=F32)


def sds(shape, dtype):
    return jax.ShapeDtypeStruct(shape, dtype)


def params(**kw):
    return pltpu.CompilerParams(vmem_limit_bytes=VMEM_BYTES, **kw)


def cost(flops, nbytes, trans=0):
    return pl.CostEstimate(flops=int(flops), bytes_accessed=int(nbytes), transcendentals=int(trans))


def unit(x):
    center = x - jnp.mean(x, axis=-1, keepdims=True)
    inverse = lax.rsqrt(jnp.mean(center * center, axis=-1, keepdims=True) + EPS)
    return center * inverse, inverse


def norm_back(grad, u, inverse, gain):
    e = grad * gain
    mean_e = jnp.mean(e, axis=-1, keepdims=True)
    mean_p = jnp.mean(e * u, axis=-1, keepdims=True)
    return inverse * (e - mean_e - u * mean_p)


def lane_group(width):
    return 128 if width % 128 == 0 else width


def tables(length, group):
    freq = 10000.0 ** (-jnp.arange(HALF, dtype=F32) / HALF)
    angles = jnp.arange(length, dtype=F32)[:, None] * freq[None, :]
    c, s = jnp.cos(angles), jnp.sin(angles)
    reps = group // HEAD_DIM
    return jnp.tile(jnp.concatenate([c, c], 1), (1, reps)), jnp.tile(jnp.concatenate([-s, s], 1), (1, reps))


def turned(a):
    width = a.shape[-1]
    lane = lax.broadcasted_iota(jnp.int32, a.shape, 1) % HEAD_DIM
    return jnp.where(lane < HALF, pltpu.roll(a, width - HALF, 1), pltpu.roll(a, HALF, 1))


def head_masks(rows, group):
    lane = lax.broadcasted_iota(jnp.int32, (rows, group), 1) // HEAD_DIM
    return [jnp.where(lane == h, 1.0, 0.0) for h in range(group // HEAD_DIM)]


def qkv_kernel(x_ref, g_ref, wq_ref, wk_ref, wv_ref, c_ref, s_ref, h_ref, q_ref, k_ref, v_ref):
    u, _ = unit(x_ref[...].astype(F32))
    h = (u * g_ref[...]).astype(BF)
    h_ref[...] = h
    reps = q_ref.shape[1] // c_ref.shape[1]
    c = jnp.concatenate([c_ref[...]] * reps, 1)
    s = jnp.concatenate([s_ref[...]] * reps, 1)
    for w_ref, o_ref in ((wq_ref, q_ref), (wk_ref, k_ref)):
        a = nn(h, w_ref[...])
        o_ref[...] = (a * c + turned(a) * s).astype(BF)
    v_ref[...] = nn(h, wv_ref[...]).astype(BF)


def qkv(x, gain, wq, wk, wv, cs, sn):
    T, D = x.shape
    W = wq.shape[1]
    tb = 256
    row = lambda n: pl.BlockSpec((tb, n), lambda i: (i, 0))
    full = lambda a: pl.BlockSpec(a.shape, lambda i: (0, 0), pipeline_mode=pl.Buffered(1))
    return pl.pallas_call(
        qkv_kernel,
        grid=(T // tb,),
        in_specs=[row(D), full(gain), full(wq), full(wk), full(wv), row(cs.shape[1]), row(cs.shape[1])],
        out_specs=[row(D), row(W), row(W), row(W)],
        out_shape=[sds((T, D), BF)] + [sds((T, W), BF)] * 3,
        compiler_params=params(),
        cost_estimate=cost(6 * T * D * W, 4 * T * D + 6 * D * W + 6 * T * W),
        name="qkv",
    )(x, gain, wq, wk, wv, cs, sn)


def attn_fwd_kernel(q_ref, k_ref, v_ref, o_ref, lse_ref):
    T, G = q_ref.shape
    qb = 256
    mult = SCALE * LOG2E
    k, v = k_ref[...], v_ref[...]
    masks = [m.astype(BF) for m in head_masks(1, G)]
    lane = lax.broadcasted_iota(jnp.int32, (qb, G), 1) // HEAD_DIM
    stat_lane = lax.broadcasted_iota(jnp.int32, (qb, 128), 1)

    def block(i, carry):
        rows = pl.ds(pl.multiple_of(i * qb, qb), qb)
        q = q_ref[rows, :]
        out = jnp.zeros((qb, G), F32)
        stats = jnp.zeros((qb, 128), F32)
        for h in range(G // HEAD_DIM):
            s = nt(q * masks[h], k)
            top = jnp.max(s, axis=-1, keepdims=True) * mult
            p = jnp.exp2(s * mult - top)
            total = jnp.sum(p, axis=-1, keepdims=True)
            o = nn(p.astype(BF), v) / total
            out = jnp.where(lane == h, o, out)
            stats = jnp.where(stat_lane == h, top + jnp.log2(total), stats)
        o_ref[rows, :] = out.astype(BF)
        lse_ref[:, rows] = jnp.transpose(stats)[:8]
        return carry

    lax.fori_loop(0, T // qb, block, 0)


def attn_fwd(q, k, v):
    T, W = q.shape
    G = lane_group(W)
    groups = W // G
    cols = pl.BlockSpec((T, G), lambda i: (0, i))
    return pl.pallas_call(
        attn_fwd_kernel,
        grid=(groups,),
        in_specs=[cols] * 3,
        out_specs=[cols, pl.BlockSpec((None, 8, T), lambda i: (i, 0, 0))],
        out_shape=[sds((T, W), BF), sds((groups, 8, T), F32)],
        compiler_params=params(),
        cost_estimate=cost(16 * T * T * W, 8 * T * W, T * T * W // HEAD_DIM),
        name="attn_fwd",
    )(q, k, v)


def attn_bwd_kernel(q_ref, k_ref, v_ref, o_ref, do_ref, lse_ref, c_ref, s_ref, dq_ref, dk_ref, dv_ref, dk_acc, dv_acc, kt_ref):
    T, G = q_ref.shape
    qb = 256
    mult = SCALE * LOG2E
    nh = G // HEAD_DIM
    k, v = k_ref[...], v_ref[...]
    kt_ref[...] = jnp.transpose(k.astype(F32)).astype(BF)
    masks = [m.astype(BF) for m in head_masks(1, G)]
    head_rows = jnp.where(
        lax.broadcasted_iota(jnp.int32, (16, G), 0) == lax.broadcasted_iota(jnp.int32, (16, G), 1) // HEAD_DIM, 1.0, 0.0
    ).astype(BF)
    dk_acc[...] = jnp.zeros_like(dk_acc)
    dv_acc[...] = jnp.zeros_like(dv_acc)

    def block(i, carry):
        rows = pl.ds(pl.multiple_of(i * qb, qb), qb)
        q = q_ref[rows, :]
        do = do_ref[rows, :]
        prod = do.astype(F32) * o_ref[rows, :].astype(F32)
        high = prod.astype(BF)
        delta = nt(head_rows, high) + nt(head_rows, (prod - high.astype(F32)).astype(BF))
        lse = lse_ref[:, rows]
        parts = []
        for h in range(nh):
            qm = q * masks[h]
            dom = do * masks[h]
            st = nt(k, qm)
            pt = jnp.exp2(st * mult - lse[h : h + 1, :])
            dpt = nt(v, dom)
            dst = (pt * (dpt - delta[h : h + 1, :])).astype(BF)
            dv_acc[...] += nn(pt.astype(BF), dom)
            dk_acc[...] += nn(dst, qm)
            parts.append(nn(kt_ref[h * HEAD_DIM : (h + 1) * HEAD_DIM, :], dst))
        dq = jnp.transpose(jnp.concatenate(parts, 0)) * SCALE
        dq_ref[rows, :] = (dq * c_ref[rows, :] - turned(dq) * s_ref[rows, :]).astype(BF)
        return carry

    lax.fori_loop(0, T // qb, block, 0)
    dk = dk_acc[...] * SCALE
    dk_ref[...] = (dk * c_ref[...] - turned(dk) * s_ref[...]).astype(BF)
    dv_ref[...] = dv_acc[...].astype(BF)


def attn_bwd(q, k, v, o, do, lse, cs, sn):
    T, W = q.shape
    G = lane_group(W)
    cols = pl.BlockSpec((T, G), lambda i: (0, i))
    tab = pl.BlockSpec((T, G), lambda i: (0, 0), pipeline_mode=pl.Buffered(1))
    return pl.pallas_call(
        attn_bwd_kernel,
        grid=(W // G,),
        in_specs=[cols] * 5 + [pl.BlockSpec((None, 8, T), lambda i: (i, 0, 0)), tab, tab],
        out_specs=[cols] * 3,
        out_shape=[sds((T, W), BF)] * 3,
        scratch_shapes=[pltpu.VMEM((T, G), F32), pltpu.VMEM((T, G), F32), pltpu.VMEM((G, T), BF)],
        compiler_params=params(),
        cost_estimate=cost(40 * T * T * W, 16 * T * W, T * T * W // HEAD_DIM),
        name="attn_bwd",
    )(q, k, v, o, do, lse, cs, sn)


def greet(n, me):
    sem = pltpu.get_barrier_semaphore()
    for d in range(1, n):
        pl.semaphore_signal(sem, 1, device_id={"tensor": me ^ d}, device_id_type=MESH_ID)
    pl.semaphore_wait(sem, n - 1)


def remote(src, dst, send, recv, target):
    return pltpu.make_async_remote_copy(src, dst, send, recv, device_id={"tensor": target}, device_id_type=MESH_ID)


def out_rs_kernel(n, a_ref, w_ref, x_ref, g_ref, after_ref, h_ref, sbuf, rbuf, ss, rs):
    me = lax.axis_index("tensor")
    C = x_ref.shape[0]
    greet(n, me)

    def part(t):
        return nn(a_ref[pl.ds(pl.multiple_of(t * C, C), C), :], w_ref[...])

    copies = {}
    for d in reversed(range(1, n)):
        t = me ^ d
        sbuf[d - 1] = part(t).astype(BF)
        copies[d] = remote(sbuf.at[d - 1], rbuf.at[d - 1], ss.at[d - 1], rs.at[d - 1], t)
        copies[d].start()
    total = part(me)
    for d in range(1, n):
        copies[d].wait_recv()
        total = total + rbuf[d - 1].astype(F32)
    after = x_ref[...].astype(F32) + total
    after_ref[...] = after
    u, _ = unit(after)
    h_ref[...] = (u * g_ref[...]).astype(BF)
    for d in range(1, n):
        copies[d].wait_send()


def out_rs(n, a, w, x, gain):
    C, D = x.shape
    T, W = a.shape
    return pl.pallas_call(
        functools.partial(out_rs_kernel, n),
        in_specs=[VSPEC] * 4,
        out_specs=[VSPEC] * 2,
        out_shape=[sds((C, D), F32), sds((C, D), BF)],
        scratch_shapes=[pltpu.VMEM((n - 1, C, D), BF)] * 2 + [pltpu.SemaphoreType.DMA((n - 1,))] * 2,
        compiler_params=params(collective_id=0, has_side_effects=True),
        cost_estimate=cost(2 * T * W * D + 2e10, 8 * C * D),
        name="out_rs",
    )(a, w, x, gain)


def ff_kernel(n, h_in, gb_hbm, wg_hbm, wu_hbm, wd_hbm, h_ref, hid_ref, dgu_ref, dh_ref,
              gb_ref, wg_ref, wu_ref, wd_ref, sbuf, rbuf, ss, rs, ss2, rs2, ls):
    me = lax.axis_index("tensor")
    C, D = h_in.shape
    F = wg_ref.shape[1]
    loads = [
        pltpu.make_async_copy(src, dst, ls.at[i])
        for i, (src, dst) in enumerate(((wg_hbm, wg_ref), (wu_hbm, wu_ref), (wd_hbm, wd_ref), (gb_hbm, gb_ref)))
    ]
    for c in loads:
        c.start()
    greet(n, me)
    gather = {}
    for d in range(1, n):
        gather[d] = remote(h_in, h_ref.at[me], ss.at[d - 1], rs.at[d - 1], me ^ d)
        gather[d].start()
    h_ref[me] = h_in[...]
    for c in loads:
        c.wait()
    tf = 256

    def chunk(t, store):
        rows = pl.ds(pl.multiple_of(t * C, C), C)
        h = h_ref[t]
        gb = gb_ref[rows, :]

        def tile(j, carry):
            cols = pl.ds(pl.multiple_of(j * tf, tf), tf)
            gate = nn(h, wg_ref[:, cols])
            up = nn(h, wu_ref[:, cols])
            dhid = nt(gb, wd_ref[cols, :])
            sig = 1.0 / (1.0 + jnp.exp(-gate))
            act = gate * sig
            hid_ref[rows, cols] = (act * up).astype(BF)
            dgu_ref[rows, cols] = (dhid * up * (sig * (1.0 + gate * (1.0 - sig)))).astype(BF)
            dgu_ref[rows, pl.ds(pl.multiple_of(F + j * tf, tf), tf)] = (dhid * act).astype(BF)
            return carry

        lax.fori_loop(0, F // tf, tile, 0)

        def back(j, carry):
            out = pl.ds(pl.multiple_of(j * tf, tf), tf)
            store(out, nt(dgu_ref[rows, :F], wg_ref[out, :]) + nt(dgu_ref[rows, F:], wu_ref[out, :]))
            return carry

        lax.fori_loop(0, D // tf, back, 0)

    def store_own(cols, val):
        dh_ref[:, cols] = val

    chunk(me, store_own)
    copies = {}
    for d in range(1, n):
        t = me ^ d
        gather[d].wait_recv()

        def store_sent(cols, val):
            sbuf[d - 1, :, cols] = val.astype(BF)

        chunk(t, store_sent)
        copies[d] = remote(sbuf.at[d - 1], rbuf.at[d - 1], ss2.at[d - 1], rs2.at[d - 1], t)
        copies[d].start()
    for d in range(1, n):
        gather[d].wait_send()
    for d in range(1, n):
        copies[d].wait_recv()
        dh_ref[...] += rbuf[d - 1].astype(F32)
    for d in range(1, n):
        copies[d].wait_send()


def ff(n, h, gb, wg, wu, wd):
    C, D = h.shape
    T = gb.shape[0]
    F = wg.shape[1]
    return pl.pallas_call(
        functools.partial(ff_kernel, n),
        in_specs=[VSPEC] + [ANYSPEC] * 4,
        out_specs=[VSPEC] * 4,
        out_shape=[sds((n, C, D), BF), sds((T, F), BF), sds((T, 2 * F), BF), sds((C, D), F32)],
        scratch_shapes=[
            pltpu.VMEM((T, D), BF),
            pltpu.VMEM((D, F), BF),
            pltpu.VMEM((D, F), BF),
            pltpu.VMEM((F, D), BF),
            pltpu.VMEM((n - 1, C, D), BF),
            pltpu.VMEM((n - 1, C, D), BF),
        ]
        + [pltpu.SemaphoreType.DMA((n - 1,))] * 4
        + [pltpu.SemaphoreType.DMA((4,))],
        compiler_params=params(collective_id=1, has_side_effects=True),
        cost_estimate=cost(10 * T * D * F + 3e10, 6 * D * F + 8 * T * D),
        name="ff",
    )(h, gb, wg, wu, wd)


def gather_kernel(n, x_in, w_ref, x_ref, da_ref, ss, rs):
    me = lax.axis_index("tensor")
    C = x_in.shape[0]
    greet(n, me)
    gather = {}
    for d in range(1, n):
        gather[d] = remote(x_in, x_ref.at[me], ss.at[d - 1], rs.at[d - 1], me ^ d)
        gather[d].start()

    def back(t, x):
        da_ref[pl.ds(pl.multiple_of(t * C, C), C), :] = nt(x, w_ref[...]).astype(BF)

    x_ref[me] = x_in[...]
    back(me, x_in[...])
    for d in range(1, n):
        gather[d].wait_recv()
        back(me ^ d, x_ref[me ^ d])
    for d in range(1, n):
        gather[d].wait_send()


def gather_back(n, x, w):
    C, D = x.shape
    W = w.shape[0]
    return pl.pallas_call(
        functools.partial(gather_kernel, n),
        in_specs=[VSPEC] * 2,
        out_specs=[VSPEC] * 2,
        out_shape=[sds((n, C, D), BF), sds((n * C, W), BF)],
        scratch_shapes=[pltpu.SemaphoreType.DMA((n - 1,))] * 2,
        compiler_params=params(collective_id=2, has_side_effects=True),
        cost_estimate=cost(2 * n * C * W * D + 2e10, 8 * C * D),
        name="gather_back",
    )(x, w)


def last_kernel(n, dq_ref, dk_ref, dv_ref, wq_ref, wk_ref, wv_ref, x_ref, da_ref, g_ref, gg_in,
                out_ref, gg_ref, sbuf, rbuf, lbuf, gbuf, gsum, ss, rs, ss2, rs2, ss3, rs3):
    me = lax.axis_index("tensor")
    C, D = x_ref.shape
    greet(n, me)

    def part(t):
        rows = pl.ds(pl.multiple_of(t * C, C), C)
        return nt(dq_ref[rows, :], wq_ref[...]) + nt(dk_ref[rows, :], wk_ref[...]) + nt(dv_ref[rows, :], wv_ref[...])

    copies = {}
    for d in reversed(range(1, n)):
        t = me ^ d
        sbuf[d - 1] = part(t).astype(BF)
        copies[d] = remote(sbuf.at[d - 1], rbuf.at[d - 1], ss.at[d - 1], rs.at[d - 1], t)
        copies[d].start()
    total = part(me)
    u, inverse = unit(x_ref[...].astype(F32))
    for d in range(1, n):
        copies[d].wait_recv()
        total = total + rbuf[d - 1].astype(F32)
    lbuf[me] = (da_ref[...] + norm_back(total, u, inverse, g_ref[...])).astype(BF)
    gather = {}
    for d in range(1, n):
        gather[d] = remote(lbuf.at[me], lbuf.at[me], ss2.at[d - 1], rs2.at[d - 1], me ^ d)
        gather[d].start()
    row = lax.broadcasted_iota(jnp.int32, (8, D), 0)
    gsum[...] = gg_in[...] + jnp.where(row == 2, jnp.sum(total * u, axis=0, keepdims=True), 0.0)
    small = {}
    for d in range(1, n):
        small[d] = remote(gsum, gbuf.at[d - 1], ss3.at[d - 1], rs3.at[d - 1], me ^ d)
        small[d].start()

    def put(t):
        out_ref[pl.ds(pl.multiple_of(t * C, C), C), :] = lbuf[t].astype(F32)

    put(me)
    for d in range(1, n):
        gather[d].wait_recv()
        put(me ^ d)
    gains = gsum[...]
    for d in range(1, n):
        small[d].wait_recv()
        gains = gains + gbuf[d - 1]
    gg_ref[...] = gains
    for d in range(1, n):
        copies[d].wait_send()
        gather[d].wait_send()
        small[d].wait_send()


def last(n, dq, dk, dv, wq, wk, wv, x, da, gain, gains):
    C, D = x.shape
    T, W = dq.shape
    return pl.pallas_call(
        functools.partial(last_kernel, n),
        in_specs=[VSPEC] * 10,
        out_specs=[VSPEC] * 2,
        out_shape=[sds((T, D), F32), sds((8, D), F32)],
        scratch_shapes=[
            pltpu.VMEM((n - 1, C, D), BF),
            pltpu.VMEM((n - 1, C, D), BF),
            pltpu.VMEM((n, C, D), BF),
            pltpu.VMEM((n - 1, 8, D), F32),
            pltpu.VMEM((8, D), F32),
        ]
        + [pltpu.SemaphoreType.DMA((n - 1,))] * 6,
        compiler_params=params(collective_id=3, has_side_effects=True),
        cost_estimate=cost(6 * T * W * D + 4e10, 8 * T * D),
        name="last",
    )(dq, dk, dv, wq, wk, wv, x, da, gain, gains)


def cross_fwd_kernel(ctx, h_ref, x_ref, wq_ref, k_ref, v_ref, wo_ref, g_ref, q_ref, o_ref, after_ref, h3_ref):
    C, HD = q_ref.shape
    KP = k_ref.shape[0]
    mult = SCALE * LOG2E
    G = 128
    masks = [m.astype(BF) for m in head_masks(1, G)]
    lane = lax.broadcasted_iota(jnp.int32, (C, G), 1) // HEAD_DIM
    valid = lax.broadcasted_iota(jnp.int32, (C, KP), 1) < ctx

    def group(g, carry):
        cols = pl.ds(pl.multiple_of(g * G, G), G)
        q = nn(h_ref[...], wq_ref[:, cols]).astype(BF)
        q_ref[:, cols] = q
        k, v = k_ref[:, cols], v_ref[:, cols]
        out = jnp.zeros((C, G), F32)
        for h in range(G // HEAD_DIM):
            s = jnp.where(valid, nt(q * masks[h], k), -1e30)
            p = jnp.exp2((s - jnp.max(s, axis=-1, keepdims=True)) * mult)
            o = nn(p.astype(BF), v) / jnp.sum(p, axis=-1, keepdims=True)
            out = jnp.where(lane == h, o, out)
        o_ref[:, cols] = out.astype(BF)
        return carry

    lax.fori_loop(0, HD // G, group, 0)
    D = h_ref.shape[1]
    tf = 256

    def project(j, carry):
        cols = pl.ds(pl.multiple_of(j * tf, tf), tf)
        after_ref[:, cols] = x_ref[:, cols] + nn(o_ref[...], wo_ref[:, cols])
        return carry

    lax.fori_loop(0, D // tf, project, 0)
    u, _ = unit(after_ref[...])
    h3_ref[...] = (u * g_ref[...]).astype(BF)


def cross_fwd(ctx, h, x, wq, k, v, wo, gain):
    C, D = h.shape
    HD = wq.shape[1]
    return pl.pallas_call(
        functools.partial(cross_fwd_kernel, ctx),
        in_specs=[VSPEC] * 7,
        out_specs=[VSPEC] * 4,
        out_shape=[sds((C, HD), BF), sds((C, HD), BF), sds((C, D), F32), sds((C, D), BF)],
        compiler_params=params(),
        cost_estimate=cost(4 * C * D * HD + 16 * C * 256 * HD, 8 * D * HD),
        name="cross_fwd",
    )(h, x, wq, k, v, wo, gain)


def cross_bwd_kernel(ctx, dh3_ref, after2_ref, cot_ref, g3_ref, wo_ref, q_ref, k_ref, v_ref, wq_ref, after1_ref, g2_ref,
                     cb_ref, dq_ref, dk_ref, dv_ref, da_ref, sb_ref, gg_ref, dh2_ref):
    C, HD = q_ref.shape
    KP = k_ref.shape[0]
    D = da_ref.shape[1]
    mult = SCALE * LOG2E
    G = 128
    masks = [m.astype(BF) for m in head_masks(1, G)]
    lane = lax.broadcasted_iota(jnp.int32, (C, G), 1) // HEAD_DIM
    valid = lax.broadcasted_iota(jnp.int32, (C, KP), 1) < ctx
    dh3 = dh3_ref[...]
    u3, inv3 = unit(after2_ref[...])
    gain3 = jnp.sum(dh3 * u3, axis=0, keepdims=True)
    da2 = cot_ref[...].astype(F32) + norm_back(dh3, u3, inv3, g3_ref[...])
    da_ref[...] = da2
    cb_ref[...] = da2.astype(BF)

    def group(g, carry):
        cols = pl.ds(pl.multiple_of(g * G, G), G)
        do = nt(cb_ref[...], wo_ref[cols, :]).astype(BF)
        q, k, v = q_ref[:, cols], k_ref[:, cols], v_ref[:, cols]
        dq = jnp.zeros((C, G), F32)
        dk = jnp.zeros((KP, G), F32)
        dv = jnp.zeros((KP, G), F32)
        for h in range(G // HEAD_DIM):
            qm = q * masks[h]
            dom = do * masks[h]
            s = jnp.where(valid, nt(qm, k), -1e30)
            p = jnp.exp2((s - jnp.max(s, axis=-1, keepdims=True)) * mult)
            p = p / jnp.sum(p, axis=-1, keepdims=True)
            dp = nt(dom, v)
            ds = (p * (dp - jnp.sum(p * dp, axis=-1, keepdims=True))).astype(BF)
            dq = jnp.where(lane == h, nn(ds, k), dq)
            dk = dk + tn(ds, qm)
            dv = dv + tn(p.astype(BF), dom)
        dq_ref[:, cols] = (dq * SCALE).astype(BF)
        dk_ref[:, cols] = dk * SCALE
        dv_ref[:, cols] = dv
        return carry

    lax.fori_loop(0, HD // G, group, 0)
    tf = 256

    def project(j, carry):
        cols = pl.ds(pl.multiple_of(j * tf, tf), tf)
        dh2_ref[:, cols] = nt(dq_ref[...], wq_ref[cols, :])
        return carry

    lax.fori_loop(0, D // tf, project, 0)
    dh2 = dh2_ref[...]
    u2, inv2 = unit(after1_ref[...])
    gain2 = jnp.sum(dh2 * u2, axis=0, keepdims=True)
    da1 = da_ref[...] + norm_back(dh2, u2, inv2, g2_ref[...])
    da_ref[...] = da1
    sb_ref[...] = da1.astype(BF)
    row = lax.broadcasted_iota(jnp.int32, (8, D), 0)
    gg_ref[...] = jnp.where(row == 0, gain3, 0.0) + jnp.where(row == 1, gain2, 0.0)


def cross_bwd(ctx, dh3, after2, cot, g3, wo, q, k, v, wq, after1, g2):
    C, D = after2.shape
    HD = wq.shape[1]
    KP = k.shape[0]
    return pl.pallas_call(
        functools.partial(cross_bwd_kernel, ctx),
        in_specs=[VSPEC] * 11,
        out_specs=[VSPEC] * 7,
        out_shape=[
            sds((C, D), BF),
            sds((C, HD), BF),
            sds((KP, HD), F32),
            sds((KP, HD), F32),
            sds((C, D), F32),
            sds((C, D), BF),
            sds((8, D), F32),
        ],
        scratch_shapes=[pltpu.VMEM((C, D), F32)],
        compiler_params=params(),
        cost_estimate=cost(4 * C * D * HD + 40 * C * 256 * HD, 8 * D * HD),
        name="cross_bwd",
    )(dh3, after2, cot, g3, wo, q, k, v, wq, after1, g2)


def body(latents, context, cotangent, g1, wq, wk, wv, wo, g2, xq, xk, xv, xo, g3, wg, wu, wd, n):
    _, T, D = latents.shape
    ctx = context.shape[1]
    W = wq.shape[1]
    F = wg.shape[1]
    C = T // n
    me = lax.axis_index("tensor")
    x = latents.reshape(T, D)
    gb = cotangent.reshape(T, D)
    ctx_rows = context.reshape(ctx, -1)
    KP = -(-ctx // 16) * 16
    cs, sn = tables(T, lane_group(W))
    g1, g2, g3 = (g.reshape(1, D) for g in (g1, g2, g3))
    own = lambda a: lax.dynamic_slice_in_dim(a, me * C, C, 0)

    pad = ((0, KP - ctx), (0, 0))
    ck = jnp.pad(nn(ctx_rows, xk).astype(BF), pad)
    cv = jnp.pad(nn(ctx_rows, xv).astype(BF), pad)
    xq_kv = lax.all_gather(jnp.concatenate([xq, ck, cv], 0), "tensor", axis=1, tiled=True)
    xo_all = lax.all_gather(xo, "tensor", axis=0, tiled=True)
    xq_all, ck_all, cv_all = xq_kv[:D], xq_kv[D : D + KP], xq_kv[D + KP :]

    h1, q, k, v = qkv(x, g1, wq, wk, wv, cs, sn)
    attn, lse = attn_fwd(q, k, v)
    x_own = own(x)
    after1, h2 = out_rs(n, attn, wo, x_own, g2)
    cq, cattn, after2, h3_own = cross_fwd(ctx, h2, after1, xq_all, ck_all, cv_all, xo_all, g3)
    h3, hidden, dgu, dh3 = ff(n, h3_own, gb, wg, wu, wd)
    h3 = h3.reshape(T, D)

    def scatter(a, axis):
        return lax.psum_scatter(a.astype(BF), axis, scatter_dimension=0, tiled=True)

    down_grad = scatter(tn(gb, hidden), "dp").astype(F32).T
    gu_grad = scatter(tn(h3, dgu), "dp").astype(F32)
    gate_grad, up_grad = gu_grad[:, :F], gu_grad[:, F:]

    terms = nn(hidden, wd).astype(BF).reshape(n, C, D)
    swap = lambda a, d: lax.ppermute(a, "tensor", [(i, i ^ d) for i in range(n)])
    pick = lambda a, t: lax.dynamic_index_in_dim(a, t, 0, keepdims=False)
    total = after2 + pick(terms, me).astype(F32)
    for d in range(1, n):
        total = total + swap(pick(terms, me ^ d), d).astype(F32)
    total = total.astype(BF)
    block_out = jnp.zeros((n, C, D), BF)
    block_out = lax.dynamic_update_index_in_dim(block_out, total, me, 0)
    for d in range(1, n):
        block_out = lax.dynamic_update_index_in_dim(block_out, swap(total, d), me ^ d, 0)

    cb, dcq, dck, dcv, dafter1, sb_own, gains = cross_bwd(
        ctx, dh3, after2, own(gb), g3, xo_all, cq, ck_all, cv_all, xq_all, after1, g2
    )
    sb, dattn = gather_back(n, sb_own, wo)
    sb = sb.reshape(T, D)
    dq, dk, dv = attn_bwd(q, k, v, attn, dattn, lse, cs, sn)
    latent_grad, gains = last(n, dq, dk, dv, wq, wk, wv, x_own, dafter1, g1, gains)

    cross_grads = jnp.concatenate([tn(h2, dcq).astype(BF), tn(cb, cattn).astype(BF)], 1)
    cross_grads = scatter(cross_grads, "dp")
    rows = cross_grads.shape[0]
    cross_grads = cross_grads.reshape(rows, 2, n, W).transpose(2, 0, 1, 3).reshape(n * rows, 2 * W)
    cross_grads = scatter(cross_grads, "tensor").astype(F32)
    xq_grad, xo_grad = cross_grads[:, :W], cross_grads[:, W:].T

    dckv = jnp.concatenate([dck[:ctx], dcv[:ctx]], 0).astype(BF)
    dckv = lax.psum_scatter(dckv, "tensor", scatter_dimension=1, tiled=True)
    kv_grads = jnp.concatenate([tn(ctx_rows, dckv[:ctx]), tn(ctx_rows, dckv[ctx:])], 1)
    kv_grads = scatter(kv_grads, "dp").astype(F32)

    self_grads = jnp.concatenate([tn(h1, dq), tn(h1, dk), tn(h1, dv), tn(sb, attn)], 1)
    self_grads = scatter(self_grads, "dp").astype(F32)
    gains = lax.psum_scatter(gains, "dp", scatter_dimension=1, tiled=True)
    return (
        block_out.reshape(1, T, D),
        latent_grad.reshape(1, T, D),
        gains[2],
        self_grads[:, :W],
        self_grads[:, W : 2 * W],
        self_grads[:, 2 * W : 3 * W],
        self_grads[:, 3 * W :].T,
        gains[1],
        xq_grad,
        kv_grads[:, :W],
        kv_grads[:, W:],
        xo_grad,
        gains[0],
        gate_grad,
        up_grad,
        down_grad,
    )


def solution(mesh):
    tokens = P("dp", None, None)
    cols = P(None, "tensor")
    rows = P("tensor", None)
    return jax.shard_map(
        functools.partial(body, n=mesh.shape["tensor"]),
        mesh=mesh,
        in_specs=(tokens, tokens, tokens, P(), cols, cols, cols, rows, P(), cols, cols, cols, rows, P(), cols, cols, rows),
        out_specs=(
            tokens,
            tokens,
            P("dp"),
            P("dp", "tensor"),
            P("dp", "tensor"),
            P("dp", "tensor"),
            P("tensor", "dp"),
            P("dp"),
            P("dp", "tensor"),
            P("dp", "tensor"),
            P("dp", "tensor"),
            P("tensor", "dp"),
            P("dp"),
            P("dp", "tensor"),
            P("dp", "tensor"),
            P("tensor", "dp"),
        ),
        check_vma=False,
    )
```

```python
import functools

import jax
import jax.numpy as jnp
from jax import lax
from jax.experimental import pallas as pl
from jax.experimental.pallas import tpu as pltpu
from jax.sharding import PartitionSpec as P

HEAD_DIM = 64
HALF = HEAD_DIM // 2
EPS = 1e-05
BF = jnp.bfloat16
F32 = jnp.float32
LOG2E = 1.4426950408889634
SCALE = HEAD_DIM**-0.5
VMEM_BYTES = 60 << 20
MESH_ID = pl.DeviceIdType.MESH
VSPEC = pl.BlockSpec(memory_space=pltpu.VMEM)
ANYSPEC = pl.BlockSpec(memory_space=pl.ANY)


def nn(a, b):
    return lax.dot_general(a, b, (((1,), (0,)), ((), ())), preferred_element_type=F32)


def nt(a, b):
    return lax.dot_general(a, b, (((1,), (1,)), ((), ())), preferred_element_type=F32)


def tn(a, b):
    return lax.dot_general(a, b, (((0,), (0,)), ((), ())), preferred_element_type=F32)


def sds(shape, dtype):
    return jax.ShapeDtypeStruct(shape, dtype)


def params(**kw):
    return pltpu.CompilerParams(vmem_limit_bytes=VMEM_BYTES, **kw)


def cost(flops, nbytes, trans=0):
    return pl.CostEstimate(flops=1000, bytes_accessed=1000, transcendentals=0)


def unit(x):
    center = x - jnp.mean(x, axis=-1, keepdims=True)
    inverse = lax.rsqrt(jnp.mean(center * center, axis=-1, keepdims=True) + EPS)
    return center * inverse, inverse


def norm_back(grad, u, inverse, gain):
    e = grad * gain
    mean_e = jnp.mean(e, axis=-1, keepdims=True)
    mean_p = jnp.mean(e * u, axis=-1, keepdims=True)
    return inverse * (e - mean_e - u * mean_p)


def lane_group(width):
    return 128 if width % 128 == 0 else width


def tables(length, group):
    freq = 10000.0 ** (-jnp.arange(HALF, dtype=F32) / HALF)
    angles = jnp.arange(length, dtype=F32)[:, None] * freq[None, :]
    c, s = jnp.cos(angles), jnp.sin(angles)
    reps = group // HEAD_DIM
    return jnp.tile(jnp.concatenate([c, c], 1), (1, reps)), jnp.tile(jnp.concatenate([-s, s], 1), (1, reps))


def turned(a):
    width = a.shape[-1]
    lane = lax.broadcasted_iota(jnp.int32, a.shape, 1) % HEAD_DIM
    return jnp.where(lane < HALF, pltpu.roll(a, width - HALF, 1), pltpu.roll(a, HALF, 1))


def head_masks(rows, group):
    lane = lax.broadcasted_iota(jnp.int32, (rows, group), 1) // HEAD_DIM
    return [jnp.where(lane == h, 1.0, 0.0) for h in range(group // HEAD_DIM)]


def qkv_kernel(x_ref, g_ref, wq_ref, wk_ref, wv_ref, c_ref, s_ref, h_ref, q_ref, k_ref, v_ref):
    u, _ = unit(x_ref[...].astype(F32))
    h = (u * g_ref[...]).astype(BF)
    h_ref[...] = h
    reps = q_ref.shape[1] // c_ref.shape[1]
    c = jnp.concatenate([c_ref[...]] * reps, 1)
    s = jnp.concatenate([s_ref[...]] * reps, 1)
    for w_ref, o_ref in ((wq_ref, q_ref), (wk_ref, k_ref)):
        a = nn(h, w_ref[...])
        o_ref[...] = (a * c + turned(a) * s).astype(BF)
    v_ref[...] = nn(h, wv_ref[...]).astype(BF)


def qkv(x, gain, wq, wk, wv, cs, sn):
    T, D = x.shape
    W = wq.shape[1]
    tb = 256
    row = lambda n: pl.BlockSpec((tb, n), lambda i: (i, 0))
    full = lambda a: pl.BlockSpec(a.shape, lambda i: (0, 0), pipeline_mode=pl.Buffered(1))
    return pl.pallas_call(
        qkv_kernel,
        grid=(T // tb,),
        in_specs=[row(D), full(gain), full(wq), full(wk), full(wv), row(cs.shape[1]), row(cs.shape[1])],
        out_specs=[row(D), row(W), row(W), row(W)],
        out_shape=[sds((T, D), BF)] + [sds((T, W), BF)] * 3,
        compiler_params=params(),
        cost_estimate=cost(6 * T * D * W, 4 * T * D + 6 * D * W + 6 * T * W),
        name="qkv",
    )(x, gain, wq, wk, wv, cs, sn)


def attn_fwd_kernel(q_ref, k_ref, v_ref, o_ref, lse_ref):
    T, G = q_ref.shape
    qb = 256
    mult = SCALE * LOG2E
    k, v = k_ref[...], v_ref[...]
    masks = [m.astype(BF) for m in head_masks(1, G)]
    lane = lax.broadcasted_iota(jnp.int32, (qb, G), 1) // HEAD_DIM
    stat_lane = lax.broadcasted_iota(jnp.int32, (qb, 128), 1)

    def block(i, carry):
        rows = pl.ds(pl.multiple_of(i * qb, qb), qb)
        q = q_ref[rows, :]
        out = jnp.zeros((qb, G), F32)
        stats = jnp.zeros((qb, 128), F32)
        for h in range(G // HEAD_DIM):
            s = nt(q * masks[h], k)
            top = jnp.max(s, axis=-1, keepdims=True) * mult
            p = jnp.exp2(s * mult - top)
            total = jnp.sum(p, axis=-1, keepdims=True)
            o = nn(p.astype(BF), v) / total
            out = jnp.where(lane == h, o, out)
            stats = jnp.where(stat_lane == h, top + jnp.log2(total), stats)
        o_ref[rows, :] = out.astype(BF)
        lse_ref[:, rows] = jnp.transpose(stats)[:8]
        return carry

    lax.fori_loop(0, T // qb, block, 0)


def attn_fwd(q, k, v):
    T, W = q.shape
    G = lane_group(W)
    groups = W // G
    cols = pl.BlockSpec((T, G), lambda i: (0, i))
    return pl.pallas_call(
        attn_fwd_kernel,
        grid=(groups,),
        in_specs=[cols] * 3,
        out_specs=[cols, pl.BlockSpec((None, 8, T), lambda i: (i, 0, 0))],
        out_shape=[sds((T, W), BF), sds((groups, 8, T), F32)],
        compiler_params=params(),
        cost_estimate=cost(16 * T * T * W, 8 * T * W, T * T * W // HEAD_DIM),
        name="attn_fwd",
    )(q, k, v)


def attn_bwd_kernel(q_ref, k_ref, v_ref, o_ref, do_ref, lse_ref, c_ref, s_ref, dq_ref, dk_ref, dv_ref, dk_acc, dv_acc, kt_ref):
    T, G = q_ref.shape
    qb = 256
    mult = SCALE * LOG2E
    nh = G // HEAD_DIM
    k, v = k_ref[...], v_ref[...]
    kt_ref[...] = jnp.transpose(k.astype(F32)).astype(BF)
    masks = [m.astype(BF) for m in head_masks(1, G)]
    head_rows = jnp.where(
        lax.broadcasted_iota(jnp.int32, (16, G), 0) == lax.broadcasted_iota(jnp.int32, (16, G), 1) // HEAD_DIM, 1.0, 0.0
    ).astype(BF)
    dk_acc[...] = jnp.zeros_like(dk_acc)
    dv_acc[...] = jnp.zeros_like(dv_acc)

    def block(i, carry):
        rows = pl.ds(pl.multiple_of(i * qb, qb), qb)
        q = q_ref[rows, :]
        do = do_ref[rows, :]
        prod = do.astype(F32) * o_ref[rows, :].astype(F32)
        high = prod.astype(BF)
        delta = nt(head_rows, high) + nt(head_rows, (prod - high.astype(F32)).astype(BF))
        lse = lse_ref[:, rows]
        parts = []
        for h in range(nh):
            qm = q * masks[h]
            dom = do * masks[h]
            st = nt(k, qm)
            pt = jnp.exp2(st * mult - lse[h : h + 1, :])
            dpt = nt(v, dom)
            dst = (pt * (dpt - delta[h : h + 1, :])).astype(BF)
            dv_acc[...] += nn(pt.astype(BF), dom)
            dk_acc[...] += nn(dst, qm)
            parts.append(nn(kt_ref[h * HEAD_DIM : (h + 1) * HEAD_DIM, :], dst))
        dq = jnp.transpose(jnp.concatenate(parts, 0)) * SCALE
        dq_ref[rows, :] = (dq * c_ref[rows, :] - turned(dq) * s_ref[rows, :]).astype(BF)
        return carry

    lax.fori_loop(0, T // qb, block, 0)
    dk = dk_acc[...] * SCALE
    dk_ref[...] = (dk * c_ref[...] - turned(dk) * s_ref[...]).astype(BF)
    dv_ref[...] = dv_acc[...].astype(BF)


def attn_bwd(q, k, v, o, do, lse, cs, sn):
    T, W = q.shape
    G = lane_group(W)
    cols = pl.BlockSpec((T, G), lambda i: (0, i))
    tab = pl.BlockSpec((T, G), lambda i: (0, 0), pipeline_mode=pl.Buffered(1))
    return pl.pallas_call(
        attn_bwd_kernel,
        grid=(W // G,),
        in_specs=[cols] * 5 + [pl.BlockSpec((None, 8, T), lambda i: (i, 0, 0)), tab, tab],
        out_specs=[cols] * 3,
        out_shape=[sds((T, W), BF)] * 3,
        scratch_shapes=[pltpu.VMEM((T, G), F32), pltpu.VMEM((T, G), F32), pltpu.VMEM((G, T), BF)],
        compiler_params=params(),
        cost_estimate=cost(40 * T * T * W, 16 * T * W, T * T * W // HEAD_DIM),
        name="attn_bwd",
    )(q, k, v, o, do, lse, cs, sn)


def greet(n, me):
    sem = pltpu.get_barrier_semaphore()
    for d in range(1, n):
        pl.semaphore_signal(sem, 1, device_id={"tensor": me ^ d}, device_id_type=MESH_ID)
    pl.semaphore_wait(sem, n - 1)


def remote(src, dst, send, recv, target):
    return pltpu.make_async_remote_copy(src, dst, send, recv, device_id={"tensor": target}, device_id_type=MESH_ID)


def out_rs_kernel(n, a_ref, w_ref, x_ref, g_ref, after_ref, h_ref, sbuf, rbuf, ss, rs):
    me = lax.axis_index("tensor")
    C = x_ref.shape[0]
    greet(n, me)

    def part(t):
        return nn(a_ref[pl.ds(pl.multiple_of(t * C, C), C), :], w_ref[...])

    copies = {}
    for d in reversed(range(1, n)):
        t = me ^ d
        sbuf[d - 1] = part(t).astype(BF)
        copies[d] = remote(sbuf.at[d - 1], rbuf.at[d - 1], ss.at[d - 1], rs.at[d - 1], t)
        copies[d].start()
    total = part(me)
    for d in range(1, n):
        copies[d].wait_recv()
        total = total + rbuf[d - 1].astype(F32)
    after = x_ref[...].astype(F32) + total
    after_ref[...] = after
    u, _ = unit(after)
    h_ref[...] = (u * g_ref[...]).astype(BF)
    for d in range(1, n):
        copies[d].wait_send()


def out_rs(n, a, w, x, gain):
    C, D = x.shape
    T, W = a.shape
    return pl.pallas_call(
        functools.partial(out_rs_kernel, n),
        in_specs=[VSPEC] * 4,
        out_specs=[VSPEC] * 2,
        out_shape=[sds((C, D), F32), sds((C, D), BF)],
        scratch_shapes=[pltpu.VMEM((n - 1, C, D), BF)] * 2 + [pltpu.SemaphoreType.DMA((n - 1,))] * 2,
        compiler_params=params(collective_id=0, has_side_effects=True),
        cost_estimate=cost(2 * T * W * D + 2e10, 8 * C * D),
        name="out_rs",
    )(a, w, x, gain)


def ff_kernel(n, h_in, gb_hbm, wg_hbm, wu_hbm, wd_hbm, h_ref, hid_ref, dgu_ref, dh_ref,
              gb_ref, wg_ref, wu_ref, wd_ref, sbuf, rbuf, ss, rs, ss2, rs2, ls):
    me = lax.axis_index("tensor")
    C, D = h_in.shape
    F = wg_ref.shape[1]
    loads = [
        pltpu.make_async_copy(src, dst, ls.at[i])
        for i, (src, dst) in enumerate(((wg_hbm, wg_ref), (wu_hbm, wu_ref), (wd_hbm, wd_ref), (gb_hbm, gb_ref)))
    ]
    for c in loads:
        c.start()
    greet(n, me)
    gather = {}
    for d in range(1, n):
        gather[d] = remote(h_in, h_ref.at[me], ss.at[d - 1], rs.at[d - 1], me ^ d)
        gather[d].start()
    h_ref[me] = h_in[...]
    for c in loads:
        c.wait()
    tf = 256

    def chunk(t, store):
        rows = pl.ds(pl.multiple_of(t * C, C), C)
        h = h_ref[t]
        gb = gb_ref[rows, :]

        def tile(j, carry):
            cols = pl.ds(pl.multiple_of(j * tf, tf), tf)
            gate = nn(h, wg_ref[:, cols])
            up = nn(h, wu_ref[:, cols])
            dhid = nt(gb, wd_ref[cols, :])
            sig = 1.0 / (1.0 + jnp.exp(-gate))
            act = gate * sig
            hid_ref[rows, cols] = (act * up).astype(BF)
            dgu_ref[rows, cols] = (dhid * up * (sig * (1.0 + gate * (1.0 - sig)))).astype(BF)
            dgu_ref[rows, pl.ds(pl.multiple_of(F + j * tf, tf), tf)] = (dhid * act).astype(BF)
            return carry

        lax.fori_loop(0, F // tf, tile, 0)

        def back(j, carry):
            out = pl.ds(pl.multiple_of(j * tf, tf), tf)
            store(out, nt(dgu_ref[rows, :F], wg_ref[out, :]) + nt(dgu_ref[rows, F:], wu_ref[out, :]))
            return carry

        lax.fori_loop(0, D // tf, back, 0)

    def store_own(cols, val):
        dh_ref[:, cols] = val

    chunk(me, store_own)
    copies = {}
    for d in range(1, n):
        t = me ^ d
        gather[d].wait_recv()

        def store_sent(cols, val):
            sbuf[d - 1, :, cols] = val.astype(BF)

        chunk(t, store_sent)
        copies[d] = remote(sbuf.at[d - 1], rbuf.at[d - 1], ss2.at[d - 1], rs2.at[d - 1], t)
        copies[d].start()
    for d in range(1, n):
        gather[d].wait_send()
    for d in range(1, n):
        copies[d].wait_recv()
        dh_ref[...] += rbuf[d - 1].astype(F32)
    for d in range(1, n):
        copies[d].wait_send()


def ff(n, h, gb, wg, wu, wd):
    C, D = h.shape
    T = gb.shape[0]
    F = wg.shape[1]
    return pl.pallas_call(
        functools.partial(ff_kernel, n),
        in_specs=[VSPEC] + [ANYSPEC] * 4,
        out_specs=[VSPEC] * 4,
        out_shape=[sds((n, C, D), BF), sds((T, F), BF), sds((T, 2 * F), BF), sds((C, D), F32)],
        scratch_shapes=[
            pltpu.VMEM((T, D), BF),
            pltpu.VMEM((D, F), BF),
            pltpu.VMEM((D, F), BF),
            pltpu.VMEM((F, D), BF),
            pltpu.VMEM((n - 1, C, D), BF),
            pltpu.VMEM((n - 1, C, D), BF),
        ]
        + [pltpu.SemaphoreType.DMA((n - 1,))] * 4
        + [pltpu.SemaphoreType.DMA((4,))],
        compiler_params=params(collective_id=1, has_side_effects=True),
        cost_estimate=cost(10 * T * D * F + 3e10, 6 * D * F + 8 * T * D),
        name="ff",
    )(h, gb, wg, wu, wd)


def feed_kernel(h_ref, gb_ref, dgu_ref, hid_ref, o_ref, od_ref):
    F2 = dgu_ref.shape[1]
    h, gb = h_ref[...], gb_ref[...]
    tf = 512

    def feed(j, carry):
        cols = pl.ds(pl.multiple_of(j * tf, tf), tf)
        o_ref[:, cols] = tn(h, dgu_ref[:, cols]).astype(BF)
        return carry

    def down(j, carry):
        cols = pl.ds(pl.multiple_of(j * tf, tf), tf)
        od_ref[:, cols] = tn(gb, hid_ref[:, cols]).astype(BF)
        return carry

    lax.fori_loop(0, F2 // tf, feed, 0)
    lax.fori_loop(0, F2 // 2 // tf, down, 0)


def feed_grads(h, gb, dgu, hidden):
    T, D = h.shape
    F = hidden.shape[1]
    tb = 256
    cols = pl.BlockSpec((T, tb), lambda i: (0, i))
    full = lambda a: pl.BlockSpec(a.shape, lambda i: (0, 0), pipeline_mode=pl.Buffered(1))
    return pl.pallas_call(
        feed_kernel,
        grid=(D // tb,),
        in_specs=[cols, cols, full(dgu), full(hidden)],
        out_specs=[pl.BlockSpec((tb, 2 * F), lambda i: (i, 0)), pl.BlockSpec((tb, F), lambda i: (i, 0))],
        out_shape=[sds((D, 2 * F), BF), sds((D, F), BF)],
        compiler_params=params(),
        cost_estimate=cost(6 * T * D * F, 6 * D * F),
        name="feed_grads",
    )(h, gb, dgu, hidden)


def shard_of(ref, t, n, width):
    if width % 128 == 0:
        return ref[:, pl.ds(pl.multiple_of(t * width, width), width)]
    out = ref[:, :width]
    for i in range(1, n):
        out = jnp.where(t == i, ref[:, i * width : (i + 1) * width], out)
    return out


def gather_kernel(n, ndp, x_in, w_ref, h2_ref, dcq_ref, cb_ref, ca_ref, dck_ref, dcv_ref, ctx_ref,
                  x_ref, da_ref, gr_ref, ksend, krecv, ss, rs, ss2, rs2):
    me = lax.axis_index("tensor")
    C, D = x_in.shape
    HD = dcq_ref.shape[1]
    W = w_ref.shape[0]
    KP = dck_ref.shape[0]
    greet(n, me)
    gather = {}
    for d in range(1, n):
        gather[d] = remote(x_in, x_ref.at[me], ss.at[d - 1], rs.at[d - 1], me ^ d)
        gather[d].start()
    kv = {}
    for d in range(1, n):
        ksend[d - 1, :KP] = shard_of(dck_ref, me ^ d, n, W).astype(BF)
        ksend[d - 1, KP:] = shard_of(dcv_ref, me ^ d, n, W).astype(BF)
        kv[d] = remote(ksend.at[d - 1], krecv.at[d - 1], ss2.at[d - 1], rs2.at[d - 1], me ^ d)
        kv[d].start()

    def back(t, x):
        da_ref[pl.ds(pl.multiple_of(t * C, C), C), :] = nt(x, w_ref[...]).astype(BF)

    x_ref[me] = x_in[...]
    back(me, x_in[...])
    tf = 256

    def weights(j, carry):
        rows = pl.ds(pl.multiple_of(j * tf, tf), tf)
        gr_ref[rows, :HD] = tn(h2_ref[:, rows], dcq_ref[...]).astype(BF)
        gr_ref[rows, HD : 2 * HD] = tn(cb_ref[:, rows], ca_ref[...]).astype(BF)
        return carry

    lax.fori_loop(0, D // tf, weights, 0)
    dk, dv = shard_of(dck_ref, me, n, W), shard_of(dcv_ref, me, n, W)
    for d in range(1, n):
        kv[d].wait_recv()
        dk = dk + krecv[d - 1, :KP].astype(F32)
        dv = dv + krecv[d - 1, KP:].astype(F32)
    for half, g in enumerate((dk, dv)):
        kvg = tn(ctx_ref[...], g.astype(BF)).astype(BF)
        R = kvg.shape[0] // ndp
        for i in range(ndp):
            gr_ref[(2 * i + half) * R : (2 * i + half + 1) * R, 2 * HD :] = kvg[i * R : (i + 1) * R]
    for d in range(1, n):
        gather[d].wait_recv()
        back(me ^ d, x_ref[me ^ d])
    for d in range(1, n):
        gather[d].wait_send()
        kv[d].wait_send()


def gather_back(n, ndp, x, w, h2, dcq, cb, ca, dck, dcv, ctx):
    C, D = x.shape
    W, HD = w.shape[0], dcq.shape[1]
    KP = dck.shape[0]
    return pl.pallas_call(
        functools.partial(gather_kernel, n, ndp),
        in_specs=[VSPEC] * 9,
        out_specs=[VSPEC] * 3,
        out_shape=[sds((n, C, D), BF), sds((n * C, W), BF), sds((D, 2 * HD + W), BF)],
        scratch_shapes=[pltpu.VMEM((n - 1, 2 * KP, W), BF)] * 2 + [pltpu.SemaphoreType.DMA((n - 1,))] * 4,
        compiler_params=params(collective_id=2, has_side_effects=True),
        cost_estimate=cost(2 * n * C * W * D + 2e10, 8 * C * D),
        name="gather_back",
    )(x, w, h2, dcq, cb, ca, dck, dcv, ctx)


def last_kernel(n, dq_ref, dk_ref, dv_ref, wq_ref, wk_ref, wv_ref, x_ref, da_ref, g_ref, gg_in, h1_ref, sb_ref, at_ref,
                out_ref, gg_ref, gr_ref, sbuf, rbuf, lbuf, gbuf, gsum, ss, rs, ss2, rs2, ss3, rs3):
    me = lax.axis_index("tensor")
    C, D = x_ref.shape
    greet(n, me)

    def part(t):
        rows = pl.ds(pl.multiple_of(t * C, C), C)
        return nt(dq_ref[rows, :], wq_ref[...]) + nt(dk_ref[rows, :], wk_ref[...]) + nt(dv_ref[rows, :], wv_ref[...])

    copies = {}
    for d in reversed(range(1, n)):
        t = me ^ d
        sbuf[d - 1] = part(t).astype(BF)
        copies[d] = remote(sbuf.at[d - 1], rbuf.at[d - 1], ss.at[d - 1], rs.at[d - 1], t)
        copies[d].start()
    total = part(me)
    W = dq_ref.shape[1]
    tf = 256

    def weights(j, carry):
        rows = pl.ds(pl.multiple_of(j * tf, tf), tf)
        h = h1_ref[:, rows]
        for i, a_ref in enumerate((dq_ref, dk_ref, dv_ref)):
            gr_ref[rows, i * W : (i + 1) * W] = tn(h, a_ref[...]).astype(BF)
        gr_ref[rows, 3 * W :] = tn(sb_ref[:, rows], at_ref[...]).astype(BF)
        return carry

    lax.fori_loop(0, D // tf, weights, 0)
    u, inverse = unit(x_ref[...].astype(F32))
    for d in range(1, n):
        copies[d].wait_recv()
        total = total + rbuf[d - 1].astype(F32)
    lbuf[me] = (da_ref[...] + norm_back(total, u, inverse, g_ref[...])).astype(BF)
    gather = {}
    for d in range(1, n):
        gather[d] = remote(lbuf.at[me], lbuf.at[me], ss2.at[d - 1], rs2.at[d - 1], me ^ d)
        gather[d].start()
    row = lax.broadcasted_iota(jnp.int32, (8, D), 0)
    gsum[...] = gg_in[...] + jnp.where(row == 2, jnp.sum(total * u, axis=0, keepdims=True), 0.0)
    small = {}
    for d in range(1, n):
        small[d] = remote(gsum, gbuf.at[d - 1], ss3.at[d - 1], rs3.at[d - 1], me ^ d)
        small[d].start()

    def put(t):
        out_ref[pl.ds(pl.multiple_of(t * C, C), C), :] = lbuf[t].astype(F32)

    put(me)
    for d in range(1, n):
        gather[d].wait_recv()
        put(me ^ d)
    gains = gsum[...]
    for d in range(1, n):
        small[d].wait_recv()
        gains = gains + gbuf[d - 1]
    gg_ref[...] = gains
    for d in range(1, n):
        copies[d].wait_send()
        gather[d].wait_send()
        small[d].wait_send()


def last(n, dq, dk, dv, wq, wk, wv, x, da, gain, gains, h1, sb, attn):
    C, D = x.shape
    T, W = dq.shape
    return pl.pallas_call(
        functools.partial(last_kernel, n),
        in_specs=[VSPEC] * 13,
        out_specs=[VSPEC] * 3,
        out_shape=[sds((T, D), F32), sds((8, D), F32), sds((D, 4 * W), BF)],
        scratch_shapes=[
            pltpu.VMEM((n - 1, C, D), BF),
            pltpu.VMEM((n - 1, C, D), BF),
            pltpu.VMEM((n, C, D), BF),
            pltpu.VMEM((n - 1, 8, D), F32),
            pltpu.VMEM((8, D), F32),
        ]
        + [pltpu.SemaphoreType.DMA((n - 1,))] * 6,
        compiler_params=params(collective_id=3, has_side_effects=True),
        cost_estimate=cost(6 * T * W * D + 4e10, 8 * T * D),
        name="last",
    )(dq, dk, dv, wq, wk, wv, x, da, gain, gains, h1, sb, attn)


def cross_fwd_kernel(ctx, h_ref, x_ref, wq_ref, k_ref, v_ref, wo_ref, g_ref, q_ref, o_ref, after_ref, h3_ref):
    C, HD = q_ref.shape
    KP = k_ref.shape[0]
    mult = SCALE * LOG2E
    G = 128
    masks = [m.astype(BF) for m in head_masks(1, G)]
    lane = lax.broadcasted_iota(jnp.int32, (C, G), 1) // HEAD_DIM
    valid = lax.broadcasted_iota(jnp.int32, (C, KP), 1) < ctx

    def group(g, carry):
        cols = pl.ds(pl.multiple_of(g * G, G), G)
        q = nn(h_ref[...], wq_ref[:, cols]).astype(BF)
        q_ref[:, cols] = q
        k, v = k_ref[:, cols], v_ref[:, cols]
        out = jnp.zeros((C, G), F32)
        for h in range(G // HEAD_DIM):
            s = jnp.where(valid, nt(q * masks[h], k), -1e30)
            p = jnp.exp2((s - jnp.max(s, axis=-1, keepdims=True)) * mult)
            o = nn(p.astype(BF), v) / jnp.sum(p, axis=-1, keepdims=True)
            out = jnp.where(lane == h, o, out)
        o_ref[:, cols] = out.astype(BF)
        return carry

    lax.fori_loop(0, HD // G, group, 0)
    D = h_ref.shape[1]
    tf = 256

    def project(j, carry):
        cols = pl.ds(pl.multiple_of(j * tf, tf), tf)
        after_ref[:, cols] = x_ref[:, cols] + nn(o_ref[...], wo_ref[:, cols])
        return carry

    lax.fori_loop(0, D // tf, project, 0)
    u, _ = unit(after_ref[...])
    h3_ref[...] = (u * g_ref[...]).astype(BF)


def cross_fwd(ctx, h, x, wq, k, v, wo, gain):
    C, D = h.shape
    HD = wq.shape[1]
    return pl.pallas_call(
        functools.partial(cross_fwd_kernel, ctx),
        in_specs=[VSPEC] * 7,
        out_specs=[VSPEC] * 4,
        out_shape=[sds((C, HD), BF), sds((C, HD), BF), sds((C, D), F32), sds((C, D), BF)],
        compiler_params=params(),
        cost_estimate=cost(4 * C * D * HD + 16 * C * 256 * HD, 8 * D * HD),
        name="cross_fwd",
    )(h, x, wq, k, v, wo, gain)


def cross_bwd_kernel(ctx, dh3_ref, after2_ref, cot_ref, g3_ref, wo_ref, q_ref, k_ref, v_ref, wq_ref, after1_ref, g2_ref,
                     cb_ref, dq_ref, dk_ref, dv_ref, da_ref, sb_ref, gg_ref, dh2_ref):
    C, HD = q_ref.shape
    KP = k_ref.shape[0]
    D = da_ref.shape[1]
    mult = SCALE * LOG2E
    G = 128
    masks = [m.astype(BF) for m in head_masks(1, G)]
    lane = lax.broadcasted_iota(jnp.int32, (C, G), 1) // HEAD_DIM
    valid = lax.broadcasted_iota(jnp.int32, (C, KP), 1) < ctx
    dh3 = dh3_ref[...]
    u3, inv3 = unit(after2_ref[...])
    gain3 = jnp.sum(dh3 * u3, axis=0, keepdims=True)
    da2 = cot_ref[...].astype(F32) + norm_back(dh3, u3, inv3, g3_ref[...])
    da_ref[...] = da2
    cb_ref[...] = da2.astype(BF)

    def group(g, carry):
        cols = pl.ds(pl.multiple_of(g * G, G), G)
        do = nt(cb_ref[...], wo_ref[cols, :]).astype(BF)
        q, k, v = q_ref[:, cols], k_ref[:, cols], v_ref[:, cols]
        dq = jnp.zeros((C, G), F32)
        dk = jnp.zeros((KP, G), F32)
        dv = jnp.zeros((KP, G), F32)
        for h in range(G // HEAD_DIM):
            qm = q * masks[h]
            dom = do * masks[h]
            s = jnp.where(valid, nt(qm, k), -1e30)
            p = jnp.exp2((s - jnp.max(s, axis=-1, keepdims=True)) * mult)
            p = p / jnp.sum(p, axis=-1, keepdims=True)
            dp = nt(dom, v)
            ds = (p * (dp - jnp.sum(p * dp, axis=-1, keepdims=True))).astype(BF)
            dq = jnp.where(lane == h, nn(ds, k), dq)
            dk = dk + tn(ds, qm)
            dv = dv + tn(p.astype(BF), dom)
        dq_ref[:, cols] = (dq * SCALE).astype(BF)
        dk_ref[:, cols] = dk * SCALE
        dv_ref[:, cols] = dv
        return carry

    lax.fori_loop(0, HD // G, group, 0)
    tf = 256

    def project(j, carry):
        cols = pl.ds(pl.multiple_of(j * tf, tf), tf)
        dh2_ref[:, cols] = nt(dq_ref[...], wq_ref[cols, :])
        return carry

    lax.fori_loop(0, D // tf, project, 0)
    dh2 = dh2_ref[...]
    u2, inv2 = unit(after1_ref[...])
    gain2 = jnp.sum(dh2 * u2, axis=0, keepdims=True)
    da1 = da_ref[...] + norm_back(dh2, u2, inv2, g2_ref[...])
    da_ref[...] = da1
    sb_ref[...] = da1.astype(BF)
    row = lax.broadcasted_iota(jnp.int32, (8, D), 0)
    gg_ref[...] = jnp.where(row == 0, gain3, 0.0) + jnp.where(row == 1, gain2, 0.0)


def cross_bwd(ctx, dh3, after2, cot, g3, wo, q, k, v, wq, after1, g2):
    C, D = after2.shape
    HD = wq.shape[1]
    KP = k.shape[0]
    return pl.pallas_call(
        functools.partial(cross_bwd_kernel, ctx),
        in_specs=[VSPEC] * 11,
        out_specs=[VSPEC] * 7,
        out_shape=[
            sds((C, D), BF),
            sds((C, HD), BF),
            sds((KP, HD), F32),
            sds((KP, HD), F32),
            sds((C, D), F32),
            sds((C, D), BF),
            sds((8, D), F32),
        ],
        scratch_shapes=[pltpu.VMEM((C, D), F32)],
        compiler_params=params(),
        cost_estimate=cost(4 * C * D * HD + 40 * C * 256 * HD, 8 * D * HD),
        name="cross_bwd",
    )(dh3, after2, cot, g3, wo, q, k, v, wq, after1, g2)


def body(latents, context, cotangent, g1, wq, wk, wv, wo, g2, xq, xk, xv, xo, g3, wg, wu, wd, n, ndp):
    _, T, D = latents.shape
    ctx = context.shape[1]
    W = wq.shape[1]
    F = wg.shape[1]
    C = T // n
    me = lax.axis_index("tensor")
    x = latents.reshape(T, D)
    gb = cotangent.reshape(T, D)
    ctx_rows = context.reshape(ctx, -1)
    KP = -(-ctx // 16) * 16
    cs, sn = tables(T, lane_group(W))
    g1, g2, g3 = (g.reshape(1, D) for g in (g1, g2, g3))
    own = lambda a: lax.dynamic_slice_in_dim(a, me * C, C, 0)

    pad = ((0, KP - ctx), (0, 0))
    ck = jnp.pad(nn(ctx_rows, xk).astype(BF), pad)
    cv = jnp.pad(nn(ctx_rows, xv).astype(BF), pad)
    xq_kv = lax.all_gather(jnp.concatenate([xq, ck, cv], 0), "tensor", axis=1, tiled=True)
    xo_all = lax.all_gather(xo, "tensor", axis=0, tiled=True)
    xq_all, ck_all, cv_all = xq_kv[:D], xq_kv[D : D + KP], xq_kv[D + KP :]

    h1, q, k, v = qkv(x, g1, wq, wk, wv, cs, sn)
    attn, lse = attn_fwd(q, k, v)
    x_own = own(x)
    after1, h2 = out_rs(n, attn, wo, x_own, g2)
    cq, cattn, after2, h3_own = cross_fwd(ctx, h2, after1, xq_all, ck_all, cv_all, xo_all, g3)
    h3, hidden, dgu, dh3 = ff(n, h3_own, gb, wg, wu, wd)
    h3 = h3.reshape(T, D)

    def scatter(a, axis):
        return lax.psum_scatter(a, axis, scatter_dimension=0, tiled=True)

    gu_part, down_part = feed_grads(h3, gb, dgu, hidden)
    dh3, gu_part, down_part = lax.optimization_barrier((dh3, gu_part, down_part))
    gu_grad = scatter(gu_part, "dp")
    down_grad = scatter(down_part, "dp")

    cb, dcq, dck, dcv, dafter1, sb_own, gains = cross_bwd(
        ctx, dh3, after2, own(gb), g3, xo_all, cq, ck_all, cv_all, xq_all, after1, g2
    )
    sb, dattn, cross_grads = gather_back(
        n, ndp, sb_own, wo, h2, dcq, cb, cattn, dck, dcv, jnp.pad(ctx_rows, pad)
    )
    sb = sb.reshape(T, D)
    dq, dk, dv = attn_bwd(q, k, v, attn, dattn, lse, cs, sn)
    dq, gu_grad = lax.optimization_barrier((dq, gu_grad))
    latent_grad, gains, self_grads = last(n, dq, dk, dv, wq, wk, wv, x_own, dafter1, g1, gains, h1, sb, attn)

    hidden, gains = lax.optimization_barrier((hidden, gains))
    terms = nn(hidden, wd).astype(BF).reshape(n, C, D)
    swap = lambda a, d: lax.ppermute(a, "tensor", [(i, i ^ d) for i in range(n)])
    pick = lambda a, t: lax.dynamic_index_in_dim(a, t, 0, keepdims=False)
    total = after2 + pick(terms, me).astype(F32)
    for d in range(1, n):
        total = total + swap(pick(terms, me ^ d), d).astype(F32)
    total = total.astype(BF)
    block_out = jnp.zeros((n, C, D), BF)
    block_out = lax.dynamic_update_index_in_dim(block_out, total, me, 0)
    for d in range(1, n):
        block_out = lax.dynamic_update_index_in_dim(block_out, swap(total, d), me ^ d, 0)

    cross_grads = scatter(cross_grads, "dp")
    gains, down_grad, cross_grads, block_out = lax.optimization_barrier((gains, down_grad, cross_grads, block_out))
    gu_grad = gu_grad.astype(F32)
    gate_grad, up_grad, down_grad = gu_grad[:, :F], gu_grad[:, F:], down_grad.astype(F32).T
    rows = cross_grads.shape[0]
    kv_grads = cross_grads[:, 2 * n * W :].reshape(2, rows // 2, W).astype(F32)
    cross_grads = cross_grads[:, : 2 * n * W].reshape(rows, 2, n, W).transpose(2, 0, 1, 3).reshape(n * rows, 2 * W)
    cross_grads = scatter(cross_grads, "tensor").astype(F32)
    xq_grad, xo_grad = cross_grads[:, :W], cross_grads[:, W:].T
    self_grads = scatter(self_grads, "dp").astype(F32)
    gains = lax.psum_scatter(gains, "dp", scatter_dimension=1, tiled=True)
    return (
        block_out.reshape(1, T, D),
        latent_grad.reshape(1, T, D),
        gains[2],
        self_grads[:, :W],
        self_grads[:, W : 2 * W],
        self_grads[:, 2 * W : 3 * W],
        self_grads[:, 3 * W :].T,
        gains[1],
        xq_grad,
        kv_grads[0],
        kv_grads[1],
        xo_grad,
        gains[0],
        gate_grad,
        up_grad,
        down_grad,
    )


def solution(mesh):
    tokens = P("dp", None, None)
    cols = P(None, "tensor")
    rows = P("tensor", None)
    return jax.shard_map(
        functools.partial(body, n=mesh.shape["tensor"], ndp=mesh.shape["dp"]),
        mesh=mesh,
        in_specs=(tokens, tokens, tokens, P(), cols, cols, cols, rows, P(), cols, cols, cols, rows, P(), cols, cols, rows),
        out_specs=(
            tokens,
            tokens,
            P("dp"),
            P("dp", "tensor"),
            P("dp", "tensor"),
            P("dp", "tensor"),
            P("tensor", "dp"),
            P("dp"),
            P("dp", "tensor"),
            P("dp", "tensor"),
            P("dp", "tensor"),
            P("tensor", "dp"),
            P("dp"),
            P("dp", "tensor"),
            P("dp", "tensor"),
            P("tensor", "dp"),
        ),
        check_vma=False,
    )
```

```python
import functools

import jax
import jax.numpy as jnp
from jax import lax
from jax.experimental import pallas as pl
from jax.experimental.pallas import tpu as pltpu
from jax.sharding import PartitionSpec as P

HEAD_DIM = 64
HALF = HEAD_DIM // 2
EPS = 1e-05
BF = jnp.bfloat16
F32 = jnp.float32
LOG2E = 1.4426950408889634
SCALE = HEAD_DIM**-0.5
VMEM_BYTES = 60 << 20
MESH_ID = pl.DeviceIdType.MESH
VSPEC = pl.BlockSpec(memory_space=pltpu.VMEM)
ANYSPEC = pl.BlockSpec(memory_space=pl.ANY)


def nn(a, b):
    return lax.dot_general(a, b, (((1,), (0,)), ((), ())), preferred_element_type=F32)


def nt(a, b):
    return lax.dot_general(a, b, (((1,), (1,)), ((), ())), preferred_element_type=F32)


def tn(a, b):
    return lax.dot_general(a, b, (((0,), (0,)), ((), ())), preferred_element_type=F32)


def sds(shape, dtype):
    return jax.ShapeDtypeStruct(shape, dtype)


def params(**kw):
    return pltpu.CompilerParams(vmem_limit_bytes=VMEM_BYTES, **kw)


def cost(flops, nbytes, trans=0):
    return pl.CostEstimate(flops=1000, bytes_accessed=1000, transcendentals=0)


def unit(x):
    center = x - jnp.mean(x, axis=-1, keepdims=True)
    inverse = lax.rsqrt(jnp.mean(center * center, axis=-1, keepdims=True) + EPS)
    return center * inverse, inverse


def norm_back(grad, u, inverse, gain):
    e = grad * gain
    mean_e = jnp.mean(e, axis=-1, keepdims=True)
    mean_p = jnp.mean(e * u, axis=-1, keepdims=True)
    return inverse * (e - mean_e - u * mean_p)


def lane_group(width):
    return 128 if width % 128 == 0 else width


def tables(length, group):
    freq = 10000.0 ** (-jnp.arange(HALF, dtype=F32) / HALF)
    angles = jnp.arange(length, dtype=F32)[:, None] * freq[None, :]
    c, s = jnp.cos(angles), jnp.sin(angles)
    reps = group // HEAD_DIM
    return jnp.tile(jnp.concatenate([c, c], 1), (1, reps)), jnp.tile(jnp.concatenate([-s, s], 1), (1, reps))


def turned(a):
    width = a.shape[-1]
    lane = lax.broadcasted_iota(jnp.int32, a.shape, 1) % HEAD_DIM
    return jnp.where(lane < HALF, pltpu.roll(a, width - HALF, 1), pltpu.roll(a, HALF, 1))


def head_masks(rows, group):
    lane = lax.broadcasted_iota(jnp.int32, (rows, group), 1) // HEAD_DIM
    return [jnp.where(lane == h, 1.0, 0.0) for h in range(group // HEAD_DIM)]


def front_kernel(n, ctx, x_ref, g_ref, wq_ref, wk_ref, wv_ref, c_ref, s_ref, xq_ref, xo_ref, ctx_ref, xk_ref, xv_ref,
                 h_ref, q_ref, k_ref, v_ref, o_ref, lse_ref, xqa_ref, xoa_ref, kva_ref,
                 kv_own, sq, rq, so, ro, sk, rk, fsq, frq, fso, fro, local):
    me = lax.axis_index("tensor")
    dp = lax.axis_index("dp")
    core = dp % 2
    partner = dp + 1 - 2 * core
    T, D = x_ref.shape
    W = q_ref.shape[1]
    KP = ctx_ref.shape[0]
    sem = pltpu.get_barrier_semaphore()
    for d in range(1, n):
        pl.semaphore_signal(sem, 1, device_id={"tensor": me ^ d}, device_id_type=MESH_ID)
    pl.semaphore_signal(sem, 1, device_id={"dp": partner}, device_id_type=MESH_ID)
    pl.semaphore_wait(sem, n)

    rows_q = pl.ds(pl.multiple_of(core * (D // 2), 16), D // 2)
    rows_o = pl.ds(pl.multiple_of(core * (W // 2), 16), W // 2)
    gq, go, gk = {}, {}, {}
    for d in range(1, n):
        gq[d] = remote(xq_ref.at[rows_q], xqa_ref.at[me, rows_q], sq.at[d - 1], rq.at[d - 1], me ^ d)
        gq[d].start()
    for d in range(1, n):
        go[d] = remote(xo_ref.at[rows_o], xoa_ref.at[me, rows_o], so.at[d - 1], ro.at[d - 1], me ^ d)
        go[d].start()
    own = [
        pltpu.make_async_copy(xq_ref, xqa_ref.at[me], local.at[0]),
        pltpu.make_async_copy(xo_ref, xoa_ref.at[me], local.at[1]),
    ]
    for copy in own:
        copy.start()
    kv_own[:KP] = nn(ctx_ref[...], xk_ref[...]).astype(BF)
    kv_own[KP:] = nn(ctx_ref[...], xv_ref[...]).astype(BF)
    for d in range(1, n):
        gk[d] = remote(kv_own, kva_ref.at[me], sk.at[d - 1], rk.at[d - 1], me ^ d)
        gk[d].start()
    kva_ref[me] = kv_own[...]

    tb = 256
    reps = W // c_ref.shape[1]

    def project(i, carry):
        rows = pl.ds(pl.multiple_of(i * tb, tb), tb)
        u, _ = unit(x_ref[rows, :].astype(F32))
        h = (u * g_ref[...]).astype(BF)
        h_ref[rows, :] = h
        c = jnp.concatenate([c_ref[rows, :]] * reps, 1)
        s = jnp.concatenate([s_ref[rows, :]] * reps, 1)
        for w_ref, out_ref in ((wq_ref, q_ref), (wk_ref, k_ref)):
            a = nn(h, w_ref[...])
            out_ref[rows, :] = (a * c + turned(a) * s).astype(BF)
        v_ref[rows, :] = nn(h, wv_ref[...]).astype(BF)
        return carry

    lax.fori_loop(0, T // tb, project, 0)

    G = lane_group(W)
    mult = SCALE * LOG2E
    masks = [m.astype(BF) for m in head_masks(1, G)]
    lane = lax.broadcasted_iota(jnp.int32, (tb, G), 1) // HEAD_DIM
    stat_lane = lax.broadcasted_iota(jnp.int32, (tb, 128), 1)

    def heads(g, carry):
        cols = pl.ds(pl.multiple_of(g * G, G), G) if G < W else slice(None)
        k, v = k_ref[:, cols], v_ref[:, cols]

        def block(i, inner):
            rows = pl.ds(pl.multiple_of(i * tb, tb), tb)
            q = q_ref[rows, cols]
            out = jnp.zeros((tb, G), F32)
            stats = jnp.zeros((tb, 128), F32)
            for h in range(G // HEAD_DIM):
                s = nt(q * masks[h], k)
                top = jnp.max(s, axis=-1, keepdims=True) * mult
                p = jnp.exp2(s * mult - top)
                total = jnp.sum(p, axis=-1, keepdims=True)
                o = nn(p.astype(BF), v) / total
                out = jnp.where(lane == h, o, out)
                stats = jnp.where(stat_lane == h, top + jnp.log2(total), stats)
            o_ref[rows, cols] = out.astype(BF)
            lse_ref[g, :, rows] = jnp.transpose(stats)[:8]
            return inner

        return lax.fori_loop(0, T // tb, block, carry)

    lax.fori_loop(0, W // G, heads, 0)

    def pass_on(ref, rows, send, recv, t):
        return pltpu.make_async_remote_copy(
            ref.at[t, rows], ref.at[t, rows], send, recv, device_id={"dp": partner}, device_id_type=MESH_ID
        )

    fq, fo = {}, {}
    for d in range(1, n):
        gq[d].wait_recv()
        fq[d] = pass_on(xqa_ref, rows_q, fsq.at[d - 1], frq.at[d - 1], me ^ d)
        fq[d].start()
    for d in range(1, n):
        go[d].wait_recv()
        fo[d] = pass_on(xoa_ref, rows_o, fso.at[d - 1], fro.at[d - 1], me ^ d)
        fo[d].start()
    for copy in own:
        copy.wait()
    for d in range(1, n):
        gk[d].wait_recv()
        fq[d].wait_recv()
        fo[d].wait_recv()
    for d in range(1, n):
        for copy in (gq[d], go[d], gk[d], fq[d], fo[d]):
            copy.wait_send()


def front(n, ctx, x, gain, wq, wk, wv, cs, sn, xq, xo, ctx_rows, xk, xv):
    T, D = x.shape
    W = wq.shape[1]
    KP = ctx_rows.shape[0]
    groups = W // lane_group(W)
    dma = pltpu.SemaphoreType.DMA((n - 1,))
    return pl.pallas_call(
        functools.partial(front_kernel, n, ctx),
        in_specs=[VSPEC] * 12,
        out_specs=[VSPEC] * 6 + [ANYSPEC] * 2 + [VSPEC],
        out_shape=[sds((T, D), BF)]
        + [sds((T, W), BF)] * 4
        + [sds((groups, 8, T), F32), sds((n, D, W), BF), sds((n, W, D), BF), sds((n, 2 * KP, W), BF)],
        scratch_shapes=[pltpu.VMEM((2 * KP, W), BF)] + [dma] * 10 + [pltpu.SemaphoreType.DMA((2,))],
        compiler_params=params(collective_id=4, has_side_effects=True),
        cost_estimate=cost(6 * T * D * W, 4 * T * D + 6 * D * W + 6 * T * W),
        name="front",
    )(x, gain, wq, wk, wv, cs, sn, xq, xo, ctx_rows, xk, xv)


def attn_bwd_kernel(q_ref, k_ref, v_ref, o_ref, do_ref, lse_ref, c_ref, s_ref, dq_ref, dk_ref, dv_ref, dk_acc, dv_acc, kt_ref):
    T, G = q_ref.shape
    qb = 256
    mult = SCALE * LOG2E
    nh = G // HEAD_DIM
    k, v = k_ref[...], v_ref[...]
    kt_ref[...] = jnp.transpose(k.astype(F32)).astype(BF)
    masks = [m.astype(BF) for m in head_masks(1, G)]
    head_rows = jnp.where(
        lax.broadcasted_iota(jnp.int32, (16, G), 0) == lax.broadcasted_iota(jnp.int32, (16, G), 1) // HEAD_DIM, 1.0, 0.0
    ).astype(BF)
    dk_acc[...] = jnp.zeros_like(dk_acc)
    dv_acc[...] = jnp.zeros_like(dv_acc)

    def block(i, carry):
        rows = pl.ds(pl.multiple_of(i * qb, qb), qb)
        q = q_ref[rows, :]
        do = do_ref[rows, :]
        prod = do.astype(F32) * o_ref[rows, :].astype(F32)
        high = prod.astype(BF)
        delta = nt(head_rows, high) + nt(head_rows, (prod - high.astype(F32)).astype(BF))
        lse = lse_ref[:, rows]
        parts = []
        for h in range(nh):
            qm = q * masks[h]
            dom = do * masks[h]
            st = nt(k, qm)
            pt = jnp.exp2(st * mult - lse[h : h + 1, :])
            dpt = nt(v, dom)
            dst = (pt * (dpt - delta[h : h + 1, :])).astype(BF)
            dv_acc[...] += nn(pt.astype(BF), dom)
            dk_acc[...] += nn(dst, qm)
            parts.append(nn(kt_ref[h * HEAD_DIM : (h + 1) * HEAD_DIM, :], dst))
        dq = jnp.transpose(jnp.concatenate(parts, 0)) * SCALE
        dq_ref[rows, :] = (dq * c_ref[rows, :] - turned(dq) * s_ref[rows, :]).astype(BF)
        return carry

    lax.fori_loop(0, T // qb, block, 0)
    dk = dk_acc[...] * SCALE
    dk_ref[...] = (dk * c_ref[...] - turned(dk) * s_ref[...]).astype(BF)
    dv_ref[...] = dv_acc[...].astype(BF)


def attn_bwd(q, k, v, o, do, lse, cs, sn):
    T, W = q.shape
    G = lane_group(W)
    cols = pl.BlockSpec((T, G), lambda i: (0, i))
    tab = pl.BlockSpec((T, G), lambda i: (0, 0), pipeline_mode=pl.Buffered(1))
    return pl.pallas_call(
        attn_bwd_kernel,
        grid=(W // G,),
        in_specs=[cols] * 5 + [pl.BlockSpec((None, 8, T), lambda i: (i, 0, 0)), tab, tab],
        out_specs=[cols] * 3,
        out_shape=[sds((T, W), BF)] * 3,
        scratch_shapes=[pltpu.VMEM((T, G), F32), pltpu.VMEM((T, G), F32), pltpu.VMEM((G, T), BF)],
        compiler_params=params(),
        cost_estimate=cost(40 * T * T * W, 16 * T * W, T * T * W // HEAD_DIM),
        name="attn_bwd",
    )(q, k, v, o, do, lse, cs, sn)


def greet(n, me):
    sem = pltpu.get_barrier_semaphore()
    for d in range(1, n):
        pl.semaphore_signal(sem, 1, device_id={"tensor": me ^ d}, device_id_type=MESH_ID)
    pl.semaphore_wait(sem, n - 1)


def remote(src, dst, send, recv, target):
    return pltpu.make_async_remote_copy(src, dst, send, recv, device_id={"tensor": target}, device_id_type=MESH_ID)


def out_rs_kernel(n, a_ref, w_ref, x_ref, g_ref, after_ref, h_ref, sbuf, rbuf, ss, rs):
    me = lax.axis_index("tensor")
    C = x_ref.shape[0]
    greet(n, me)

    def part(t):
        return nn(a_ref[pl.ds(pl.multiple_of(t * C, C), C), :], w_ref[...])

    copies = {}
    for d in reversed(range(1, n)):
        t = me ^ d
        sbuf[d - 1] = part(t).astype(BF)
        copies[d] = remote(sbuf.at[d - 1], rbuf.at[d - 1], ss.at[d - 1], rs.at[d - 1], t)
        copies[d].start()
    total = part(me)
    for d in range(1, n):
        copies[d].wait_recv()
        total = total + rbuf[d - 1].astype(F32)
    after = x_ref[...].astype(F32) + total
    after_ref[...] = after
    u, _ = unit(after)
    h_ref[...] = (u * g_ref[...]).astype(BF)
    for d in range(1, n):
        copies[d].wait_send()


def out_rs(n, a, w, x, gain):
    C, D = x.shape
    T, W = a.shape
    return pl.pallas_call(
        functools.partial(out_rs_kernel, n),
        in_specs=[VSPEC] * 4,
        out_specs=[VSPEC] * 2,
        out_shape=[sds((C, D), F32), sds((C, D), BF)],
        scratch_shapes=[pltpu.VMEM((n - 1, C, D), BF)] * 2 + [pltpu.SemaphoreType.DMA((n - 1,))] * 2,
        compiler_params=params(collective_id=0, has_side_effects=True),
        cost_estimate=cost(2 * T * W * D + 2e10, 8 * C * D),
        name="out_rs",
    )(a, w, x, gain)


def ff_kernel(n, h_in, gb_hbm, wg_hbm, wu_hbm, wd_hbm, h_ref, hid_ref, dgu_ref, dh_ref,
              gb_ref, wg_ref, wu_ref, wd_ref, sbuf, rbuf, ss, rs, ss2, rs2, ls):
    me = lax.axis_index("tensor")
    C, D = h_in.shape
    F = wg_ref.shape[1]
    loads = [
        pltpu.make_async_copy(src, dst, ls.at[i])
        for i, (src, dst) in enumerate(((wg_hbm, wg_ref), (wu_hbm, wu_ref), (wd_hbm, wd_ref), (gb_hbm, gb_ref)))
    ]
    for c in loads:
        c.start()
    greet(n, me)
    gather = {}
    for d in range(1, n):
        gather[d] = remote(h_in, h_ref.at[me], ss.at[d - 1], rs.at[d - 1], me ^ d)
        gather[d].start()
    h_ref[me] = h_in[...]
    for c in loads:
        c.wait()
    tf = 256

    def chunk(t, store):
        rows = pl.ds(pl.multiple_of(t * C, C), C)
        h = h_ref[t]
        gb = gb_ref[rows, :]

        def tile(j, carry):
            cols = pl.ds(pl.multiple_of(j * tf, tf), tf)
            gate = nn(h, wg_ref[:, cols])
            up = nn(h, wu_ref[:, cols])
            dhid = nt(gb, wd_ref[cols, :])
            sig = 1.0 / (1.0 + jnp.exp(-gate))
            act = gate * sig
            hid_ref[rows, cols] = (act * up).astype(BF)
            dgu_ref[rows, cols] = (dhid * up * (sig * (1.0 + gate * (1.0 - sig)))).astype(BF)
            dgu_ref[rows, pl.ds(pl.multiple_of(F + j * tf, tf), tf)] = (dhid * act).astype(BF)
            return carry

        lax.fori_loop(0, F // tf, tile, 0)

        def back(j, carry):
            out = pl.ds(pl.multiple_of(j * tf, tf), tf)
            store(out, nt(dgu_ref[rows, :F], wg_ref[out, :]) + nt(dgu_ref[rows, F:], wu_ref[out, :]))
            return carry

        lax.fori_loop(0, D // tf, back, 0)

    def store_own(cols, val):
        dh_ref[:, cols] = val

    chunk(me, store_own)
    copies = {}
    for d in range(1, n):
        t = me ^ d
        gather[d].wait_recv()

        def store_sent(cols, val):
            sbuf[d - 1, :, cols] = val.astype(BF)

        chunk(t, store_sent)
        copies[d] = remote(sbuf.at[d - 1], rbuf.at[d - 1], ss2.at[d - 1], rs2.at[d - 1], t)
        copies[d].start()
    for d in range(1, n):
        gather[d].wait_send()
    for d in range(1, n):
        copies[d].wait_recv()
        dh_ref[...] += rbuf[d - 1].astype(F32)
    for d in range(1, n):
        copies[d].wait_send()


def ff(n, h, gb, wg, wu, wd):
    C, D = h.shape
    T = gb.shape[0]
    F = wg.shape[1]
    return pl.pallas_call(
        functools.partial(ff_kernel, n),
        in_specs=[VSPEC] + [ANYSPEC] * 4,
        out_specs=[VSPEC] * 4,
        out_shape=[sds((n, C, D), BF), sds((T, F), BF), sds((T, 2 * F), BF), sds((C, D), F32)],
        scratch_shapes=[
            pltpu.VMEM((T, D), BF),
            pltpu.VMEM((D, F), BF),
            pltpu.VMEM((D, F), BF),
            pltpu.VMEM((F, D), BF),
            pltpu.VMEM((n - 1, C, D), BF),
            pltpu.VMEM((n - 1, C, D), BF),
        ]
        + [pltpu.SemaphoreType.DMA((n - 1,))] * 4
        + [pltpu.SemaphoreType.DMA((4,))],
        compiler_params=params(collective_id=1, has_side_effects=True),
        cost_estimate=cost(10 * T * D * F + 3e10, 6 * D * F + 8 * T * D),
        name="ff",
    )(h, gb, wg, wu, wd)


def feed_kernel(h_ref, gb_ref, dgu_ref, hid_ref, o_ref, od_ref):
    F2 = dgu_ref.shape[1]
    h, gb = h_ref[...], gb_ref[...]
    tf = 512

    def feed(j, carry):
        cols = pl.ds(pl.multiple_of(j * tf, tf), tf)
        o_ref[:, cols] = tn(h, dgu_ref[:, cols]).astype(BF)
        return carry

    def down(j, carry):
        cols = pl.ds(pl.multiple_of(j * tf, tf), tf)
        od_ref[:, cols] = tn(gb, hid_ref[:, cols]).astype(BF)
        return carry

    lax.fori_loop(0, F2 // tf, feed, 0)
    lax.fori_loop(0, F2 // 2 // tf, down, 0)


def feed_grads(h, gb, dgu, hidden):
    T, D = h.shape
    F = hidden.shape[1]
    tb = 256
    cols = pl.BlockSpec((T, tb), lambda i: (0, i))
    full = lambda a: pl.BlockSpec(a.shape, lambda i: (0, 0), pipeline_mode=pl.Buffered(1))
    return pl.pallas_call(
        feed_kernel,
        grid=(D // tb,),
        in_specs=[cols, cols, full(dgu), full(hidden)],
        out_specs=[pl.BlockSpec((tb, 2 * F), lambda i: (i, 0)), pl.BlockSpec((tb, F), lambda i: (i, 0))],
        out_shape=[sds((D, 2 * F), BF), sds((D, F), BF)],
        compiler_params=params(),
        cost_estimate=cost(6 * T * D * F, 6 * D * F),
        name="feed_grads",
    )(h, gb, dgu, hidden)


def gather_kernel(n, ndp, x_in, w_ref, h2_ref, dcq_ref, cb_ref, ca_ref, dkv_ref, ctx_ref,
                  x_ref, da_ref, gr_ref, ksend, krecv, ss, rs, ss2, rs2):
    me = lax.axis_index("tensor")
    C, D = x_in.shape
    W = w_ref.shape[0]
    HD = n * W
    KP = ctx_ref.shape[0]
    greet(n, me)
    gather = {}
    for d in range(1, n):
        gather[d] = remote(x_in, x_ref.at[me], ss.at[d - 1], rs.at[d - 1], me ^ d)
        gather[d].start()
    kv = {}
    for d in range(1, n):
        ksend[d - 1] = dkv_ref[me ^ d].astype(BF)
        kv[d] = remote(ksend.at[d - 1], krecv.at[d - 1], ss2.at[d - 1], rs2.at[d - 1], me ^ d)
        kv[d].start()

    def back(t, x):
        da_ref[pl.ds(pl.multiple_of(t * C, C), C), :] = nt(x, w_ref[...]).astype(BF)

    x_ref[me] = x_in[...]
    back(me, x_in[...])
    tf = 256

    def weights(j, carry):
        rows = pl.ds(pl.multiple_of(j * tf, tf), tf)
        h2, cb = h2_ref[:, rows], cb_ref[:, rows]
        for t in range(n):
            gr_ref[rows, t * W : (t + 1) * W] = tn(h2, dcq_ref[t]).astype(BF)
            gr_ref[rows, HD + t * W : HD + (t + 1) * W] = tn(cb, ca_ref[t]).astype(BF)
        return carry

    lax.fori_loop(0, D // tf, weights, 0)
    dkv = dkv_ref[me]
    for d in range(1, n):
        kv[d].wait_recv()
        dkv = dkv + krecv[d - 1].astype(F32)
    for half in range(2):
        kvg = tn(ctx_ref[...], dkv[half * KP : (half + 1) * KP].astype(BF)).astype(BF)
        R = kvg.shape[0] // ndp
        for i in range(ndp):
            gr_ref[(2 * i + half) * R : (2 * i + half + 1) * R, 2 * HD :] = kvg[i * R : (i + 1) * R]
    for d in range(1, n):
        gather[d].wait_recv()
        back(me ^ d, x_ref[me ^ d])
    for d in range(1, n):
        gather[d].wait_send()
        kv[d].wait_send()


def gather_back(n, ndp, x, w, h2, dcq, cb, ca, dkv, ctx):
    C, D = x.shape
    W = w.shape[0]
    KP = ctx.shape[0]
    return pl.pallas_call(
        functools.partial(gather_kernel, n, ndp),
        in_specs=[VSPEC] * 8,
        out_specs=[VSPEC] * 3,
        out_shape=[sds((n, C, D), BF), sds((n * C, W), BF), sds((D, (2 * n + 1) * W), BF)],
        scratch_shapes=[pltpu.VMEM((n - 1, 2 * KP, W), BF)] * 2 + [pltpu.SemaphoreType.DMA((n - 1,))] * 4,
        compiler_params=params(collective_id=2, has_side_effects=True),
        cost_estimate=cost(2 * n * C * W * D + 2e10, 8 * C * D),
        name="gather_back",
    )(x, w, h2, dcq, cb, ca, dkv, ctx)


def last_kernel(n, dq_ref, dk_ref, dv_ref, wq_ref, wk_ref, wv_ref, x_ref, da_ref, g_ref, gg_in, h1_ref, sb_ref, at_ref,
                lbuf, gr_ref, sbuf, rbuf, gbuf, gsum, ss, rs, ss2, rs2, ss3, rs3):
    me = lax.axis_index("tensor")
    C, D = x_ref.shape
    greet(n, me)

    def part(t):
        rows = pl.ds(pl.multiple_of(t * C, C), C)
        return nt(dq_ref[rows, :], wq_ref[...]) + nt(dk_ref[rows, :], wk_ref[...]) + nt(dv_ref[rows, :], wv_ref[...])

    copies = {}
    for d in reversed(range(1, n)):
        t = me ^ d
        sbuf[d - 1] = part(t).astype(BF)
        copies[d] = remote(sbuf.at[d - 1], rbuf.at[d - 1], ss.at[d - 1], rs.at[d - 1], t)
        copies[d].start()
    total = part(me)
    W = dq_ref.shape[1]
    tf = 256

    def weights(j, carry):
        rows = pl.ds(pl.multiple_of(j * tf, tf), tf)
        h = h1_ref[:, rows]
        for i, a_ref in enumerate((dq_ref, dk_ref, dv_ref)):
            gr_ref[rows, i * W : (i + 1) * W] = tn(h, a_ref[...]).astype(BF)
        gr_ref[rows, 3 * W : 4 * W] = tn(sb_ref[:, rows], at_ref[...]).astype(BF)
        return carry

    lax.fori_loop(0, D // tf, weights, 0)
    u, inverse = unit(x_ref[...].astype(F32))
    for d in range(1, n):
        copies[d].wait_recv()
        total = total + rbuf[d - 1].astype(F32)
    lbuf[me] = (da_ref[...] + norm_back(total, u, inverse, g_ref[...])).astype(BF)
    gather = {}
    for d in range(1, n):
        gather[d] = remote(lbuf.at[me], lbuf.at[me], ss2.at[d - 1], rs2.at[d - 1], me ^ d)
        gather[d].start()
    row = lax.broadcasted_iota(jnp.int32, (8, D), 0)
    gsum[...] = gg_in[...] + jnp.where(row == 2, jnp.sum(total * u, axis=0, keepdims=True), 0.0)
    small = {}
    for d in range(1, n):
        small[d] = remote(gsum, gbuf.at[d - 1], ss3.at[d - 1], rs3.at[d - 1], me ^ d)
        small[d].start()

    gains = gsum[...]
    for d in range(1, n):
        small[d].wait_recv()
        gains = gains + gbuf[d - 1]
    gains = jnp.concatenate([gains, jnp.zeros((120, D), F32)], 0)
    gr_ref[:, 4 * W :] = jnp.transpose(gains).astype(BF)
    for d in range(1, n):
        gather[d].wait_recv()
    for d in range(1, n):
        copies[d].wait_send()
        gather[d].wait_send()
        small[d].wait_send()


def last(n, dq, dk, dv, wq, wk, wv, x, da, gain, gains, h1, sb, attn):
    C, D = x.shape
    T, W = dq.shape
    return pl.pallas_call(
        functools.partial(last_kernel, n),
        in_specs=[VSPEC] * 13,
        out_specs=[VSPEC] * 2,
        out_shape=[sds((n, C, D), BF), sds((D, 4 * W + 128), BF)],
        scratch_shapes=[
            pltpu.VMEM((n - 1, C, D), BF),
            pltpu.VMEM((n - 1, C, D), BF),
            pltpu.VMEM((n - 1, 8, D), F32),
            pltpu.VMEM((8, D), F32),
        ]
        + [pltpu.SemaphoreType.DMA((n - 1,))] * 6,
        compiler_params=params(collective_id=3, has_side_effects=True),
        cost_estimate=cost(6 * T * W * D + 4e10, 8 * T * D),
        name="last",
    )(dq, dk, dv, wq, wk, wv, x, da, gain, gains, h1, sb, attn)


def cross_fwd_kernel(n, ctx, h_ref, x_ref, wq_ref, kv_ref, wo_ref, g_ref, q_ref, o_ref, after_ref, h3_ref):
    _, C, W = q_ref.shape
    KP = kv_ref.shape[1] // 2
    mult = SCALE * LOG2E
    G = lane_group(W)
    per = W // G
    masks = [m.astype(BF) for m in head_masks(1, G)]
    lane = lax.broadcasted_iota(jnp.int32, (C, G), 1) // HEAD_DIM
    valid = lax.broadcasted_iota(jnp.int32, (C, KP), 1) < ctx

    def group(g, carry):
        t = g // per
        cols = pl.ds(pl.multiple_of(g % per * G, G), G) if per > 1 else slice(None)
        q = nn(h_ref[...], wq_ref[t, :, cols]).astype(BF)
        q_ref[t, :, cols] = q
        k, v = kv_ref[t, :KP, cols], kv_ref[t, KP:, cols]
        out = jnp.zeros((C, G), F32)
        for h in range(G // HEAD_DIM):
            s = jnp.where(valid, nt(q * masks[h], k), -1e30)
            p = jnp.exp2((s - jnp.max(s, axis=-1, keepdims=True)) * mult)
            o = nn(p.astype(BF), v) / jnp.sum(p, axis=-1, keepdims=True)
            out = jnp.where(lane == h, o, out)
        o_ref[t, :, cols] = out.astype(BF)
        return carry

    lax.fori_loop(0, n * per, group, 0)
    D = h_ref.shape[1]
    tf = 256

    def project(j, carry):
        cols = pl.ds(pl.multiple_of(j * tf, tf), tf)
        total = nn(o_ref[0], wo_ref[0, :, cols])
        for t in range(1, n):
            total = total + nn(o_ref[t], wo_ref[t, :, cols])
        after_ref[:, cols] = x_ref[:, cols] + total
        return carry

    lax.fori_loop(0, D // tf, project, 0)
    u, _ = unit(after_ref[...])
    h3_ref[...] = (u * g_ref[...]).astype(BF)


def cross_fwd(ctx, h, x, wq, kv, wo, gain):
    C, D = h.shape
    n, W = wq.shape[0], wq.shape[2]
    return pl.pallas_call(
        functools.partial(cross_fwd_kernel, n, ctx),
        in_specs=[VSPEC] * 6,
        out_specs=[VSPEC] * 4,
        out_shape=[sds((n, C, W), BF), sds((n, C, W), BF), sds((C, D), F32), sds((C, D), BF)],
        compiler_params=params(),
        cost_estimate=cost(4 * C * D * n * W + 16 * C * 256 * n * W, 8 * D * n * W),
        name="cross_fwd",
    )(h, x, wq, kv, wo, gain)


def cross_bwd_kernel(n, ctx, dh3_ref, after2_ref, cot_ref, g3_ref, wo_ref, q_ref, kv_ref, wq_ref, after1_ref, g2_ref,
                     cb_ref, dq_ref, dkv_ref, da_ref, sb_ref, gg_ref, dh2_ref):
    _, C, W = q_ref.shape
    KP = kv_ref.shape[1] // 2
    D = da_ref.shape[1]
    mult = SCALE * LOG2E
    G = lane_group(W)
    per = W // G
    masks = [m.astype(BF) for m in head_masks(1, G)]
    lane = lax.broadcasted_iota(jnp.int32, (C, G), 1) // HEAD_DIM
    valid = lax.broadcasted_iota(jnp.int32, (C, KP), 1) < ctx
    dh3 = dh3_ref[...]
    u3, inv3 = unit(after2_ref[...])
    gain3 = jnp.sum(dh3 * u3, axis=0, keepdims=True)
    da2 = cot_ref[...].astype(F32) + norm_back(dh3, u3, inv3, g3_ref[...])
    da_ref[...] = da2
    cb_ref[...] = da2.astype(BF)

    def group(g, carry):
        t = g // per
        cols = pl.ds(pl.multiple_of(g % per * G, G), G) if per > 1 else slice(None)
        do = nt(cb_ref[...], wo_ref[t, cols, :]).astype(BF)
        q, k, v = q_ref[t, :, cols], kv_ref[t, :KP, cols], kv_ref[t, KP:, cols]
        dq = jnp.zeros((C, G), F32)
        dk = jnp.zeros((KP, G), F32)
        dv = jnp.zeros((KP, G), F32)
        for h in range(G // HEAD_DIM):
            qm = q * masks[h]
            dom = do * masks[h]
            s = jnp.where(valid, nt(qm, k), -1e30)
            p = jnp.exp2((s - jnp.max(s, axis=-1, keepdims=True)) * mult)
            p = p / jnp.sum(p, axis=-1, keepdims=True)
            dp = nt(dom, v)
            ds = (p * (dp - jnp.sum(p * dp, axis=-1, keepdims=True))).astype(BF)
            dq = jnp.where(lane == h, nn(ds, k), dq)
            dk = dk + tn(ds, qm)
            dv = dv + tn(p.astype(BF), dom)
        dq_ref[t, :, cols] = (dq * SCALE).astype(BF)
        dkv_ref[t, :KP, cols] = dk * SCALE
        dkv_ref[t, KP:, cols] = dv
        return carry

    lax.fori_loop(0, n * per, group, 0)
    tf = 256

    def project(j, carry):
        cols = pl.ds(pl.multiple_of(j * tf, tf), tf)
        total = nt(dq_ref[0], wq_ref[0, cols, :])
        for t in range(1, n):
            total = total + nt(dq_ref[t], wq_ref[t, cols, :])
        dh2_ref[:, cols] = total
        return carry

    lax.fori_loop(0, D // tf, project, 0)
    dh2 = dh2_ref[...]
    u2, inv2 = unit(after1_ref[...])
    gain2 = jnp.sum(dh2 * u2, axis=0, keepdims=True)
    da1 = da_ref[...] + norm_back(dh2, u2, inv2, g2_ref[...])
    da_ref[...] = da1
    sb_ref[...] = da1.astype(BF)
    row = lax.broadcasted_iota(jnp.int32, (8, D), 0)
    gg_ref[...] = jnp.where(row == 0, gain3, 0.0) + jnp.where(row == 1, gain2, 0.0)


def cross_bwd(ctx, dh3, after2, cot, g3, wo, q, kv, wq, after1, g2):
    C, D = after2.shape
    n, W = wq.shape[0], wq.shape[2]
    return pl.pallas_call(
        functools.partial(cross_bwd_kernel, n, ctx),
        in_specs=[VSPEC] * 10,
        out_specs=[VSPEC] * 6,
        out_shape=[
            sds((C, D), BF),
            sds((n, C, W), BF),
            sds(kv.shape, F32),
            sds((C, D), F32),
            sds((C, D), BF),
            sds((8, D), F32),
        ],
        scratch_shapes=[pltpu.VMEM((C, D), F32)],
        compiler_params=params(),
        cost_estimate=cost(4 * C * D * n * W + 40 * C * 256 * n * W, 8 * D * n * W),
        name="cross_bwd",
    )(dh3, after2, cot, g3, wo, q, kv, wq, after1, g2)


def swap_sum_kernel(n, a_ref, o_ref, rbuf, ss, rs):
    me = lax.axis_index("tensor")
    greet(n, me)
    copies = {}
    for d in range(1, n):
        copies[d] = remote(a_ref.at[me ^ d], rbuf.at[d - 1], ss.at[d - 1], rs.at[d - 1], me ^ d)
        copies[d].start()
    total = a_ref[me].astype(F32)
    for d in range(1, n):
        copies[d].wait_recv()
        total = total + rbuf[d - 1].astype(F32)
    o_ref[...] = total
    for d in range(1, n):
        copies[d].wait_send()


def swap_sum(a):
    n, R, N = a.shape
    return pl.pallas_call(
        functools.partial(swap_sum_kernel, n),
        in_specs=[VSPEC],
        out_specs=VSPEC,
        out_shape=sds((R, N), F32),
        scratch_shapes=[pltpu.VMEM((n - 1, R, N), BF)] + [pltpu.SemaphoreType.DMA((n - 1,))] * 2,
        compiler_params=params(collective_id=5, has_side_effects=True),
        cost_estimate=cost(n * R * N, 8 * R * N),
        name="swap_sum",
    )(a)


def body(latents, context, cotangent, g1, wq, wk, wv, wo, g2, xq, xk, xv, xo, g3, wg, wu, wd, n, ndp):
    _, T, D = latents.shape
    ctx = context.shape[1]
    W = wq.shape[1]
    F = wg.shape[1]
    C = T // n
    me = lax.axis_index("tensor")
    x = latents.reshape(T, D)
    gb = cotangent.reshape(T, D)
    ctx_rows = context.reshape(ctx, -1)
    KP = -(-ctx // 16) * 16
    cs, sn = tables(T, lane_group(W))
    g1, g2, g3 = (g.reshape(1, D) for g in (g1, g2, g3))
    own = lambda a: lax.dynamic_slice_in_dim(a, me * C, C, 0)

    ctx_pad = jnp.pad(ctx_rows, ((0, KP - ctx), (0, 0)))
    h1, q, k, v, attn, lse, xq_all, xo_all, kv_all = front(n, ctx, x, g1, wq, wk, wv, cs, sn, xq, xo, ctx_pad, xk, xv)
    x_own = own(x)
    after1, h2 = out_rs(n, attn, wo, x_own, g2)
    cq, cattn, after2, h3_own = cross_fwd(ctx, h2, after1, xq_all, kv_all, xo_all, g3)
    h3, hidden, dgu, dh3 = ff(n, h3_own, gb, wg, wu, wd)
    h3 = h3.reshape(T, D)

    def scatter(a, axis):
        return lax.psum_scatter(a, axis, scatter_dimension=0, tiled=True)

    gu_part, down_part = feed_grads(h3, gb, dgu, hidden)
    dh3, gu_part, down_part = lax.optimization_barrier((dh3, gu_part, down_part))
    gu_grad = scatter(gu_part, "dp")
    down_grad = scatter(down_part, "dp")

    cb, dcq, dckv, dafter1, sb_own, gains = cross_bwd(
        ctx, dh3, after2, own(gb), g3, xo_all, cq, kv_all, xq_all, after1, g2
    )
    sb, dattn, cross_grads = gather_back(n, ndp, sb_own, wo, h2, dcq, cb, cattn, dckv, ctx_pad)
    sb = sb.reshape(T, D)
    dq, dk, dv = attn_bwd(q, k, v, attn, dattn, lse, cs, sn)
    dq, gu_grad = lax.optimization_barrier((dq, gu_grad))
    latent_grad, self_grads = last(n, dq, dk, dv, wq, wk, wv, x_own, dafter1, g1, gains, h1, sb, attn)
    self_grads = scatter(self_grads, "dp")

    hidden, latent_grad = lax.optimization_barrier((hidden, latent_grad))
    terms = nn(hidden, wd).astype(BF).reshape(n, C, D)
    swap = lambda a, d: lax.ppermute(a, "tensor", [(i, i ^ d) for i in range(n)])
    pick = lambda a, t: lax.dynamic_index_in_dim(a, t, 0, keepdims=False)
    total = after2 + pick(terms, me).astype(F32)
    for d in range(1, n):
        total = total + swap(pick(terms, me ^ d), d).astype(F32)
    total = total.astype(BF)
    block_out = jnp.zeros((n, C, D), BF)
    block_out = lax.dynamic_update_index_in_dim(block_out, total, me, 0)
    for d in range(1, n):
        block_out = lax.dynamic_update_index_in_dim(block_out, swap(total, d), me ^ d, 0)

    cross_grads = scatter(cross_grads, "dp")
    cross_grads, down_grad, block_out = lax.optimization_barrier((cross_grads, down_grad, block_out))
    gu_grad = gu_grad.astype(F32)
    gate_grad, up_grad, down_grad = gu_grad[:, :F], gu_grad[:, F:], down_grad.astype(F32).T
    rows = cross_grads.shape[0]
    kv_grads = cross_grads[:, 2 * n * W :].reshape(2, rows // 2, W).astype(F32)
    cross_grads = cross_grads[:, : 2 * n * W].reshape(rows, 2, n, W).transpose(2, 0, 1, 3).reshape(n, rows, 2 * W)
    cross_grads = swap_sum(cross_grads)
    xq_grad, xo_grad = cross_grads[:, :W], cross_grads[:, W:].T
    self_grads = self_grads.astype(F32)
    gains = self_grads[:, 4 * W :]
    return (
        block_out.reshape(1, T, D),
        latent_grad.astype(F32).reshape(1, T, D),
        gains[:, 2],
        self_grads[:, :W],
        self_grads[:, W : 2 * W],
        self_grads[:, 2 * W : 3 * W],
        self_grads[:, 3 * W : 4 * W].T,
        gains[:, 1],
        xq_grad,
        kv_grads[0],
        kv_grads[1],
        xo_grad,
        gains[:, 0],
        gate_grad,
        up_grad,
        down_grad,
    )


def solution(mesh):
    tokens = P("dp", None, None)
    cols = P(None, "tensor")
    rows = P("tensor", None)
    return jax.shard_map(
        functools.partial(body, n=mesh.shape["tensor"], ndp=mesh.shape["dp"]),
        mesh=mesh,
        in_specs=(tokens, tokens, tokens, P(), cols, cols, cols, rows, P(), cols, cols, cols, rows, P(), cols, cols, rows),
        out_specs=(
            tokens,
            tokens,
            P("dp"),
            P("dp", "tensor"),
            P("dp", "tensor"),
            P("dp", "tensor"),
            P("tensor", "dp"),
            P("dp"),
            P("dp", "tensor"),
            P("dp", "tensor"),
            P("dp", "tensor"),
            P("tensor", "dp"),
            P("dp"),
            P("dp", "tensor"),
            P("dp", "tensor"),
            P("tensor", "dp"),
        ),
        check_vma=False,
    )
```

```python
import functools

import jax
import jax.numpy as jnp
from jax import lax
from jax.experimental import pallas as pl
from jax.experimental.pallas import tpu as pltpu
from jax.sharding import PartitionSpec as P

HEAD_DIM = 64
HALF = HEAD_DIM // 2
EPS = 1e-05
BF = jnp.bfloat16
F32 = jnp.float32
LOG2E = 1.4426950408889634
SCALE = HEAD_DIM**-0.5
VMEM_BYTES = 60 << 20
MESH_ID = pl.DeviceIdType.MESH
VSPEC = pl.BlockSpec(memory_space=pltpu.VMEM)
ANYSPEC = pl.BlockSpec(memory_space=pl.ANY)


def nn(a, b):
    return lax.dot_general(a, b, (((1,), (0,)), ((), ())), preferred_element_type=F32)


def nt(a, b):
    return lax.dot_general(a, b, (((1,), (1,)), ((), ())), preferred_element_type=F32)


def tn(a, b):
    return lax.dot_general(a, b, (((0,), (0,)), ((), ())), preferred_element_type=F32)


def sds(shape, dtype):
    return jax.ShapeDtypeStruct(shape, dtype)


def params(**kw):
    return pltpu.CompilerParams(vmem_limit_bytes=VMEM_BYTES, **kw)


def cost(flops, nbytes, trans=0):
    return pl.CostEstimate(flops=1000, bytes_accessed=1000, transcendentals=0)


def unit(x):
    center = x - jnp.mean(x, axis=-1, keepdims=True)
    inverse = lax.rsqrt(jnp.mean(center * center, axis=-1, keepdims=True) + EPS)
    return center * inverse, inverse


def norm_back(grad, u, inverse, gain):
    e = grad * gain
    mean_e = jnp.mean(e, axis=-1, keepdims=True)
    mean_p = jnp.mean(e * u, axis=-1, keepdims=True)
    return inverse * (e - mean_e - u * mean_p)


def lane_group(width):
    return 128 if width % 128 == 0 else width


def tables(length, group):
    freq = 10000.0 ** (-jnp.arange(HALF, dtype=F32) / HALF)
    angles = jnp.arange(length, dtype=F32)[:, None] * freq[None, :]
    c, s = jnp.cos(angles), jnp.sin(angles)
    reps = group // HEAD_DIM
    return jnp.tile(jnp.concatenate([c, c], 1), (1, reps)), jnp.tile(jnp.concatenate([-s, s], 1), (1, reps))


def turned(a):
    width = a.shape[-1]
    lane = lax.broadcasted_iota(jnp.int32, a.shape, 1) % HEAD_DIM
    return jnp.where(lane < HALF, pltpu.roll(a, width - HALF, 1), pltpu.roll(a, HALF, 1))


def head_masks(rows, group):
    lane = lax.broadcasted_iota(jnp.int32, (rows, group), 1) // HEAD_DIM
    return [jnp.where(lane == h, 1.0, 0.0) for h in range(group // HEAD_DIM)]


def front_kernel(n, ctx, x_ref, g_ref, wq_ref, wk_ref, wv_ref, c_ref, s_ref, xq_ref, xo_ref, ctx_ref, xk_ref, xv_ref,
                 h_ref, q_ref, k_ref, v_ref, o_ref, lse_ref, xqa_ref, xoa_ref, kva_ref,
                 kv_own, sq, rq, so, ro, sk, rk, fsq, frq, fso, fro, local):
    me = lax.axis_index("tensor")
    dp = lax.axis_index("dp")
    core = dp % 2
    partner = dp + 1 - 2 * core
    T, D = x_ref.shape
    W = q_ref.shape[1]
    KP = ctx_ref.shape[0]
    sem = pltpu.get_barrier_semaphore()
    for d in range(1, n):
        pl.semaphore_signal(sem, 1, device_id={"tensor": me ^ d}, device_id_type=MESH_ID)
    pl.semaphore_signal(sem, 1, device_id={"dp": partner}, device_id_type=MESH_ID)
    pl.semaphore_wait(sem, n)

    rows_q = pl.ds(pl.multiple_of(core * (D // 2), 16), D // 2)
    rows_o = pl.ds(pl.multiple_of(core * (W // 2), 16), W // 2)
    def quarter(ref, rows):
        return lambda t, i: ref.at[t, pl.ds(pl.multiple_of(core * (rows // 2) + i * (rows // 4), 16), rows // 4)]

    gq = Gather(n, me, xq_ref.at[rows_q], lambda t: xqa_ref.at[t, rows_q], quarter(xqa_ref, D), sq, rq)
    go = Gather(n, me, xo_ref.at[rows_o], lambda t: xoa_ref.at[t, rows_o], quarter(xoa_ref, W), so, ro)
    gk = Gather(n, me, kv_own, lambda t: kva_ref.at[t], lambda t, i: kva_ref.at[t, pl.ds(i * KP, KP)], sk, rk)
    gq.start()
    go.start()
    own = [
        pltpu.make_async_copy(xq_ref, xqa_ref.at[me], local.at[0]),
        pltpu.make_async_copy(xo_ref, xoa_ref.at[me], local.at[1]),
    ]
    for copy in own:
        copy.start()
    kv_own[:KP] = nn(ctx_ref[...], xk_ref[...]).astype(BF)
    kv_own[KP:] = nn(ctx_ref[...], xv_ref[...]).astype(BF)
    gk.start()
    kva_ref[me] = kv_own[...]

    tb = 256
    reps = W // c_ref.shape[1]

    def project(i, carry):
        rows = pl.ds(pl.multiple_of(i * tb, tb), tb)
        u, _ = unit(x_ref[rows, :].astype(F32))
        h = (u * g_ref[...]).astype(BF)
        h_ref[rows, :] = h
        c = jnp.concatenate([c_ref[rows, :]] * reps, 1)
        s = jnp.concatenate([s_ref[rows, :]] * reps, 1)
        for w_ref, out_ref in ((wq_ref, q_ref), (wk_ref, k_ref)):
            a = nn(h, w_ref[...])
            out_ref[rows, :] = (a * c + turned(a) * s).astype(BF)
        v_ref[rows, :] = nn(h, wv_ref[...]).astype(BF)
        return carry

    lax.fori_loop(0, T // tb, project, 0)
    gq.relay()

    G = lane_group(W)
    mult = SCALE * LOG2E
    masks = [m.astype(BF) for m in head_masks(1, G)]
    lane = lax.broadcasted_iota(jnp.int32, (tb, G), 1) // HEAD_DIM
    stat_lane = lax.broadcasted_iota(jnp.int32, (tb, 128), 1)

    def heads(g, carry):
        cols = pl.ds(pl.multiple_of(g * G, G), G) if G < W else slice(None)
        k, v = k_ref[:, cols], v_ref[:, cols]

        def block(i, inner):
            rows = pl.ds(pl.multiple_of(i * tb, tb), tb)
            q = q_ref[rows, cols]
            out = jnp.zeros((tb, G), F32)
            stats = jnp.zeros((tb, 128), F32)
            for h in range(G // HEAD_DIM):
                s = nt(q * masks[h], k)
                top = jnp.max(s, axis=-1, keepdims=True) * mult
                p = jnp.exp2(s * mult - top)
                total = jnp.sum(p, axis=-1, keepdims=True)
                o = nn(p.astype(BF), v) / total
                out = jnp.where(lane == h, o, out)
                stats = jnp.where(stat_lane == h, top + jnp.log2(total), stats)
            o_ref[rows, cols] = out.astype(BF)
            lse_ref[g, :, rows] = jnp.transpose(stats)[:8]
            return inner

        return lax.fori_loop(0, T // tb, block, carry)

    lax.fori_loop(0, W // G, heads, 0)

    def pass_on(ref, rows, send, recv, t):
        return pltpu.make_async_remote_copy(
            ref.at[t, rows], ref.at[t, rows], send, recv, device_id={"dp": partner}, device_id_type=MESH_ID
        )

    go.relay()
    gk.relay()
    passed = []
    for gather, ref, rows, send, recv in ((gq, xqa_ref, rows_q, fsq, frq), (go, xoa_ref, rows_o, fso, fro)):
        for d in range(1, n):
            gather.wait(d)
            copy = pass_on(ref, rows, send.at[d - 1], recv.at[d - 1], me ^ d)
            copy.start()
            passed.append(copy)
    for copy in own:
        copy.wait()
    for d in range(1, n):
        gk.wait(d)
    for copy in passed:
        copy.wait_recv()
    for copy in (gq, go, gk):
        copy.finish()
    for copy in passed:
        copy.wait_send()


def front(n, ctx, x, gain, wq, wk, wv, cs, sn, xq, xo, ctx_rows, xk, xv):
    T, D = x.shape
    W = wq.shape[1]
    KP = ctx_rows.shape[0]
    groups = W // lane_group(W)
    link, pair = pltpu.SemaphoreType.DMA((links(n),)), pltpu.SemaphoreType.DMA((n - 1,))
    return pl.pallas_call(
        functools.partial(front_kernel, n, ctx),
        in_specs=[VSPEC] * 12,
        out_specs=[VSPEC] * 6 + [ANYSPEC] * 2 + [VSPEC],
        out_shape=[sds((T, D), BF)]
        + [sds((T, W), BF)] * 4
        + [sds((groups, 8, T), F32), sds((n, D, W), BF), sds((n, W, D), BF), sds((n, 2 * KP, W), BF)],
        scratch_shapes=[pltpu.VMEM((2 * KP, W), BF)] + [link] * 6 + [pair] * 4 + [pltpu.SemaphoreType.DMA((2,))],
        compiler_params=params(collective_id=4, has_side_effects=True),
        cost_estimate=cost(6 * T * D * W, 4 * T * D + 6 * D * W + 6 * T * W),
        name="front",
    )(x, gain, wq, wk, wv, cs, sn, xq, xo, ctx_rows, xk, xv)


def attn_bwd_kernel(q_ref, k_ref, v_ref, o_ref, do_ref, lse_ref, c_ref, s_ref, dq_ref, dk_ref, dv_ref, dk_acc, dv_acc, kt_ref):
    T, G = q_ref.shape
    qb = 256
    mult = SCALE * LOG2E
    nh = G // HEAD_DIM
    k, v = k_ref[...], v_ref[...]
    kt_ref[...] = jnp.transpose(k.astype(F32)).astype(BF)
    masks = [m.astype(BF) for m in head_masks(1, G)]
    head_rows = jnp.where(
        lax.broadcasted_iota(jnp.int32, (16, G), 0) == lax.broadcasted_iota(jnp.int32, (16, G), 1) // HEAD_DIM, 1.0, 0.0
    ).astype(BF)
    dk_acc[...] = jnp.zeros_like(dk_acc)
    dv_acc[...] = jnp.zeros_like(dv_acc)

    def block(i, carry):
        rows = pl.ds(pl.multiple_of(i * qb, qb), qb)
        q = q_ref[rows, :]
        do = do_ref[rows, :]
        prod = do.astype(F32) * o_ref[rows, :].astype(F32)
        high = prod.astype(BF)
        delta = nt(head_rows, high) + nt(head_rows, (prod - high.astype(F32)).astype(BF))
        lse = lse_ref[:, rows]
        parts = []
        for h in range(nh):
            qm = q * masks[h]
            dom = do * masks[h]
            st = nt(k, qm)
            pt = jnp.exp2(st * mult - lse[h : h + 1, :])
            dpt = nt(v, dom)
            dst = (pt * (dpt - delta[h : h + 1, :])).astype(BF)
            dv_acc[...] += nn(pt.astype(BF), dom)
            dk_acc[...] += nn(dst, qm)
            parts.append(nn(kt_ref[h * HEAD_DIM : (h + 1) * HEAD_DIM, :], dst))
        dq = jnp.transpose(jnp.concatenate(parts, 0)) * SCALE
        dq_ref[rows, :] = (dq * c_ref[rows, :] - turned(dq) * s_ref[rows, :]).astype(BF)
        return carry

    lax.fori_loop(0, T // qb, block, 0)
    dk = dk_acc[...] * SCALE
    dk_ref[...] = (dk * c_ref[...] - turned(dk) * s_ref[...]).astype(BF)
    dv_ref[...] = dv_acc[...].astype(BF)


def attn_bwd(q, k, v, o, do, lse, cs, sn):
    T, W = q.shape
    G = lane_group(W)
    cols = pl.BlockSpec((T, G), lambda i: (0, i))
    tab = pl.BlockSpec((T, G), lambda i: (0, 0), pipeline_mode=pl.Buffered(1))
    return pl.pallas_call(
        attn_bwd_kernel,
        grid=(W // G,),
        in_specs=[cols] * 5 + [pl.BlockSpec((None, 8, T), lambda i: (i, 0, 0)), tab, tab],
        out_specs=[cols] * 3,
        out_shape=[sds((T, W), BF)] * 3,
        scratch_shapes=[pltpu.VMEM((T, G), F32), pltpu.VMEM((T, G), F32), pltpu.VMEM((G, T), BF)],
        compiler_params=params(),
        cost_estimate=cost(40 * T * T * W, 16 * T * W, T * T * W // HEAD_DIM),
        name="attn_bwd",
    )(q, k, v, o, do, lse, cs, sn)


def greet(n, me):
    sem = pltpu.get_barrier_semaphore()
    for d in range(1, n):
        pl.semaphore_signal(sem, 1, device_id={"tensor": me ^ d}, device_id_type=MESH_ID)
    pl.semaphore_wait(sem, n - 1)


def remote(src, dst, send, recv, target):
    return pltpu.make_async_remote_copy(src, dst, send, recv, device_id={"tensor": target}, device_id_type=MESH_ID)


def links(n):
    return 4 if n == 4 else n - 1


class Gather:
    def __init__(self, n, me, src, slot, half, ss, rs):
        self.n, self.me, self.half, self.ss, self.rs = n, me, half, ss, rs
        self.copies = {
            d: remote(src, slot(me), ss.at[d - 1], rs.at[d - 1], me ^ d) for d in (range(1, n) if n != 4 else (1, 2))
        }
        self.passed = []

    def start(self):
        for copy in self.copies.values():
            copy.start()

    def relay(self):
        if self.n == 4:
            for i, d in enumerate((1, 2)):
                self.copies[d].wait_recv()
                block = self.half(self.me ^ d, i)
                copy = remote(block, block, self.ss.at[2 + i], self.rs.at[2 + i], self.me ^ (3 - d))
                copy.start()
                self.passed.append(copy)

    def wait(self, d):
        if self.n != 4:
            self.copies[d].wait_recv()
        elif d == 3:
            for copy in self.passed:
                copy.wait_recv()

    def finish(self):
        for copy in (*self.copies.values(), *self.passed):
            copy.wait_send()


def reduce_bufs(n, C, D):
    shape = (6, C, D // 2) if n == 4 else (n - 1, C, D)
    return [pltpu.VMEM(shape, BF)] * 2 + [pltpu.SemaphoreType.DMA((shape[0],))] * 2


def reduce_parts(n, me, part, filler, sbuf, rbuf, ss, rs):
    copies = {}

    def send(i, val, d):
        sbuf[i] = val.astype(BF)
        copies[i] = remote(sbuf.at[i], rbuf.at[i], ss.at[i], rs.at[i], me ^ d)
        copies[i].start()

    def got(i):
        copies[i].wait_recv()
        return rbuf[i].astype(F32)

    if n == 4:
        across = part(me ^ 3)
        H = across.shape[1] // 2
        send(0, across[:, :H], 1)
        send(2, across[:, H:], 2)
        one = part(me ^ 1)
        send(1, one[:, :H], 1)
        two = part(me ^ 2)
        send(3, two[:, H:], 2)
        total = part(me)
        filler()
        send(4, two[:, :H] + got(0), 2)
        send(5, one[:, H:] + got(2), 1)
        total = jnp.concatenate([total[:, :H] + got(1) + got(4), total[:, H:] + got(3) + got(5)], 1)
    else:
        for d in reversed(range(1, n)):
            send(d - 1, part(me ^ d), d)
        total = part(me)
        filler()
        for d in range(1, n):
            total = total + got(d - 1)
    return total, copies


def out_rs_kernel(n, a_ref, w_ref, x_ref, g_ref, after_ref, h_ref, sbuf, rbuf, ss, rs):
    me = lax.axis_index("tensor")
    C = x_ref.shape[0]
    greet(n, me)

    def part(t):
        return nn(a_ref[pl.ds(pl.multiple_of(t * C, C), C), :], w_ref[...])

    total, copies = reduce_parts(n, me, part, lambda: None, sbuf, rbuf, ss, rs)
    after = x_ref[...].astype(F32) + total
    after_ref[...] = after
    u, _ = unit(after)
    h_ref[...] = (u * g_ref[...]).astype(BF)
    for copy in copies.values():
        copy.wait_send()


def out_rs(n, a, w, x, gain):
    C, D = x.shape
    T, W = a.shape
    return pl.pallas_call(
        functools.partial(out_rs_kernel, n),
        in_specs=[VSPEC] * 4,
        out_specs=[VSPEC] * 2,
        out_shape=[sds((C, D), F32), sds((C, D), BF)],
        scratch_shapes=reduce_bufs(n, C, D),
        compiler_params=params(collective_id=0, has_side_effects=True),
        cost_estimate=cost(2 * T * W * D + 2e10, 8 * C * D),
        name="out_rs",
    )(a, w, x, gain)


def ff_kernel(n, h_in, gb_hbm, wg_hbm, wu_hbm, wd_hbm, h_ref, hid_ref, dgu_ref, dh_ref,
              gb_ref, wg_ref, wu_ref, wd_ref, sbuf, rbuf, ss, rs, ss2, rs2, ls):
    me = lax.axis_index("tensor")
    C, D = h_in.shape
    F = wg_ref.shape[1]
    loads = [
        pltpu.make_async_copy(src, dst, ls.at[i])
        for i, (src, dst) in enumerate(((wg_hbm, wg_ref), (wu_hbm, wu_ref), (wd_hbm, wd_ref), (gb_hbm, gb_ref)))
    ]
    for c in loads:
        c.start()
    greet(n, me)
    gather = Gather(n, me, h_in, lambda t: h_ref.at[t], lambda t, i: h_ref.at[t, pl.ds(i * C // 2, C // 2)], ss, rs)
    gather.start()
    h_ref[me] = h_in[...]
    for c in loads:
        c.wait()
    tf = 256

    def chunk(t, store):
        rows = pl.ds(pl.multiple_of(t * C, C), C)
        h = h_ref[t]
        gb = gb_ref[rows, :]

        def tile(j, carry):
            cols = pl.ds(pl.multiple_of(j * tf, tf), tf)
            gate = nn(h, wg_ref[:, cols])
            up = nn(h, wu_ref[:, cols])
            dhid = nt(gb, wd_ref[cols, :])
            sig = 1.0 / (1.0 + jnp.exp(-gate))
            act = gate * sig
            hid_ref[rows, cols] = (act * up).astype(BF)
            dgu_ref[rows, cols] = (dhid * up * (sig * (1.0 + gate * (1.0 - sig)))).astype(BF)
            dgu_ref[rows, pl.ds(pl.multiple_of(F + j * tf, tf), tf)] = (dhid * act).astype(BF)
            return carry

        lax.fori_loop(0, F // tf, tile, 0)

        def back(j, carry):
            out = pl.ds(pl.multiple_of(j * tf, tf), tf)
            store(out, nt(dgu_ref[rows, :F], wg_ref[out, :]) + nt(dgu_ref[rows, F:], wu_ref[out, :]))
            return carry

        lax.fori_loop(0, D // tf, back, 0)

    def store_own(cols, val):
        dh_ref[:, cols] = val

    chunk(me, store_own)
    gather.relay()
    copies = {}
    for d in range(1, n):
        t = me ^ d
        gather.wait(d)

        def store_sent(cols, val):
            sbuf[d - 1, :, cols] = val.astype(BF)

        chunk(t, store_sent)
        copies[d] = remote(sbuf.at[d - 1], rbuf.at[d - 1], ss2.at[d - 1], rs2.at[d - 1], t)
        copies[d].start()
    gather.finish()
    for d in range(1, n):
        copies[d].wait_recv()
        dh_ref[...] += rbuf[d - 1].astype(F32)
    for d in range(1, n):
        copies[d].wait_send()


def ff(n, h, gb, wg, wu, wd):
    C, D = h.shape
    T = gb.shape[0]
    F = wg.shape[1]
    return pl.pallas_call(
        functools.partial(ff_kernel, n),
        in_specs=[VSPEC] + [ANYSPEC] * 4,
        out_specs=[VSPEC] * 4,
        out_shape=[sds((n, C, D), BF), sds((T, F), BF), sds((T, 2 * F), BF), sds((C, D), F32)],
        scratch_shapes=[
            pltpu.VMEM((T, D), BF),
            pltpu.VMEM((D, F), BF),
            pltpu.VMEM((D, F), BF),
            pltpu.VMEM((F, D), BF),
            pltpu.VMEM((n - 1, C, D), BF),
            pltpu.VMEM((n - 1, C, D), BF),
        ]
        + [pltpu.SemaphoreType.DMA((links(n),))] * 2
        + [pltpu.SemaphoreType.DMA((n - 1,))] * 2
        + [pltpu.SemaphoreType.DMA((4,))],
        compiler_params=params(collective_id=1, has_side_effects=True),
        cost_estimate=cost(10 * T * D * F + 3e10, 6 * D * F + 8 * T * D),
        name="ff",
    )(h, gb, wg, wu, wd)


def down_kernel(gb_ref, hid_ref, o_ref):
    gb = gb_ref[...]
    tf = 512 if hid_ref.shape[1] % 512 == 0 else 256

    def down(j, carry):
        cols = pl.ds(pl.multiple_of(j * tf, tf), tf)
        o_ref[:, cols] = tn(gb, hid_ref[:, cols]).astype(BF)
        return carry

    lax.fori_loop(0, hid_ref.shape[1] // tf, down, 0)


def down_grads(gb, hidden):
    T, D = gb.shape
    F = hidden.shape[1]
    tb = 256
    return pl.pallas_call(
        down_kernel,
        grid=(D // tb,),
        in_specs=[
            pl.BlockSpec((T, tb), lambda i: (0, i)),
            pl.BlockSpec(hidden.shape, lambda i: (0, 0), pipeline_mode=pl.Buffered(1)),
        ],
        out_specs=pl.BlockSpec((tb, F), lambda i: (i, 0)),
        out_shape=sds((D, F), BF),
        compiler_params=params(),
        cost_estimate=cost(2 * T * D * F, 2 * D * F),
        name="down_grads",
    )(gb, hidden)


def feed_kernel(n, hid_ref, wd_ref, after_ref, h_ref, dgu_ref, out_ref, gr_ref, sbuf, rbuf, ss, rs):
    me = lax.axis_index("tensor")
    C, D = after_ref.shape
    F2 = dgu_ref.shape[1]
    greet(n, me)

    def part(t):
        return nn(hid_ref[pl.ds(pl.multiple_of(t * C, C), C), :], wd_ref[...])

    tb, tf = 256, 512

    def tile(j, carry):
        cols = pl.ds(pl.multiple_of(j * tf, tf), tf)
        for i in range(D // tb):
            rows = slice(i * tb, (i + 1) * tb)
            gr_ref[rows, cols] = tn(h_ref[:, rows], dgu_ref[:, cols]).astype(BF)
        return carry

    def filler():
        lax.fori_loop(0, F2 // tf, tile, 0)

    total, copies = reduce_parts(n, me, part, filler, sbuf, rbuf, ss, rs)
    out_ref[...] = (after_ref[...] + total).astype(BF)
    for copy in copies.values():
        copy.wait_send()


def feed_grads(n, hidden, wd, after, h, dgu):
    C, D = after.shape
    T, F2 = dgu.shape
    return pl.pallas_call(
        functools.partial(feed_kernel, n),
        in_specs=[VSPEC] * 5,
        out_specs=[VSPEC] * 2,
        out_shape=[sds((C, D), BF), sds((D, F2), BF)],
        scratch_shapes=reduce_bufs(n, C, D),
        compiler_params=params(collective_id=6, has_side_effects=True),
        cost_estimate=cost(3 * T * D * F2, 6 * D * F2),
        name="feed_grads",
    )(hidden, wd, after, h, dgu)


def gather_kernel(n, ndp, x_in, w_ref, h2_ref, dcq_ref, cb_ref, ca_ref, dkv_ref, ctx_ref,
                  x_ref, da_ref, gr_ref, ksend, krecv, ss, rs, ss2, rs2):
    me = lax.axis_index("tensor")
    C, D = x_in.shape
    W = w_ref.shape[0]
    HD = n * W
    KP = ctx_ref.shape[0]
    greet(n, me)
    gather = Gather(n, me, x_in, lambda t: x_ref.at[t], lambda t, i: x_ref.at[t, pl.ds(i * C // 2, C // 2)], ss, rs)
    gather.start()
    kv = {}
    for d in range(1, n):
        ksend[d - 1] = dkv_ref[me ^ d].astype(BF)
        kv[d] = remote(ksend.at[d - 1], krecv.at[d - 1], ss2.at[d - 1], rs2.at[d - 1], me ^ d)
        kv[d].start()

    def back(t, x):
        da_ref[pl.ds(pl.multiple_of(t * C, C), C), :] = nt(x, w_ref[...]).astype(BF)

    x_ref[me] = x_in[...]
    back(me, x_in[...])
    tf = 256

    def weights(j, carry):
        rows = pl.ds(pl.multiple_of(j * tf, tf), tf)
        h2, cb = h2_ref[:, rows], cb_ref[:, rows]
        for t in range(n):
            gr_ref[rows, t * W : (t + 1) * W] = tn(h2, dcq_ref[t]).astype(BF)
            gr_ref[rows, HD + t * W : HD + (t + 1) * W] = tn(cb, ca_ref[t]).astype(BF)
        return carry

    lax.fori_loop(0, D // tf, weights, 0)
    gather.relay()
    dkv = dkv_ref[me]
    for d in range(1, n):
        kv[d].wait_recv()
        dkv = dkv + krecv[d - 1].astype(F32)
    for half in range(2):
        kvg = tn(ctx_ref[...], dkv[half * KP : (half + 1) * KP].astype(BF)).astype(BF)
        R = kvg.shape[0] // ndp
        for i in range(ndp):
            gr_ref[(2 * i + half) * R : (2 * i + half + 1) * R, 2 * HD :] = kvg[i * R : (i + 1) * R]
    for d in range(1, n):
        gather.wait(d)
        back(me ^ d, x_ref[me ^ d])
    gather.finish()
    for d in range(1, n):
        kv[d].wait_send()


def gather_back(n, ndp, x, w, h2, dcq, cb, ca, dkv, ctx):
    C, D = x.shape
    W = w.shape[0]
    KP = ctx.shape[0]
    return pl.pallas_call(
        functools.partial(gather_kernel, n, ndp),
        in_specs=[VSPEC] * 8,
        out_specs=[VSPEC] * 3,
        out_shape=[sds((n, C, D), BF), sds((n * C, W), BF), sds((D, (2 * n + 1) * W), BF)],
        scratch_shapes=[pltpu.VMEM((n - 1, 2 * KP, W), BF)] * 2
        + [pltpu.SemaphoreType.DMA((links(n),))] * 2
        + [pltpu.SemaphoreType.DMA((n - 1,))] * 2,
        compiler_params=params(collective_id=2, has_side_effects=True),
        cost_estimate=cost(2 * n * C * W * D + 2e10, 8 * C * D),
        name="gather_back",
    )(x, w, h2, dcq, cb, ca, dkv, ctx)


def last_kernel(n, dq_ref, dk_ref, dv_ref, wq_ref, wk_ref, wv_ref, x_ref, da_ref, g_ref, gg_in, h1_ref, sb_ref, at_ref,
                lbuf, gr_ref, sbuf, rbuf, gbuf, gsum, ss, rs, ss2, rs2, ss3, rs3):
    me = lax.axis_index("tensor")
    C, D = x_ref.shape
    greet(n, me)

    def part(t):
        rows = pl.ds(pl.multiple_of(t * C, C), C)
        return nt(dq_ref[rows, :], wq_ref[...]) + nt(dk_ref[rows, :], wk_ref[...]) + nt(dv_ref[rows, :], wv_ref[...])

    W = dq_ref.shape[1]
    tf = 256

    def weights(j, carry):
        rows = pl.ds(pl.multiple_of(j * tf, tf), tf)
        h = h1_ref[:, rows]
        for i, a_ref in enumerate((dq_ref, dk_ref, dv_ref)):
            gr_ref[rows, i * W : (i + 1) * W] = tn(h, a_ref[...]).astype(BF)
        gr_ref[rows, 3 * W : 4 * W] = tn(sb_ref[:, rows], at_ref[...]).astype(BF)
        return carry

    def filler():
        lax.fori_loop(0, D // tf, weights, 0)

    total, copies = reduce_parts(n, me, part, filler, sbuf, rbuf, ss, rs)
    u, inverse = unit(x_ref[...].astype(F32))
    lbuf[me] = (da_ref[...] + norm_back(total, u, inverse, g_ref[...])).astype(BF)
    gather = Gather(
        n, me, lbuf.at[me], lambda t: lbuf.at[t], lambda t, i: lbuf.at[t, pl.ds(i * C // 2, C // 2)], ss2, rs2
    )
    gather.start()
    row = lax.broadcasted_iota(jnp.int32, (8, D), 0)
    gsum[...] = gg_in[...] + jnp.where(row == 2, jnp.sum(total * u, axis=0, keepdims=True), 0.0)
    small = {}
    for d in range(1, n):
        small[d] = remote(gsum, gbuf.at[d - 1], ss3.at[d - 1], rs3.at[d - 1], me ^ d)
        small[d].start()

    gains = gsum[...]
    for d in range(1, n):
        small[d].wait_recv()
        gains = gains + gbuf[d - 1]
    gains = jnp.concatenate([gains, jnp.zeros((120, D), F32)], 0)
    gr_ref[:, 4 * W :] = jnp.transpose(gains).astype(BF)
    gather.relay()
    for d in range(1, n):
        gather.wait(d)
    gather.finish()
    for copy in copies.values():
        copy.wait_send()
    for d in range(1, n):
        small[d].wait_send()


def last(n, dq, dk, dv, wq, wk, wv, x, da, gain, gains, h1, sb, attn):
    C, D = x.shape
    T, W = dq.shape
    return pl.pallas_call(
        functools.partial(last_kernel, n),
        in_specs=[VSPEC] * 13,
        out_specs=[VSPEC] * 2,
        out_shape=[sds((n, C, D), BF), sds((D, 4 * W + 128), BF)],
        scratch_shapes=reduce_bufs(n, C, D)[:2]
        + [pltpu.VMEM((n - 1, 8, D), F32), pltpu.VMEM((8, D), F32)]
        + reduce_bufs(n, C, D)[2:]
        + [pltpu.SemaphoreType.DMA((links(n),))] * 2
        + [pltpu.SemaphoreType.DMA((n - 1,))] * 2,
        compiler_params=params(collective_id=3, has_side_effects=True),
        cost_estimate=cost(6 * T * W * D + 4e10, 8 * T * D),
        name="last",
    )(dq, dk, dv, wq, wk, wv, x, da, gain, gains, h1, sb, attn)


def cross_fwd_kernel(n, ctx, h_ref, x_ref, wq_ref, kv_ref, wo_ref, g_ref, q_ref, o_ref, after_ref, h3_ref):
    _, C, W = q_ref.shape
    KP = kv_ref.shape[1] // 2
    mult = SCALE * LOG2E
    G = lane_group(W)
    per = W // G
    masks = [m.astype(BF) for m in head_masks(1, G)]
    lane = lax.broadcasted_iota(jnp.int32, (C, G), 1) // HEAD_DIM
    valid = lax.broadcasted_iota(jnp.int32, (C, KP), 1) < ctx

    def group(g, carry):
        t = g // per
        cols = pl.ds(pl.multiple_of(g % per * G, G), G) if per > 1 else slice(None)
        q = nn(h_ref[...], wq_ref[t, :, cols]).astype(BF)
        q_ref[t, :, cols] = q
        k, v = kv_ref[t, :KP, cols], kv_ref[t, KP:, cols]
        out = jnp.zeros((C, G), F32)
        for h in range(G // HEAD_DIM):
            s = jnp.where(valid, nt(q * masks[h], k), -1e30)
            p = jnp.exp2((s - jnp.max(s, axis=-1, keepdims=True)) * mult)
            o = nn(p.astype(BF), v) / jnp.sum(p, axis=-1, keepdims=True)
            out = jnp.where(lane == h, o, out)
        o_ref[t, :, cols] = out.astype(BF)
        return carry

    lax.fori_loop(0, n * per, group, 0)
    D = h_ref.shape[1]
    tf = 256

    def project(j, carry):
        cols = pl.ds(pl.multiple_of(j * tf, tf), tf)
        total = nn(o_ref[0], wo_ref[0, :, cols])
        for t in range(1, n):
            total = total + nn(o_ref[t], wo_ref[t, :, cols])
        after_ref[:, cols] = x_ref[:, cols] + total
        return carry

    lax.fori_loop(0, D // tf, project, 0)
    u, _ = unit(after_ref[...])
    h3_ref[...] = (u * g_ref[...]).astype(BF)


def cross_fwd(ctx, h, x, wq, kv, wo, gain):
    C, D = h.shape
    n, W = wq.shape[0], wq.shape[2]
    return pl.pallas_call(
        functools.partial(cross_fwd_kernel, n, ctx),
        in_specs=[VSPEC] * 6,
        out_specs=[VSPEC] * 4,
        out_shape=[sds((n, C, W), BF), sds((n, C, W), BF), sds((C, D), F32), sds((C, D), BF)],
        compiler_params=params(),
        cost_estimate=cost(4 * C * D * n * W + 16 * C * 256 * n * W, 8 * D * n * W),
        name="cross_fwd",
    )(h, x, wq, kv, wo, gain)


def cross_bwd_kernel(n, ctx, dh3_ref, after2_ref, cot_ref, g3_ref, wo_ref, q_ref, kv_ref, wq_ref, after1_ref, g2_ref, bo_in,
                     cb_ref, dq_ref, dkv_ref, da_ref, sb_ref, gg_ref, bo_ref, dh2_ref, ss, rs):
    me = lax.axis_index("tensor")
    _, C, W = q_ref.shape
    KP = kv_ref.shape[1] // 2
    D = da_ref.shape[1]
    mult = SCALE * LOG2E
    G = lane_group(W)
    per = W // G
    masks = [m.astype(BF) for m in head_masks(1, G)]
    lane = lax.broadcasted_iota(jnp.int32, (C, G), 1) // HEAD_DIM
    valid = lax.broadcasted_iota(jnp.int32, (C, KP), 1) < ctx
    greet(n, me)
    gather = Gather(n, me, bo_in, lambda t: bo_ref.at[t], lambda t, i: bo_ref.at[t, pl.ds(i * C // 2, C // 2)], ss, rs)
    gather.start()
    bo_ref[me] = bo_in[...]
    dh3 = dh3_ref[...]
    u3, inv3 = unit(after2_ref[...])
    gain3 = jnp.sum(dh3 * u3, axis=0, keepdims=True)
    da2 = cot_ref[...].astype(F32) + norm_back(dh3, u3, inv3, g3_ref[...])
    da_ref[...] = da2
    cb_ref[...] = da2.astype(BF)

    def group(g, carry):
        t = g // per
        cols = pl.ds(pl.multiple_of(g % per * G, G), G) if per > 1 else slice(None)
        do = nt(cb_ref[...], wo_ref[t, cols, :]).astype(BF)
        q, k, v = q_ref[t, :, cols], kv_ref[t, :KP, cols], kv_ref[t, KP:, cols]
        dq = jnp.zeros((C, G), F32)
        dk = jnp.zeros((KP, G), F32)
        dv = jnp.zeros((KP, G), F32)
        for h in range(G // HEAD_DIM):
            qm = q * masks[h]
            dom = do * masks[h]
            s = jnp.where(valid, nt(qm, k), -1e30)
            p = jnp.exp2((s - jnp.max(s, axis=-1, keepdims=True)) * mult)
            p = p / jnp.sum(p, axis=-1, keepdims=True)
            dp = nt(dom, v)
            ds = (p * (dp - jnp.sum(p * dp, axis=-1, keepdims=True))).astype(BF)
            dq = jnp.where(lane == h, nn(ds, k), dq)
            dk = dk + tn(ds, qm)
            dv = dv + tn(p.astype(BF), dom)
        dq_ref[t, :, cols] = (dq * SCALE).astype(BF)
        dkv_ref[t, :KP, cols] = dk * SCALE
        dkv_ref[t, KP:, cols] = dv
        return carry

    lax.fori_loop(0, n * per, group, 0)
    gather.relay()
    tf = 256

    def project(j, carry):
        cols = pl.ds(pl.multiple_of(j * tf, tf), tf)
        total = nt(dq_ref[0], wq_ref[0, cols, :])
        for t in range(1, n):
            total = total + nt(dq_ref[t], wq_ref[t, cols, :])
        dh2_ref[:, cols] = total
        return carry

    lax.fori_loop(0, D // tf, project, 0)
    dh2 = dh2_ref[...]
    u2, inv2 = unit(after1_ref[...])
    gain2 = jnp.sum(dh2 * u2, axis=0, keepdims=True)
    da1 = da_ref[...] + norm_back(dh2, u2, inv2, g2_ref[...])
    da_ref[...] = da1
    sb_ref[...] = da1.astype(BF)
    row = lax.broadcasted_iota(jnp.int32, (8, D), 0)
    gg_ref[...] = jnp.where(row == 0, gain3, 0.0) + jnp.where(row == 1, gain2, 0.0)
    for d in range(1, n):
        gather.wait(d)
    gather.finish()


def cross_bwd(ctx, dh3, after2, cot, g3, wo, q, kv, wq, after1, g2, bo):
    C, D = after2.shape
    n, W = wq.shape[0], wq.shape[2]
    return pl.pallas_call(
        functools.partial(cross_bwd_kernel, n, ctx),
        in_specs=[VSPEC] * 11,
        out_specs=[VSPEC] * 7,
        out_shape=[
            sds((C, D), BF),
            sds((n, C, W), BF),
            sds(kv.shape, F32),
            sds((C, D), F32),
            sds((C, D), BF),
            sds((8, D), F32),
            sds((n, C, D), BF),
        ],
        scratch_shapes=[pltpu.VMEM((C, D), F32)] + [pltpu.SemaphoreType.DMA((links(n),))] * 2,
        compiler_params=params(collective_id=7, has_side_effects=True),
        cost_estimate=cost(4 * C * D * n * W + 40 * C * 256 * n * W, 8 * D * n * W),
        name="cross_bwd",
    )(dh3, after2, cot, g3, wo, q, kv, wq, after1, g2, bo)


def swap_sum_kernel(n, a_ref, o_ref, rbuf, ss, rs):
    me = lax.axis_index("tensor")
    greet(n, me)
    copies = {}
    for d in range(1, n):
        copies[d] = remote(a_ref.at[me ^ d], rbuf.at[d - 1], ss.at[d - 1], rs.at[d - 1], me ^ d)
        copies[d].start()
    total = a_ref[me].astype(F32)
    for d in range(1, n):
        copies[d].wait_recv()
        total = total + rbuf[d - 1].astype(F32)
    o_ref[...] = total
    for d in range(1, n):
        copies[d].wait_send()


def swap_sum(a):
    n, R, N = a.shape
    return pl.pallas_call(
        functools.partial(swap_sum_kernel, n),
        in_specs=[VSPEC],
        out_specs=VSPEC,
        out_shape=sds((R, N), F32),
        scratch_shapes=[pltpu.VMEM((n - 1, R, N), BF)] + [pltpu.SemaphoreType.DMA((n - 1,))] * 2,
        compiler_params=params(collective_id=5, has_side_effects=True),
        cost_estimate=cost(n * R * N, 8 * R * N),
        name="swap_sum",
    )(a)


def body(latents, context, cotangent, g1, wq, wk, wv, wo, g2, xq, xk, xv, xo, g3, wg, wu, wd, n, ndp):
    _, T, D = latents.shape
    ctx = context.shape[1]
    W = wq.shape[1]
    F = wg.shape[1]
    C = T // n
    me = lax.axis_index("tensor")
    x = latents.reshape(T, D)
    gb = cotangent.reshape(T, D)
    ctx_rows = context.reshape(ctx, -1)
    KP = -(-ctx // 16) * 16
    cs, sn = tables(T, lane_group(W))
    g1, g2, g3 = (g.reshape(1, D) for g in (g1, g2, g3))
    own = lambda a: lax.dynamic_slice_in_dim(a, me * C, C, 0)

    ctx_pad = jnp.pad(ctx_rows, ((0, KP - ctx), (0, 0)))
    h1, q, k, v, attn, lse, xq_all, xo_all, kv_all = front(n, ctx, x, g1, wq, wk, wv, cs, sn, xq, xo, ctx_pad, xk, xv)
    x_own = own(x)
    after1, h2 = out_rs(n, attn, wo, x_own, g2)
    cq, cattn, after2, h3_own = cross_fwd(ctx, h2, after1, xq_all, kv_all, xo_all, g3)
    h3, hidden, dgu, dh3 = ff(n, h3_own, gb, wg, wu, wd)
    h3 = h3.reshape(T, D)

    def scatter(a, axis):
        return lax.psum_scatter(a, axis, scatter_dimension=0, tiled=True)

    down_part = down_grads(gb, hidden)
    down_part, dgu = lax.optimization_barrier((down_part, dgu))
    down_grad = scatter(down_part, "dp")
    out_own, gu_part = feed_grads(n, hidden, wd, after2, h3, dgu)
    dh3, gu_part = lax.optimization_barrier((dh3, gu_part))
    gu_grad = scatter(gu_part, "dp")

    cb, dcq, dckv, dafter1, sb_own, gains, block_out = cross_bwd(
        ctx, dh3, after2, own(gb), g3, xo_all, cq, kv_all, xq_all, after1, g2, out_own
    )
    sb, dattn, cross_grads = gather_back(n, ndp, sb_own, wo, h2, dcq, cb, cattn, dckv, ctx_pad)
    sb = sb.reshape(T, D)
    dq, dk, dv = attn_bwd(q, k, v, attn, dattn, lse, cs, sn)
    dq, down_grad = lax.optimization_barrier((dq, down_grad))
    latent_grad, self_grads = last(n, dq, dk, dv, wq, wk, wv, x_own, dafter1, g1, gains, h1, sb, attn)
    self_grads = scatter(self_grads, "dp")

    cross_grads = scatter(cross_grads, "dp")
    cross_grads, gu_grad = lax.optimization_barrier((cross_grads, gu_grad))
    gu_grad = gu_grad.astype(F32)
    gate_grad, up_grad, down_grad = gu_grad[:, :F], gu_grad[:, F:], down_grad.astype(F32).T
    rows = cross_grads.shape[0]
    kv_grads = cross_grads[:, 2 * n * W :].reshape(2, rows // 2, W).astype(F32)
    cross_grads = cross_grads[:, : 2 * n * W].reshape(rows, 2, n, W).transpose(2, 0, 1, 3).reshape(n, rows, 2 * W)
    cross_grads = swap_sum(cross_grads)
    cross_grads, self_grads = lax.optimization_barrier((cross_grads, self_grads))
    xq_grad, xo_grad = cross_grads[:, :W], cross_grads[:, W:].T
    self_grads = self_grads.astype(F32)
    gains = self_grads[:, 4 * W :]
    return (
        block_out.reshape(1, T, D),
        latent_grad.astype(F32).reshape(1, T, D),
        gains[:, 2],
        self_grads[:, :W],
        self_grads[:, W : 2 * W],
        self_grads[:, 2 * W : 3 * W],
        self_grads[:, 3 * W : 4 * W].T,
        gains[:, 1],
        xq_grad,
        kv_grads[0],
        kv_grads[1],
        xo_grad,
        gains[:, 0],
        gate_grad,
        up_grad,
        down_grad,
    )


def solution(mesh):
    tokens = P("dp", None, None)
    cols = P(None, "tensor")
    rows = P("tensor", None)
    return jax.shard_map(
        functools.partial(body, n=mesh.shape["tensor"], ndp=mesh.shape["dp"]),
        mesh=mesh,
        in_specs=(tokens, tokens, tokens, P(), cols, cols, cols, rows, P(), cols, cols, cols, rows, P(), cols, cols, rows),
        out_specs=(
            tokens,
            tokens,
            P("dp"),
            P("dp", "tensor"),
            P("dp", "tensor"),
            P("dp", "tensor"),
            P("tensor", "dp"),
            P("dp"),
            P("dp", "tensor"),
            P("dp", "tensor"),
            P("dp", "tensor"),
            P("tensor", "dp"),
            P("dp"),
            P("dp", "tensor"),
            P("dp", "tensor"),
            P("tensor", "dp"),
        ),
        check_vma=False,
    )
```

```python
import functools

import jax
import jax.numpy as jnp
from jax import lax
from jax.experimental import pallas as pl
from jax.experimental.pallas import tpu as pltpu
from jax.sharding import PartitionSpec as P

HEAD_DIM = 64
HALF = HEAD_DIM // 2
EPS = 1e-05
BF = jnp.bfloat16
F32 = jnp.float32
LOG2E = 1.4426950408889634
SCALE = HEAD_DIM**-0.5
VMEM_BYTES = 60 << 20
MESH_ID = pl.DeviceIdType.MESH
VSPEC = pl.BlockSpec(memory_space=pltpu.VMEM)
ANYSPEC = pl.BlockSpec(memory_space=pl.ANY)


def nn(a, b):
    return lax.dot_general(a, b, (((1,), (0,)), ((), ())), preferred_element_type=F32)


def nt(a, b):
    return lax.dot_general(a, b, (((1,), (1,)), ((), ())), preferred_element_type=F32)


def tn(a, b):
    return lax.dot_general(a, b, (((0,), (0,)), ((), ())), preferred_element_type=F32)


def sds(shape, dtype):
    return jax.ShapeDtypeStruct(shape, dtype)


def params(**kw):
    return pltpu.CompilerParams(vmem_limit_bytes=VMEM_BYTES, **kw)


def cost(flops, nbytes, trans=0):
    return pl.CostEstimate(flops=1000, bytes_accessed=1000, transcendentals=0)


def unit(x):
    center = x - jnp.mean(x, axis=-1, keepdims=True)
    inverse = lax.rsqrt(jnp.mean(center * center, axis=-1, keepdims=True) + EPS)
    return center * inverse, inverse


def norm_back(grad, u, inverse, gain):
    e = grad * gain
    mean_e = jnp.mean(e, axis=-1, keepdims=True)
    mean_p = jnp.mean(e * u, axis=-1, keepdims=True)
    return inverse * (e - mean_e - u * mean_p)


def lane_group(width):
    return 128 if width % 128 == 0 else width


def tables(length, group):
    freq = 10000.0 ** (-jnp.arange(HALF, dtype=F32) / HALF)
    angles = jnp.arange(length, dtype=F32)[:, None] * freq[None, :]
    c, s = jnp.cos(angles), jnp.sin(angles)
    reps = group // HEAD_DIM
    return jnp.tile(jnp.concatenate([c, c], 1), (1, reps)), jnp.tile(jnp.concatenate([-s, s], 1), (1, reps))


def turned(a):
    width = a.shape[-1]
    lane = lax.broadcasted_iota(jnp.int32, a.shape, 1) % HEAD_DIM
    return jnp.where(lane < HALF, pltpu.roll(a, width - HALF, 1), pltpu.roll(a, HALF, 1))


def head_masks(rows, group):
    lane = lax.broadcasted_iota(jnp.int32, (rows, group), 1) // HEAD_DIM
    return [jnp.where(lane == h, 1.0, 0.0) for h in range(group // HEAD_DIM)]


def front_kernel(n, ctx, x_ref, g_ref, wq_ref, wk_ref, wv_ref, c_ref, s_ref, xq_ref, xo_ref, ctx_ref, xk_ref, xv_ref,
                 h_ref, q_ref, k_ref, v_ref, o_ref, lse_ref, xqa_ref, xoa_ref, kva_ref,
                 kv_own, sq, rq, so, ro, sk, rk, fsq, frq, fso, fro, local):
    me = lax.axis_index("tensor")
    dp = lax.axis_index("dp")
    core = dp % 2
    partner = dp + 1 - 2 * core
    T, D = x_ref.shape
    W = q_ref.shape[1]
    KP = ctx_ref.shape[0]
    greet(n, me, [partner])

    rows_q = pl.ds(pl.multiple_of(core * (D // 2), 16), D // 2)
    rows_o = pl.ds(pl.multiple_of(core * (W // 2), 16), W // 2)
    def quarter(ref, rows):
        return lambda t, i: ref.at[t, pl.ds(pl.multiple_of(core * (rows // 2) + i * (rows // 4), 16), rows // 4)]

    gq = Gather(n, me, xq_ref.at[rows_q], lambda t: xqa_ref.at[t, rows_q], quarter(xqa_ref, D), sq, rq)
    go = Gather(n, me, xo_ref.at[rows_o], lambda t: xoa_ref.at[t, rows_o], quarter(xoa_ref, W), so, ro)
    gk = Gather(n, me, kv_own, lambda t: kva_ref.at[t], lambda t, i: kva_ref.at[t, pl.ds(i * KP, KP)], sk, rk)
    gq.start()
    go.start()
    own = [
        pltpu.make_async_copy(xq_ref, xqa_ref.at[me], local.at[0]),
        pltpu.make_async_copy(xo_ref, xoa_ref.at[me], local.at[1]),
    ]
    for copy in own:
        copy.start()
    kv_own[:KP] = nn(ctx_ref[...], xk_ref[...]).astype(BF)
    kv_own[KP:] = nn(ctx_ref[...], xv_ref[...]).astype(BF)
    gk.start()
    kva_ref[me] = kv_own[...]

    tb = 256
    reps = W // c_ref.shape[1]

    def project(i, carry):
        rows = pl.ds(pl.multiple_of(i * tb, tb), tb)
        u, _ = unit(x_ref[rows, :].astype(F32))
        h = (u * g_ref[...]).astype(BF)
        h_ref[rows, :] = h
        c = jnp.concatenate([c_ref[rows, :]] * reps, 1)
        s = jnp.concatenate([s_ref[rows, :]] * reps, 1)
        for w_ref, out_ref in ((wq_ref, q_ref), (wk_ref, k_ref)):
            a = nn(h, w_ref[...])
            out_ref[rows, :] = (a * c + turned(a) * s).astype(BF)
        v_ref[rows, :] = nn(h, wv_ref[...]).astype(BF)
        return carry

    lax.fori_loop(0, T // tb, project, 0)
    gq.relay()

    G = lane_group(W)
    mult = SCALE * LOG2E
    masks = [m.astype(BF) for m in head_masks(1, G)]
    lane = lax.broadcasted_iota(jnp.int32, (tb, G), 1) // HEAD_DIM
    stat_lane = lax.broadcasted_iota(jnp.int32, (tb, 128), 1)

    def heads(g, carry):
        cols = pl.ds(pl.multiple_of(g * G, G), G) if G < W else slice(None)
        k, v = k_ref[:, cols], v_ref[:, cols]

        def block(i, inner):
            rows = pl.ds(pl.multiple_of(i * tb, tb), tb)
            q = q_ref[rows, cols]
            out = jnp.zeros((tb, G), F32)
            stats = jnp.zeros((tb, 128), F32)
            for h in range(G // HEAD_DIM):
                s = nt(q * masks[h], k)
                top = jnp.max(s, axis=-1, keepdims=True) * mult
                p = jnp.exp2(s * mult - top)
                total = jnp.sum(p, axis=-1, keepdims=True)
                o = nn(p.astype(BF), v) / total
                out = jnp.where(lane == h, o, out)
                stats = jnp.where(stat_lane == h, top + jnp.log2(total), stats)
            o_ref[rows, cols] = out.astype(BF)
            lse_ref[g, :, rows] = jnp.transpose(stats)[:8]
            return inner

        return lax.fori_loop(0, T // tb, block, carry)

    lax.fori_loop(0, W // G, heads, 0)

    go.relay()
    gk.relay()
    passed = []
    for gather, ref, rows, send, recv in ((gq, xqa_ref, rows_q, fsq, frq), (go, xoa_ref, rows_o, fso, fro)):
        for d in range(1, n):
            gather.wait(d)
            block = ref.at[me ^ d, rows]
            copy = to_dp(block, block, send.at[d - 1], recv.at[d - 1], partner)
            copy.start()
            passed.append(copy)
    for copy in own:
        copy.wait()
    for d in range(1, n):
        gk.wait(d)
    for copy in passed:
        copy.wait_recv()
    for copy in (gq, go, gk):
        copy.finish()
    for copy in passed:
        copy.wait_send()


def front(n, ctx, x, gain, wq, wk, wv, cs, sn, xq, xo, ctx_rows, xk, xv):
    T, D = x.shape
    W = wq.shape[1]
    KP = ctx_rows.shape[0]
    groups = W // lane_group(W)
    link, pair = pltpu.SemaphoreType.DMA((links(n),)), pltpu.SemaphoreType.DMA((n - 1,))
    return pl.pallas_call(
        functools.partial(front_kernel, n, ctx),
        in_specs=[VSPEC] * 12,
        out_specs=[VSPEC] * 6 + [ANYSPEC] * 2 + [VSPEC],
        out_shape=[sds((T, D), BF)]
        + [sds((T, W), BF)] * 4
        + [sds((groups, 8, T), F32), sds((n, D, W), BF), sds((n, W, D), BF), sds((n, 2 * KP, W), BF)],
        scratch_shapes=[pltpu.VMEM((2 * KP, W), BF)] + [link] * 6 + [pair] * 4 + [pltpu.SemaphoreType.DMA((2,))],
        compiler_params=params(collective_id=4, has_side_effects=True),
        cost_estimate=cost(6 * T * D * W, 4 * T * D + 6 * D * W + 6 * T * W),
        name="front",
    )(x, gain, wq, wk, wv, cs, sn, xq, xo, ctx_rows, xk, xv)


def greet(n, me, dps=()):
    sem = pltpu.get_barrier_semaphore()
    for d in range(1, n):
        pl.semaphore_signal(sem, 1, device_id={"tensor": me ^ d}, device_id_type=MESH_ID)
    for dp in dps:
        pl.semaphore_signal(sem, 1, device_id={"dp": dp}, device_id_type=MESH_ID)
    pl.semaphore_wait(sem, n - 1 + len(dps))


def to_dp(src, dst, send, recv, target):
    return pltpu.make_async_remote_copy(src, dst, send, recv, device_id={"dp": target}, device_id_type=MESH_ID)


def remote(src, dst, send, recv, target):
    return pltpu.make_async_remote_copy(src, dst, send, recv, device_id={"tensor": target}, device_id_type=MESH_ID)


def links(n):
    return 4 if n == 4 else n - 1


class Gather:
    def __init__(self, n, me, src, slot, half, ss, rs):
        self.n, self.me, self.half, self.ss, self.rs = n, me, half, ss, rs
        self.copies = {
            d: remote(src, slot(me), ss.at[d - 1], rs.at[d - 1], me ^ d) for d in (range(1, n) if n != 4 else (1, 2))
        }
        self.passed = []

    def start(self):
        for copy in self.copies.values():
            copy.start()

    def relay(self):
        if self.n == 4:
            for i, d in enumerate((1, 2)):
                self.copies[d].wait_recv()
                block = self.half(self.me ^ d, i)
                copy = remote(block, block, self.ss.at[2 + i], self.rs.at[2 + i], self.me ^ (3 - d))
                copy.start()
                self.passed.append(copy)

    def wait(self, d):
        if self.n != 4:
            self.copies[d].wait_recv()
        elif d == 3:
            for copy in self.passed:
                copy.wait_recv()

    def finish(self):
        for copy in (*self.copies.values(), *self.passed):
            copy.wait_send()


def reduce_bufs(n, C, D):
    shape = (6, C, D // 2) if n == 4 else (n - 1, C, D)
    return [pltpu.VMEM(shape, BF)] * 2 + [pltpu.SemaphoreType.DMA((shape[0],))] * 2


def reduce_parts(n, me, part, filler, sbuf, rbuf, ss, rs):
    copies = {}

    def send(i, val, d):
        sbuf[i] = val.astype(BF)
        copies[i] = remote(sbuf.at[i], rbuf.at[i], ss.at[i], rs.at[i], me ^ d)
        copies[i].start()

    def got(i):
        copies[i].wait_recv()
        return rbuf[i].astype(F32)

    if n == 4:
        across = part(me ^ 3)
        H = across.shape[1] // 2
        send(0, across[:, :H], 1)
        send(2, across[:, H:], 2)
        one = part(me ^ 1)
        send(1, one[:, :H], 1)
        two = part(me ^ 2)
        send(3, two[:, H:], 2)
        total = part(me)
        filler()
        send(4, two[:, :H] + got(0), 2)
        send(5, one[:, H:] + got(2), 1)
        total = jnp.concatenate([total[:, :H] + got(1) + got(4), total[:, H:] + got(3) + got(5)], 1)
    else:
        for d in reversed(range(1, n)):
            send(d - 1, part(me ^ d), d)
        total = part(me)
        filler()
        for d in range(1, n):
            total = total + got(d - 1)
    return total, copies


class ShardSum:
    def __init__(self, n, me, a, sbuf, rbuf, ss, rs):
        self.n, self.me, self.a, self.sbuf, self.rbuf, self.ss, self.rs = n, me, a, sbuf, rbuf, ss, rs
        self.copies = {}

    def send(self, i, src, d):
        self.copies[i] = remote(src, self.rbuf.at[i], self.ss.at[i], self.rs.at[i], self.me ^ d)
        self.copies[i].start()

    def got(self, i):
        self.copies[i].wait_recv()
        return self.rbuf[i].astype(F32)

    def halves(self, d):
        H = self.a.shape[1] // 2
        return self.a.at[self.me ^ d, pl.ds(0, H)], self.a.at[self.me ^ d, pl.ds(H, H)]

    def start(self):
        if self.n == 4:
            self.send(0, self.halves(3)[0], 1)
            self.send(2, self.halves(3)[1], 2)
            self.send(1, self.halves(1)[0], 1)
            self.send(3, self.halves(2)[1], 2)
        else:
            for d in range(1, self.n):
                self.send(d - 1, self.a.at[self.me ^ d], d)

    def middle(self):
        if self.n == 4:
            self.sbuf[0] = (self.halves(2)[0][...].astype(F32) + self.got(0)).astype(BF)
            self.send(4, self.sbuf.at[0], 2)
            self.sbuf[1] = (self.halves(1)[1][...].astype(F32) + self.got(2)).astype(BF)
            self.send(5, self.sbuf.at[1], 1)

    def store(self, out_ref):
        if self.n == 4:
            H = self.a.shape[1] // 2
            own = self.halves(0)
            out_ref[:H] = (own[0][...].astype(F32) + self.got(1) + self.got(4)).astype(BF)
            out_ref[H:] = (own[1][...].astype(F32) + self.got(3) + self.got(5)).astype(BF)
        else:
            total = self.a[self.me].astype(F32)
            for d in range(1, self.n):
                total = total + self.got(d - 1)
            out_ref[...] = total.astype(BF)
        for copy in self.copies.values():
            copy.wait_send()


def out_rs_kernel(n, a_ref, w_ref, x_ref, g_ref, after_ref, h_ref, sbuf, rbuf, ss, rs):
    me = lax.axis_index("tensor")
    C = x_ref.shape[0]
    greet(n, me)

    def part(t):
        return nn(a_ref[pl.ds(pl.multiple_of(t * C, C), C), :], w_ref[...])

    total, copies = reduce_parts(n, me, part, lambda: None, sbuf, rbuf, ss, rs)
    after = x_ref[...].astype(F32) + total
    after_ref[...] = after
    u, _ = unit(after)
    h_ref[...] = (u * g_ref[...]).astype(BF)
    for copy in copies.values():
        copy.wait_send()


def out_rs(n, a, w, x, gain):
    C, D = x.shape
    T, W = a.shape
    return pl.pallas_call(
        functools.partial(out_rs_kernel, n),
        in_specs=[VSPEC] * 4,
        out_specs=[VSPEC] * 2,
        out_shape=[sds((C, D), F32), sds((C, D), BF)],
        scratch_shapes=reduce_bufs(n, C, D),
        compiler_params=params(collective_id=0, has_side_effects=True),
        cost_estimate=cost(2 * T * W * D + 2e10, 8 * C * D),
        name="out_rs",
    )(a, w, x, gain)


def ff_kernel(n, h_in, gb_hbm, wg_hbm, wu_hbm, wd_hbm, h_ref, hid_ref, dgu_ref, dh_ref,
              gb_ref, wg_ref, wu_ref, wd_ref, sbuf, rbuf, ss, rs, ss2, rs2, ls):
    me = lax.axis_index("tensor")
    C, D = h_in.shape
    F = wg_ref.shape[1]
    loads = [
        pltpu.make_async_copy(src, dst, ls.at[i])
        for i, (src, dst) in enumerate(((wg_hbm, wg_ref), (wu_hbm, wu_ref), (wd_hbm, wd_ref), (gb_hbm, gb_ref)))
    ]
    for c in loads:
        c.start()
    greet(n, me)
    gather = Gather(n, me, h_in, lambda t: h_ref.at[t], lambda t, i: h_ref.at[t, pl.ds(i * C // 2, C // 2)], ss, rs)
    gather.start()
    h_ref[me] = h_in[...]
    for c in loads:
        c.wait()
    tf = 256

    def chunk(t, store):
        rows = pl.ds(pl.multiple_of(t * C, C), C)
        h = h_ref[t]
        gb = gb_ref[rows, :]

        def tile(j, carry):
            cols = pl.ds(pl.multiple_of(j * tf, tf), tf)
            gate = nn(h, wg_ref[:, cols])
            up = nn(h, wu_ref[:, cols])
            dhid = nt(gb, wd_ref[cols, :])
            sig = 1.0 / (1.0 + jnp.exp(-gate))
            act = gate * sig
            hid_ref[rows, cols] = (act * up).astype(BF)
            dgu_ref[rows, cols] = (dhid * up * (sig * (1.0 + gate * (1.0 - sig)))).astype(BF)
            dgu_ref[rows, pl.ds(pl.multiple_of(F + j * tf, tf), tf)] = (dhid * act).astype(BF)
            return carry

        lax.fori_loop(0, F // tf, tile, 0)

        def back(j, carry):
            out = pl.ds(pl.multiple_of(j * tf, tf), tf)
            store(out, nt(dgu_ref[rows, :F], wg_ref[out, :]) + nt(dgu_ref[rows, F:], wu_ref[out, :]))
            return carry

        lax.fori_loop(0, D // tf, back, 0)

    def store_own(cols, val):
        dh_ref[:, cols] = val

    chunk(me, store_own)
    gather.relay()
    copies = {}
    for d in range(1, n):
        t = me ^ d
        gather.wait(d)

        def store_sent(cols, val):
            sbuf[d - 1, :, cols] = val.astype(BF)

        chunk(t, store_sent)
        copies[d] = remote(sbuf.at[d - 1], rbuf.at[d - 1], ss2.at[d - 1], rs2.at[d - 1], t)
        copies[d].start()
    gather.finish()
    for d in range(1, n):
        copies[d].wait_recv()
        dh_ref[...] += rbuf[d - 1].astype(F32)
    for d in range(1, n):
        copies[d].wait_send()


def ff(n, h, gb, wg, wu, wd):
    C, D = h.shape
    T = gb.shape[0]
    F = wg.shape[1]
    return pl.pallas_call(
        functools.partial(ff_kernel, n),
        in_specs=[VSPEC] + [ANYSPEC] * 4,
        out_specs=[VSPEC] * 4,
        out_shape=[sds((n, C, D), BF), sds((T, F), BF), sds((T, 2 * F), BF), sds((C, D), F32)],
        scratch_shapes=[
            pltpu.VMEM((T, D), BF),
            pltpu.VMEM((D, F), BF),
            pltpu.VMEM((D, F), BF),
            pltpu.VMEM((F, D), BF),
            pltpu.VMEM((n - 1, C, D), BF),
            pltpu.VMEM((n - 1, C, D), BF),
        ]
        + [pltpu.SemaphoreType.DMA((links(n),))] * 2
        + [pltpu.SemaphoreType.DMA((n - 1,))] * 2
        + [pltpu.SemaphoreType.DMA((4,))],
        compiler_params=params(collective_id=1, has_side_effects=True),
        cost_estimate=cost(10 * T * D * F + 3e10, 6 * D * F + 8 * T * D),
        name="ff",
    )(h, gb, wg, wu, wd)


def down_kernel(gb_ref, hid_ref, o_ref):
    gb = gb_ref[...]
    tf = 512 if hid_ref.shape[1] % 512 == 0 else 256

    def down(j, carry):
        cols = pl.ds(pl.multiple_of(j * tf, tf), tf)
        o_ref[:, cols] = tn(gb, hid_ref[:, cols]).astype(BF)
        return carry

    lax.fori_loop(0, hid_ref.shape[1] // tf, down, 0)


def down_grads(gb, hidden):
    T, D = gb.shape
    F = hidden.shape[1]
    tb = 256
    return pl.pallas_call(
        down_kernel,
        grid=(D // tb,),
        in_specs=[
            pl.BlockSpec((T, tb), lambda i: (0, i)),
            pl.BlockSpec(hidden.shape, lambda i: (0, 0), pipeline_mode=pl.Buffered(1)),
        ],
        out_specs=pl.BlockSpec((tb, F), lambda i: (i, 0)),
        out_shape=sds((D, F), BF),
        compiler_params=params(),
        cost_estimate=cost(2 * T * D * F, 2 * D * F),
        name="down_grads",
    )(gb, hidden)


def feed_kernel(n, hid_ref, wd_ref, after_ref, h_ref, dgu_ref, out_ref, gr_ref, sbuf, rbuf, ss, rs):
    me = lax.axis_index("tensor")
    C, D = after_ref.shape
    F2 = dgu_ref.shape[1]
    greet(n, me)

    def part(t):
        return nn(hid_ref[pl.ds(pl.multiple_of(t * C, C), C), :], wd_ref[...])

    tb, tf = 256, 512

    def tile(j, carry):
        cols = pl.ds(pl.multiple_of(j * tf, tf), tf)
        for i in range(D // tb):
            rows = slice(i * tb, (i + 1) * tb)
            gr_ref[rows, cols] = tn(h_ref[:, rows], dgu_ref[:, cols]).astype(BF)
        return carry

    def filler():
        lax.fori_loop(0, F2 // tf, tile, 0)

    total, copies = reduce_parts(n, me, part, filler, sbuf, rbuf, ss, rs)
    out_ref[...] = (after_ref[...] + total).astype(BF)
    for copy in copies.values():
        copy.wait_send()


def feed_grads(n, hidden, wd, after, h, dgu):
    C, D = after.shape
    T, F2 = dgu.shape
    return pl.pallas_call(
        functools.partial(feed_kernel, n),
        in_specs=[VSPEC] * 5,
        out_specs=[VSPEC] * 2,
        out_shape=[sds((C, D), BF), sds((D, F2), BF)],
        scratch_shapes=reduce_bufs(n, C, D),
        compiler_params=params(collective_id=6, has_side_effects=True),
        cost_estimate=cost(3 * T * D * F2, 6 * D * F2),
        name="feed_grads",
    )(hidden, wd, after, h, dgu)


def gather_kernel(n, ndp, x_in, w_ref, h2_ref, dcq_ref, cb_ref, ca_ref, dkv_ref, ctx_ref, x_ref, da_ref, gr_ref, kv_ref,
                  buf, other, ksend, krecv, ss, rs, ss2, rs2, pair):
    me = lax.axis_index("tensor")
    dp = lax.axis_index("dp")
    core = dp % 2
    partner = dp + 1 - 2 * core
    C, D = x_in.shape
    W = w_ref.shape[0]
    KP = ctx_ref.shape[0]
    R = D // ndp
    greet(n, me, [partner])
    gather = Gather(n, me, x_in, lambda t: x_ref.at[t], lambda t, i: x_ref.at[t, pl.ds(i * C // 2, C // 2)], ss, rs)
    gather.start()
    kv = {}
    for d in range(1, n):
        ksend[d - 1] = dkv_ref[me ^ d].astype(BF)
        kv[d] = remote(ksend.at[d - 1], krecv.at[d - 1], ss2.at[d - 1], rs2.at[d - 1], me ^ d)
        kv[d].start()

    def back(t, x):
        da_ref[pl.ds(pl.multiple_of(t * C, C), C), :] = nt(x, w_ref[...]).astype(BF)

    x_ref[me] = x_in[...]
    back(me, x_in[...])

    for j in range(ndp // 2):
        h2, cb = h2_ref[:, 2 * R * j : 2 * R * (j + 1)], cb_ref[:, 2 * R * j : 2 * R * (j + 1)]

        def weights(t, carry):
            for i, (a, b) in enumerate(((h2, dcq_ref[t]), (cb, ca_ref[t]))):
                res = tn(a, b).astype(BF)
                for c in range(2):
                    buf[c, t, j * R : (j + 1) * R, i * W : (i + 1) * W] = res[c * R : (c + 1) * R]
            return carry

        lax.fori_loop(0, n, weights, 0)
    swap = to_dp(buf.at[1 - core], other, pair.at[0], pair.at[1], partner)
    swap.start()
    gather.relay()
    dkv = dkv_ref[me]
    for d in range(1, n):
        kv[d].wait_recv()
        dkv = dkv + krecv[d - 1].astype(F32)
    for half in range(2):
        kvg = tn(ctx_ref[...], dkv[half * KP : (half + 1) * KP].astype(BF)).astype(BF)
        S = kvg.shape[0] // ndp
        for i in range(ndp):
            kv_ref[(2 * i + half) * S : (2 * i + half + 1) * S] = kvg[i * S : (i + 1) * S]
    for d in range(1, n):
        gather.wait(d)
        back(me ^ d, x_ref[me ^ d])
    swap.wait_recv()

    def add(t, carry):
        gr_ref[t] = (buf[core, t].astype(F32) + other[t].astype(F32)).astype(BF)
        return carry

    lax.fori_loop(0, n, add, 0)
    gather.finish()
    for d in range(1, n):
        kv[d].wait_send()
    swap.wait_send()


def gather_back(n, ndp, x, w, h2, dcq, cb, ca, dkv, ctx):
    C, D = x.shape
    W = w.shape[0]
    KP = ctx.shape[0]
    half = (n, D // 2, 2 * W)
    return pl.pallas_call(
        functools.partial(gather_kernel, n, ndp),
        in_specs=[VSPEC] * 8,
        out_specs=[VSPEC] * 4,
        out_shape=[sds((n, C, D), BF), sds((n * C, W), BF), sds(half, BF), sds((2 * ctx.shape[1], W), BF)],
        scratch_shapes=[pltpu.VMEM((2, *half), BF), pltpu.VMEM(half, BF)]
        + [pltpu.VMEM((n - 1, 2 * KP, W), BF)] * 2
        + [pltpu.SemaphoreType.DMA((links(n),))] * 2
        + [pltpu.SemaphoreType.DMA((n - 1,))] * 2
        + [pltpu.SemaphoreType.DMA((2,))],
        compiler_params=params(collective_id=2, has_side_effects=True),
        cost_estimate=cost(2 * n * C * W * D + 2e10, 8 * C * D),
        name="gather_back",
    )(x, w, h2, dcq, cb, ca, dkv, ctx)


def attn_bwd_kernel(n, q_ref, k_ref, v_ref, o_ref, do_ref, lse_ref, c_ref, s_ref, h_ref, sb_ref, kv_ref, a_ref,
                    dq_ref, dk_ref, dv_ref, gr_ref, x_ref, dk_acc, dv_acc, kt_ref, sbuf, rbuf, ss, rs):
    me = lax.axis_index("tensor")
    T, W = q_ref.shape
    G = lane_group(W)
    qb = 256
    mult = SCALE * LOG2E
    nh = G // HEAD_DIM
    greet(n, me)
    shards = ShardSum(n, me, a_ref, sbuf, rbuf, ss, rs)
    shards.start()
    masks = [m.astype(BF) for m in head_masks(1, G)]
    head_rows = jnp.where(
        lax.broadcasted_iota(jnp.int32, (16, G), 0) == lax.broadcasted_iota(jnp.int32, (16, G), 1) // HEAD_DIM, 1.0, 0.0
    ).astype(BF)

    def heads(g, outer):
        cols = pl.ds(pl.multiple_of(g * G, G), G) if G < W else slice(None)
        k, v = k_ref[:, cols], v_ref[:, cols]
        kt_ref[...] = jnp.transpose(k.astype(F32)).astype(BF)
        dk_acc[...] = jnp.zeros_like(dk_acc)
        dv_acc[...] = jnp.zeros_like(dv_acc)

        def block(i, carry):
            rows = pl.ds(pl.multiple_of(i * qb, qb), qb)
            q = q_ref[rows, cols]
            do = do_ref[rows, cols]
            prod = do.astype(F32) * o_ref[rows, cols].astype(F32)
            high = prod.astype(BF)
            delta = nt(head_rows, high) + nt(head_rows, (prod - high.astype(F32)).astype(BF))
            lse = lse_ref[g, :, rows]
            parts = []
            for h in range(nh):
                qm = q * masks[h]
                dom = do * masks[h]
                st = nt(k, qm)
                pt = jnp.exp2(st * mult - lse[h : h + 1, :])
                dpt = nt(v, dom)
                dst = (pt * (dpt - delta[h : h + 1, :])).astype(BF)
                dv_acc[...] += nn(pt.astype(BF), dom)
                dk_acc[...] += nn(dst, qm)
                parts.append(nn(kt_ref[h * HEAD_DIM : (h + 1) * HEAD_DIM, :], dst))
            dq = jnp.transpose(jnp.concatenate(parts, 0)) * SCALE
            dq_ref[rows, cols] = (dq * c_ref[rows, :] - turned(dq) * s_ref[rows, :]).astype(BF)
            return carry

        lax.fori_loop(0, T // qb, block, 0)
        dk = dk_acc[...] * SCALE
        dk_ref[:, cols] = (dk * c_ref[...] - turned(dk) * s_ref[...]).astype(BF)
        dv_ref[:, cols] = dv_acc[...].astype(BF)
        return outer

    lax.fori_loop(0, W // G, heads, 0)
    shards.middle()
    tf = 256

    def weights(j, carry):
        rows = pl.ds(pl.multiple_of(j * tf, tf), tf)
        h = h_ref[:, rows]
        for i, g_ref in enumerate((dq_ref, dk_ref, dv_ref)):
            gr_ref[rows, i * W : (i + 1) * W] = tn(h, g_ref[...]).astype(BF)
        gr_ref[rows, 3 * W : 4 * W] = tn(sb_ref[:, rows], o_ref[...]).astype(BF)
        gr_ref[rows, 4 * W :] = kv_ref[rows, :]
        return carry

    lax.fori_loop(0, gr_ref.shape[0] // tf, weights, 0)
    shards.store(x_ref)


def attn_bwd(n, q, k, v, o, do, lse, cs, sn, h, sb, kv, a):
    T, W = q.shape
    D = h.shape[1]
    G = lane_group(W)
    _, R, N = a.shape
    slots = 6 if n == 4 else n - 1
    H = R // 2 if n == 4 else R
    return pl.pallas_call(
        functools.partial(attn_bwd_kernel, n),
        in_specs=[VSPEC] * 12,
        out_specs=[VSPEC] * 5,
        out_shape=[sds((T, W), BF)] * 3 + [sds((D, 5 * W), BF), sds((R, N), BF)],
        scratch_shapes=[pltpu.VMEM((T, G), F32), pltpu.VMEM((T, G), F32), pltpu.VMEM((G, T), BF)]
        + [pltpu.VMEM((2, H, N), BF), pltpu.VMEM((slots, H, N), BF)]
        + [pltpu.SemaphoreType.DMA((slots,))] * 2,
        compiler_params=params(collective_id=5, has_side_effects=True),
        cost_estimate=cost(40 * T * T * W, 16 * T * W, T * T * W // HEAD_DIM),
        name="attn_bwd",
    )(q, k, v, o, do, lse, cs, sn, h, sb, kv, a)


def last_kernel(n, ndp, dq_ref, dk_ref, dv_ref, wq_ref, wk_ref, wv_ref, x_ref, da_ref, g_ref, gg_in,
                lbuf, gg_ref, sbuf, rbuf, gbuf, gsum, gown, gall, ss, rs, ss2, rs2, ss3, rs3, ss4, rs4):
    me = lax.axis_index("tensor")
    dp = lax.axis_index("dp")
    C, D = x_ref.shape
    R = D // ndp
    others = [(dp + i) % ndp for i in range(1, ndp)]
    greet(n, me, others)

    def part(t):
        rows = pl.ds(pl.multiple_of(t * C, C), C)
        return nt(dq_ref[rows, :], wq_ref[...]) + nt(dk_ref[rows, :], wk_ref[...]) + nt(dv_ref[rows, :], wv_ref[...])

    total, copies = reduce_parts(n, me, part, lambda: None, sbuf, rbuf, ss, rs)
    u, inverse = unit(x_ref[...].astype(F32))
    lbuf[me] = (da_ref[...] + norm_back(total, u, inverse, g_ref[...])).astype(BF)
    gather = Gather(
        n, me, lbuf.at[me], lambda t: lbuf.at[t], lambda t, i: lbuf.at[t, pl.ds(i * C // 2, C // 2)], ss2, rs2
    )
    gather.start()
    row = lax.broadcasted_iota(jnp.int32, (8, D), 0)
    gsum[...] = gg_in[...] + jnp.where(row == 2, jnp.sum(total * u, axis=0, keepdims=True), 0.0)
    small = {}
    for d in range(1, n):
        small[d] = remote(gsum, gbuf.at[d - 1], ss3.at[d - 1], rs3.at[d - 1], me ^ d)
        small[d].start()
    gains = gsum[...]
    for d in range(1, n):
        small[d].wait_recv()
        gains = gains + gbuf[d - 1]
    for i in range(ndp):
        gown[i] = gains[:, i * R : (i + 1) * R]
    sums = []
    for i, other in enumerate(others):
        sums.append(to_dp(gown.at[other], gall.at[i], ss4.at[i], rs4.at[i], other))
        sums[i].start()
    mine = gown[dp]
    for i in range(ndp - 1):
        sums[i].wait_recv()
        mine = mine + gall[i]
    gg_ref[...] = mine
    gather.relay()
    for d in range(1, n):
        gather.wait(d)
    gather.finish()
    for copy in (*copies.values(), *small.values(), *sums):
        copy.wait_send()


def last(n, ndp, dq, dk, dv, wq, wk, wv, x, da, gain, gains):
    C, D = x.shape
    T, W = dq.shape
    return pl.pallas_call(
        functools.partial(last_kernel, n, ndp),
        in_specs=[VSPEC] * 10,
        out_specs=[VSPEC] * 2,
        out_shape=[sds((n, C, D), BF), sds((8, D // ndp), F32)],
        scratch_shapes=reduce_bufs(n, C, D)[:2]
        + [pltpu.VMEM((n - 1, 8, D), F32), pltpu.VMEM((8, D), F32)]
        + [pltpu.VMEM((ndp, 8, D // ndp), F32), pltpu.VMEM((ndp - 1, 8, D // ndp), F32)]
        + reduce_bufs(n, C, D)[2:]
        + [pltpu.SemaphoreType.DMA((links(n),))] * 2
        + [pltpu.SemaphoreType.DMA((n - 1,))] * 2
        + [pltpu.SemaphoreType.DMA((ndp - 1,))] * 2,
        compiler_params=params(collective_id=3, has_side_effects=True),
        cost_estimate=cost(6 * T * W * D + 4e10, 8 * T * D),
        name="last",
    )(dq, dk, dv, wq, wk, wv, x, da, gain, gains)


def cross_fwd_kernel(n, ctx, h_ref, x_ref, wq_ref, kv_ref, wo_ref, g_ref, q_ref, o_ref, after_ref, h3_ref):
    _, C, W = q_ref.shape
    KP = kv_ref.shape[1] // 2
    mult = SCALE * LOG2E
    G = lane_group(W)
    per = W // G
    masks = [m.astype(BF) for m in head_masks(1, G)]
    lane = lax.broadcasted_iota(jnp.int32, (C, G), 1) // HEAD_DIM
    valid = lax.broadcasted_iota(jnp.int32, (C, KP), 1) < ctx

    def group(g, carry):
        t = g // per
        cols = pl.ds(pl.multiple_of(g % per * G, G), G) if per > 1 else slice(None)
        q = nn(h_ref[...], wq_ref[t, :, cols]).astype(BF)
        q_ref[t, :, cols] = q
        k, v = kv_ref[t, :KP, cols], kv_ref[t, KP:, cols]
        out = jnp.zeros((C, G), F32)
        for h in range(G // HEAD_DIM):
            s = jnp.where(valid, nt(q * masks[h], k), -1e30)
            p = jnp.exp2((s - jnp.max(s, axis=-1, keepdims=True)) * mult)
            o = nn(p.astype(BF), v) / jnp.sum(p, axis=-1, keepdims=True)
            out = jnp.where(lane == h, o, out)
        o_ref[t, :, cols] = out.astype(BF)
        return carry

    lax.fori_loop(0, n * per, group, 0)
    D = h_ref.shape[1]
    tf = 256

    def project(j, carry):
        cols = pl.ds(pl.multiple_of(j * tf, tf), tf)
        total = nn(o_ref[0], wo_ref[0, :, cols])
        for t in range(1, n):
            total = total + nn(o_ref[t], wo_ref[t, :, cols])
        after_ref[:, cols] = x_ref[:, cols] + total
        return carry

    lax.fori_loop(0, D // tf, project, 0)
    u, _ = unit(after_ref[...])
    h3_ref[...] = (u * g_ref[...]).astype(BF)


def cross_fwd(ctx, h, x, wq, kv, wo, gain):
    C, D = h.shape
    n, W = wq.shape[0], wq.shape[2]
    return pl.pallas_call(
        functools.partial(cross_fwd_kernel, n, ctx),
        in_specs=[VSPEC] * 6,
        out_specs=[VSPEC] * 4,
        out_shape=[sds((n, C, W), BF), sds((n, C, W), BF), sds((C, D), F32), sds((C, D), BF)],
        compiler_params=params(),
        cost_estimate=cost(4 * C * D * n * W + 16 * C * 256 * n * W, 8 * D * n * W),
        name="cross_fwd",
    )(h, x, wq, kv, wo, gain)


def cross_bwd_kernel(n, ctx, dh3_ref, after2_ref, cot_ref, g3_ref, wo_ref, q_ref, kv_ref, wq_ref, after1_ref, g2_ref, bo_in,
                     cb_ref, dq_ref, dkv_ref, da_ref, sb_ref, gg_ref, bo_ref, dh2_ref, ss, rs):
    me = lax.axis_index("tensor")
    _, C, W = q_ref.shape
    KP = kv_ref.shape[1] // 2
    D = da_ref.shape[1]
    mult = SCALE * LOG2E
    G = lane_group(W)
    per = W // G
    masks = [m.astype(BF) for m in head_masks(1, G)]
    lane = lax.broadcasted_iota(jnp.int32, (C, G), 1) // HEAD_DIM
    valid = lax.broadcasted_iota(jnp.int32, (C, KP), 1) < ctx
    greet(n, me)
    gather = Gather(n, me, bo_in, lambda t: bo_ref.at[t], lambda t, i: bo_ref.at[t, pl.ds(i * C // 2, C // 2)], ss, rs)
    gather.start()
    bo_ref[me] = bo_in[...]
    dh3 = dh3_ref[...]
    u3, inv3 = unit(after2_ref[...])
    gain3 = jnp.sum(dh3 * u3, axis=0, keepdims=True)
    da2 = cot_ref[...].astype(F32) + norm_back(dh3, u3, inv3, g3_ref[...])
    da_ref[...] = da2
    cb_ref[...] = da2.astype(BF)

    def group(g, carry):
        t = g // per
        cols = pl.ds(pl.multiple_of(g % per * G, G), G) if per > 1 else slice(None)
        do = nt(cb_ref[...], wo_ref[t, cols, :]).astype(BF)
        q, k, v = q_ref[t, :, cols], kv_ref[t, :KP, cols], kv_ref[t, KP:, cols]
        dq = jnp.zeros((C, G), F32)
        dk = jnp.zeros((KP, G), F32)
        dv = jnp.zeros((KP, G), F32)
        for h in range(G // HEAD_DIM):
            qm = q * masks[h]
            dom = do * masks[h]
            s = jnp.where(valid, nt(qm, k), -1e30)
            p = jnp.exp2((s - jnp.max(s, axis=-1, keepdims=True)) * mult)
            p = p / jnp.sum(p, axis=-1, keepdims=True)
            dp = nt(dom, v)
            ds = (p * (dp - jnp.sum(p * dp, axis=-1, keepdims=True))).astype(BF)
            dq = jnp.where(lane == h, nn(ds, k), dq)
            dk = dk + tn(ds, qm)
            dv = dv + tn(p.astype(BF), dom)
        dq_ref[t, :, cols] = (dq * SCALE).astype(BF)
        dkv_ref[t, :KP, cols] = dk * SCALE
        dkv_ref[t, KP:, cols] = dv
        return carry

    lax.fori_loop(0, n * per, group, 0)
    gather.relay()
    tf = 256

    def project(j, carry):
        cols = pl.ds(pl.multiple_of(j * tf, tf), tf)
        total = nt(dq_ref[0], wq_ref[0, cols, :])
        for t in range(1, n):
            total = total + nt(dq_ref[t], wq_ref[t, cols, :])
        dh2_ref[:, cols] = total
        return carry

    lax.fori_loop(0, D // tf, project, 0)
    dh2 = dh2_ref[...]
    u2, inv2 = unit(after1_ref[...])
    gain2 = jnp.sum(dh2 * u2, axis=0, keepdims=True)
    da1 = da_ref[...] + norm_back(dh2, u2, inv2, g2_ref[...])
    da_ref[...] = da1
    sb_ref[...] = da1.astype(BF)
    row = lax.broadcasted_iota(jnp.int32, (8, D), 0)
    gg_ref[...] = jnp.where(row == 0, gain3, 0.0) + jnp.where(row == 1, gain2, 0.0)
    for d in range(1, n):
        gather.wait(d)
    gather.finish()


def cross_bwd(ctx, dh3, after2, cot, g3, wo, q, kv, wq, after1, g2, bo):
    C, D = after2.shape
    n, W = wq.shape[0], wq.shape[2]
    return pl.pallas_call(
        functools.partial(cross_bwd_kernel, n, ctx),
        in_specs=[VSPEC] * 11,
        out_specs=[VSPEC] * 7,
        out_shape=[
            sds((C, D), BF),
            sds((n, C, W), BF),
            sds(kv.shape, F32),
            sds((C, D), F32),
            sds((C, D), BF),
            sds((8, D), F32),
            sds((n, C, D), BF),
        ],
        scratch_shapes=[pltpu.VMEM((C, D), F32)] + [pltpu.SemaphoreType.DMA((links(n),))] * 2,
        compiler_params=params(collective_id=7, has_side_effects=True),
        cost_estimate=cost(4 * C * D * n * W + 40 * C * 256 * n * W, 8 * D * n * W),
        name="cross_bwd",
    )(dh3, after2, cot, g3, wo, q, kv, wq, after1, g2, bo)


def body(latents, context, cotangent, g1, wq, wk, wv, wo, g2, xq, xk, xv, xo, g3, wg, wu, wd, n, ndp):
    _, T, D = latents.shape
    ctx = context.shape[1]
    W = wq.shape[1]
    F = wg.shape[1]
    C = T // n
    me = lax.axis_index("tensor")
    x = latents.reshape(T, D)
    gb = cotangent.reshape(T, D)
    ctx_rows = context.reshape(ctx, -1)
    KP = -(-ctx // 16) * 16
    cs, sn = tables(T, lane_group(W))
    g1, g2, g3 = (g.reshape(1, D) for g in (g1, g2, g3))
    own = lambda a: lax.dynamic_slice_in_dim(a, me * C, C, 0)

    ctx_pad = jnp.pad(ctx_rows, ((0, KP - ctx), (0, 0)))
    h1, q, k, v, attn, lse, xq_all, xo_all, kv_all = front(n, ctx, x, g1, wq, wk, wv, cs, sn, xq, xo, ctx_pad, xk, xv)
    x_own = own(x)
    after1, h2 = out_rs(n, attn, wo, x_own, g2)
    cq, cattn, after2, h3_own = cross_fwd(ctx, h2, after1, xq_all, kv_all, xo_all, g3)
    h3, hidden, dgu, dh3 = ff(n, h3_own, gb, wg, wu, wd)
    h3 = h3.reshape(T, D)

    def scatter(a, axis):
        return lax.psum_scatter(a, axis, scatter_dimension=0, tiled=True)

    down_part = down_grads(gb, hidden)
    down_part, dgu = lax.optimization_barrier((down_part, dgu))
    down_grad = scatter(down_part, "dp")
    out_own, gu_part = feed_grads(n, hidden, wd, after2, h3, dgu)
    dh3, gu_part = lax.optimization_barrier((dh3, gu_part))
    gu_grad = scatter(gu_part, "dp")

    cb, dcq, dckv, dafter1, sb_own, gains, block_out = cross_bwd(
        ctx, dh3, after2, own(gb), g3, xo_all, cq, kv_all, xq_all, after1, g2, out_own
    )
    sb_own, down_grad = lax.optimization_barrier((sb_own, down_grad))
    sb, dattn, cross_part, kv_part = gather_back(n, ndp, sb_own, wo, h2, dcq, cb, cattn, dckv, ctx_pad)
    sb = sb.reshape(T, D)
    dq, dk, dv, self_part, cross_part = attn_bwd(
        n, q, k, v, attn, dattn, lse, cs, sn, h1, sb, kv_part, cross_part
    )
    cores = [[i for i in range(ndp) if i % 2 == c] for c in range(2)]
    cross_grads = lax.psum_scatter(cross_part, "dp", scatter_dimension=0, axis_index_groups=cores, tiled=True)
    self_grads = scatter(self_part, "dp")
    dq, gu_grad = lax.optimization_barrier((dq, gu_grad))
    latent_grad, gains = last(n, ndp, dq, dk, dv, wq, wk, wv, x_own, dafter1, g1, gains)

    cross_grads, self_grads, gains = lax.optimization_barrier((cross_grads, self_grads, gains))
    gu_grad = gu_grad.astype(F32)
    gate_grad, up_grad, down_grad = gu_grad[:, :F], gu_grad[:, F:], down_grad.astype(F32).T
    cross_grads = cross_grads.astype(F32)
    xq_grad, xo_grad = cross_grads[:, :W], cross_grads[:, W:].T
    self_grads = self_grads.astype(F32)
    kv_grads = self_grads[:, 4 * W :].reshape(2, D // ndp // 2, W)
    return (
        block_out.reshape(1, T, D),
        latent_grad.astype(F32).reshape(1, T, D),
        gains[2],
        self_grads[:, :W],
        self_grads[:, W : 2 * W],
        self_grads[:, 2 * W : 3 * W],
        self_grads[:, 3 * W : 4 * W].T,
        gains[1],
        xq_grad,
        kv_grads[0],
        kv_grads[1],
        xo_grad,
        gains[0],
        gate_grad,
        up_grad,
        down_grad,
    )


def solution(mesh):
    tokens = P("dp", None, None)
    cols = P(None, "tensor")
    rows = P("tensor", None)
    return jax.shard_map(
        functools.partial(body, n=mesh.shape["tensor"], ndp=mesh.shape["dp"]),
        mesh=mesh,
        in_specs=(tokens, tokens, tokens, P(), cols, cols, cols, rows, P(), cols, cols, cols, rows, P(), cols, cols, rows),
        out_specs=(
            tokens,
            tokens,
            P("dp"),
            P("dp", "tensor"),
            P("dp", "tensor"),
            P("dp", "tensor"),
            P("tensor", "dp"),
            P("dp"),
            P("dp", "tensor"),
            P("dp", "tensor"),
            P("dp", "tensor"),
            P("tensor", "dp"),
            P("dp"),
            P("dp", "tensor"),
            P("dp", "tensor"),
            P("tensor", "dp"),
        ),
        check_vma=False,
    )
```

```python
import functools

import jax
import jax.numpy as jnp
from jax import lax
from jax.experimental import pallas as pl
from jax.experimental.pallas import tpu as pltpu
from jax.sharding import PartitionSpec as P

HEAD_DIM = 64
HALF = HEAD_DIM // 2
EPS = 1e-05
BF = jnp.bfloat16
F32 = jnp.float32
LOG2E = 1.4426950408889634
SCALE = HEAD_DIM**-0.5
VMEM_BYTES = 60 << 20
MESH_ID = pl.DeviceIdType.MESH
VSPEC = pl.BlockSpec(memory_space=pltpu.VMEM)
ANYSPEC = pl.BlockSpec(memory_space=pl.ANY)


def nn(a, b):
    return lax.dot_general(a, b, (((1,), (0,)), ((), ())), preferred_element_type=F32)


def nt(a, b):
    return lax.dot_general(a, b, (((1,), (1,)), ((), ())), preferred_element_type=F32)


def tn(a, b):
    return lax.dot_general(a, b, (((0,), (0,)), ((), ())), preferred_element_type=F32)


def sds(shape, dtype):
    return jax.ShapeDtypeStruct(shape, dtype)


def params(**kw):
    return pltpu.CompilerParams(vmem_limit_bytes=VMEM_BYTES, **kw)


def cost(flops, nbytes, trans=0):
    return pl.CostEstimate(flops=1000, bytes_accessed=1000, transcendentals=0)


def unit(x):
    center = x - jnp.mean(x, axis=-1, keepdims=True)
    inverse = lax.rsqrt(jnp.mean(center * center, axis=-1, keepdims=True) + EPS)
    return center * inverse, inverse


def norm_back(grad, u, inverse, gain):
    e = grad * gain
    mean_e = jnp.mean(e, axis=-1, keepdims=True)
    mean_p = jnp.mean(e * u, axis=-1, keepdims=True)
    return inverse * (e - mean_e - u * mean_p)


def lane_group(width):
    return 128 if width % 128 == 0 else width


def tables(length, group):
    freq = jnp.tile(10000.0 ** (-jnp.arange(HALF, dtype=F32) / HALF), group // HALF)
    angles = lax.broadcasted_iota(F32, (length, group), 0) * freq[None, :]
    front = lax.broadcasted_iota(jnp.int32, (length, group), 1) % HEAD_DIM < HALF
    return jnp.cos(angles), jnp.where(front, -1.0, 1.0) * jnp.sin(angles)


def turned(a):
    width = a.shape[-1]
    lane = lax.broadcasted_iota(jnp.int32, a.shape, 1) % HEAD_DIM
    return jnp.where(lane < HALF, pltpu.roll(a, width - HALF, 1), pltpu.roll(a, HALF, 1))


def head_masks(rows, group):
    lane = lax.broadcasted_iota(jnp.int32, (rows, group), 1) // HEAD_DIM
    return [jnp.where(lane == h, 1.0, 0.0) for h in range(group // HEAD_DIM)]


def greet(n, me, dps=()):
    sem = pltpu.get_barrier_semaphore()
    for d in range(1, n):
        pl.semaphore_signal(sem, 1, device_id={"tensor": me ^ d}, device_id_type=MESH_ID)
    for dp in dps:
        pl.semaphore_signal(sem, 1, device_id={"dp": dp}, device_id_type=MESH_ID)
    pl.semaphore_wait(sem, n - 1 + len(dps))


def to_dp(src, dst, send, recv, target):
    return pltpu.make_async_remote_copy(src, dst, send, recv, device_id={"dp": target}, device_id_type=MESH_ID)


def remote(src, dst, send, recv, target):
    return pltpu.make_async_remote_copy(src, dst, send, recv, device_id={"tensor": target}, device_id_type=MESH_ID)


class Late:
    def __init__(self, src, dst, sem):
        self.dst, self.copy = dst, pltpu.make_async_copy(src, dst, sem)
        self.copy.start()

    def __call__(self):
        self.copy.wait()
        return self.dst


def held(*arrays):
    return [pltpu.VMEM(a.shape, a.dtype) for a in arrays] + [pltpu.SemaphoreType.DMA((len(arrays),))]


def rows_of(ref, t, C):
    return ref.at[pl.ds(pl.multiple_of(t * C, C), C)]


def links(n):
    return 4 if n == 4 else n - 1


class Gather:
    def __init__(self, n, me, src, slot, half, ss, rs):
        self.n, self.me, self.half, self.ss, self.rs = n, me, half, ss, rs
        self.copies = {
            d: remote(src, slot(me), ss.at[d - 1], rs.at[d - 1], me ^ d) for d in (range(1, n) if n != 4 else (1, 2))
        }
        self.passed = []

    def start(self):
        for copy in self.copies.values():
            copy.start()

    def relay(self):
        if self.n == 4:
            for i, d in enumerate((1, 2)):
                self.copies[d].wait_recv()
                block = self.half(self.me ^ d, i)
                copy = remote(block, block, self.ss.at[2 + i], self.rs.at[2 + i], self.me ^ (3 - d))
                copy.start()
                self.passed.append(copy)

    def wait(self, d):
        if self.n != 4:
            self.copies[d].wait_recv()
        elif d == 3:
            for copy in self.passed:
                copy.wait_recv()

    def finish(self):
        for copy in (*self.copies.values(), *self.passed):
            copy.wait_send()


def reduce_bufs(n, C, D):
    shape = (6, C, D // 2) if n == 4 else (n - 1, C, D)
    return [pltpu.VMEM(shape, BF)] * 2 + [pltpu.SemaphoreType.DMA((shape[0],))] * 2


def reduce_parts(n, me, part, filler, sbuf, rbuf, ss, rs):
    copies = {}

    def send(i, val, d):
        sbuf[i] = val.astype(BF)
        copies[i] = remote(sbuf.at[i], rbuf.at[i], ss.at[i], rs.at[i], me ^ d)
        copies[i].start()

    def got(i):
        copies[i].wait_recv()
        return rbuf[i].astype(F32)

    if n == 4:
        across = part(me ^ 3)
        H = across.shape[1] // 2
        send(0, across[:, :H], 1)
        send(2, across[:, H:], 2)
        one = part(me ^ 1)
        send(1, one[:, :H], 1)
        two = part(me ^ 2)
        send(3, two[:, H:], 2)
        total = part(me)
        filler()
        send(4, two[:, :H] + got(0), 2)
        send(5, one[:, H:] + got(2), 1)
        total = jnp.concatenate([total[:, :H] + got(1) + got(4), total[:, H:] + got(3) + got(5)], 1)
    else:
        for d in reversed(range(1, n)):
            send(d - 1, part(me ^ d), d)
        total = part(me)
        filler()
        for d in range(1, n):
            total = total + got(d - 1)
    return total, copies


class ShardSum:
    def __init__(self, n, me, a, sbuf, rbuf, ss, rs):
        self.n, self.me, self.a, self.sbuf, self.rbuf, self.ss, self.rs = n, me, a, sbuf, rbuf, ss, rs
        self.copies = {}

    def send(self, i, src, d):
        self.copies[i] = remote(src, self.rbuf.at[i], self.ss.at[i], self.rs.at[i], self.me ^ d)
        self.copies[i].start()

    def got(self, i):
        self.copies[i].wait_recv()
        return self.rbuf[i].astype(F32)

    def halves(self, d, a=None):
        a = self.a if a is None else a
        H = a.shape[1] // 2
        return a.at[self.me ^ d, pl.ds(0, H)], a.at[self.me ^ d, pl.ds(H, H)]

    def start(self, a):
        if self.n == 4:
            self.send(0, self.halves(3, a)[0], 1)
            self.send(2, self.halves(3, a)[1], 2)
            self.send(1, self.halves(1, a)[0], 1)
            self.send(3, self.halves(2, a)[1], 2)
        else:
            for d in range(1, self.n):
                self.send(d - 1, a.at[self.me ^ d], d)

    def middle(self):
        if self.n == 4:
            self.sbuf[0] = (self.halves(2)[0][...].astype(F32) + self.got(0)).astype(BF)
            self.send(4, self.sbuf.at[0], 2)
            self.sbuf[1] = (self.halves(1)[1][...].astype(F32) + self.got(2)).astype(BF)
            self.send(5, self.sbuf.at[1], 1)

    def store(self, out_ref):
        if self.n == 4:
            H = self.a.shape[1] // 2
            own = self.halves(0)
            out_ref[:H] = (own[0][...].astype(F32) + self.got(1) + self.got(4)).astype(BF)
            out_ref[H:] = (own[1][...].astype(F32) + self.got(3) + self.got(5)).astype(BF)
        else:
            total = self.a[self.me].astype(F32)
            for d in range(1, self.n):
                total = total + self.got(d - 1)
            out_ref[...] = total.astype(BF)
        for copy in self.copies.values():
            copy.wait_send()


def front_kernel(n, ctx, x_hbm, g_ref, wq_hbm, wk_hbm, wv_hbm, c_ref, s_ref, xq_ref, xo_ref, ctx_ref, xk_hbm, xv_hbm,
                 h_hbm, q_hbm, k_hbm, v_hbm, o_ref, lse_ref, xqa_ref, xoa_ref, kva_ref,
                 kv_own, sq, rq, so, ro, sk, rk, fsq, frq, fso, fro, local,
                 x_buf, wq_buf, wk_buf, wv_buf, xk_buf, xv_buf, lsem, h_ref, q_ref, k_ref, v_ref, osem):
    xk, xv, x, wq, wk, wv = (
        Late(src, dst, lsem.at[i])
        for i, (src, dst) in enumerate(
            (
                (xk_hbm, xk_buf),
                (xv_hbm, xv_buf),
                (x_hbm, x_buf),
                (wq_hbm, wq_buf),
                (wk_hbm, wk_buf),
                (wv_hbm, wv_buf),
            )
        )
    )
    me = lax.axis_index("tensor")
    dp = lax.axis_index("dp")
    core = dp % 2
    partner = dp + 1 - 2 * core
    T, D = x_hbm.shape
    W = q_ref.shape[1]
    KP = ctx_ref.shape[0]
    greet(n, me, [partner])

    rows_q = pl.ds(pl.multiple_of(core * (D // 2), 16), D // 2)
    rows_o = pl.ds(pl.multiple_of(core * (W // 2), 16), W // 2)
    def quarter(ref, rows):
        return lambda t, i: ref.at[t, pl.ds(pl.multiple_of(core * (rows // 2) + i * (rows // 4), 16), rows // 4)]

    gq = Gather(n, me, xq_ref.at[rows_q], lambda t: xqa_ref.at[t, rows_q], quarter(xqa_ref, D), sq, rq)
    go = Gather(n, me, xo_ref.at[rows_o], lambda t: xoa_ref.at[t, rows_o], quarter(xoa_ref, W), so, ro)
    gk = Gather(n, me, kv_own, lambda t: kva_ref.at[t], lambda t, i: kva_ref.at[t, pl.ds(i * KP, KP)], sk, rk)
    gq.start()
    go.start()
    own = [
        pltpu.make_async_copy(xq_ref, xqa_ref.at[me], local.at[0]),
        pltpu.make_async_copy(xo_ref, xoa_ref.at[me], local.at[1]),
    ]
    for copy in own:
        copy.start()
    kv_own[:KP] = nn(ctx_ref[...], xk()[...]).astype(BF)
    kv_own[KP:] = nn(ctx_ref[...], xv()[...]).astype(BF)
    gk.start()
    kva_ref[me] = kv_own[...]

    tb = 256
    reps = W // c_ref.shape[1]
    x_ref, wq_ref, wk_ref, wv_ref = x(), wq(), wk(), wv()

    def project(i, carry):
        rows = pl.ds(pl.multiple_of(i * tb, tb), tb)
        u, _ = unit(x_ref[rows, :].astype(F32))
        h = (u * g_ref[...].reshape(1, D)).astype(BF)
        h_ref[rows, :] = h
        c = jnp.concatenate([c_ref[rows, :]] * reps, 1)
        s = jnp.concatenate([s_ref[rows, :]] * reps, 1)
        for w_ref, out_ref in ((wq_ref, q_ref), (wk_ref, k_ref)):
            a = nn(h, w_ref[...])
            out_ref[rows, :] = (a * c + turned(a) * s).astype(BF)
        v_ref[rows, :] = nn(h, wv_ref[...]).astype(BF)
        return carry

    lax.fori_loop(0, T // tb, project, 0)
    kept = [
        pltpu.make_async_copy(src, dst, osem.at[i])
        for i, (src, dst) in enumerate(((h_ref, h_hbm), (q_ref, q_hbm), (k_ref, k_hbm), (v_ref, v_hbm)))
    ]
    for copy in kept:
        copy.start()
    gq.relay()

    G = lane_group(W)
    mult = SCALE * LOG2E
    masks = [m.astype(BF) for m in head_masks(1, G)]
    lane = lax.broadcasted_iota(jnp.int32, (tb, G), 1) // HEAD_DIM
    stat_lane = lax.broadcasted_iota(jnp.int32, (tb, 128), 1)

    def heads(g, carry):
        cols = pl.ds(pl.multiple_of(g * G, G), G) if G < W else slice(None)
        k, v = k_ref[:, cols], v_ref[:, cols]

        def block(i, inner):
            rows = pl.ds(pl.multiple_of(i * tb, tb), tb)
            q = q_ref[rows, cols]
            out = jnp.zeros((tb, G), F32)
            stats = jnp.zeros((tb, 128), F32)
            for h in range(G // HEAD_DIM):
                s = nt(q * masks[h], k)
                top = jnp.max(s, axis=-1, keepdims=True) * mult
                p = jnp.exp2(s * mult - top)
                total = jnp.sum(p, axis=-1, keepdims=True)
                o = nn(p.astype(BF), v) / total
                out = jnp.where(lane == h, o, out)
                stats = jnp.where(stat_lane == h, top + jnp.log2(total), stats)
            o_ref[rows, cols] = out.astype(BF)
            lse_ref[g, :, rows] = jnp.transpose(stats)[:8]
            return inner

        return lax.fori_loop(0, T // tb, block, carry)

    lax.fori_loop(0, W // G, heads, 0)

    go.relay()
    gk.relay()
    passed = []
    for gather, ref, rows, send, recv in ((gq, xqa_ref, rows_q, fsq, frq), (go, xoa_ref, rows_o, fso, fro)):
        for d in range(1, n):
            gather.wait(d)
            block = ref.at[me ^ d, rows]
            copy = to_dp(block, block, send.at[d - 1], recv.at[d - 1], partner)
            copy.start()
            passed.append(copy)
    for copy in (*own, *kept):
        copy.wait()
    for d in range(1, n):
        gk.wait(d)
    for copy in passed:
        copy.wait_recv()
    for copy in (gq, go, gk):
        copy.finish()
    for copy in passed:
        copy.wait_send()


def front(n, ctx, x, gain, wq, wk, wv, cs, sn, xq, xo, ctx_rows, xk, xv):
    T, D = x.shape
    W = wq.shape[1]
    KP = ctx_rows.shape[0]
    groups = W // lane_group(W)
    link, pair = pltpu.SemaphoreType.DMA((links(n),)), pltpu.SemaphoreType.DMA((n - 1,))
    return pl.pallas_call(
        functools.partial(front_kernel, n, ctx),
        in_specs=[ANYSPEC, VSPEC] + [ANYSPEC] * 3 + [VSPEC] * 5 + [ANYSPEC] * 2,
        out_specs=[ANYSPEC] * 4 + [VSPEC] * 2 + [ANYSPEC] * 2 + [VSPEC],
        out_shape=[sds((T, D), BF)]
        + [sds((T, W), BF)] * 4
        + [sds((groups, 8, T), F32), sds((n, D, W), BF), sds((n, W, D), BF), sds((n, 2 * KP, W), BF)],
        scratch_shapes=[pltpu.VMEM((2 * KP, W), BF)] + [link] * 6 + [pair] * 4 + [pltpu.SemaphoreType.DMA((2,))]
        + held(x, wq, wk, wv, xk, xv)
        + held(sds((T, D), BF), *[sds((T, W), BF)] * 3),
        compiler_params=params(collective_id=4, has_side_effects=True),
        cost_estimate=cost(6 * T * D * W, 4 * T * D + 6 * D * W + 6 * T * W),
        name="front",
    )(x, gain, wq, wk, wv, cs, sn, xq, xo, ctx_rows, xk, xv)


def out_rs_kernel(n, a_ref, w_ref, x_hbm, g_ref, after_ref, h_ref, sbuf, rbuf, ss, rs, x_buf, lsem):
    me = lax.axis_index("tensor")
    C, D = x_buf.shape
    x = Late(rows_of(x_hbm, me, C), x_buf, lsem.at[0])
    greet(n, me)

    def part(t):
        return nn(a_ref[pl.ds(pl.multiple_of(t * C, C), C), :], w_ref[...])

    total, copies = reduce_parts(n, me, part, lambda: None, sbuf, rbuf, ss, rs)
    after = x()[...].astype(F32) + total
    after_ref[...] = after
    u, _ = unit(after)
    h_ref[...] = (u * g_ref[...].reshape(1, D)).astype(BF)
    for copy in copies.values():
        copy.wait_send()


def out_rs(n, a, w, x, gain):
    T, D = x.shape
    C = T // n
    W = a.shape[1]
    return pl.pallas_call(
        functools.partial(out_rs_kernel, n),
        in_specs=[VSPEC, VSPEC, ANYSPEC, VSPEC],
        out_specs=[VSPEC] * 2,
        out_shape=[sds((C, D), F32), sds((C, D), BF)],
        scratch_shapes=reduce_bufs(n, C, D) + held(sds((C, D), BF)),
        compiler_params=params(collective_id=0, has_side_effects=True),
        cost_estimate=cost(2 * T * W * D + 2e10, 8 * C * D),
        name="out_rs",
    )(a, w, x, gain)


def ff_kernel(n, h_in, gb_hbm, wg_hbm, wu_hbm, wd_hbm, h_hbm, hid_hbm, dgu_hbm, dh_ref,
              gb_ref, wg_ref, wu_ref, wd_ref, sbuf, rbuf, ss, rs, ss2, rs2, ls, h_ref, hid_ref, dgu_ref, osem):
    me = lax.axis_index("tensor")
    C, D = h_in.shape
    F = wg_ref.shape[1]
    loads = [
        pltpu.make_async_copy(src, dst, ls.at[i])
        for i, (src, dst) in enumerate(((wg_hbm, wg_ref), (wu_hbm, wu_ref), (wd_hbm, wd_ref), (gb_hbm, gb_ref)))
    ]
    for c in loads:
        c.start()
    greet(n, me)
    gather = Gather(n, me, h_in, lambda t: h_ref.at[t], lambda t, i: h_ref.at[t, pl.ds(i * C // 2, C // 2)], ss, rs)
    gather.start()
    h_ref[me] = h_in[...]
    for c in loads:
        c.wait()
    tf = 256

    def chunk(t, store):
        rows = pl.ds(pl.multiple_of(t * C, C), C)
        h = h_ref[t]
        gb = gb_ref[rows, :]

        def tile(j, carry):
            cols = pl.ds(pl.multiple_of(j * tf, tf), tf)
            gate = nn(h, wg_ref[:, cols])
            up = nn(h, wu_ref[:, cols])
            dhid = nt(gb, wd_ref[cols, :])
            sig = 1.0 / (1.0 + jnp.exp(-gate))
            act = gate * sig
            hid_ref[rows, cols] = (act * up).astype(BF)
            dgu_ref[rows, cols] = (dhid * up * (sig * (1.0 + gate * (1.0 - sig)))).astype(BF)
            dgu_ref[rows, pl.ds(pl.multiple_of(F + j * tf, tf), tf)] = (dhid * act).astype(BF)
            return carry

        lax.fori_loop(0, F // tf, tile, 0)

        def back(j, carry):
            out = pl.ds(pl.multiple_of(j * tf, tf), tf)
            store(out, nt(dgu_ref[rows, :F], wg_ref[out, :]) + nt(dgu_ref[rows, F:], wu_ref[out, :]))
            return carry

        lax.fori_loop(0, D // tf, back, 0)

    def store_own(cols, val):
        dh_ref[:, cols] = val

    kept = []

    def keep(i, t):
        pieces = [(h_ref.at[t], h_hbm.at[t])]
        pieces += [(rows_of(a, t, C), rows_of(b, t, C)) for a, b in ((hid_ref, hid_hbm), (dgu_ref, dgu_hbm))]
        for k, (src, dst) in enumerate(pieces):
            kept.append(pltpu.make_async_copy(src, dst, osem.at[i, k]))
            kept[-1].start()

    chunk(me, store_own)
    keep(0, me)
    gather.relay()
    copies = {}
    for d in range(1, n):
        t = me ^ d
        gather.wait(d)

        def store_sent(cols, val):
            sbuf[d - 1, :, cols] = val.astype(BF)

        chunk(t, store_sent)
        keep(d, t)
        copies[d] = remote(sbuf.at[d - 1], rbuf.at[d - 1], ss2.at[d - 1], rs2.at[d - 1], t)
        copies[d].start()
    gather.finish()
    for d in range(1, n):
        copies[d].wait_recv()
        dh_ref[...] += rbuf[d - 1].astype(F32)
    for d in range(1, n):
        copies[d].wait_send()
    for copy in kept:
        copy.wait()


def ff(n, h, gb, wg, wu, wd):
    C, D = h.shape
    T = gb.shape[0]
    F = wg.shape[1]
    return pl.pallas_call(
        functools.partial(ff_kernel, n),
        in_specs=[VSPEC] + [ANYSPEC] * 4,
        out_specs=[ANYSPEC] * 3 + [VSPEC],
        out_shape=[sds((n, C, D), BF), sds((T, F), BF), sds((T, 2 * F), BF), sds((C, D), F32)],
        scratch_shapes=[
            pltpu.VMEM((T, D), BF),
            pltpu.VMEM((D, F), BF),
            pltpu.VMEM((D, F), BF),
            pltpu.VMEM((F, D), BF),
            pltpu.VMEM((n - 1, C, D), BF),
            pltpu.VMEM((n - 1, C, D), BF),
        ]
        + [pltpu.SemaphoreType.DMA((links(n),))] * 2
        + [pltpu.SemaphoreType.DMA((n - 1,))] * 2
        + [pltpu.SemaphoreType.DMA((4,))]
        + [pltpu.VMEM((n, C, D), BF), pltpu.VMEM((T, F), BF), pltpu.VMEM((T, 2 * F), BF)]
        + [pltpu.SemaphoreType.DMA((n, 3))],
        compiler_params=params(collective_id=1, has_side_effects=True),
        cost_estimate=cost(10 * T * D * F + 3e10, 6 * D * F + 8 * T * D),
        name="ff",
    )(h, gb, wg, wu, wd)


def down_kernel(gb_ref, hid_ref, o_ref):
    gb = gb_ref[...]
    tf = 512 if hid_ref.shape[1] % 512 == 0 else 256

    def down(j, carry):
        cols = pl.ds(pl.multiple_of(j * tf, tf), tf)
        o_ref[:, cols] = tn(gb, hid_ref[:, cols]).astype(BF)
        return carry

    lax.fori_loop(0, hid_ref.shape[1] // tf, down, 0)


def down_grads(gb, hidden):
    T, D = gb.shape
    F = hidden.shape[1]
    tb = 256
    return pl.pallas_call(
        down_kernel,
        grid=(D // tb,),
        in_specs=[
            pl.BlockSpec((T, tb), lambda i: (0, i)),
            pl.BlockSpec(hidden.shape, lambda i: (0, 0), pipeline_mode=pl.Buffered(1)),
        ],
        out_specs=pl.BlockSpec((tb, F), lambda i: (i, 0)),
        out_shape=sds((D, F), BF),
        compiler_params=params(),
        cost_estimate=cost(2 * T * D * F, 2 * D * F),
        name="down_grads",
    )(gb, hidden)


def feed_kernel(n, hid_ref, wd_ref, after_hbm, h_hbm, dgu_hbm, out_ref, gr_hbm,
                sbuf, rbuf, ss, rs, h_ref, dgu_ref, after_ref, lsem, gr_ref, osem):
    me = lax.axis_index("tensor")
    h, dgu, after = (
        Late(src, dst, lsem.at[i])
        for i, (src, dst) in enumerate(((h_hbm, h_ref), (dgu_hbm, dgu_ref), (after_hbm, after_ref)))
    )
    C, D = after_ref.shape
    F2 = dgu_ref.shape[1]
    greet(n, me)

    def part(t):
        return nn(hid_ref[pl.ds(pl.multiple_of(t * C, C), C), :], wd_ref[...])

    tb, tf = 256, 512

    def tile(j, carry):
        cols = pl.ds(pl.multiple_of(j * tf, tf), tf)
        for i in range(D // tb):
            rows = slice(i * tb, (i + 1) * tb)
            gr_ref[rows, cols] = tn(h_ref[:, rows], dgu_ref[:, cols]).astype(BF)
        leave(j).start()
        return carry

    def leave(j):
        cols = pl.ds(pl.multiple_of(j * tf, tf), tf)
        return pltpu.make_async_copy(gr_ref.at[:, cols], gr_hbm.at[:, cols], osem.at[j])

    def filler():
        h()
        dgu()
        lax.fori_loop(0, F2 // tf, tile, 0)

    total, copies = reduce_parts(n, me, part, filler, sbuf, rbuf, ss, rs)
    out_ref[...] = (after()[...] + total).astype(BF)
    for copy in copies.values():
        copy.wait_send()
    for j in range(F2 // tf):
        leave(j).wait()


def feed_grads(n, hidden, wd, after, h, dgu):
    C, D = after.shape
    T, F2 = dgu.shape
    return pl.pallas_call(
        functools.partial(feed_kernel, n),
        in_specs=[VSPEC] * 2 + [ANYSPEC] * 3,
        out_specs=[VSPEC, ANYSPEC],
        out_shape=[sds((C, D), BF), sds((D, F2), BF)],
        scratch_shapes=reduce_bufs(n, C, D)
        + held(h, dgu, after)
        + [pltpu.VMEM((D, F2), BF), pltpu.SemaphoreType.DMA((F2 // 512,))],
        compiler_params=params(collective_id=6, has_side_effects=True),
        cost_estimate=cost(3 * T * D * F2, 6 * D * F2),
        name="feed_grads",
    )(hidden, wd, after, h, dgu)


def gather_kernel(n, ndp, x_in, w_ref, h2_ref, dcq_ref, cb_ref, ca_ref, dkv_ref, ctx_ref, at_ref, x_hbm, da_ref, gr_hbm, kv_ref,
                  buf, other, ksend, krecv, ss, rs, ss2, rs2, pair, x_ref, acc, gr_ref, osem, gsem):
    me = lax.axis_index("tensor")
    dp = lax.axis_index("dp")
    core = dp % 2
    partner = dp + 1 - 2 * core
    C, D = x_in.shape
    W = w_ref.shape[0]
    KP = ctx_ref.shape[0]
    R = D // ndp
    greet(n, me, [partner])
    gather = Gather(n, me, x_in, lambda t: x_ref.at[t], lambda t, i: x_ref.at[t, pl.ds(i * C // 2, C // 2)], ss, rs)
    gather.start()
    kv = {}
    for d in range(1, n):
        ksend[d - 1] = dkv_ref[me ^ d].astype(BF)
        kv[d] = remote(ksend.at[d - 1], krecv.at[d - 1], ss2.at[d - 1], rs2.at[d - 1], me ^ d)
        kv[d].start()

    kept = []

    def back(i, t):
        rows = pl.ds(pl.multiple_of(t * C, C), C)
        x = x_ref[t]
        kept.append(pltpu.make_async_copy(x_ref.at[t], x_hbm.at[t], osem.at[i]))
        kept[-1].start()
        da_ref[rows, :] = nt(x, w_ref[...]).astype(BF)
        term = tn(x, at_ref[rows, :])
        if i == 0:
            acc[...] = term
        else:
            acc[...] += term

    x_ref[me] = x_in[...]
    back(0, me)

    for j in range(ndp // 2):
        h2, cb = h2_ref[:, 2 * R * j : 2 * R * (j + 1)], cb_ref[:, 2 * R * j : 2 * R * (j + 1)]

        def weights(t, carry):
            for i, (a, b) in enumerate(((h2, dcq_ref[t]), (cb, ca_ref[t]))):
                res = tn(a, b).astype(BF)
                for c in range(2):
                    buf[c, t, j * R : (j + 1) * R, i * W : (i + 1) * W] = res[c * R : (c + 1) * R]
            return carry

        lax.fori_loop(0, n, weights, 0)
    swap = to_dp(buf.at[1 - core], other, pair.at[0], pair.at[1], partner)
    swap.start()
    gather.relay()
    dkv = dkv_ref[me]
    for d in range(1, n):
        kv[d].wait_recv()
        dkv = dkv + krecv[d - 1].astype(F32)
    for half in range(2):
        kvg = tn(ctx_ref[...], dkv[half * KP : (half + 1) * KP].astype(BF)).astype(BF)
        S = kvg.shape[0] // ndp
        for i in range(ndp):
            kv_ref[(2 * i + half) * S : (2 * i + half + 1) * S, W:] = kvg[i * S : (i + 1) * S]
    for d in range(1, n - 1):
        gather.wait(d)
        back(d, me ^ d)
    swap.wait_recv()

    def leave(t):
        return pltpu.make_async_copy(gr_ref.at[t], gr_hbm.at[t], gsem.at[t])

    def add(t, carry):
        gr_ref[t] = (buf[core, t].astype(F32) + other[t].astype(F32)).astype(BF)
        leave(t).start()
        return carry

    lax.fori_loop(0, n, add, 0)
    gather.wait(n - 1)
    back(n - 1, me ^ (n - 1))
    kv_ref[:, :W] = acc[...].astype(BF)
    gather.finish()
    for copy in kept:
        copy.wait()
    for t in range(n):
        leave(t).wait()
    for d in range(1, n):
        kv[d].wait_send()
    swap.wait_send()


def gather_back(n, ndp, x, w, h2, dcq, cb, ca, dkv, ctx, attn):
    C, D = x.shape
    W = w.shape[0]
    KP = ctx.shape[0]
    half = (n, D // 2, 2 * W)
    return pl.pallas_call(
        functools.partial(gather_kernel, n, ndp),
        in_specs=[VSPEC] * 9,
        out_specs=[ANYSPEC, VSPEC, ANYSPEC, VSPEC],
        out_shape=[sds((n, C, D), BF), sds((n * C, W), BF), sds(half, BF), sds((D, 2 * W), BF)],
        scratch_shapes=[pltpu.VMEM((2, *half), BF), pltpu.VMEM(half, BF)]
        + [pltpu.VMEM((n - 1, 2 * KP, W), BF)] * 2
        + [pltpu.SemaphoreType.DMA((links(n),))] * 2
        + [pltpu.SemaphoreType.DMA((n - 1,))] * 2
        + [pltpu.SemaphoreType.DMA((2,))]
        + [pltpu.VMEM((n, C, D), BF), pltpu.VMEM((D, W), F32), pltpu.VMEM(half, BF)]
        + [pltpu.SemaphoreType.DMA((n,))] * 2,
        compiler_params=params(collective_id=2, has_side_effects=True),
        cost_estimate=cost(2 * n * C * W * D + 2e10, 8 * C * D),
        name="gather_back",
    )(x, w, h2, dcq, cb, ca, dkv, ctx, attn)


def attn_bwd_kernel(n, q_ref, k_ref, v_ref, o_ref, do_ref, lse_ref, c_ref, s_ref, h_hbm, a_hbm,
                    dq_ref, dk_ref, dv_ref, gr_hbm, x_ref, dk_acc, dv_acc, kt_ref, sbuf, rbuf, ss, rs,
                    a_ref, h_ref, lsem, gr_ref, osem):
    me = lax.axis_index("tensor")
    T, W = q_ref.shape
    G = lane_group(W)
    qb = 256
    mult = SCALE * LOG2E
    nh = G // HEAD_DIM
    greet(n, me)
    shards = ShardSum(n, me, a_ref, sbuf, rbuf, ss, rs)
    shards.start(a_hbm)
    a, h_all = Late(a_hbm, a_ref, lsem.at[0]), Late(h_hbm, h_ref, lsem.at[1])
    masks = [m.astype(BF) for m in head_masks(1, G)]
    head_rows = jnp.where(
        lax.broadcasted_iota(jnp.int32, (16, G), 0) == lax.broadcasted_iota(jnp.int32, (16, G), 1) // HEAD_DIM, 1.0, 0.0
    ).astype(BF)

    def heads(g, outer):
        cols = pl.ds(pl.multiple_of(g * G, G), G) if G < W else slice(None)
        k, v = k_ref[:, cols], v_ref[:, cols]
        kt_ref[...] = jnp.transpose(k.astype(F32)).astype(BF)
        dk_acc[...] = jnp.zeros_like(dk_acc)
        dv_acc[...] = jnp.zeros_like(dv_acc)

        def block(i, carry):
            rows = pl.ds(pl.multiple_of(i * qb, qb), qb)
            q = q_ref[rows, cols]
            do = do_ref[rows, cols]
            prod = do.astype(F32) * o_ref[rows, cols].astype(F32)
            high = prod.astype(BF)
            delta = nt(head_rows, high) + nt(head_rows, (prod - high.astype(F32)).astype(BF))
            lse = lse_ref[g, :, rows]
            parts = []
            for h in range(nh):
                qm = q * masks[h]
                dom = do * masks[h]
                st = nt(k, qm)
                pt = jnp.exp2(st * mult - lse[h : h + 1, :])
                dpt = nt(v, dom)
                dst = (pt * (dpt - delta[h : h + 1, :])).astype(BF)
                dv_acc[...] += nn(pt.astype(BF), dom)
                dk_acc[...] += nn(dst, qm)
                parts.append(nn(kt_ref[h * HEAD_DIM : (h + 1) * HEAD_DIM, :], dst))
            dq = jnp.transpose(jnp.concatenate(parts, 0)) * SCALE
            dq_ref[rows, cols] = (dq * c_ref[rows, :] - turned(dq) * s_ref[rows, :]).astype(BF)
            return carry

        lax.fori_loop(0, T // qb, block, 0)
        dk = dk_acc[...] * SCALE
        dk_ref[:, cols] = (dk * c_ref[...] - turned(dk) * s_ref[...]).astype(BF)
        dv_ref[:, cols] = dv_acc[...].astype(BF)
        return outer

    lax.fori_loop(0, W // G, heads, 0)
    a()
    shards.middle()
    h_all()
    tf = 256

    def leave(j):
        rows = pl.ds(pl.multiple_of(j * tf, tf), tf)
        return pltpu.make_async_copy(gr_ref.at[rows], gr_hbm.at[rows], osem.at[j])

    def weights(j, carry):
        rows = pl.ds(pl.multiple_of(j * tf, tf), tf)
        h = h_ref[:, rows]
        for i, g_ref in enumerate((dq_ref, dk_ref, dv_ref)):
            gr_ref[rows, i * W : (i + 1) * W] = tn(h, g_ref[...]).astype(BF)
        leave(j).start()
        return carry

    lax.fori_loop(0, gr_ref.shape[0] // tf, weights, 0)
    shards.store(x_ref)
    for j in range(gr_ref.shape[0] // tf):
        leave(j).wait()


def attn_bwd(n, q, k, v, o, do, lse, cs, sn, h, a):
    T, W = q.shape
    D = h.shape[1]
    G = lane_group(W)
    _, R, N = a.shape
    slots = 6 if n == 4 else n - 1
    H = R // 2 if n == 4 else R
    return pl.pallas_call(
        functools.partial(attn_bwd_kernel, n),
        in_specs=[VSPEC] * 8 + [ANYSPEC] * 2,
        out_specs=[VSPEC] * 3 + [ANYSPEC, VSPEC],
        out_shape=[sds((T, W), BF)] * 3 + [sds((D, 3 * W), BF), sds((R, N), BF)],
        scratch_shapes=[pltpu.VMEM((T, G), F32), pltpu.VMEM((T, G), F32), pltpu.VMEM((G, T), BF)]
        + [pltpu.VMEM((2, H, N), BF), pltpu.VMEM((slots, H, N), BF)]
        + [pltpu.SemaphoreType.DMA((slots,))] * 2
        + held(a, h)
        + [pltpu.VMEM((D, 3 * W), BF), pltpu.SemaphoreType.DMA((D // 256,))],
        compiler_params=params(collective_id=5, has_side_effects=True),
        cost_estimate=cost(40 * T * T * W, 16 * T * W, T * T * W // HEAD_DIM),
        name="attn_bwd",
    )(q, k, v, o, do, lse, cs, sn, h, a)


def last_kernel(n, ndp, dq_ref, dk_ref, dv_ref, wq_ref, wk_ref, wv_ref, x_hbm, da_ref, g_ref, gg_in,
                lbuf, gg_ref, sbuf, rbuf, gbuf, gsum, gown, gall, ss, rs, ss2, rs2, ss3, rs3, ss4, rs4, x_buf, lsem):
    me = lax.axis_index("tensor")
    dp = lax.axis_index("dp")
    C, D = x_buf.shape
    x = Late(rows_of(x_hbm, me, C), x_buf, lsem.at[0])
    R = D // ndp
    others = [(dp + i) % ndp for i in range(1, ndp)]
    greet(n, me, others)

    def part(t):
        rows = pl.ds(pl.multiple_of(t * C, C), C)
        return nt(dq_ref[rows, :], wq_ref[...]) + nt(dk_ref[rows, :], wk_ref[...]) + nt(dv_ref[rows, :], wv_ref[...])

    total, copies = reduce_parts(n, me, part, lambda: None, sbuf, rbuf, ss, rs)
    u, inverse = unit(x()[...].astype(F32))
    row = lax.broadcasted_iota(jnp.int32, (8, D), 0)
    gsum[...] = gg_in[...] + jnp.where(row == 2, jnp.sum(total * u, axis=0, keepdims=True), 0.0)
    small = {}
    for d in range(1, n):
        small[d] = remote(gsum, gbuf.at[d - 1], ss3.at[d - 1], rs3.at[d - 1], me ^ d)
        small[d].start()
    lbuf[me] = (da_ref[...] + norm_back(total, u, inverse, g_ref[...].reshape(1, D))).astype(BF)
    gather = Gather(
        n, me, lbuf.at[me], lambda t: lbuf.at[t], lambda t, i: lbuf.at[t, pl.ds(i * C // 2, C // 2)], ss2, rs2
    )
    gather.start()
    gains = gsum[...]
    for d in range(1, n):
        small[d].wait_recv()
        gains = gains + gbuf[d - 1]
    for i in range(ndp):
        gown[i] = gains[:, i * R : (i + 1) * R]
    sums = []
    for i, other in enumerate(others):
        sums.append(to_dp(gown.at[other], gall.at[i], ss4.at[i], rs4.at[i], other))
        sums[i].start()
    gather.relay()
    mine = gown[dp]
    for i in range(ndp - 1):
        sums[i].wait_recv()
        mine = mine + gall[i]
    gg_ref[...] = mine
    for d in range(1, n):
        gather.wait(d)
    gather.finish()
    for copy in (*copies.values(), *small.values(), *sums):
        copy.wait_send()


def last(n, ndp, dq, dk, dv, wq, wk, wv, x, da, gain, gains):
    T, W = dq.shape
    C, D = da.shape
    return pl.pallas_call(
        functools.partial(last_kernel, n, ndp),
        in_specs=[VSPEC] * 6 + [ANYSPEC] + [VSPEC] * 3,
        out_specs=[VSPEC] * 2,
        out_shape=[sds((n, C, D), BF), sds((8, D // ndp), F32)],
        scratch_shapes=reduce_bufs(n, C, D)[:2]
        + [pltpu.VMEM((n - 1, 8, D), F32), pltpu.VMEM((8, D), F32)]
        + [pltpu.VMEM((ndp, 8, D // ndp), F32), pltpu.VMEM((ndp - 1, 8, D // ndp), F32)]
        + reduce_bufs(n, C, D)[2:]
        + [pltpu.SemaphoreType.DMA((links(n),))] * 2
        + [pltpu.SemaphoreType.DMA((n - 1,))] * 2
        + [pltpu.SemaphoreType.DMA((ndp - 1,))] * 2
        + held(sds((C, D), BF)),
        compiler_params=params(collective_id=3, has_side_effects=True),
        cost_estimate=cost(6 * T * W * D + 4e10, 8 * T * D),
        name="last",
    )(dq, dk, dv, wq, wk, wv, x, da, gain, gains)


def cross_fwd_kernel(n, ctx, h_ref, x_ref, wq_ref, kv_ref, wo_hbm, g_ref, q_ref, o_ref, after_ref, h3_ref, wo_ref, lsem):
    wo = Late(wo_hbm, wo_ref, lsem.at[0])
    _, C, W = q_ref.shape
    KP = kv_ref.shape[1] // 2
    mult = SCALE * LOG2E
    G = lane_group(W)
    per = W // G
    masks = [m.astype(BF) for m in head_masks(1, G)]
    lane = lax.broadcasted_iota(jnp.int32, (C, G), 1) // HEAD_DIM
    valid = lax.broadcasted_iota(jnp.int32, (C, KP), 1) < ctx

    def group(g, carry):
        t = g // per
        cols = pl.ds(pl.multiple_of(g % per * G, G), G) if per > 1 else slice(None)
        q = nn(h_ref[...], wq_ref[t, :, cols]).astype(BF)
        q_ref[t, :, cols] = q
        k, v = kv_ref[t, :KP, cols], kv_ref[t, KP:, cols]
        out = jnp.zeros((C, G), F32)
        for h in range(G // HEAD_DIM):
            s = jnp.where(valid, nt(q * masks[h], k), -1e30)
            p = jnp.exp2((s - jnp.max(s, axis=-1, keepdims=True)) * mult)
            o = nn(p.astype(BF), v) / jnp.sum(p, axis=-1, keepdims=True)
            out = jnp.where(lane == h, o, out)
        o_ref[t, :, cols] = out.astype(BF)
        return carry

    lax.fori_loop(0, n * per, group, 0)
    D = h_ref.shape[1]
    tf = 256
    wo()

    def project(j, carry):
        cols = pl.ds(pl.multiple_of(j * tf, tf), tf)
        total = nn(o_ref[0], wo_ref[0, :, cols])
        for t in range(1, n):
            total = total + nn(o_ref[t], wo_ref[t, :, cols])
        after_ref[:, cols] = x_ref[:, cols] + total
        return carry

    lax.fori_loop(0, D // tf, project, 0)
    u, _ = unit(after_ref[...])
    h3_ref[...] = (u * g_ref[...].reshape(1, D)).astype(BF)


def cross_fwd(ctx, h, x, wq, kv, wo, gain):
    C, D = h.shape
    n, W = wq.shape[0], wq.shape[2]
    return pl.pallas_call(
        functools.partial(cross_fwd_kernel, n, ctx),
        in_specs=[VSPEC] * 4 + [ANYSPEC, VSPEC],
        out_specs=[VSPEC] * 4,
        out_shape=[sds((n, C, W), BF), sds((n, C, W), BF), sds((C, D), F32), sds((C, D), BF)],
        scratch_shapes=held(wo),
        compiler_params=params(),
        cost_estimate=cost(4 * C * D * n * W + 16 * C * 256 * n * W, 8 * D * n * W),
        name="cross_fwd",
    )(h, x, wq, kv, wo, gain)


def cross_bwd_kernel(n, ctx, dh3_ref, after2_ref, cot_hbm, g3_ref, wo_hbm, q_ref, kv_ref, wq_hbm, after1_hbm, g2_ref, bo_in,
                     cb_ref, dq_ref, dkv_ref, da_ref, sb_ref, gg_ref, bo_ref, dh2_ref, ss, rs,
                     cot_buf, wo_ref, wq_ref, after1_buf, lsem):
    me = lax.axis_index("tensor")
    cot, wo, wq, after1 = (
        Late(src, dst, lsem.at[i])
        for i, (src, dst) in enumerate(
            (
                (rows_of(cot_hbm, me, cot_buf.shape[0]), cot_buf),
                (wo_hbm, wo_ref),
                (wq_hbm, wq_ref),
                (after1_hbm, after1_buf),
            )
        )
    )
    _, C, W = q_ref.shape
    KP = kv_ref.shape[1] // 2
    D = da_ref.shape[1]
    mult = SCALE * LOG2E
    G = lane_group(W)
    per = W // G
    masks = [m.astype(BF) for m in head_masks(1, G)]
    lane = lax.broadcasted_iota(jnp.int32, (C, G), 1) // HEAD_DIM
    valid = lax.broadcasted_iota(jnp.int32, (C, KP), 1) < ctx
    greet(n, me)
    gather = Gather(n, me, bo_in, lambda t: bo_ref.at[t], lambda t, i: bo_ref.at[t, pl.ds(i * C // 2, C // 2)], ss, rs)
    gather.start()
    bo_ref[me] = bo_in[...]
    dh3 = dh3_ref[...]
    u3, inv3 = unit(after2_ref[...])
    gain3 = jnp.sum(dh3 * u3, axis=0, keepdims=True)
    da2 = cot()[...].astype(F32) + norm_back(dh3, u3, inv3, g3_ref[...].reshape(1, D))
    da_ref[...] = da2
    cb_ref[...] = da2.astype(BF)
    wo()

    def group(g, carry):
        t = g // per
        cols = pl.ds(pl.multiple_of(g % per * G, G), G) if per > 1 else slice(None)
        do = nt(cb_ref[...], wo_ref[t, cols, :]).astype(BF)
        q, k, v = q_ref[t, :, cols], kv_ref[t, :KP, cols], kv_ref[t, KP:, cols]
        dq = jnp.zeros((C, G), F32)
        dk = jnp.zeros((KP, G), F32)
        dv = jnp.zeros((KP, G), F32)
        for h in range(G // HEAD_DIM):
            qm = q * masks[h]
            dom = do * masks[h]
            s = jnp.where(valid, nt(qm, k), -1e30)
            p = jnp.exp2((s - jnp.max(s, axis=-1, keepdims=True)) * mult)
            p = p / jnp.sum(p, axis=-1, keepdims=True)
            dp = nt(dom, v)
            ds = (p * (dp - jnp.sum(p * dp, axis=-1, keepdims=True))).astype(BF)
            dq = jnp.where(lane == h, nn(ds, k), dq)
            dk = dk + tn(ds, qm)
            dv = dv + tn(p.astype(BF), dom)
        dq_ref[t, :, cols] = (dq * SCALE).astype(BF)
        dkv_ref[t, :KP, cols] = dk * SCALE
        dkv_ref[t, KP:, cols] = dv
        return carry

    lax.fori_loop(0, n * per, group, 0)
    gather.relay()
    wq()
    tf = 256

    def project(j, carry):
        cols = pl.ds(pl.multiple_of(j * tf, tf), tf)
        total = nt(dq_ref[0], wq_ref[0, cols, :])
        for t in range(1, n):
            total = total + nt(dq_ref[t], wq_ref[t, cols, :])
        dh2_ref[:, cols] = total
        return carry

    lax.fori_loop(0, D // tf, project, 0)
    dh2 = dh2_ref[...]
    u2, inv2 = unit(after1()[...])
    gain2 = jnp.sum(dh2 * u2, axis=0, keepdims=True)
    da1 = da_ref[...] + norm_back(dh2, u2, inv2, g2_ref[...].reshape(1, D))
    da_ref[...] = da1
    sb_ref[...] = da1.astype(BF)
    row = lax.broadcasted_iota(jnp.int32, (8, D), 0)
    gg_ref[...] = jnp.where(row == 0, gain3, 0.0) + jnp.where(row == 1, gain2, 0.0)
    for d in range(1, n):
        gather.wait(d)
    gather.finish()


def cross_bwd(ctx, dh3, after2, cot, g3, wo, q, kv, wq, after1, g2, bo):
    C, D = after2.shape
    n, W = wq.shape[0], wq.shape[2]
    return pl.pallas_call(
        functools.partial(cross_bwd_kernel, n, ctx),
        in_specs=[VSPEC, VSPEC, ANYSPEC, VSPEC, ANYSPEC, VSPEC, VSPEC, ANYSPEC, ANYSPEC, VSPEC, VSPEC],
        out_specs=[VSPEC] * 7,
        out_shape=[
            sds((C, D), BF),
            sds((n, C, W), BF),
            sds(kv.shape, F32),
            sds((C, D), F32),
            sds((C, D), BF),
            sds((8, D), F32),
            sds((n, C, D), BF),
        ],
        scratch_shapes=[pltpu.VMEM((C, D), F32)]
        + [pltpu.SemaphoreType.DMA((links(n),))] * 2
        + held(sds((C, D), BF), wo, wq, after1),
        compiler_params=params(collective_id=7, has_side_effects=True),
        cost_estimate=cost(4 * C * D * n * W + 40 * C * 256 * n * W, 8 * D * n * W),
        name="cross_bwd",
    )(dh3, after2, cot, g3, wo, q, kv, wq, after1, g2, bo)


def body(latents, context, cotangent, g1, wq, wk, wv, wo, g2, xq, xk, xv, xo, g3, wg, wu, wd, n, ndp):
    _, T, D = latents.shape
    ctx = context.shape[1]
    W = wq.shape[1]
    F = wg.shape[1]
    C = T // n
    x = latents.reshape(T, D)
    gb = cotangent.reshape(T, D)
    ctx_rows = context.reshape(ctx, -1)
    KP = -(-ctx // 16) * 16
    cs, sn = tables(T, lane_group(W))

    ctx_pad = jnp.pad(ctx_rows, ((0, KP - ctx), (0, 0)))
    h1, q, k, v, attn, lse, xq_all, xo_all, kv_all = front(n, ctx, x, g1, wq, wk, wv, cs, sn, xq, xo, ctx_pad, xk, xv)
    after1, h2 = out_rs(n, attn, wo, x, g2)
    cq, cattn, after2, h3_own = cross_fwd(ctx, h2, after1, xq_all, kv_all, xo_all, g3)
    h3, hidden, dgu, dh3 = ff(n, h3_own, gb, wg, wu, wd)
    h3 = h3.reshape(T, D)

    def scatter(a, axis):
        return lax.psum_scatter(a, axis, scatter_dimension=0, tiled=True)

    down_part = down_grads(gb, hidden)
    down_part, dgu = lax.optimization_barrier((down_part, dgu))
    down_grad = scatter(down_part, "dp")
    out_own, gu_part = feed_grads(n, hidden, wd, after2, h3, dgu)
    dh3, gu_part = lax.optimization_barrier((dh3, gu_part))
    gu_grad = scatter(gu_part, "dp")

    cb, dcq, dckv, dafter1, sb_own, gains, block_out = cross_bwd(
        ctx, dh3, after2, gb, g3, xo_all, cq, kv_all, xq_all, after1, g2, out_own
    )
    sb_own, down_grad = lax.optimization_barrier((sb_own, down_grad))
    sb, dattn, cross_part, early_part = gather_back(n, ndp, sb_own, wo, h2, dcq, cb, cattn, dckv, ctx_pad, attn)
    early_grads = scatter(early_part, "dp")
    dq, dk, dv, self_part, cross_part = attn_bwd(n, q, k, v, attn, dattn, lse, cs, sn, h1, cross_part)
    cores = [[i for i in range(ndp) if i % 2 == c] for c in range(2)]
    cross_grads = lax.psum_scatter(cross_part, "dp", scatter_dimension=0, axis_index_groups=cores, tiled=True)
    self_grads = scatter(self_part, "dp")
    dq, gu_grad = lax.optimization_barrier((dq, gu_grad))
    latent_grad, gains = last(n, ndp, dq, dk, dv, wq, wk, wv, x, dafter1, g1, gains)

    latent_grad = latent_grad.astype(F32)
    gu_grad = gu_grad.astype(F32)
    gate_grad, up_grad, down_grad = gu_grad[:, :F], gu_grad[:, F:], down_grad.astype(F32).T
    early_grads, gains, latent_grad, gate_grad, up_grad = lax.optimization_barrier(
        (early_grads, gains, latent_grad, gate_grad, up_grad)
    )
    early_grads = early_grads.astype(F32)
    so_grad, kv_grads = early_grads[:, :W].T, early_grads[:, W:].reshape(2, D // ndp // 2, W)
    cross_grads, so_grad, kv_grads = lax.optimization_barrier((cross_grads, so_grad, kv_grads))
    cross_grads = cross_grads.astype(F32)
    xq_grad, xo_grad = cross_grads[:, :W], cross_grads[:, W:].T
    self_grads, xq_grad, xo_grad = lax.optimization_barrier((self_grads, xq_grad, xo_grad))
    self_grads = self_grads.astype(F32)
    return (
        block_out.reshape(1, T, D),
        latent_grad.reshape(1, T, D),
        gains[2],
        self_grads[:, :W],
        self_grads[:, W : 2 * W],
        self_grads[:, 2 * W : 3 * W],
        so_grad,
        gains[1],
        xq_grad,
        kv_grads[0],
        kv_grads[1],
        xo_grad,
        gains[0],
        gate_grad,
        up_grad,
        down_grad,
    )


def solution(mesh):
    tokens = P("dp", None, None)
    cols = P(None, "tensor")
    rows = P("tensor", None)
    return jax.shard_map(
        functools.partial(body, n=mesh.shape["tensor"], ndp=mesh.shape["dp"]),
        mesh=mesh,
        in_specs=(tokens, tokens, tokens, P(), cols, cols, cols, rows, P(), cols, cols, cols, rows, P(), cols, cols, rows),
        out_specs=(
            tokens,
            tokens,
            P("dp"),
            P("dp", "tensor"),
            P("dp", "tensor"),
            P("dp", "tensor"),
            P("tensor", "dp"),
            P("dp"),
            P("dp", "tensor"),
            P("dp", "tensor"),
            P("dp", "tensor"),
            P("tensor", "dp"),
            P("dp"),
            P("dp", "tensor"),
            P("dp", "tensor"),
            P("tensor", "dp"),
        ),
        check_vma=False,
    )
```

```python
import functools

import jax
import jax.numpy as jnp
from jax import lax
from jax.experimental import pallas as pl
from jax.experimental.pallas import tpu as pltpu
from jax.sharding import PartitionSpec as P

HEAD_DIM = 64
HALF = HEAD_DIM // 2
EPS = 1e-05
BF = jnp.bfloat16
F32 = jnp.float32
LOG2E = 1.4426950408889634
SCALE = HEAD_DIM**-0.5
VMEM_BYTES = 60 << 20
MESH_ID = pl.DeviceIdType.MESH
VSPEC = pl.BlockSpec(memory_space=pltpu.VMEM)
ANYSPEC = pl.BlockSpec(memory_space=pl.ANY)


def nn(a, b):
    return lax.dot_general(a, b, (((1,), (0,)), ((), ())), preferred_element_type=F32)


def nt(a, b):
    return lax.dot_general(a, b, (((1,), (1,)), ((), ())), preferred_element_type=F32)


def tn(a, b):
    return lax.dot_general(a, b, (((0,), (0,)), ((), ())), preferred_element_type=F32)


def sds(shape, dtype):
    return jax.ShapeDtypeStruct(shape, dtype)


def params(**kw):
    return pltpu.CompilerParams(vmem_limit_bytes=VMEM_BYTES, **kw)


def cost(flops, nbytes, trans=0):
    return pl.CostEstimate(flops=1000, bytes_accessed=1000, transcendentals=0)


def unit(x):
    center = x - jnp.mean(x, axis=-1, keepdims=True)
    inverse = lax.rsqrt(jnp.mean(center * center, axis=-1, keepdims=True) + EPS)
    return center * inverse, inverse


def norm_back(grad, u, inverse, gain):
    e = grad * gain
    mean_e = jnp.mean(e, axis=-1, keepdims=True)
    mean_p = jnp.mean(e * u, axis=-1, keepdims=True)
    return inverse * (e - mean_e - u * mean_p)


def lane_group(width):
    return 128 if width % 128 == 0 else width


def tables(length, group):
    freq = jnp.tile(10000.0 ** (-jnp.arange(HALF, dtype=F32) / HALF), group // HALF)
    angles = lax.broadcasted_iota(F32, (length, group), 0) * freq[None, :]
    front = lax.broadcasted_iota(jnp.int32, (length, group), 1) % HEAD_DIM < HALF
    return jnp.cos(angles), jnp.where(front, -1.0, 1.0) * jnp.sin(angles)


def turned(a):
    width = a.shape[-1]
    lane = lax.broadcasted_iota(jnp.int32, a.shape, 1) % HEAD_DIM
    return jnp.where(lane < HALF, pltpu.roll(a, width - HALF, 1), pltpu.roll(a, HALF, 1))


def head_masks(rows, group):
    lane = lax.broadcasted_iota(jnp.int32, (rows, group), 1) // HEAD_DIM
    return [jnp.where(lane == h, 1.0, 0.0) for h in range(group // HEAD_DIM)]


def greet(n, me, dps=()):
    sem = pltpu.get_barrier_semaphore()
    for d in range(1, n):
        pl.semaphore_signal(sem, 1, device_id={"tensor": me ^ d}, device_id_type=MESH_ID)
    for dp in dps:
        pl.semaphore_signal(sem, 1, device_id={"dp": dp}, device_id_type=MESH_ID)
    pl.semaphore_wait(sem, n - 1 + len(dps))


def to_dp(src, dst, send, recv, target):
    return pltpu.make_async_remote_copy(src, dst, send, recv, device_id={"dp": target}, device_id_type=MESH_ID)


def remote(src, dst, send, recv, target):
    return pltpu.make_async_remote_copy(src, dst, send, recv, device_id={"tensor": target}, device_id_type=MESH_ID)


class Late:
    def __init__(self, src, dst, sem):
        self.dst, self.copy = dst, pltpu.make_async_copy(src, dst, sem)
        self.copy.start()

    def __call__(self):
        self.copy.wait()
        return self.dst


def held(*arrays):
    return [pltpu.VMEM(a.shape, a.dtype) for a in arrays] + [pltpu.SemaphoreType.DMA((len(arrays),))]


def rows_of(ref, t, C):
    return ref.at[pl.ds(pl.multiple_of(t * C, C), C)]


def links(n):
    return 4 if n == 4 else n - 1


class Gather:
    def __init__(self, n, me, src, slot, half, ss, rs):
        self.n, self.me, self.half, self.ss, self.rs = n, me, half, ss, rs
        self.copies = {
            d: remote(src, slot(me), ss.at[d - 1], rs.at[d - 1], me ^ d) for d in (range(1, n) if n != 4 else (1, 2))
        }
        self.passed = []

    def start(self):
        for copy in self.copies.values():
            copy.start()

    def relay(self):
        if self.n == 4:
            for i, d in enumerate((1, 2)):
                self.copies[d].wait_recv()
                block = self.half(self.me ^ d, i)
                copy = remote(block, block, self.ss.at[2 + i], self.rs.at[2 + i], self.me ^ (3 - d))
                copy.start()
                self.passed.append(copy)

    def wait(self, d):
        if self.n != 4:
            self.copies[d].wait_recv()
        elif d == 3:
            for copy in self.passed:
                copy.wait_recv()

    def finish(self):
        for copy in (*self.copies.values(), *self.passed):
            copy.wait_send()


def reduce_bufs(n, C, D):
    shape = (6, C, D // 2) if n == 4 else (n - 1, C, D)
    return [pltpu.VMEM(shape, BF)] * 2 + [pltpu.SemaphoreType.DMA((shape[0],))] * 2


def reduce_parts(n, me, part, filler, sbuf, rbuf, ss, rs):
    copies = {}

    def send(i, val, d):
        sbuf[i] = val.astype(BF)
        copies[i] = remote(sbuf.at[i], rbuf.at[i], ss.at[i], rs.at[i], me ^ d)
        copies[i].start()

    def got(i):
        copies[i].wait_recv()
        return rbuf[i].astype(F32)

    if n == 4:
        across = part(me ^ 3)
        H = across.shape[1] // 2
        send(0, across[:, :H], 1)
        send(2, across[:, H:], 2)
        one = part(me ^ 1)
        send(1, one[:, :H], 1)
        two = part(me ^ 2)
        send(3, two[:, H:], 2)
        total = part(me)
        filler()
        send(4, two[:, :H] + got(0), 2)
        send(5, one[:, H:] + got(2), 1)
        total = jnp.concatenate([total[:, :H] + got(1) + got(4), total[:, H:] + got(3) + got(5)], 1)
    else:
        for d in reversed(range(1, n)):
            send(d - 1, part(me ^ d), d)
        total = part(me)
        filler()
        for d in range(1, n):
            total = total + got(d - 1)
    return total, copies


class ShardSum:
    def __init__(self, n, me, a, sbuf, rbuf, ss, rs):
        self.n, self.me, self.a, self.sbuf, self.rbuf, self.ss, self.rs = n, me, a, sbuf, rbuf, ss, rs
        self.copies = {}

    def send(self, i, src, d):
        self.copies[i] = remote(src, self.rbuf.at[i], self.ss.at[i], self.rs.at[i], self.me ^ d)
        self.copies[i].start()

    def got(self, i):
        self.copies[i].wait_recv()
        return self.rbuf[i].astype(F32)

    def halves(self, d, a=None):
        a = self.a if a is None else a
        H = a.shape[1] // 2
        return a.at[self.me ^ d, pl.ds(0, H)], a.at[self.me ^ d, pl.ds(H, H)]

    def start(self, a):
        if self.n == 4:
            self.send(0, self.halves(3, a)[0], 1)
            self.send(2, self.halves(3, a)[1], 2)
            self.send(1, self.halves(1, a)[0], 1)
            self.send(3, self.halves(2, a)[1], 2)
        else:
            for d in range(1, self.n):
                self.send(d - 1, a.at[self.me ^ d], d)

    def middle(self):
        if self.n == 4:
            self.sbuf[0] = (self.halves(2)[0][...].astype(F32) + self.got(0)).astype(BF)
            self.send(4, self.sbuf.at[0], 2)
            self.sbuf[1] = (self.halves(1)[1][...].astype(F32) + self.got(2)).astype(BF)
            self.send(5, self.sbuf.at[1], 1)

    def store(self, out_ref):
        if self.n == 4:
            H = self.a.shape[1] // 2
            own = self.halves(0)
            out_ref[:H] = (own[0][...].astype(F32) + self.got(1) + self.got(4)).astype(BF)
            out_ref[H:] = (own[1][...].astype(F32) + self.got(3) + self.got(5)).astype(BF)
        else:
            total = self.a[self.me].astype(F32)
            for d in range(1, self.n):
                total = total + self.got(d - 1)
            out_ref[...] = total.astype(BF)
        for copy in self.copies.values():
            copy.wait_send()


def front_kernel(n, ctx, x_hbm, g_ref, wq_hbm, wk_hbm, wv_hbm, c_ref, s_ref, xq_ref, xo_ref, ctx_ref, xk_hbm, xv_hbm,
                 h_hbm, q_hbm, k_hbm, v_hbm, o_ref, lse_ref, xqa_ref, xoa_ref, kva_ref,
                 kv_own, sq, rq, so, ro, sk, rk, fsq, frq, fso, fro, local,
                 x_buf, wq_buf, wk_buf, wv_buf, xk_buf, xv_buf, lsem, h_ref, q_ref, k_ref, v_ref, osem):
    xk, xv, x, wq, wk, wv = (
        Late(src, dst, lsem.at[i])
        for i, (src, dst) in enumerate(
            (
                (xk_hbm, xk_buf),
                (xv_hbm, xv_buf),
                (x_hbm, x_buf),
                (wq_hbm, wq_buf),
                (wk_hbm, wk_buf),
                (wv_hbm, wv_buf),
            )
        )
    )
    me = lax.axis_index("tensor")
    dp = lax.axis_index("dp")
    core = dp % 2
    partner = dp + 1 - 2 * core
    T, D = x_hbm.shape
    W = q_ref.shape[1]
    KP = ctx_ref.shape[0]
    greet(n, me, [partner])

    rows_q = pl.ds(pl.multiple_of(core * (D // 2), 16), D // 2)
    rows_o = pl.ds(pl.multiple_of(core * (W // 2), 16), W // 2)
    def quarter(ref, rows):
        return lambda t, i: ref.at[t, pl.ds(pl.multiple_of(core * (rows // 2) + i * (rows // 4), 16), rows // 4)]

    gq = Gather(n, me, xq_ref.at[rows_q], lambda t: xqa_ref.at[t, rows_q], quarter(xqa_ref, D), sq, rq)
    go = Gather(n, me, xo_ref.at[rows_o], lambda t: xoa_ref.at[t, rows_o], quarter(xoa_ref, W), so, ro)
    gk = Gather(n, me, kv_own, lambda t: kva_ref.at[t], lambda t, i: kva_ref.at[t, pl.ds(i * KP, KP)], sk, rk)
    gq.start()
    go.start()
    own = [
        pltpu.make_async_copy(xq_ref, xqa_ref.at[me], local.at[0]),
        pltpu.make_async_copy(xo_ref, xoa_ref.at[me], local.at[1]),
    ]
    for copy in own:
        copy.start()
    kv_own[:KP] = nn(ctx_ref[...], xk()[...]).astype(BF)
    kv_own[KP:] = nn(ctx_ref[...], xv()[...]).astype(BF)
    gk.start()
    kva_ref[me] = kv_own[...]

    tb = 256
    reps = W // c_ref.shape[1]
    x_ref, wq_ref, wk_ref, wv_ref = x(), wq(), wk(), wv()

    def project(i, carry):
        rows = pl.ds(pl.multiple_of(i * tb, tb), tb)
        u, _ = unit(x_ref[rows, :].astype(F32))
        h = (u * g_ref[...].reshape(1, D)).astype(BF)
        h_ref[rows, :] = h
        c = jnp.concatenate([c_ref[rows, :]] * reps, 1)
        s = jnp.concatenate([s_ref[rows, :]] * reps, 1)
        for w_ref, out_ref in ((wq_ref, q_ref), (wk_ref, k_ref)):
            a = nn(h, w_ref[...])
            out_ref[rows, :] = (a * c + turned(a) * s).astype(BF)
        v_ref[rows, :] = nn(h, wv_ref[...]).astype(BF)
        return carry

    lax.fori_loop(0, T // tb, project, 0)
    kept = [
        pltpu.make_async_copy(src, dst, osem.at[i])
        for i, (src, dst) in enumerate(((h_ref, h_hbm), (q_ref, q_hbm), (k_ref, k_hbm), (v_ref, v_hbm)))
    ]
    for copy in kept:
        copy.start()
    gq.relay()

    G = lane_group(W)
    mult = SCALE * LOG2E
    masks = [m.astype(BF) for m in head_masks(1, G)]
    lane = lax.broadcasted_iota(jnp.int32, (tb, G), 1) // HEAD_DIM
    stat_lane = lax.broadcasted_iota(jnp.int32, (tb, 128), 1)

    def heads(g, carry):
        cols = pl.ds(pl.multiple_of(g * G, G), G) if G < W else slice(None)
        k, v = k_ref[:, cols], v_ref[:, cols]

        def block(i, inner):
            rows = pl.ds(pl.multiple_of(i * tb, tb), tb)
            q = q_ref[rows, cols]
            out = jnp.zeros((tb, G), F32)
            stats = jnp.zeros((tb, 128), F32)
            for h in range(G // HEAD_DIM):
                s = nt(q * masks[h], k)
                top = jnp.max(s, axis=-1, keepdims=True) * mult
                p = jnp.exp2(s * mult - top)
                total = jnp.sum(p, axis=-1, keepdims=True)
                o = nn(p.astype(BF), v) / total
                out = jnp.where(lane == h, o, out)
                stats = jnp.where(stat_lane == h, top + jnp.log2(total), stats)
            o_ref[rows, cols] = out.astype(BF)
            lse_ref[g, :, rows] = jnp.transpose(stats)[:8]
            return inner

        return lax.fori_loop(0, T // tb, block, carry)

    lax.fori_loop(0, W // G, heads, 0)

    go.relay()
    gk.relay()
    passed = []
    for gather, ref, rows, send, recv in ((gq, xqa_ref, rows_q, fsq, frq), (go, xoa_ref, rows_o, fso, fro)):
        for d in range(1, n):
            gather.wait(d)
            block = ref.at[me ^ d, rows]
            copy = to_dp(block, block, send.at[d - 1], recv.at[d - 1], partner)
            copy.start()
            passed.append(copy)
    for copy in (*own, *kept):
        copy.wait()
    for d in range(1, n):
        gk.wait(d)
    for copy in passed:
        copy.wait_recv()
    for copy in (gq, go, gk):
        copy.finish()
    for copy in passed:
        copy.wait_send()


def front(n, ctx, x, gain, wq, wk, wv, cs, sn, xq, xo, ctx_rows, xk, xv):
    T, D = x.shape
    W = wq.shape[1]
    KP = ctx_rows.shape[0]
    groups = W // lane_group(W)
    link, pair = pltpu.SemaphoreType.DMA((links(n),)), pltpu.SemaphoreType.DMA((n - 1,))
    return pl.pallas_call(
        functools.partial(front_kernel, n, ctx),
        in_specs=[ANYSPEC, VSPEC] + [ANYSPEC] * 3 + [VSPEC] * 5 + [ANYSPEC] * 2,
        out_specs=[ANYSPEC] * 4 + [VSPEC] * 2 + [ANYSPEC] * 2 + [VSPEC],
        out_shape=[sds((T, D), BF)]
        + [sds((T, W), BF)] * 4
        + [sds((groups, 8, T), F32), sds((n, D, W), BF), sds((n, W, D), BF), sds((n, 2 * KP, W), BF)],
        scratch_shapes=[pltpu.VMEM((2 * KP, W), BF)] + [link] * 6 + [pair] * 4 + [pltpu.SemaphoreType.DMA((2,))]
        + held(x, wq, wk, wv, xk, xv)
        + held(sds((T, D), BF), *[sds((T, W), BF)] * 3),
        compiler_params=params(collective_id=4, has_side_effects=True),
        cost_estimate=cost(6 * T * D * W, 4 * T * D + 6 * D * W + 6 * T * W),
        name="front",
    )(x, gain, wq, wk, wv, cs, sn, xq, xo, ctx_rows, xk, xv)


def out_rs_kernel(n, a_ref, w_ref, x_hbm, g_ref, after_ref, h_ref, sbuf, rbuf, ss, rs, x_buf, lsem):
    me = lax.axis_index("tensor")
    C, D = x_buf.shape
    x = Late(rows_of(x_hbm, me, C), x_buf, lsem.at[0])
    greet(n, me)

    def part(t):
        return nn(a_ref[pl.ds(pl.multiple_of(t * C, C), C), :], w_ref[...])

    total, copies = reduce_parts(n, me, part, lambda: None, sbuf, rbuf, ss, rs)
    after = x()[...].astype(F32) + total
    after_ref[...] = after
    u, _ = unit(after)
    h_ref[...] = (u * g_ref[...].reshape(1, D)).astype(BF)
    for copy in copies.values():
        copy.wait_send()


def out_rs(n, a, w, x, gain):
    T, D = x.shape
    C = T // n
    W = a.shape[1]
    return pl.pallas_call(
        functools.partial(out_rs_kernel, n),
        in_specs=[VSPEC, VSPEC, ANYSPEC, VSPEC],
        out_specs=[VSPEC] * 2,
        out_shape=[sds((C, D), F32), sds((C, D), BF)],
        scratch_shapes=reduce_bufs(n, C, D) + held(sds((C, D), BF)),
        compiler_params=params(collective_id=0, has_side_effects=True),
        cost_estimate=cost(2 * T * W * D + 2e10, 8 * C * D),
        name="out_rs",
    )(a, w, x, gain)


def ff_kernel(n, h_in, gb_hbm, wg_hbm, wu_hbm, wd_hbm, h_hbm, hid_hbm, dgu_hbm, dh_ref,
              gb_ref, wg_ref, wu_ref, wd_ref, sbuf, rbuf, ss, rs, ss2, rs2, ls, h_ref, hid_ref, dgu_ref, osem):
    me = lax.axis_index("tensor")
    C, D = h_in.shape
    F = wg_ref.shape[1]
    loads = [
        pltpu.make_async_copy(src, dst, ls.at[i])
        for i, (src, dst) in enumerate(((wg_hbm, wg_ref), (wu_hbm, wu_ref), (wd_hbm, wd_ref), (gb_hbm, gb_ref)))
    ]
    for c in loads:
        c.start()
    greet(n, me)
    gather = Gather(n, me, h_in, lambda t: h_ref.at[t], lambda t, i: h_ref.at[t, pl.ds(i * C // 2, C // 2)], ss, rs)
    gather.start()
    h_ref[me] = h_in[...]
    for c in loads:
        c.wait()
    tf = 512

    def chunk(t, store):
        rows = pl.ds(pl.multiple_of(t * C, C), C)
        h = h_ref[t]
        gb = gb_ref[rows, :]

        def tile(j, carry):
            cols = pl.ds(pl.multiple_of(j * tf, tf), tf)
            gate = nn(h, wg_ref[:, cols])
            up = nn(h, wu_ref[:, cols])
            dhid = nt(gb, wd_ref[cols, :])
            sig = 1.0 / (1.0 + jnp.exp(-gate))
            act = gate * sig
            hid_ref[rows, cols] = (act * up).astype(BF)
            dgu_ref[rows, cols] = (dhid * up * (sig * (1.0 + gate * (1.0 - sig)))).astype(BF)
            dgu_ref[rows, pl.ds(pl.multiple_of(F + j * tf, tf), tf)] = (dhid * act).astype(BF)
            return carry

        lax.fori_loop(0, F // tf, tile, 0)

        def back(j, carry):
            out = pl.ds(pl.multiple_of(j * tf, tf), tf)
            store(out, nt(dgu_ref[rows, :F], wg_ref[out, :]) + nt(dgu_ref[rows, F:], wu_ref[out, :]))
            return carry

        lax.fori_loop(0, D // tf, back, 0)

    def store_own(cols, val):
        dh_ref[:, cols] = val

    kept = []

    def keep(i, t):
        pieces = [(h_ref.at[t], h_hbm.at[t])]
        pieces += [(rows_of(a, t, C), rows_of(b, t, C)) for a, b in ((hid_ref, hid_hbm), (dgu_ref, dgu_hbm))]
        for k, (src, dst) in enumerate(pieces):
            kept.append(pltpu.make_async_copy(src, dst, osem.at[i, k]))
            kept[-1].start()

    chunk(me, store_own)
    keep(0, me)
    gather.relay()
    copies = {}
    for d in range(1, n):
        t = me ^ d
        gather.wait(d)

        def store_sent(cols, val):
            sbuf[d - 1, :, cols] = val.astype(BF)

        chunk(t, store_sent)
        keep(d, t)
        copies[d] = remote(sbuf.at[d - 1], rbuf.at[d - 1], ss2.at[d - 1], rs2.at[d - 1], t)
        copies[d].start()
    gather.finish()
    for d in range(1, n):
        copies[d].wait_recv()
        dh_ref[...] += rbuf[d - 1].astype(F32)
    for d in range(1, n):
        copies[d].wait_send()
    for copy in kept:
        copy.wait()


def ff(n, h, gb, wg, wu, wd):
    C, D = h.shape
    T = gb.shape[0]
    F = wg.shape[1]
    return pl.pallas_call(
        functools.partial(ff_kernel, n),
        in_specs=[VSPEC] + [ANYSPEC] * 4,
        out_specs=[ANYSPEC] * 3 + [VSPEC],
        out_shape=[sds((n, C, D), BF), sds((T, F), BF), sds((T, 2 * F), BF), sds((C, D), F32)],
        scratch_shapes=[
            pltpu.VMEM((T, D), BF),
            pltpu.VMEM((D, F), BF),
            pltpu.VMEM((D, F), BF),
            pltpu.VMEM((F, D), BF),
            pltpu.VMEM((n - 1, C, D), BF),
            pltpu.VMEM((n - 1, C, D), BF),
        ]
        + [pltpu.SemaphoreType.DMA((links(n),))] * 2
        + [pltpu.SemaphoreType.DMA((n - 1,))] * 2
        + [pltpu.SemaphoreType.DMA((4,))]
        + [pltpu.VMEM((n, C, D), BF), pltpu.VMEM((T, F), BF), pltpu.VMEM((T, 2 * F), BF)]
        + [pltpu.SemaphoreType.DMA((n, 3))],
        compiler_params=params(collective_id=1, has_side_effects=True),
        cost_estimate=cost(10 * T * D * F + 3e10, 6 * D * F + 8 * T * D),
        name="ff",
    )(h, gb, wg, wu, wd)


def down_kernel(gb_ref, hid_ref, o_ref):
    gb = gb_ref[...]
    tf = 512 if hid_ref.shape[1] % 512 == 0 else 256

    def down(j, carry):
        cols = pl.ds(pl.multiple_of(j * tf, tf), tf)
        o_ref[:, cols] = tn(gb, hid_ref[:, cols]).astype(BF)
        return carry

    lax.fori_loop(0, hid_ref.shape[1] // tf, down, 0)


def down_grads(gb, hidden):
    T, D = gb.shape
    F = hidden.shape[1]
    tb = 512
    return pl.pallas_call(
        down_kernel,
        grid=(D // tb,),
        in_specs=[
            pl.BlockSpec((T, tb), lambda i: (0, i)),
            pl.BlockSpec(hidden.shape, lambda i: (0, 0), pipeline_mode=pl.Buffered(1)),
        ],
        out_specs=pl.BlockSpec((tb, F), lambda i: (i, 0)),
        out_shape=sds((D, F), BF),
        compiler_params=params(),
        cost_estimate=cost(2 * T * D * F, 2 * D * F),
        name="down_grads",
    )(gb, hidden)


def feed_kernel(n, hid_ref, wd_ref, after_hbm, h_hbm, dgu_hbm, out_ref, gr_hbm,
                sbuf, rbuf, ss, rs, h_ref, dgu_ref, after_ref, lsem, gr_ref, osem):
    me = lax.axis_index("tensor")
    h, dgu, after = (
        Late(src, dst, lsem.at[i])
        for i, (src, dst) in enumerate(((h_hbm, h_ref), (dgu_hbm, dgu_ref), (after_hbm, after_ref)))
    )
    C, D = after_ref.shape
    F2 = dgu_ref.shape[1]
    greet(n, me)

    def part(t):
        return nn(hid_ref[pl.ds(pl.multiple_of(t * C, C), C), :], wd_ref[...])

    tb, tf = 512, 512

    def tile(j, carry):
        cols = pl.ds(pl.multiple_of(j * tf, tf), tf)
        for i in range(D // tb):
            rows = slice(i * tb, (i + 1) * tb)
            gr_ref[rows, cols] = tn(h_ref[:, rows], dgu_ref[:, cols]).astype(BF)
        leave(j).start()
        return carry

    def leave(j):
        cols = pl.ds(pl.multiple_of(j * tf, tf), tf)
        return pltpu.make_async_copy(gr_ref.at[:, cols], gr_hbm.at[:, cols], osem.at[j])

    def filler():
        h()
        dgu()
        lax.fori_loop(0, F2 // tf, tile, 0)

    total, copies = reduce_parts(n, me, part, filler, sbuf, rbuf, ss, rs)
    out_ref[...] = (after()[...] + total).astype(BF)
    for copy in copies.values():
        copy.wait_send()
    for j in range(F2 // tf):
        leave(j).wait()


def feed_grads(n, hidden, wd, after, h, dgu):
    C, D = after.shape
    T, F2 = dgu.shape
    return pl.pallas_call(
        functools.partial(feed_kernel, n),
        in_specs=[VSPEC] * 2 + [ANYSPEC] * 3,
        out_specs=[VSPEC, ANYSPEC],
        out_shape=[sds((C, D), BF), sds((D, F2), BF)],
        scratch_shapes=reduce_bufs(n, C, D)
        + held(h, dgu, after)
        + [pltpu.VMEM((D, F2), BF), pltpu.SemaphoreType.DMA((F2 // 512,))],
        compiler_params=params(collective_id=6, has_side_effects=True),
        cost_estimate=cost(3 * T * D * F2, 6 * D * F2),
        name="feed_grads",
    )(hidden, wd, after, h, dgu)


def gather_kernel(n, ndp, x_in, w_ref, h2_ref, dcq_ref, cb_ref, ca_ref, dkv_ref, ctx_ref, at_ref, x_hbm, da_ref, gr_hbm, kv_ref,
                  buf, other, ksend, krecv, ss, rs, ss2, rs2, pair, x_ref, acc, gr_ref, osem, gsem):
    me = lax.axis_index("tensor")
    dp = lax.axis_index("dp")
    core = dp % 2
    partner = dp + 1 - 2 * core
    C, D = x_in.shape
    W = w_ref.shape[0]
    KP = ctx_ref.shape[0]
    R = D // ndp
    greet(n, me, [partner])
    gather = Gather(n, me, x_in, lambda t: x_ref.at[t], lambda t, i: x_ref.at[t, pl.ds(i * C // 2, C // 2)], ss, rs)
    gather.start()
    kv = {}
    for d in range(1, n):
        ksend[d - 1] = dkv_ref[me ^ d].astype(BF)
        kv[d] = remote(ksend.at[d - 1], krecv.at[d - 1], ss2.at[d - 1], rs2.at[d - 1], me ^ d)
        kv[d].start()

    kept = []

    def back(i, t):
        rows = pl.ds(pl.multiple_of(t * C, C), C)
        x = x_ref[t]
        kept.append(pltpu.make_async_copy(x_ref.at[t], x_hbm.at[t], osem.at[i]))
        kept[-1].start()
        da_ref[rows, :] = nt(x, w_ref[...]).astype(BF)
        term = tn(x, at_ref[rows, :])
        if i == 0:
            acc[...] = term
        else:
            acc[...] += term

    x_ref[me] = x_in[...]
    back(0, me)

    for j in range(ndp // 2):
        h2, cb = h2_ref[:, 2 * R * j : 2 * R * (j + 1)], cb_ref[:, 2 * R * j : 2 * R * (j + 1)]

        def weights(t, carry):
            for i, (a, b) in enumerate(((h2, dcq_ref[t]), (cb, ca_ref[t]))):
                res = tn(a, b).astype(BF)
                for c in range(2):
                    buf[c, t, j * R : (j + 1) * R, i * W : (i + 1) * W] = res[c * R : (c + 1) * R]
            return carry

        lax.fori_loop(0, n, weights, 0)
    swap = to_dp(buf.at[1 - core], other, pair.at[0], pair.at[1], partner)
    swap.start()
    gather.relay()
    dkv = dkv_ref[me]
    for d in range(1, n):
        kv[d].wait_recv()
        dkv = dkv + krecv[d - 1].astype(F32)
    for half in range(2):
        kvg = tn(ctx_ref[...], dkv[half * KP : (half + 1) * KP].astype(BF)).astype(BF)
        S = kvg.shape[0] // ndp
        for i in range(ndp):
            kv_ref[(2 * i + half) * S : (2 * i + half + 1) * S, W:] = kvg[i * S : (i + 1) * S]
    for d in range(1, n - 1):
        gather.wait(d)
        back(d, me ^ d)
    swap.wait_recv()

    def leave(t):
        return pltpu.make_async_copy(gr_ref.at[t], gr_hbm.at[t], gsem.at[t])

    def add(t, carry):
        gr_ref[t] = (buf[core, t].astype(F32) + other[t].astype(F32)).astype(BF)
        leave(t).start()
        return carry

    lax.fori_loop(0, n, add, 0)
    gather.wait(n - 1)
    back(n - 1, me ^ (n - 1))
    kv_ref[:, :W] = acc[...].astype(BF)
    gather.finish()
    for copy in kept:
        copy.wait()
    for t in range(n):
        leave(t).wait()
    for d in range(1, n):
        kv[d].wait_send()
    swap.wait_send()


def gather_back(n, ndp, x, w, h2, dcq, cb, ca, dkv, ctx, attn):
    C, D = x.shape
    W = w.shape[0]
    KP = ctx.shape[0]
    half = (n, D // 2, 2 * W)
    return pl.pallas_call(
        functools.partial(gather_kernel, n, ndp),
        in_specs=[VSPEC] * 9,
        out_specs=[ANYSPEC, VSPEC, ANYSPEC, VSPEC],
        out_shape=[sds((n, C, D), BF), sds((n * C, W), BF), sds(half, BF), sds((D, 2 * W), BF)],
        scratch_shapes=[pltpu.VMEM((2, *half), BF), pltpu.VMEM(half, BF)]
        + [pltpu.VMEM((n - 1, 2 * KP, W), BF)] * 2
        + [pltpu.SemaphoreType.DMA((links(n),))] * 2
        + [pltpu.SemaphoreType.DMA((n - 1,))] * 2
        + [pltpu.SemaphoreType.DMA((2,))]
        + [pltpu.VMEM((n, C, D), BF), pltpu.VMEM((D, W), F32), pltpu.VMEM(half, BF)]
        + [pltpu.SemaphoreType.DMA((n,))] * 2,
        compiler_params=params(collective_id=2, has_side_effects=True),
        cost_estimate=cost(2 * n * C * W * D + 2e10, 8 * C * D),
        name="gather_back",
    )(x, w, h2, dcq, cb, ca, dkv, ctx, attn)


def attn_bwd_kernel(n, q_ref, k_ref, v_ref, o_ref, do_ref, lse_ref, c_ref, s_ref, h_hbm, e_hbm, a_hbm,
                    dq_ref, dk_ref, dv_ref, gr_hbm, x_ref, dk_acc, dv_acc, kt_ref, sbuf, rbuf, ss, rs,
                    a_ref, h_ref, e_ref, lsem, gr_ref, osem):
    me = lax.axis_index("tensor")
    T, W = q_ref.shape
    G = lane_group(W)
    qb = 256
    mult = SCALE * LOG2E
    nh = G // HEAD_DIM
    greet(n, me)
    shards = ShardSum(n, me, a_ref, sbuf, rbuf, ss, rs)
    shards.start(a_hbm)
    a, h_all, early = (
        Late(src, dst, lsem.at[i]) for i, (src, dst) in enumerate(((a_hbm, a_ref), (h_hbm, h_ref), (e_hbm, e_ref)))
    )
    masks = [m.astype(BF) for m in head_masks(1, G)]
    head_rows = jnp.where(
        lax.broadcasted_iota(jnp.int32, (16, G), 0) == lax.broadcasted_iota(jnp.int32, (16, G), 1) // HEAD_DIM, 1.0, 0.0
    ).astype(BF)

    def heads(g, outer):
        cols = pl.ds(pl.multiple_of(g * G, G), G) if G < W else slice(None)
        k, v = k_ref[:, cols], v_ref[:, cols]
        kt_ref[...] = jnp.transpose(k.astype(F32)).astype(BF)
        dk_acc[...] = jnp.zeros_like(dk_acc)
        dv_acc[...] = jnp.zeros_like(dv_acc)

        def block(i, carry):
            rows = pl.ds(pl.multiple_of(i * qb, qb), qb)
            q = q_ref[rows, cols]
            do = do_ref[rows, cols]
            prod = do.astype(F32) * o_ref[rows, cols].astype(F32)
            high = prod.astype(BF)
            delta = nt(head_rows, high) + nt(head_rows, (prod - high.astype(F32)).astype(BF))
            lse = lse_ref[g, :, rows]
            parts = []
            for h in range(nh):
                qm = q * masks[h]
                dom = do * masks[h]
                st = nt(k, qm)
                pt = jnp.exp2(st * mult - lse[h : h + 1, :])
                dpt = nt(v, dom)
                dst = (pt * (dpt - delta[h : h + 1, :])).astype(BF)
                dv_acc[...] += nn(pt.astype(BF), dom)
                dk_acc[...] += nn(dst, qm)
                parts.append(nn(kt_ref[h * HEAD_DIM : (h + 1) * HEAD_DIM, :], dst))
            dq = jnp.transpose(jnp.concatenate(parts, 0)) * SCALE
            dq_ref[rows, cols] = (dq * c_ref[rows, :] - turned(dq) * s_ref[rows, :]).astype(BF)
            return carry

        lax.fori_loop(0, T // qb, block, 0)
        dk = dk_acc[...] * SCALE
        dk_ref[:, cols] = (dk * c_ref[...] - turned(dk) * s_ref[...]).astype(BF)
        dv_ref[:, cols] = dv_acc[...].astype(BF)
        return outer

    lax.fori_loop(0, W // G, heads, 0)
    a()
    shards.middle()
    h_all()
    early()
    tf = 256

    def leave(j):
        rows = pl.ds(pl.multiple_of(j * tf, tf), tf)
        return pltpu.make_async_copy(gr_ref.at[rows], gr_hbm.at[rows], osem.at[j])

    def weights(j, carry):
        rows = pl.ds(pl.multiple_of(j * tf, tf), tf)
        h = h_ref[:, rows]
        for i, g_ref in enumerate((dq_ref, dk_ref, dv_ref)):
            gr_ref[rows, i * W : (i + 1) * W] = tn(h, g_ref[...]).astype(BF)
        gr_ref[rows, 3 * W :] = e_ref[rows, :]
        leave(j).start()
        return carry

    lax.fori_loop(0, gr_ref.shape[0] // tf, weights, 0)
    shards.store(x_ref)
    for j in range(gr_ref.shape[0] // tf):
        leave(j).wait()


def attn_bwd(n, q, k, v, o, do, lse, cs, sn, h, early, a):
    T, W = q.shape
    D = h.shape[1]
    G = lane_group(W)
    _, R, N = a.shape
    slots = 6 if n == 4 else n - 1
    H = R // 2 if n == 4 else R
    return pl.pallas_call(
        functools.partial(attn_bwd_kernel, n),
        in_specs=[VSPEC] * 8 + [ANYSPEC] * 3,
        out_specs=[VSPEC] * 3 + [ANYSPEC, VSPEC],
        out_shape=[sds((T, W), BF)] * 3 + [sds((D, 5 * W), BF), sds((R, N), BF)],
        scratch_shapes=[pltpu.VMEM((T, G), F32), pltpu.VMEM((T, G), F32), pltpu.VMEM((G, T), BF)]
        + [pltpu.VMEM((2, H, N), BF), pltpu.VMEM((slots, H, N), BF)]
        + [pltpu.SemaphoreType.DMA((slots,))] * 2
        + held(a, h, early)
        + [pltpu.VMEM((D, 5 * W), BF), pltpu.SemaphoreType.DMA((D // 256,))],
        compiler_params=params(collective_id=5, has_side_effects=True),
        cost_estimate=cost(40 * T * T * W, 16 * T * W, T * T * W // HEAD_DIM),
        name="attn_bwd",
    )(q, k, v, o, do, lse, cs, sn, h, early, a)


def last_kernel(n, ndp, dq_ref, dk_ref, dv_ref, wq_ref, wk_ref, wv_ref, x_hbm, da_ref, g_ref, gg_in,
                lbuf, gg_ref, sbuf, rbuf, gbuf, gsum, gown, gall, ss, rs, ss2, rs2, ss3, rs3, ss4, rs4, x_buf, lsem):
    me = lax.axis_index("tensor")
    dp = lax.axis_index("dp")
    C, D = x_buf.shape
    x = Late(rows_of(x_hbm, me, C), x_buf, lsem.at[0])
    R = D // ndp
    others = [(dp + i) % ndp for i in range(1, ndp)]
    greet(n, me, others)

    def part(t):
        rows = pl.ds(pl.multiple_of(t * C, C), C)
        return nt(dq_ref[rows, :], wq_ref[...]) + nt(dk_ref[rows, :], wk_ref[...]) + nt(dv_ref[rows, :], wv_ref[...])

    total, copies = reduce_parts(n, me, part, lambda: None, sbuf, rbuf, ss, rs)
    u, inverse = unit(x()[...].astype(F32))
    row = lax.broadcasted_iota(jnp.int32, (8, D), 0)
    gsum[...] = gg_in[...] + jnp.where(row == 2, jnp.sum(total * u, axis=0, keepdims=True), 0.0)
    small = {}
    for d in range(1, n):
        small[d] = remote(gsum, gbuf.at[d - 1], ss3.at[d - 1], rs3.at[d - 1], me ^ d)
        small[d].start()
    lbuf[me] = (da_ref[...] + norm_back(total, u, inverse, g_ref[...].reshape(1, D))).astype(BF)
    gather = Gather(
        n, me, lbuf.at[me], lambda t: lbuf.at[t], lambda t, i: lbuf.at[t, pl.ds(i * C // 2, C // 2)], ss2, rs2
    )
    gather.start()
    gains = gsum[...]
    for d in range(1, n):
        small[d].wait_recv()
        gains = gains + gbuf[d - 1]
    for i in range(ndp):
        gown[i] = gains[:, i * R : (i + 1) * R]
    sums = []
    for i, other in enumerate(others):
        sums.append(to_dp(gown.at[other], gall.at[i], ss4.at[i], rs4.at[i], other))
        sums[i].start()
    gather.relay()
    mine = gown[dp]
    for i in range(ndp - 1):
        sums[i].wait_recv()
        mine = mine + gall[i]
    gg_ref[...] = mine
    for d in range(1, n):
        gather.wait(d)
    gather.finish()
    for copy in (*copies.values(), *small.values(), *sums):
        copy.wait_send()


def last(n, ndp, dq, dk, dv, wq, wk, wv, x, da, gain, gains):
    T, W = dq.shape
    C, D = da.shape
    return pl.pallas_call(
        functools.partial(last_kernel, n, ndp),
        in_specs=[VSPEC] * 6 + [ANYSPEC] + [VSPEC] * 3,
        out_specs=[VSPEC] * 2,
        out_shape=[sds((n, C, D), BF), sds((8, D // ndp), F32)],
        scratch_shapes=reduce_bufs(n, C, D)[:2]
        + [pltpu.VMEM((n - 1, 8, D), F32), pltpu.VMEM((8, D), F32)]
        + [pltpu.VMEM((ndp, 8, D // ndp), F32), pltpu.VMEM((ndp - 1, 8, D // ndp), F32)]
        + reduce_bufs(n, C, D)[2:]
        + [pltpu.SemaphoreType.DMA((links(n),))] * 2
        + [pltpu.SemaphoreType.DMA((n - 1,))] * 2
        + [pltpu.SemaphoreType.DMA((ndp - 1,))] * 2
        + held(sds((C, D), BF)),
        compiler_params=params(collective_id=3, has_side_effects=True),
        cost_estimate=cost(6 * T * W * D + 4e10, 8 * T * D),
        name="last",
    )(dq, dk, dv, wq, wk, wv, x, da, gain, gains)


def cross_fwd_kernel(n, ctx, h_ref, x_ref, wq_ref, kv_ref, wo_hbm, g_ref, q_ref, o_ref, after_ref, h3_ref, wo_ref, lsem):
    wo = Late(wo_hbm, wo_ref, lsem.at[0])
    _, C, W = q_ref.shape
    KP = kv_ref.shape[1] // 2
    mult = SCALE * LOG2E
    G = lane_group(W)
    per = W // G
    masks = [m.astype(BF) for m in head_masks(1, G)]
    lane = lax.broadcasted_iota(jnp.int32, (C, G), 1) // HEAD_DIM
    valid = lax.broadcasted_iota(jnp.int32, (C, KP), 1) < ctx

    def group(t, j):
        cols = slice(j * G, (j + 1) * G)
        q = nn(h_ref[...], wq_ref[t, :, cols]).astype(BF)
        q_ref[t, :, cols] = q
        k, v = kv_ref[t, :KP, cols], kv_ref[t, KP:, cols]
        out = jnp.zeros((C, G), F32)
        for h in range(G // HEAD_DIM):
            s = jnp.where(valid, nt(q * masks[h], k), -1e30)
            p = jnp.exp2((s - jnp.max(s, axis=-1, keepdims=True)) * mult)
            o = nn(p.astype(BF), v) / jnp.sum(p, axis=-1, keepdims=True)
            out = jnp.where(lane == h, o, out)
        o_ref[t, :, cols] = out.astype(BF)

    def shard(t, carry):
        for j in range(per):
            group(t, j)
        return carry

    lax.fori_loop(0, n, shard, 0)
    D = h_ref.shape[1]
    tf = 256
    wo()

    def project(j, carry):
        cols = pl.ds(pl.multiple_of(j * tf, tf), tf)
        total = nn(o_ref[0], wo_ref[0, :, cols])
        for t in range(1, n):
            total = total + nn(o_ref[t], wo_ref[t, :, cols])
        after_ref[:, cols] = x_ref[:, cols] + total
        return carry

    lax.fori_loop(0, D // tf, project, 0)
    u, _ = unit(after_ref[...])
    h3_ref[...] = (u * g_ref[...].reshape(1, D)).astype(BF)


def cross_fwd(ctx, h, x, wq, kv, wo, gain):
    C, D = h.shape
    n, W = wq.shape[0], wq.shape[2]
    return pl.pallas_call(
        functools.partial(cross_fwd_kernel, n, ctx),
        in_specs=[VSPEC] * 4 + [ANYSPEC, VSPEC],
        out_specs=[VSPEC] * 4,
        out_shape=[sds((n, C, W), BF), sds((n, C, W), BF), sds((C, D), F32), sds((C, D), BF)],
        scratch_shapes=held(wo),
        compiler_params=params(),
        cost_estimate=cost(4 * C * D * n * W + 16 * C * 256 * n * W, 8 * D * n * W),
        name="cross_fwd",
    )(h, x, wq, kv, wo, gain)


def cross_bwd_kernel(n, ctx, dh3_ref, after2_ref, cot_hbm, g3_ref, wo_hbm, q_ref, kv_ref, wq_hbm, after1_hbm, g2_ref, bo_in,
                     cb_ref, dq_ref, dkv_ref, da_ref, sb_ref, gg_ref, bo_ref, dh2_ref, ss, rs,
                     cot_buf, wo_ref, wq_ref, after1_buf, lsem):
    me = lax.axis_index("tensor")
    cot, wo, wq, after1 = (
        Late(src, dst, lsem.at[i])
        for i, (src, dst) in enumerate(
            (
                (rows_of(cot_hbm, me, cot_buf.shape[0]), cot_buf),
                (wo_hbm, wo_ref),
                (wq_hbm, wq_ref),
                (after1_hbm, after1_buf),
            )
        )
    )
    _, C, W = q_ref.shape
    KP = kv_ref.shape[1] // 2
    D = da_ref.shape[1]
    mult = SCALE * LOG2E
    G = lane_group(W)
    per = W // G
    masks = [m.astype(BF) for m in head_masks(1, G)]
    lane = lax.broadcasted_iota(jnp.int32, (C, G), 1) // HEAD_DIM
    valid = lax.broadcasted_iota(jnp.int32, (C, KP), 1) < ctx
    greet(n, me)
    gather = Gather(n, me, bo_in, lambda t: bo_ref.at[t], lambda t, i: bo_ref.at[t, pl.ds(i * C // 2, C // 2)], ss, rs)
    gather.start()
    bo_ref[me] = bo_in[...]
    dh3 = dh3_ref[...]
    u3, inv3 = unit(after2_ref[...])
    gain3 = jnp.sum(dh3 * u3, axis=0, keepdims=True)
    da2 = cot()[...].astype(F32) + norm_back(dh3, u3, inv3, g3_ref[...].reshape(1, D))
    da_ref[...] = da2
    cb_ref[...] = da2.astype(BF)
    wo()

    def group(t, j):
        cols = slice(j * G, (j + 1) * G)
        do = nt(cb_ref[...], wo_ref[t, cols, :]).astype(BF)
        q, k, v = q_ref[t, :, cols], kv_ref[t, :KP, cols], kv_ref[t, KP:, cols]
        dq = jnp.zeros((C, G), F32)
        dk = jnp.zeros((KP, G), F32)
        dv = jnp.zeros((KP, G), F32)
        for h in range(G // HEAD_DIM):
            qm = q * masks[h]
            dom = do * masks[h]
            s = jnp.where(valid, nt(qm, k), -1e30)
            p = jnp.exp2((s - jnp.max(s, axis=-1, keepdims=True)) * mult)
            p = p / jnp.sum(p, axis=-1, keepdims=True)
            dp = nt(dom, v)
            ds = (p * (dp - jnp.sum(p * dp, axis=-1, keepdims=True))).astype(BF)
            dq = jnp.where(lane == h, nn(ds, k), dq)
            dk = dk + tn(ds, qm)
            dv = dv + tn(p.astype(BF), dom)
        dq_ref[t, :, cols] = (dq * SCALE).astype(BF)
        dkv_ref[t, :KP, cols] = dk * SCALE
        dkv_ref[t, KP:, cols] = dv

    def shard(t, carry):
        for j in range(per):
            group(t, j)
        return carry

    lax.fori_loop(0, n, shard, 0)
    gather.relay()
    wq()
    tf = 256

    def project(j, carry):
        cols = pl.ds(pl.multiple_of(j * tf, tf), tf)
        total = nt(dq_ref[0], wq_ref[0, cols, :])
        for t in range(1, n):
            total = total + nt(dq_ref[t], wq_ref[t, cols, :])
        dh2_ref[:, cols] = total
        return carry

    lax.fori_loop(0, D // tf, project, 0)
    dh2 = dh2_ref[...]
    u2, inv2 = unit(after1()[...])
    gain2 = jnp.sum(dh2 * u2, axis=0, keepdims=True)
    da1 = da_ref[...] + norm_back(dh2, u2, inv2, g2_ref[...].reshape(1, D))
    da_ref[...] = da1
    sb_ref[...] = da1.astype(BF)
    row = lax.broadcasted_iota(jnp.int32, (8, D), 0)
    gg_ref[...] = jnp.where(row == 0, gain3, 0.0) + jnp.where(row == 1, gain2, 0.0)
    for d in range(1, n):
        gather.wait(d)
    gather.finish()


def cross_bwd(ctx, dh3, after2, cot, g3, wo, q, kv, wq, after1, g2, bo):
    C, D = after2.shape
    n, W = wq.shape[0], wq.shape[2]
    return pl.pallas_call(
        functools.partial(cross_bwd_kernel, n, ctx),
        in_specs=[VSPEC, VSPEC, ANYSPEC, VSPEC, ANYSPEC, VSPEC, VSPEC, ANYSPEC, ANYSPEC, VSPEC, VSPEC],
        out_specs=[VSPEC] * 7,
        out_shape=[
            sds((C, D), BF),
            sds((n, C, W), BF),
            sds(kv.shape, F32),
            sds((C, D), F32),
            sds((C, D), BF),
            sds((8, D), F32),
            sds((n, C, D), BF),
        ],
        scratch_shapes=[pltpu.VMEM((C, D), F32)]
        + [pltpu.SemaphoreType.DMA((links(n),))] * 2
        + held(sds((C, D), BF), wo, wq, after1),
        compiler_params=params(collective_id=7, has_side_effects=True),
        cost_estimate=cost(4 * C * D * n * W + 40 * C * 256 * n * W, 8 * D * n * W),
        name="cross_bwd",
    )(dh3, after2, cot, g3, wo, q, kv, wq, after1, g2, bo)


def body(latents, context, cotangent, g1, wq, wk, wv, wo, g2, xq, xk, xv, xo, g3, wg, wu, wd, n, ndp):
    _, T, D = latents.shape
    ctx = context.shape[1]
    W = wq.shape[1]
    F = wg.shape[1]
    C = T // n
    x = latents.reshape(T, D)
    gb = cotangent.reshape(T, D)
    ctx_rows = context.reshape(ctx, -1)
    KP = -(-ctx // 16) * 16
    cs, sn = tables(T, lane_group(W))

    ctx_pad = jnp.pad(ctx_rows, ((0, KP - ctx), (0, 0)))
    h1, q, k, v, attn, lse, xq_all, xo_all, kv_all = front(n, ctx, x, g1, wq, wk, wv, cs, sn, xq, xo, ctx_pad, xk, xv)
    after1, h2 = out_rs(n, attn, wo, x, g2)
    cq, cattn, after2, h3_own = cross_fwd(ctx, h2, after1, xq_all, kv_all, xo_all, g3)
    h3, hidden, dgu, dh3 = ff(n, h3_own, gb, wg, wu, wd)
    h3 = h3.reshape(T, D)

    def scatter(a, axis):
        return lax.psum_scatter(a, axis, scatter_dimension=0, tiled=True)

    down_part = down_grads(gb, hidden)
    down_part, dgu = lax.optimization_barrier((down_part, dgu))
    down_grad = scatter(down_part, "dp")
    out_own, gu_part = feed_grads(n, hidden, wd, after2, h3, dgu)
    dh3, gu_part = lax.optimization_barrier((dh3, gu_part))
    gu_grad = scatter(gu_part, "dp")

    cb, dcq, dckv, dafter1, sb_own, gains, block_out = cross_bwd(
        ctx, dh3, after2, gb, g3, xo_all, cq, kv_all, xq_all, after1, g2, out_own
    )
    sb_own, down_grad = lax.optimization_barrier((sb_own, down_grad))
    sb, dattn, cross_part, early_part = gather_back(n, ndp, sb_own, wo, h2, dcq, cb, cattn, dckv, ctx_pad, attn)
    dq, dk, dv, self_part, cross_part = attn_bwd(n, q, k, v, attn, dattn, lse, cs, sn, h1, early_part, cross_part)
    cores = [[i for i in range(ndp) if i % 2 == c] for c in range(2)]
    cross_grads = lax.psum_scatter(cross_part, "dp", scatter_dimension=0, axis_index_groups=cores, tiled=True)
    self_grads = scatter(self_part, "dp")
    dq, gu_grad = lax.optimization_barrier((dq, gu_grad))
    latent_grad, gains = last(n, ndp, dq, dk, dv, wq, wk, wv, x, dafter1, g1, gains)

    latent_grad = latent_grad.astype(F32)
    gu_grad = gu_grad.astype(F32)
    gate_grad, up_grad, down_grad = gu_grad[:, :F], gu_grad[:, F:], down_grad.astype(F32).T
    cross_grads, gains, latent_grad, gate_grad, up_grad = lax.optimization_barrier(
        (cross_grads, gains, latent_grad, gate_grad, up_grad)
    )
    cross_grads = cross_grads.astype(F32)
    xq_grad, xo_grad = cross_grads[:, :W], cross_grads[:, W:].T
    self_grads, xq_grad, xo_grad = lax.optimization_barrier((self_grads, xq_grad, xo_grad))
    self_grads = self_grads.astype(F32)
    so_grad, kv_grads = self_grads[:, 3 * W : 4 * W].T, self_grads[:, 4 * W :].reshape(2, D // ndp // 2, W)
    return (
        block_out.reshape(1, T, D),
        latent_grad.reshape(1, T, D),
        gains[2],
        self_grads[:, :W],
        self_grads[:, W : 2 * W],
        self_grads[:, 2 * W : 3 * W],
        so_grad,
        gains[1],
        xq_grad,
        kv_grads[0],
        kv_grads[1],
        xo_grad,
        gains[0],
        gate_grad,
        up_grad,
        down_grad,
    )


def solution(mesh):
    tokens = P("dp", None, None)
    cols = P(None, "tensor")
    rows = P("tensor", None)
    return jax.shard_map(
        functools.partial(body, n=mesh.shape["tensor"], ndp=mesh.shape["dp"]),
        mesh=mesh,
        in_specs=(tokens, tokens, tokens, P(), cols, cols, cols, rows, P(), cols, cols, cols, rows, P(), cols, cols, rows),
        out_specs=(
            tokens,
            tokens,
            P("dp"),
            P("dp", "tensor"),
            P("dp", "tensor"),
            P("dp", "tensor"),
            P("tensor", "dp"),
            P("dp"),
            P("dp", "tensor"),
            P("dp", "tensor"),
            P("dp", "tensor"),
            P("tensor", "dp"),
            P("dp"),
            P("dp", "tensor"),
            P("dp", "tensor"),
            P("tensor", "dp"),
        ),
        check_vma=False,
    )
```

```python
import functools

import jax
import jax.numpy as jnp
from jax import lax
from jax.experimental import pallas as pl
from jax.experimental.pallas import tpu as pltpu
from jax.sharding import PartitionSpec as P

HEAD_DIM = 64
HALF = HEAD_DIM // 2
EPS = 1e-05
BF = jnp.bfloat16
F32 = jnp.float32
LOG2E = 1.4426950408889634
SCALE = HEAD_DIM**-0.5
VMEM_BYTES = 60 << 20
MESH_ID = pl.DeviceIdType.MESH
VSPEC = pl.BlockSpec(memory_space=pltpu.VMEM)
ANYSPEC = pl.BlockSpec(memory_space=pl.ANY)


def nn(a, b):
    return lax.dot_general(a, b, (((1,), (0,)), ((), ())), preferred_element_type=F32)


def nt(a, b):
    return lax.dot_general(a, b, (((1,), (1,)), ((), ())), preferred_element_type=F32)


def tn(a, b):
    return lax.dot_general(a, b, (((0,), (0,)), ((), ())), preferred_element_type=F32)


def sds(shape, dtype):
    return jax.ShapeDtypeStruct(shape, dtype)


def params(**kw):
    return pltpu.CompilerParams(vmem_limit_bytes=VMEM_BYTES, **kw)


def cost(flops, nbytes, trans=0):
    return pl.CostEstimate(flops=1000, bytes_accessed=1000, transcendentals=0)


def unit(x):
    center = x - jnp.mean(x, axis=-1, keepdims=True)
    inverse = lax.rsqrt(jnp.mean(center * center, axis=-1, keepdims=True) + EPS)
    return center * inverse, inverse


def norm_back(grad, u, inverse, gain):
    e = grad * gain
    mean_e = jnp.mean(e, axis=-1, keepdims=True)
    mean_p = jnp.mean(e * u, axis=-1, keepdims=True)
    return inverse * (e - mean_e - u * mean_p)


def lane_group(width):
    return 128 if width % 128 == 0 else width


def tables(length, group):
    freq = jnp.tile(10000.0 ** (-jnp.arange(HALF, dtype=F32) / HALF), group // HALF)
    angles = lax.broadcasted_iota(F32, (length, group), 0) * freq[None, :]
    front = lax.broadcasted_iota(jnp.int32, (length, group), 1) % HEAD_DIM < HALF
    return jnp.cos(angles), jnp.where(front, -1.0, 1.0) * jnp.sin(angles)


def turned(a):
    width = a.shape[-1]
    lane = lax.broadcasted_iota(jnp.int32, a.shape, 1) % HEAD_DIM
    return jnp.where(lane < HALF, pltpu.roll(a, width - HALF, 1), pltpu.roll(a, HALF, 1))


def head_masks(rows, group):
    lane = lax.broadcasted_iota(jnp.int32, (rows, group), 1) // HEAD_DIM
    return [jnp.where(lane == h, 1.0, 0.0) for h in range(group // HEAD_DIM)]


def greet(n, me, dps=()):
    sem = pltpu.get_barrier_semaphore()
    for d in range(1, n):
        pl.semaphore_signal(sem, 1, device_id={"tensor": me ^ d}, device_id_type=MESH_ID)
    for dp in dps:
        pl.semaphore_signal(sem, 1, device_id={"dp": dp}, device_id_type=MESH_ID)
    pl.semaphore_wait(sem, n - 1 + len(dps))


def to_dp(src, dst, send, recv, target):
    return pltpu.make_async_remote_copy(src, dst, send, recv, device_id={"dp": target}, device_id_type=MESH_ID)


def remote(src, dst, send, recv, target):
    return pltpu.make_async_remote_copy(src, dst, send, recv, device_id={"tensor": target}, device_id_type=MESH_ID)


class Late:
    def __init__(self, src, dst, sem):
        self.dst, self.copy = dst, pltpu.make_async_copy(src, dst, sem)
        self.copy.start()

    def __call__(self):
        self.copy.wait()
        return self.dst


def held(*arrays):
    return [pltpu.VMEM(a.shape, a.dtype) for a in arrays] + [pltpu.SemaphoreType.DMA((len(arrays),))]


def rows_of(ref, t, C):
    return ref.at[pl.ds(pl.multiple_of(t * C, C), C)]


def links(n):
    return 4 if n == 4 else n - 1


class Gather:
    def __init__(self, n, me, src, slot, half, ss, rs):
        self.n, self.me, self.half, self.ss, self.rs = n, me, half, ss, rs
        self.copies = {
            d: remote(src, slot(me), ss.at[d - 1], rs.at[d - 1], me ^ d) for d in (range(1, n) if n != 4 else (1, 2))
        }
        self.passed = []

    def start(self):
        for copy in self.copies.values():
            copy.start()

    def relay(self):
        if self.n == 4:
            for i, d in enumerate((1, 2)):
                self.copies[d].wait_recv()
                block = self.half(self.me ^ d, i)
                copy = remote(block, block, self.ss.at[2 + i], self.rs.at[2 + i], self.me ^ (3 - d))
                copy.start()
                self.passed.append(copy)

    def wait(self, d):
        if self.n != 4:
            self.copies[d].wait_recv()
        elif d == 3:
            for copy in self.passed:
                copy.wait_recv()

    def finish(self):
        for copy in (*self.copies.values(), *self.passed):
            copy.wait_send()


def reduce_bufs(n, C, D):
    shape = (6, C, D // 2) if n == 4 else (n - 1, C, D)
    return [pltpu.VMEM(shape, BF)] * 2 + [pltpu.SemaphoreType.DMA((shape[0],))] * 2


def reduce_parts(n, me, part, filler, sbuf, rbuf, ss, rs):
    copies = {}

    def send(i, val, d):
        sbuf[i] = val.astype(BF)
        copies[i] = remote(sbuf.at[i], rbuf.at[i], ss.at[i], rs.at[i], me ^ d)
        copies[i].start()

    def got(i):
        copies[i].wait_recv()
        return rbuf[i].astype(F32)

    if n == 4:
        across = part(me ^ 3)
        H = across.shape[1] // 2
        send(0, across[:, :H], 1)
        send(2, across[:, H:], 2)
        one = part(me ^ 1)
        send(1, one[:, :H], 1)
        two = part(me ^ 2)
        send(3, two[:, H:], 2)
        total = part(me)
        filler()
        send(4, two[:, :H] + got(0), 2)
        send(5, one[:, H:] + got(2), 1)
        total = jnp.concatenate([total[:, :H] + got(1) + got(4), total[:, H:] + got(3) + got(5)], 1)
    else:
        for d in reversed(range(1, n)):
            send(d - 1, part(me ^ d), d)
        total = part(me)
        filler()
        for d in range(1, n):
            total = total + got(d - 1)
    return total, copies


class ShardSum:
    def __init__(self, n, me, a, sbuf, rbuf, ss, rs):
        self.n, self.me, self.a, self.sbuf, self.rbuf, self.ss, self.rs = n, me, a, sbuf, rbuf, ss, rs
        self.copies = {}

    def send(self, i, src, d):
        self.copies[i] = remote(src, self.rbuf.at[i], self.ss.at[i], self.rs.at[i], self.me ^ d)
        self.copies[i].start()

    def got(self, i):
        self.copies[i].wait_recv()
        return self.rbuf[i].astype(F32)

    def halves(self, d, a=None):
        a = self.a if a is None else a
        H = a.shape[1] // 2
        return a.at[self.me ^ d, pl.ds(0, H)], a.at[self.me ^ d, pl.ds(H, H)]

    def start(self, a):
        if self.n == 4:
            self.send(0, self.halves(3, a)[0], 1)
            self.send(2, self.halves(3, a)[1], 2)
            self.send(1, self.halves(1, a)[0], 1)
            self.send(3, self.halves(2, a)[1], 2)
        else:
            for d in range(1, self.n):
                self.send(d - 1, a.at[self.me ^ d], d)

    def middle(self):
        if self.n == 4:
            self.sbuf[0] = (self.halves(2)[0][...].astype(F32) + self.got(0)).astype(BF)
            self.send(4, self.sbuf.at[0], 2)
            self.sbuf[1] = (self.halves(1)[1][...].astype(F32) + self.got(2)).astype(BF)
            self.send(5, self.sbuf.at[1], 1)

    def store(self, out_ref):
        if self.n == 4:
            H = self.a.shape[1] // 2
            own = self.halves(0)
            out_ref[:H] = (own[0][...].astype(F32) + self.got(1) + self.got(4)).astype(BF)
            out_ref[H:] = (own[1][...].astype(F32) + self.got(3) + self.got(5)).astype(BF)
        else:
            total = self.a[self.me].astype(F32)
            for d in range(1, self.n):
                total = total + self.got(d - 1)
            out_ref[...] = total.astype(BF)
        for copy in self.copies.values():
            copy.wait_send()


def front_kernel(n, ctx, x_hbm, g_ref, wq_hbm, wk_hbm, wv_hbm, c_ref, s_ref, xq_ref, xo_ref, ctx_ref, xk_hbm, xv_hbm,
                 h_hbm, q_hbm, k_hbm, v_hbm, o_ref, lse_ref, xqa_ref, xoa_ref, kva_ref,
                 kv_own, sq, rq, so, ro, sk, rk, fsq, frq, fso, fro, local,
                 x_buf, wq_buf, wk_buf, wv_buf, xk_buf, xv_buf, lsem, h_ref, q_ref, k_ref, v_ref, osem):
    xk, xv, x, wq, wk, wv = (
        Late(src, dst, lsem.at[i])
        for i, (src, dst) in enumerate(
            (
                (xk_hbm, xk_buf),
                (xv_hbm, xv_buf),
                (x_hbm, x_buf),
                (wq_hbm, wq_buf),
                (wk_hbm, wk_buf),
                (wv_hbm, wv_buf),
            )
        )
    )
    me = lax.axis_index("tensor")
    dp = lax.axis_index("dp")
    core = dp % 2
    partner = dp + 1 - 2 * core
    T, D = x_hbm.shape
    W = q_ref.shape[1]
    KP = ctx_ref.shape[0]
    greet(n, me, [partner])

    rows_q = pl.ds(pl.multiple_of(core * (D // 2), 16), D // 2)
    rows_o = pl.ds(pl.multiple_of(core * (W // 2), 16), W // 2)
    def quarter(ref, rows):
        return lambda t, i: ref.at[t, pl.ds(pl.multiple_of(core * (rows // 2) + i * (rows // 4), 16), rows // 4)]

    gq = Gather(n, me, xq_ref.at[rows_q], lambda t: xqa_ref.at[t, rows_q], quarter(xqa_ref, D), sq, rq)
    go = Gather(n, me, xo_ref.at[rows_o], lambda t: xoa_ref.at[t, rows_o], quarter(xoa_ref, W), so, ro)
    gk = Gather(n, me, kv_own, lambda t: kva_ref.at[t], lambda t, i: kva_ref.at[t, pl.ds(i * KP, KP)], sk, rk)
    gq.start()
    go.start()
    own = [
        pltpu.make_async_copy(xq_ref, xqa_ref.at[me], local.at[0]),
        pltpu.make_async_copy(xo_ref, xoa_ref.at[me], local.at[1]),
    ]
    for copy in own:
        copy.start()
    kv_own[:KP] = nn(ctx_ref[...], xk()[...]).astype(BF)
    kv_own[KP:] = nn(ctx_ref[...], xv()[...]).astype(BF)
    gk.start()
    kva_ref[me] = kv_own[...]

    tb = 256
    reps = W // c_ref.shape[1]
    x_ref, wq_ref, wk_ref, wv_ref = x(), wq(), wk(), wv()

    def project(i, carry):
        rows = pl.ds(pl.multiple_of(i * tb, tb), tb)
        u, _ = unit(x_ref[rows, :].astype(F32))
        h = (u * g_ref[...].reshape(1, D)).astype(BF)
        h_ref[rows, :] = h
        c = jnp.concatenate([c_ref[rows, :]] * reps, 1)
        s = jnp.concatenate([s_ref[rows, :]] * reps, 1)
        for w_ref, out_ref in ((wq_ref, q_ref), (wk_ref, k_ref)):
            a = nn(h, w_ref[...])
            out_ref[rows, :] = (a * c + turned(a) * s).astype(BF)
        v_ref[rows, :] = nn(h, wv_ref[...]).astype(BF)
        return carry

    lax.fori_loop(0, T // tb, project, 0)
    kept = [
        pltpu.make_async_copy(src, dst, osem.at[i])
        for i, (src, dst) in enumerate(((h_ref, h_hbm), (q_ref, q_hbm), (k_ref, k_hbm), (v_ref, v_hbm)))
    ]
    for copy in kept:
        copy.start()
    gq.relay()

    G = lane_group(W)
    mult = SCALE * LOG2E
    masks = [m.astype(BF) for m in head_masks(1, G)]
    lane = lax.broadcasted_iota(jnp.int32, (tb, G), 1) // HEAD_DIM
    stat_lane = lax.broadcasted_iota(jnp.int32, (tb, 128), 1)

    def heads(g, carry):
        cols = pl.ds(pl.multiple_of(g * G, G), G) if G < W else slice(None)
        k, v = k_ref[:, cols], v_ref[:, cols]

        def block(i, inner):
            rows = pl.ds(pl.multiple_of(i * tb, tb), tb)
            q = q_ref[rows, cols]
            out = jnp.zeros((tb, G), F32)
            stats = jnp.zeros((tb, 128), F32)
            for h in range(G // HEAD_DIM):
                s = nt(q * masks[h], k)
                top = jnp.max(s, axis=-1, keepdims=True) * mult
                p = jnp.exp2(s * mult - top)
                total = jnp.sum(p, axis=-1, keepdims=True)
                o = nn(p.astype(BF), v) / total
                out = jnp.where(lane == h, o, out)
                stats = jnp.where(stat_lane == h, top + jnp.log2(total), stats)
            o_ref[rows, cols] = out.astype(BF)
            lse_ref[g, :, rows] = jnp.transpose(stats)[:8]
            return inner

        return lax.fori_loop(0, T // tb, block, carry)

    lax.fori_loop(0, W // G, heads, 0)

    go.relay()
    gk.relay()
    passed = []
    for gather, ref, rows, send, recv in ((gq, xqa_ref, rows_q, fsq, frq), (go, xoa_ref, rows_o, fso, fro)):
        for d in range(1, n):
            gather.wait(d)
            block = ref.at[me ^ d, rows]
            copy = to_dp(block, block, send.at[d - 1], recv.at[d - 1], partner)
            copy.start()
            passed.append(copy)
    for copy in (*own, *kept):
        copy.wait()
    for d in range(1, n):
        gk.wait(d)
    for copy in passed:
        copy.wait_recv()
    for copy in (gq, go, gk):
        copy.finish()
    for copy in passed:
        copy.wait_send()


def front(n, ctx, x, gain, wq, wk, wv, cs, sn, xq, xo, ctx_rows, xk, xv):
    T, D = x.shape
    W = wq.shape[1]
    KP = ctx_rows.shape[0]
    groups = W // lane_group(W)
    link, pair = pltpu.SemaphoreType.DMA((links(n),)), pltpu.SemaphoreType.DMA((n - 1,))
    return pl.pallas_call(
        functools.partial(front_kernel, n, ctx),
        in_specs=[ANYSPEC, VSPEC] + [ANYSPEC] * 3 + [VSPEC] * 5 + [ANYSPEC] * 2,
        out_specs=[ANYSPEC] * 4 + [VSPEC] * 2 + [ANYSPEC] * 2 + [VSPEC],
        out_shape=[sds((T, D), BF)]
        + [sds((T, W), BF)] * 4
        + [sds((groups, 8, T), F32), sds((n, D, W), BF), sds((n, W, D), BF), sds((n, 2 * KP, W), BF)],
        scratch_shapes=[pltpu.VMEM((2 * KP, W), BF)] + [link] * 6 + [pair] * 4 + [pltpu.SemaphoreType.DMA((2,))]
        + held(x, wq, wk, wv, xk, xv)
        + held(sds((T, D), BF), *[sds((T, W), BF)] * 3),
        compiler_params=params(collective_id=4, has_side_effects=True),
        cost_estimate=cost(6 * T * D * W, 4 * T * D + 6 * D * W + 6 * T * W),
        name="front",
    )(x, gain, wq, wk, wv, cs, sn, xq, xo, ctx_rows, xk, xv)


def out_rs_kernel(n, a_ref, w_ref, x_hbm, g_ref, after_ref, h_ref, sbuf, rbuf, ss, rs, x_buf, lsem):
    me = lax.axis_index("tensor")
    C, D = x_buf.shape
    x = Late(rows_of(x_hbm, me, C), x_buf, lsem.at[0])
    greet(n, me)

    def part(t):
        return nn(a_ref[pl.ds(pl.multiple_of(t * C, C), C), :], w_ref[...])

    total, copies = reduce_parts(n, me, part, lambda: None, sbuf, rbuf, ss, rs)
    after = x()[...].astype(F32) + total
    after_ref[...] = after
    u, _ = unit(after)
    h_ref[...] = (u * g_ref[...].reshape(1, D)).astype(BF)
    for copy in copies.values():
        copy.wait_send()


def out_rs(n, a, w, x, gain):
    T, D = x.shape
    C = T // n
    W = a.shape[1]
    return pl.pallas_call(
        functools.partial(out_rs_kernel, n),
        in_specs=[VSPEC, VSPEC, ANYSPEC, VSPEC],
        out_specs=[VSPEC] * 2,
        out_shape=[sds((C, D), F32), sds((C, D), BF)],
        scratch_shapes=reduce_bufs(n, C, D) + held(sds((C, D), BF)),
        compiler_params=params(collective_id=0, has_side_effects=True),
        cost_estimate=cost(2 * T * W * D + 2e10, 8 * C * D),
        name="out_rs",
    )(a, w, x, gain)


def ff_kernel(n, h_in, gb_hbm, wg_hbm, wu_hbm, wd_hbm, h_hbm, hid_hbm, dgu_hbm, dh_ref, gd_hbm,
              gb_ref, wg_ref, wu_ref, wd_ref, sbuf, rbuf, ss, rs, ss2, rs2, ls, h_ref, hid_ref, dgu_ref, osem, gd_ref, gsem):
    me = lax.axis_index("tensor")
    C, D = h_in.shape
    F = wg_ref.shape[1]
    loads = [
        pltpu.make_async_copy(src, dst, ls.at[i])
        for i, (src, dst) in enumerate(((wg_hbm, wg_ref), (wu_hbm, wu_ref), (wd_hbm, wd_ref), (gb_hbm, gb_ref)))
    ]
    for c in loads:
        c.start()
    greet(n, me)
    gather = Gather(n, me, h_in, lambda t: h_ref.at[t], lambda t, i: h_ref.at[t, pl.ds(i * C // 2, C // 2)], ss, rs)
    gather.start()
    h_ref[me] = h_in[...]
    for c in loads:
        c.wait()
    tf = 512

    def chunk(t, store):
        rows = pl.ds(pl.multiple_of(t * C, C), C)
        h = h_ref[t]
        gb = gb_ref[rows, :]

        def tile(j, carry):
            cols = pl.ds(pl.multiple_of(j * tf, tf), tf)
            gate = nn(h, wg_ref[:, cols])
            up = nn(h, wu_ref[:, cols])
            dhid = nt(gb, wd_ref[cols, :])
            sig = 1.0 / (1.0 + jnp.exp(-gate))
            act = gate * sig
            hid_ref[rows, cols] = (act * up).astype(BF)
            dgu_ref[rows, cols] = (dhid * up * (sig * (1.0 + gate * (1.0 - sig)))).astype(BF)
            dgu_ref[rows, pl.ds(pl.multiple_of(F + j * tf, tf), tf)] = (dhid * act).astype(BF)
            return carry

        lax.fori_loop(0, F // tf, tile, 0)

        def back(j, carry):
            out = pl.ds(pl.multiple_of(j * tf, tf), tf)
            store(out, nt(dgu_ref[rows, :F], wg_ref[out, :]) + nt(dgu_ref[rows, F:], wu_ref[out, :]))
            return carry

        lax.fori_loop(0, D // tf, back, 0)

    def store_own(cols, val):
        dh_ref[:, cols] = val

    kept = []

    def keep(i, t):
        pieces = [(h_ref.at[t], h_hbm.at[t])]
        pieces += [(rows_of(a, t, C), rows_of(b, t, C)) for a, b in ((hid_ref, hid_hbm), (dgu_ref, dgu_hbm))]
        for k, (src, dst) in enumerate(pieces):
            kept.append(pltpu.make_async_copy(src, dst, osem.at[i, k]))
            kept[-1].start()

    chunk(me, store_own)
    keep(0, me)
    gather.relay()
    copies = {}
    for d in range(1, n):
        t = me ^ d
        gather.wait(d)

        def store_sent(cols, val):
            sbuf[d - 1, :, cols] = val.astype(BF)

        chunk(t, store_sent)
        keep(d, t)
        copies[d] = remote(sbuf.at[d - 1], rbuf.at[d - 1], ss2.at[d - 1], rs2.at[d - 1], t)
        copies[d].start()
    gather.finish()

    def leave(i):
        return pltpu.make_async_copy(rows_of(gd_ref, i, td), rows_of(gd_hbm, i, td), gsem.at[i])

    td = 512
    tg = 512 if F % 512 == 0 else 256

    def down(i, carry):
        g = gb_ref[:, pl.ds(pl.multiple_of(i * td, td), td)]
        for j in range(F // tg):
            cols = slice(j * tg, (j + 1) * tg)
            gd_ref[pl.ds(pl.multiple_of(i * td, td), td), cols] = tn(g, hid_ref[:, cols]).astype(BF)
        leave(i).start()
        return carry

    lax.fori_loop(0, D // td, down, 0)
    for d in range(1, n):
        copies[d].wait_recv()
        dh_ref[...] += rbuf[d - 1].astype(F32)
    for d in range(1, n):
        copies[d].wait_send()
    for copy in kept:
        copy.wait()
    for i in range(D // td):
        leave(i).wait()


def ff(n, h, gb, wg, wu, wd):
    C, D = h.shape
    T = gb.shape[0]
    F = wg.shape[1]
    return pl.pallas_call(
        functools.partial(ff_kernel, n),
        in_specs=[VSPEC] + [ANYSPEC] * 4,
        out_specs=[ANYSPEC] * 3 + [VSPEC, ANYSPEC],
        out_shape=[sds((n, C, D), BF), sds((T, F), BF), sds((T, 2 * F), BF), sds((C, D), F32), sds((D, F), BF)],
        scratch_shapes=[
            pltpu.VMEM((T, D), BF),
            pltpu.VMEM((D, F), BF),
            pltpu.VMEM((D, F), BF),
            pltpu.VMEM((F, D), BF),
            pltpu.VMEM((n - 1, C, D), BF),
            pltpu.VMEM((n - 1, C, D), BF),
        ]
        + [pltpu.SemaphoreType.DMA((links(n),))] * 2
        + [pltpu.SemaphoreType.DMA((n - 1,))] * 2
        + [pltpu.SemaphoreType.DMA((4,))]
        + [pltpu.VMEM((n, C, D), BF), pltpu.VMEM((T, F), BF), pltpu.VMEM((T, 2 * F), BF)]
        + [pltpu.SemaphoreType.DMA((n, 3))]
        + [pltpu.VMEM((D, F), BF), pltpu.SemaphoreType.DMA((D // 512,))],
        compiler_params=params(collective_id=1, has_side_effects=True),
        cost_estimate=cost(10 * T * D * F + 3e10, 6 * D * F + 8 * T * D),
        name="ff",
    )(h, gb, wg, wu, wd)


def feed_kernel(n, hid_ref, wd_ref, after_hbm, h_hbm, dgu_hbm, out_ref, gr_hbm,
                sbuf, rbuf, ss, rs, h_ref, dgu_ref, after_ref, lsem, gr_ref, osem):
    me = lax.axis_index("tensor")
    h, dgu, after = (
        Late(src, dst, lsem.at[i])
        for i, (src, dst) in enumerate(((h_hbm, h_ref), (dgu_hbm, dgu_ref), (after_hbm, after_ref)))
    )
    C, D = after_ref.shape
    F2 = dgu_ref.shape[1]
    greet(n, me)

    def part(t):
        return nn(hid_ref[pl.ds(pl.multiple_of(t * C, C), C), :], wd_ref[...])

    tb, tf = 512, 512

    def tile(j, carry):
        cols = pl.ds(pl.multiple_of(j * tf, tf), tf)
        for i in range(D // tb):
            rows = slice(i * tb, (i + 1) * tb)
            gr_ref[rows, cols] = tn(h_ref[:, rows], dgu_ref[:, cols]).astype(BF)
        leave(j).start()
        return carry

    def leave(j):
        cols = pl.ds(pl.multiple_of(j * tf, tf), tf)
        return pltpu.make_async_copy(gr_ref.at[:, cols], gr_hbm.at[:, cols], osem.at[j])

    def filler():
        h()
        dgu()
        lax.fori_loop(0, F2 // tf, tile, 0)

    total, copies = reduce_parts(n, me, part, filler, sbuf, rbuf, ss, rs)
    out_ref[...] = (after()[...] + total).astype(BF)
    for copy in copies.values():
        copy.wait_send()
    for j in range(F2 // tf):
        leave(j).wait()


def feed_grads(n, hidden, wd, after, h, dgu):
    C, D = after.shape
    T, F2 = dgu.shape
    return pl.pallas_call(
        functools.partial(feed_kernel, n),
        in_specs=[VSPEC] * 2 + [ANYSPEC] * 3,
        out_specs=[VSPEC, ANYSPEC],
        out_shape=[sds((C, D), BF), sds((D, F2), BF)],
        scratch_shapes=reduce_bufs(n, C, D)
        + held(h, dgu, after)
        + [pltpu.VMEM((D, F2), BF), pltpu.SemaphoreType.DMA((F2 // 512,))],
        compiler_params=params(collective_id=6, has_side_effects=True),
        cost_estimate=cost(3 * T * D * F2, 6 * D * F2),
        name="feed_grads",
    )(hidden, wd, after, h, dgu)


def gather_kernel(n, ndp, x_in, w_ref, h2_ref, dcq_ref, cb_ref, ca_ref, dkv_ref, ctx_ref, at_ref, x_hbm, da_ref, gr_hbm, kv_ref,
                  buf, other, ksend, krecv, ss, rs, ss2, rs2, pair, x_ref, acc, gr_ref, osem, gsem):
    me = lax.axis_index("tensor")
    dp = lax.axis_index("dp")
    core = dp % 2
    partner = dp + 1 - 2 * core
    C, D = x_in.shape
    W = w_ref.shape[0]
    KP = ctx_ref.shape[0]
    R = D // ndp
    greet(n, me, [partner])
    gather = Gather(n, me, x_in, lambda t: x_ref.at[t], lambda t, i: x_ref.at[t, pl.ds(i * C // 2, C // 2)], ss, rs)
    gather.start()
    kv = {}
    for d in range(1, n):
        ksend[d - 1] = dkv_ref[me ^ d].astype(BF)
        kv[d] = remote(ksend.at[d - 1], krecv.at[d - 1], ss2.at[d - 1], rs2.at[d - 1], me ^ d)
        kv[d].start()

    kept = []

    def back(i, t):
        rows = pl.ds(pl.multiple_of(t * C, C), C)
        x = x_ref[t]
        kept.append(pltpu.make_async_copy(x_ref.at[t], x_hbm.at[t], osem.at[i]))
        kept[-1].start()
        da_ref[rows, :] = nt(x, w_ref[...]).astype(BF)
        term = tn(x, at_ref[rows, :])
        if i == 0:
            acc[...] = term
        else:
            acc[...] += term

    x_ref[me] = x_in[...]
    back(0, me)

    for j in range(ndp // 2):
        h2, cb = h2_ref[:, 2 * R * j : 2 * R * (j + 1)], cb_ref[:, 2 * R * j : 2 * R * (j + 1)]

        def weights(t, carry):
            for i, (a, b) in enumerate(((h2, dcq_ref[t]), (cb, ca_ref[t]))):
                res = tn(a, b).astype(BF)
                for c in range(2):
                    buf[c, t, j * R : (j + 1) * R, i * W : (i + 1) * W] = res[c * R : (c + 1) * R]
            return carry

        lax.fori_loop(0, n, weights, 0)
    swap = to_dp(buf.at[1 - core], other, pair.at[0], pair.at[1], partner)
    swap.start()
    gather.relay()
    dkv = dkv_ref[me]
    for d in range(1, n):
        kv[d].wait_recv()
        dkv = dkv + krecv[d - 1].astype(F32)
    for half in range(2):
        kvg = tn(ctx_ref[...], dkv[half * KP : (half + 1) * KP].astype(BF)).astype(BF)
        S = kvg.shape[0] // ndp
        for i in range(ndp):
            kv_ref[(2 * i + half) * S : (2 * i + half + 1) * S, W:] = kvg[i * S : (i + 1) * S]
    for d in range(1, n - 1):
        gather.wait(d)
        back(d, me ^ d)
    swap.wait_recv()

    def leave(t):
        return pltpu.make_async_copy(gr_ref.at[t], gr_hbm.at[t], gsem.at[t])

    def add(t, carry):
        gr_ref[t] = (buf[core, t].astype(F32) + other[t].astype(F32)).astype(BF)
        leave(t).start()
        return carry

    lax.fori_loop(0, n, add, 0)
    gather.wait(n - 1)
    back(n - 1, me ^ (n - 1))
    kv_ref[:, :W] = acc[...].astype(BF)
    gather.finish()
    for copy in kept:
        copy.wait()
    for t in range(n):
        leave(t).wait()
    for d in range(1, n):
        kv[d].wait_send()
    swap.wait_send()


def gather_back(n, ndp, x, w, h2, dcq, cb, ca, dkv, ctx, attn):
    C, D = x.shape
    W = w.shape[0]
    KP = ctx.shape[0]
    half = (n, D // 2, 2 * W)
    return pl.pallas_call(
        functools.partial(gather_kernel, n, ndp),
        in_specs=[VSPEC] * 9,
        out_specs=[ANYSPEC, VSPEC, ANYSPEC, VSPEC],
        out_shape=[sds((n, C, D), BF), sds((n * C, W), BF), sds(half, BF), sds((D, 2 * W), BF)],
        scratch_shapes=[pltpu.VMEM((2, *half), BF), pltpu.VMEM(half, BF)]
        + [pltpu.VMEM((n - 1, 2 * KP, W), BF)] * 2
        + [pltpu.SemaphoreType.DMA((links(n),))] * 2
        + [pltpu.SemaphoreType.DMA((n - 1,))] * 2
        + [pltpu.SemaphoreType.DMA((2,))]
        + [pltpu.VMEM((n, C, D), BF), pltpu.VMEM((D, W), F32), pltpu.VMEM(half, BF)]
        + [pltpu.SemaphoreType.DMA((n,))] * 2,
        compiler_params=params(collective_id=2, has_side_effects=True),
        cost_estimate=cost(2 * n * C * W * D + 2e10, 8 * C * D),
        name="gather_back",
    )(x, w, h2, dcq, cb, ca, dkv, ctx, attn)


def attn_bwd_kernel(n, ndp, q_ref, k_ref, v_ref, o_ref, do_ref, lse_ref, c_ref, s_ref, h_hbm, e_hbm, a_hbm,
                    dq_ref, dk_ref, dv_ref, gr_hbm, dk_acc, dv_acc, kt_ref, sbuf, rbuf, ss, rs,
                    a_ref, h_ref, e_ref, lsem, gr_ref, osem, x_ref):
    me = lax.axis_index("tensor")
    T, W = q_ref.shape
    G = lane_group(W)
    qb = 256
    mult = SCALE * LOG2E
    nh = G // HEAD_DIM
    greet(n, me)
    shards = ShardSum(n, me, a_ref, sbuf, rbuf, ss, rs)
    shards.start(a_hbm)
    a, h_all, early = (
        Late(src, dst, lsem.at[i]) for i, (src, dst) in enumerate(((a_hbm, a_ref), (h_hbm, h_ref), (e_hbm, e_ref)))
    )
    masks = [m.astype(BF) for m in head_masks(1, G)]
    head_rows = jnp.where(
        lax.broadcasted_iota(jnp.int32, (16, G), 0) == lax.broadcasted_iota(jnp.int32, (16, G), 1) // HEAD_DIM, 1.0, 0.0
    ).astype(BF)

    def heads(g, outer):
        cols = pl.ds(pl.multiple_of(g * G, G), G) if G < W else slice(None)
        k, v = k_ref[:, cols], v_ref[:, cols]
        kt_ref[...] = jnp.transpose(k.astype(F32)).astype(BF)
        dk_acc[...] = jnp.zeros_like(dk_acc)
        dv_acc[...] = jnp.zeros_like(dv_acc)

        def block(i, carry):
            rows = pl.ds(pl.multiple_of(i * qb, qb), qb)
            q = q_ref[rows, cols]
            do = do_ref[rows, cols]
            prod = do.astype(F32) * o_ref[rows, cols].astype(F32)
            high = prod.astype(BF)
            delta = nt(head_rows, high) + nt(head_rows, (prod - high.astype(F32)).astype(BF))
            lse = lse_ref[g, :, rows]
            parts = []
            for h in range(nh):
                qm = q * masks[h]
                dom = do * masks[h]
                st = nt(k, qm)
                pt = jnp.exp2(st * mult - lse[h : h + 1, :])
                dpt = nt(v, dom)
                dst = (pt * (dpt - delta[h : h + 1, :])).astype(BF)
                dv_acc[...] += nn(pt.astype(BF), dom)
                dk_acc[...] += nn(dst, qm)
                parts.append(nn(kt_ref[h * HEAD_DIM : (h + 1) * HEAD_DIM, :], dst))
            dq = jnp.transpose(jnp.concatenate(parts, 0)) * SCALE
            dq_ref[rows, cols] = (dq * c_ref[rows, :] - turned(dq) * s_ref[rows, :]).astype(BF)
            return carry

        lax.fori_loop(0, T // qb, block, 0)
        dk = dk_acc[...] * SCALE
        dk_ref[:, cols] = (dk * c_ref[...] - turned(dk) * s_ref[...]).astype(BF)
        dv_ref[:, cols] = dv_acc[...].astype(BF)
        return outer

    lax.fori_loop(0, W // G, heads, 0)
    a()
    shards.middle()
    h_all()
    early()
    tf = 256
    cut = 5 * W if W % 128 == 0 else 0

    def leave(j):
        rows = pl.ds(pl.multiple_of(j * tf, tf), tf)
        return pltpu.make_async_copy(gr_ref.at[rows, :cut], gr_hbm.at[rows, :cut], osem.at[j])

    def weights(j, carry):
        rows = pl.ds(pl.multiple_of(j * tf, tf), tf)
        h = h_ref[:, rows]
        for i, g_ref in enumerate((dq_ref, dk_ref, dv_ref)):
            gr_ref[rows, i * W : (i + 1) * W] = tn(h, g_ref[...]).astype(BF)
        gr_ref[rows, 3 * W : 5 * W] = e_ref[rows, :]
        if cut:
            leave(j).start()
        return carry

    lax.fori_loop(0, gr_ref.shape[0] // tf, weights, 0)
    shards.store(x_ref)
    core = lax.axis_index("dp") % 2
    R = gr_ref.shape[0] // ndp
    for i in range(ndp // 2):
        gr_ref[pl.ds(pl.multiple_of((2 * i + core) * R, 16), R), 5 * W :] = x_ref[i * R : (i + 1) * R]
        gr_ref[pl.ds(pl.multiple_of((2 * i + 1 - core) * R, 16), R), 5 * W :] = jnp.zeros((R, 2 * W), BF)
    final = pltpu.make_async_copy(gr_ref.at[:, cut:], gr_hbm.at[:, cut:], osem.at[gr_ref.shape[0] // tf])
    final.start()
    if cut:
        for j in range(gr_ref.shape[0] // tf):
            leave(j).wait()
    final.wait()


def attn_bwd(n, ndp, q, k, v, o, do, lse, cs, sn, h, early, a):
    T, W = q.shape
    D = h.shape[1]
    G = lane_group(W)
    _, R, N = a.shape
    slots = 6 if n == 4 else n - 1
    H = R // 2 if n == 4 else R
    return pl.pallas_call(
        functools.partial(attn_bwd_kernel, n, ndp),
        in_specs=[VSPEC] * 8 + [ANYSPEC] * 3,
        out_specs=[VSPEC] * 3 + [ANYSPEC],
        out_shape=[sds((T, W), BF)] * 3 + [sds((D, 7 * W), BF)],
        scratch_shapes=[pltpu.VMEM((T, G), F32), pltpu.VMEM((T, G), F32), pltpu.VMEM((G, T), BF)]
        + [pltpu.VMEM((2, H, N), BF), pltpu.VMEM((slots, H, N), BF)]
        + [pltpu.SemaphoreType.DMA((slots,))] * 2
        + held(a, h, early)
        + [pltpu.VMEM((D, 7 * W), BF), pltpu.SemaphoreType.DMA((D // 256 + 1,)), pltpu.VMEM((R, N), BF)],
        compiler_params=params(collective_id=5, has_side_effects=True),
        cost_estimate=cost(40 * T * T * W, 16 * T * W, T * T * W // HEAD_DIM),
        name="attn_bwd",
    )(q, k, v, o, do, lse, cs, sn, h, early, a)


def last_kernel(n, ndp, dq_ref, dk_ref, dv_ref, wq_ref, wk_ref, wv_ref, x_hbm, da_ref, g_ref, gg_in,
                lbuf, gg_ref, sbuf, rbuf, gbuf, gsum, gown, gall, ss, rs, ss2, rs2, ss3, rs3, ss4, rs4, x_buf, lsem):
    me = lax.axis_index("tensor")
    dp = lax.axis_index("dp")
    C, D = x_buf.shape
    x = Late(rows_of(x_hbm, me, C), x_buf, lsem.at[0])
    R = D // ndp
    others = [(dp + i) % ndp for i in range(1, ndp)]
    greet(n, me, others)

    def part(t):
        rows = pl.ds(pl.multiple_of(t * C, C), C)
        return nt(dq_ref[rows, :], wq_ref[...]) + nt(dk_ref[rows, :], wk_ref[...]) + nt(dv_ref[rows, :], wv_ref[...])

    total, copies = reduce_parts(n, me, part, lambda: None, sbuf, rbuf, ss, rs)
    u, inverse = unit(x()[...].astype(F32))
    row = lax.broadcasted_iota(jnp.int32, (8, D), 0)
    gsum[...] = gg_in[...] + jnp.where(row == 2, jnp.sum(total * u, axis=0, keepdims=True), 0.0)
    small = {}
    for d in range(1, n):
        small[d] = remote(gsum, gbuf.at[d - 1], ss3.at[d - 1], rs3.at[d - 1], me ^ d)
        small[d].start()
    lbuf[me] = (da_ref[...] + norm_back(total, u, inverse, g_ref[...].reshape(1, D))).astype(BF)
    gather = Gather(
        n, me, lbuf.at[me], lambda t: lbuf.at[t], lambda t, i: lbuf.at[t, pl.ds(i * C // 2, C // 2)], ss2, rs2
    )
    gather.start()
    gains = gsum[...]
    for d in range(1, n):
        small[d].wait_recv()
        gains = gains + gbuf[d - 1]
    for i in range(ndp):
        gown[i] = gains[:, i * R : (i + 1) * R]
    sums = []
    for i, other in enumerate(others):
        sums.append(to_dp(gown.at[other], gall.at[i], ss4.at[i], rs4.at[i], other))
        sums[i].start()
    gather.relay()
    mine = gown[dp]
    for i in range(ndp - 1):
        sums[i].wait_recv()
        mine = mine + gall[i]
    gg_ref[...] = mine
    for d in range(1, n):
        gather.wait(d)
    gather.finish()
    for copy in (*copies.values(), *small.values(), *sums):
        copy.wait_send()


def last(n, ndp, dq, dk, dv, wq, wk, wv, x, da, gain, gains):
    T, W = dq.shape
    C, D = da.shape
    return pl.pallas_call(
        functools.partial(last_kernel, n, ndp),
        in_specs=[VSPEC] * 6 + [ANYSPEC] + [VSPEC] * 3,
        out_specs=[VSPEC] * 2,
        out_shape=[sds((n, C, D), BF), sds((8, D // ndp), F32)],
        scratch_shapes=reduce_bufs(n, C, D)[:2]
        + [pltpu.VMEM((n - 1, 8, D), F32), pltpu.VMEM((8, D), F32)]
        + [pltpu.VMEM((ndp, 8, D // ndp), F32), pltpu.VMEM((ndp - 1, 8, D // ndp), F32)]
        + reduce_bufs(n, C, D)[2:]
        + [pltpu.SemaphoreType.DMA((links(n),))] * 2
        + [pltpu.SemaphoreType.DMA((n - 1,))] * 2
        + [pltpu.SemaphoreType.DMA((ndp - 1,))] * 2
        + held(sds((C, D), BF)),
        compiler_params=params(collective_id=3, has_side_effects=True),
        cost_estimate=cost(6 * T * W * D + 4e10, 8 * T * D),
        name="last",
    )(dq, dk, dv, wq, wk, wv, x, da, gain, gains)


def cross_fwd_kernel(n, ctx, h_ref, x_ref, wq_ref, kv_ref, wo_hbm, g_ref, q_ref, o_ref, after_ref, h3_ref, wo_ref, lsem):
    wo = Late(wo_hbm, wo_ref, lsem.at[0])
    _, C, W = q_ref.shape
    KP = kv_ref.shape[1] // 2
    mult = SCALE * LOG2E
    G = lane_group(W)
    per = W // G
    masks = [m.astype(BF) for m in head_masks(1, G)]
    lane = lax.broadcasted_iota(jnp.int32, (C, G), 1) // HEAD_DIM
    valid = lax.broadcasted_iota(jnp.int32, (C, KP), 1) < ctx

    def group(t, j):
        cols = slice(j * G, (j + 1) * G)
        q = nn(h_ref[...], wq_ref[t, :, cols]).astype(BF)
        q_ref[t, :, cols] = q
        k, v = kv_ref[t, :KP, cols], kv_ref[t, KP:, cols]
        out = jnp.zeros((C, G), F32)
        for h in range(G // HEAD_DIM):
            s = jnp.where(valid, nt(q * masks[h], k), -1e30)
            p = jnp.exp2((s - jnp.max(s, axis=-1, keepdims=True)) * mult)
            o = nn(p.astype(BF), v) / jnp.sum(p, axis=-1, keepdims=True)
            out = jnp.where(lane == h, o, out)
        o_ref[t, :, cols] = out.astype(BF)

    def shard(t, carry):
        for j in range(per):
            group(t, j)
        return carry

    lax.fori_loop(0, n, shard, 0)
    D = h_ref.shape[1]
    tf = 256
    wo()

    def project(j, carry):
        cols = pl.ds(pl.multiple_of(j * tf, tf), tf)
        total = nn(o_ref[0], wo_ref[0, :, cols])
        for t in range(1, n):
            total = total + nn(o_ref[t], wo_ref[t, :, cols])
        after_ref[:, cols] = x_ref[:, cols] + total
        return carry

    lax.fori_loop(0, D // tf, project, 0)
    u, _ = unit(after_ref[...])
    h3_ref[...] = (u * g_ref[...].reshape(1, D)).astype(BF)


def cross_fwd(ctx, h, x, wq, kv, wo, gain):
    C, D = h.shape
    n, W = wq.shape[0], wq.shape[2]
    return pl.pallas_call(
        functools.partial(cross_fwd_kernel, n, ctx),
        in_specs=[VSPEC] * 4 + [ANYSPEC, VSPEC],
        out_specs=[VSPEC] * 4,
        out_shape=[sds((n, C, W), BF), sds((n, C, W), BF), sds((C, D), F32), sds((C, D), BF)],
        scratch_shapes=held(wo),
        compiler_params=params(),
        cost_estimate=cost(4 * C * D * n * W + 16 * C * 256 * n * W, 8 * D * n * W),
        name="cross_fwd",
    )(h, x, wq, kv, wo, gain)


def cross_bwd_kernel(n, ctx, dh3_ref, after2_ref, cot_hbm, g3_ref, wo_hbm, q_ref, kv_ref, wq_hbm, after1_hbm, g2_ref, bo_in,
                     cb_ref, dq_ref, dkv_ref, da_ref, sb_ref, gg_ref, bo_ref, dh2_ref, ss, rs,
                     cot_buf, wo_ref, wq_ref, after1_buf, lsem):
    me = lax.axis_index("tensor")
    cot, wo, wq, after1 = (
        Late(src, dst, lsem.at[i])
        for i, (src, dst) in enumerate(
            (
                (rows_of(cot_hbm, me, cot_buf.shape[0]), cot_buf),
                (wo_hbm, wo_ref),
                (wq_hbm, wq_ref),
                (after1_hbm, after1_buf),
            )
        )
    )
    _, C, W = q_ref.shape
    KP = kv_ref.shape[1] // 2
    D = da_ref.shape[1]
    mult = SCALE * LOG2E
    G = lane_group(W)
    per = W // G
    masks = [m.astype(BF) for m in head_masks(1, G)]
    lane = lax.broadcasted_iota(jnp.int32, (C, G), 1) // HEAD_DIM
    valid = lax.broadcasted_iota(jnp.int32, (C, KP), 1) < ctx
    greet(n, me)
    gather = Gather(n, me, bo_in, lambda t: bo_ref.at[t], lambda t, i: bo_ref.at[t, pl.ds(i * C // 2, C // 2)], ss, rs)
    gather.start()
    bo_ref[me] = bo_in[...]
    dh3 = dh3_ref[...]
    u3, inv3 = unit(after2_ref[...])
    gain3 = jnp.sum(dh3 * u3, axis=0, keepdims=True)
    da2 = cot()[...].astype(F32) + norm_back(dh3, u3, inv3, g3_ref[...].reshape(1, D))
    da_ref[...] = da2
    cb_ref[...] = da2.astype(BF)
    wo()

    def group(t, j):
        cols = slice(j * G, (j + 1) * G)
        do = nt(cb_ref[...], wo_ref[t, cols, :]).astype(BF)
        q, k, v = q_ref[t, :, cols], kv_ref[t, :KP, cols], kv_ref[t, KP:, cols]
        dq = jnp.zeros((C, G), F32)
        dk = jnp.zeros((KP, G), F32)
        dv = jnp.zeros((KP, G), F32)
        for h in range(G // HEAD_DIM):
            qm = q * masks[h]
            dom = do * masks[h]
            s = jnp.where(valid, nt(qm, k), -1e30)
            p = jnp.exp2((s - jnp.max(s, axis=-1, keepdims=True)) * mult)
            p = p / jnp.sum(p, axis=-1, keepdims=True)
            dp = nt(dom, v)
            ds = (p * (dp - jnp.sum(p * dp, axis=-1, keepdims=True))).astype(BF)
            dq = jnp.where(lane == h, nn(ds, k), dq)
            dk = dk + tn(ds, qm)
            dv = dv + tn(p.astype(BF), dom)
        dq_ref[t, :, cols] = (dq * SCALE).astype(BF)
        dkv_ref[t, :KP, cols] = dk * SCALE
        dkv_ref[t, KP:, cols] = dv

    def shard(t, carry):
        for j in range(per):
            group(t, j)
        return carry

    lax.fori_loop(0, n, shard, 0)
    gather.relay()
    wq()
    tf = 256

    def project(j, carry):
        cols = pl.ds(pl.multiple_of(j * tf, tf), tf)
        total = nt(dq_ref[0], wq_ref[0, cols, :])
        for t in range(1, n):
            total = total + nt(dq_ref[t], wq_ref[t, cols, :])
        dh2_ref[:, cols] = total
        return carry

    lax.fori_loop(0, D // tf, project, 0)
    dh2 = dh2_ref[...]
    u2, inv2 = unit(after1()[...])
    gain2 = jnp.sum(dh2 * u2, axis=0, keepdims=True)
    da1 = da_ref[...] + norm_back(dh2, u2, inv2, g2_ref[...].reshape(1, D))
    da_ref[...] = da1
    sb_ref[...] = da1.astype(BF)
    row = lax.broadcasted_iota(jnp.int32, (8, D), 0)
    gg_ref[...] = jnp.where(row == 0, gain3, 0.0) + jnp.where(row == 1, gain2, 0.0)
    for d in range(1, n):
        gather.wait(d)
    gather.finish()


def cross_bwd(ctx, dh3, after2, cot, g3, wo, q, kv, wq, after1, g2, bo):
    C, D = after2.shape
    n, W = wq.shape[0], wq.shape[2]
    return pl.pallas_call(
        functools.partial(cross_bwd_kernel, n, ctx),
        in_specs=[VSPEC, VSPEC, ANYSPEC, VSPEC, ANYSPEC, VSPEC, VSPEC, ANYSPEC, ANYSPEC, VSPEC, VSPEC],
        out_specs=[VSPEC] * 7,
        out_shape=[
            sds((C, D), BF),
            sds((n, C, W), BF),
            sds(kv.shape, F32),
            sds((C, D), F32),
            sds((C, D), BF),
            sds((8, D), F32),
            sds((n, C, D), BF),
        ],
        scratch_shapes=[pltpu.VMEM((C, D), F32)]
        + [pltpu.SemaphoreType.DMA((links(n),))] * 2
        + held(sds((C, D), BF), wo, wq, after1),
        compiler_params=params(collective_id=7, has_side_effects=True),
        cost_estimate=cost(4 * C * D * n * W + 40 * C * 256 * n * W, 8 * D * n * W),
        name="cross_bwd",
    )(dh3, after2, cot, g3, wo, q, kv, wq, after1, g2, bo)


def body(latents, context, cotangent, g1, wq, wk, wv, wo, g2, xq, xk, xv, xo, g3, wg, wu, wd, n, ndp):
    _, T, D = latents.shape
    ctx = context.shape[1]
    W = wq.shape[1]
    F = wg.shape[1]
    C = T // n
    x = latents.reshape(T, D)
    gb = cotangent.reshape(T, D)
    ctx_rows = context.reshape(ctx, -1)
    KP = -(-ctx // 16) * 16
    cs, sn = tables(T, lane_group(W))

    ctx_pad = jnp.pad(ctx_rows, ((0, KP - ctx), (0, 0)))
    h1, q, k, v, attn, lse, xq_all, xo_all, kv_all = front(n, ctx, x, g1, wq, wk, wv, cs, sn, xq, xo, ctx_pad, xk, xv)
    after1, h2 = out_rs(n, attn, wo, x, g2)
    cq, cattn, after2, h3_own = cross_fwd(ctx, h2, after1, xq_all, kv_all, xo_all, g3)
    h3, hidden, dgu, dh3, down_part = ff(n, h3_own, gb, wg, wu, wd)
    h3 = h3.reshape(T, D)

    def scatter(a, axis):
        return lax.psum_scatter(a, axis, scatter_dimension=0, tiled=True)

    down_grad = scatter(down_part, "dp")
    out_own, gu_part = feed_grads(n, hidden, wd, after2, h3, dgu)
    dh3, gu_part = lax.optimization_barrier((dh3, gu_part))
    gu_grad = scatter(gu_part, "dp")

    cb, dcq, dckv, dafter1, sb_own, gains, block_out = cross_bwd(
        ctx, dh3, after2, gb, g3, xo_all, cq, kv_all, xq_all, after1, g2, out_own
    )
    sb_own, down_grad = lax.optimization_barrier((sb_own, down_grad))
    sb, dattn, cross_part, early_part = gather_back(n, ndp, sb_own, wo, h2, dcq, cb, cattn, dckv, ctx_pad, attn)
    dq, dk, dv, self_part = attn_bwd(n, ndp, q, k, v, attn, dattn, lse, cs, sn, h1, early_part, cross_part)
    self_grads = scatter(self_part, "dp")
    dq, gu_grad = lax.optimization_barrier((dq, gu_grad))
    latent_grad, gains = last(n, ndp, dq, dk, dv, wq, wk, wv, x, dafter1, g1, gains)

    latent_grad = latent_grad.astype(F32)
    gu_grad = gu_grad.astype(F32)
    gate_grad, up_grad, down_grad = gu_grad[:, :F], gu_grad[:, F:], down_grad.astype(F32).T
    self_grads, gains, latent_grad, gate_grad, up_grad, down_grad = lax.optimization_barrier(
        (self_grads, gains, latent_grad, gate_grad, up_grad, down_grad)
    )
    self_grads = self_grads.astype(F32)
    so_grad, kv_grads = self_grads[:, 3 * W : 4 * W].T, self_grads[:, 4 * W : 5 * W].reshape(2, D // ndp // 2, W)
    xq_grad, xo_grad = self_grads[:, 5 * W : 6 * W], self_grads[:, 6 * W :].T
    return (
        block_out.reshape(1, T, D),
        latent_grad.reshape(1, T, D),
        gains[2],
        self_grads[:, :W],
        self_grads[:, W : 2 * W],
        self_grads[:, 2 * W : 3 * W],
        so_grad,
        gains[1],
        xq_grad,
        kv_grads[0],
        kv_grads[1],
        xo_grad,
        gains[0],
        gate_grad,
        up_grad,
        down_grad,
    )


def solution(mesh):
    tokens = P("dp", None, None)
    cols = P(None, "tensor")
    rows = P("tensor", None)
    return jax.shard_map(
        functools.partial(body, n=mesh.shape["tensor"], ndp=mesh.shape["dp"]),
        mesh=mesh,
        in_specs=(tokens, tokens, tokens, P(), cols, cols, cols, rows, P(), cols, cols, cols, rows, P(), cols, cols, rows),
        out_specs=(
            tokens,
            tokens,
            P("dp"),
            P("dp", "tensor"),
            P("dp", "tensor"),
            P("dp", "tensor"),
            P("tensor", "dp"),
            P("dp"),
            P("dp", "tensor"),
            P("dp", "tensor"),
            P("dp", "tensor"),
            P("tensor", "dp"),
            P("dp"),
            P("dp", "tensor"),
            P("dp", "tensor"),
            P("tensor", "dp"),
        ),
        check_vma=False,
    )
```

```python
import functools

import jax
import jax.numpy as jnp
from jax import lax
from jax.experimental import pallas as pl
from jax.experimental.pallas import tpu as pltpu
from jax.sharding import PartitionSpec as P

HEAD_DIM = 64
HALF = HEAD_DIM // 2
EPS = 1e-05
BF = jnp.bfloat16
F32 = jnp.float32
LOG2E = 1.4426950408889634
SCALE = HEAD_DIM**-0.5
VMEM_BYTES = 60 << 20
MESH_ID = pl.DeviceIdType.MESH
VSPEC = pl.BlockSpec(memory_space=pltpu.VMEM)
ANYSPEC = pl.BlockSpec(memory_space=pl.ANY)


def nn(a, b):
    return lax.dot_general(a, b, (((1,), (0,)), ((), ())), preferred_element_type=F32)


def nt(a, b):
    return lax.dot_general(a, b, (((1,), (1,)), ((), ())), preferred_element_type=F32)


def tn(a, b):
    return lax.dot_general(a, b, (((0,), (0,)), ((), ())), preferred_element_type=F32)


def sds(shape, dtype):
    return jax.ShapeDtypeStruct(shape, dtype)


def params(**kw):
    return pltpu.CompilerParams(vmem_limit_bytes=VMEM_BYTES, **kw)


def cost(flops, nbytes, trans=0):
    return pl.CostEstimate(flops=1000, bytes_accessed=1000, transcendentals=0)


def unit(x):
    center = x - jnp.mean(x, axis=-1, keepdims=True)
    inverse = lax.rsqrt(jnp.mean(center * center, axis=-1, keepdims=True) + EPS)
    return center * inverse, inverse


def norm_back(grad, u, inverse, gain):
    e = grad * gain
    mean_e = jnp.mean(e, axis=-1, keepdims=True)
    mean_p = jnp.mean(e * u, axis=-1, keepdims=True)
    return inverse * (e - mean_e - u * mean_p)


def lane_group(width):
    return 128 if width % 128 == 0 else width


def tables(length, group):
    freq = jnp.tile(10000.0 ** (-jnp.arange(HALF, dtype=F32) / HALF), group // HALF)
    angles = lax.broadcasted_iota(F32, (length, group), 0) * freq[None, :]
    front = lax.broadcasted_iota(jnp.int32, (length, group), 1) % HEAD_DIM < HALF
    return jnp.cos(angles), jnp.where(front, -1.0, 1.0) * jnp.sin(angles)


def turned(a):
    width = a.shape[-1]
    lane = lax.broadcasted_iota(jnp.int32, a.shape, 1) % HEAD_DIM
    return jnp.where(lane < HALF, pltpu.roll(a, width - HALF, 1), pltpu.roll(a, HALF, 1))


def head_masks(rows, group):
    lane = lax.broadcasted_iota(jnp.int32, (rows, group), 1) // HEAD_DIM
    return [jnp.where(lane == h, 1.0, 0.0) for h in range(group // HEAD_DIM)]


def greet(n, me, dps=()):
    sem = pltpu.get_barrier_semaphore()
    for d in range(1, n):
        pl.semaphore_signal(sem, 1, device_id={"tensor": me ^ d}, device_id_type=MESH_ID)
    for dp in dps:
        pl.semaphore_signal(sem, 1, device_id={"dp": dp}, device_id_type=MESH_ID)
    pl.semaphore_wait(sem, n - 1 + len(dps))


def to_dp(src, dst, send, recv, target):
    return pltpu.make_async_remote_copy(src, dst, send, recv, device_id={"dp": target}, device_id_type=MESH_ID)


def remote(src, dst, send, recv, target):
    return pltpu.make_async_remote_copy(src, dst, send, recv, device_id={"tensor": target}, device_id_type=MESH_ID)


class Late:
    def __init__(self, src, dst, sem):
        self.dst, self.copy = dst, pltpu.make_async_copy(src, dst, sem)
        self.copy.start()

    def __call__(self):
        self.copy.wait()
        return self.dst


def held(*arrays):
    return [pltpu.VMEM(a.shape, a.dtype) for a in arrays] + [pltpu.SemaphoreType.DMA((len(arrays),))]


def rows_of(ref, t, C):
    return ref.at[pl.ds(pl.multiple_of(t * C, C), C)]


def links(n):
    return 4 if n == 4 else n - 1


class Gather:
    def __init__(self, n, me, src, slot, half, ss, rs):
        self.n, self.me, self.half, self.ss, self.rs = n, me, half, ss, rs
        self.copies = {
            d: remote(src, slot(me), ss.at[d - 1], rs.at[d - 1], me ^ d) for d in (range(1, n) if n != 4 else (1, 2))
        }
        self.passed = []

    def start(self):
        for copy in self.copies.values():
            copy.start()

    def relay(self):
        if self.n == 4:
            for i, d in enumerate((1, 2)):
                self.copies[d].wait_recv()
                block = self.half(self.me ^ d, i)
                copy = remote(block, block, self.ss.at[2 + i], self.rs.at[2 + i], self.me ^ (3 - d))
                copy.start()
                self.passed.append(copy)

    def wait(self, d):
        if self.n != 4:
            self.copies[d].wait_recv()
        elif d == 3:
            for copy in self.passed:
                copy.wait_recv()

    def finish(self):
        for copy in (*self.copies.values(), *self.passed):
            copy.wait_send()


def reduce_bufs(n, C, D):
    shape = (6, C, D // 2) if n == 4 else (n - 1, C, D)
    return [pltpu.VMEM(shape, BF)] * 2 + [pltpu.SemaphoreType.DMA((shape[0],))] * 2


def reduce_parts(n, me, part, filler, sbuf, rbuf, ss, rs):
    copies = {}

    def send(i, val, d):
        sbuf[i] = val.astype(BF)
        copies[i] = remote(sbuf.at[i], rbuf.at[i], ss.at[i], rs.at[i], me ^ d)
        copies[i].start()

    def got(i):
        copies[i].wait_recv()
        return rbuf[i].astype(F32)

    if n == 4:
        across = part(me ^ 3)
        H = across.shape[1] // 2
        send(0, across[:, :H], 1)
        send(2, across[:, H:], 2)
        one = part(me ^ 1)
        send(1, one[:, :H], 1)
        two = part(me ^ 2)
        send(3, two[:, H:], 2)
        total = part(me)
        filler()
        send(4, two[:, :H] + got(0), 2)
        send(5, one[:, H:] + got(2), 1)
        total = jnp.concatenate([total[:, :H] + got(1) + got(4), total[:, H:] + got(3) + got(5)], 1)
    else:
        for d in reversed(range(1, n)):
            send(d - 1, part(me ^ d), d)
        total = part(me)
        filler()
        for d in range(1, n):
            total = total + got(d - 1)
    return total, copies


class ShardSum:
    def __init__(self, n, me, a, sbuf, rbuf, ss, rs):
        self.n, self.me, self.a, self.sbuf, self.rbuf, self.ss, self.rs = n, me, a, sbuf, rbuf, ss, rs
        self.copies = {}

    def send(self, i, src, d):
        self.copies[i] = remote(src, self.rbuf.at[i], self.ss.at[i], self.rs.at[i], self.me ^ d)
        self.copies[i].start()

    def got(self, i):
        self.copies[i].wait_recv()
        return self.rbuf[i].astype(F32)

    def halves(self, d, a=None):
        a = self.a if a is None else a
        H = a.shape[1] // 2
        return a.at[self.me ^ d, pl.ds(0, H)], a.at[self.me ^ d, pl.ds(H, H)]

    def start(self, a):
        if self.n == 4:
            self.send(0, self.halves(3, a)[0], 1)
            self.send(2, self.halves(3, a)[1], 2)
            self.send(1, self.halves(1, a)[0], 1)
            self.send(3, self.halves(2, a)[1], 2)
        else:
            for d in range(1, self.n):
                self.send(d - 1, a.at[self.me ^ d], d)

    def middle(self):
        if self.n == 4:
            self.sbuf[0] = (self.halves(2)[0][...].astype(F32) + self.got(0)).astype(BF)
            self.send(4, self.sbuf.at[0], 2)
            self.sbuf[1] = (self.halves(1)[1][...].astype(F32) + self.got(2)).astype(BF)
            self.send(5, self.sbuf.at[1], 1)

    def store(self, out_ref):
        if self.n == 4:
            H = self.a.shape[1] // 2
            own = self.halves(0)
            out_ref[:H] = (own[0][...].astype(F32) + self.got(1) + self.got(4)).astype(BF)
            out_ref[H:] = (own[1][...].astype(F32) + self.got(3) + self.got(5)).astype(BF)
        else:
            total = self.a[self.me].astype(F32)
            for d in range(1, self.n):
                total = total + self.got(d - 1)
            out_ref[...] = total.astype(BF)
        for copy in self.copies.values():
            copy.wait_send()


def front_kernel(n, ctx, x_hbm, g_ref, wq_hbm, wk_hbm, wv_hbm, c_ref, s_ref, xq_ref, xo_ref, ctx_ref, xk_hbm, xv_hbm,
                 h_hbm, q_hbm, k_hbm, v_hbm, o_ref, lse_ref, xqa_ref, xoa_ref, kva_ref,
                 kv_own, sq, rq, so, ro, sk, rk, fsq, frq, fso, fro, local,
                 x_buf, wq_buf, wk_buf, wv_buf, xk_buf, xv_buf, lsem, h_ref, q_ref, k_ref, v_ref, osem):
    xk, xv, x, wq, wk, wv = (
        Late(src, dst, lsem.at[i])
        for i, (src, dst) in enumerate(
            (
                (xk_hbm, xk_buf),
                (xv_hbm, xv_buf),
                (x_hbm, x_buf),
                (wq_hbm, wq_buf),
                (wk_hbm, wk_buf),
                (wv_hbm, wv_buf),
            )
        )
    )
    me = lax.axis_index("tensor")
    dp = lax.axis_index("dp")
    core = dp % 2
    partner = dp + 1 - 2 * core
    T, D = x_hbm.shape
    W = q_ref.shape[1]
    KP = ctx_ref.shape[0]
    greet(n, me, [partner])

    rows_q = pl.ds(pl.multiple_of(core * (D // 2), 16), D // 2)
    rows_o = pl.ds(pl.multiple_of(core * (W // 2), 16), W // 2)
    def quarter(ref, rows):
        return lambda t, i: ref.at[t, pl.ds(pl.multiple_of(core * (rows // 2) + i * (rows // 4), 16), rows // 4)]

    gq = Gather(n, me, xq_ref.at[rows_q], lambda t: xqa_ref.at[t, rows_q], quarter(xqa_ref, D), sq, rq)
    go = Gather(n, me, xo_ref.at[rows_o], lambda t: xoa_ref.at[t, rows_o], quarter(xoa_ref, W), so, ro)
    gk = Gather(n, me, kv_own, lambda t: kva_ref.at[t], lambda t, i: kva_ref.at[t, pl.ds(i * KP, KP)], sk, rk)
    gq.start()
    go.start()
    own = [
        pltpu.make_async_copy(xq_ref, xqa_ref.at[me], local.at[0]),
        pltpu.make_async_copy(xo_ref, xoa_ref.at[me], local.at[1]),
    ]
    for copy in own:
        copy.start()
    kv_own[:KP] = nn(ctx_ref[...], xk()[...]).astype(BF)
    kv_own[KP:] = nn(ctx_ref[...], xv()[...]).astype(BF)
    gk.start()
    kva_ref[me] = kv_own[...]

    tb = 256
    reps = W // c_ref.shape[1]
    x_ref, wq_ref, wk_ref, wv_ref = x(), wq(), wk(), wv()

    def project(i, carry):
        rows = pl.ds(pl.multiple_of(i * tb, tb), tb)
        u, _ = unit(x_ref[rows, :].astype(F32))
        h = (u * g_ref[...].reshape(1, D)).astype(BF)
        h_ref[rows, :] = h
        c = jnp.concatenate([c_ref[rows, :]] * reps, 1)
        s = jnp.concatenate([s_ref[rows, :]] * reps, 1)
        for w_ref, out_ref in ((wq_ref, q_ref), (wk_ref, k_ref)):
            a = nn(h, w_ref[...])
            out_ref[rows, :] = (a * c + turned(a) * s).astype(BF)
        v_ref[rows, :] = nn(h, wv_ref[...]).astype(BF)
        return carry

    lax.fori_loop(0, T // tb, project, 0)
    kept = [
        pltpu.make_async_copy(src, dst, osem.at[i])
        for i, (src, dst) in enumerate(((h_ref, h_hbm), (q_ref, q_hbm), (k_ref, k_hbm), (v_ref, v_hbm)))
    ]
    for copy in kept:
        copy.start()
    gq.relay()

    G = lane_group(W)
    mult = SCALE * LOG2E
    masks = [m.astype(BF) for m in head_masks(1, G)]
    lane = lax.broadcasted_iota(jnp.int32, (tb, G), 1) // HEAD_DIM
    stat_lane = lax.broadcasted_iota(jnp.int32, (tb, 128), 1)

    def heads(g, carry):
        cols = pl.ds(pl.multiple_of(g * G, G), G) if G < W else slice(None)
        k, v = k_ref[:, cols], v_ref[:, cols]

        def block(i, inner):
            rows = pl.ds(pl.multiple_of(i * tb, tb), tb)
            q = q_ref[rows, cols]
            out = jnp.zeros((tb, G), F32)
            stats = jnp.zeros((tb, 128), F32)
            for h in range(G // HEAD_DIM):
                s = nt(q * masks[h], k)
                top = jnp.max(s, axis=-1, keepdims=True) * mult
                p = jnp.exp2(s * mult - top)
                total = jnp.sum(p, axis=-1, keepdims=True)
                o = nn(p.astype(BF), v) / total
                out = jnp.where(lane == h, o, out)
                stats = jnp.where(stat_lane == h, top + jnp.log2(total), stats)
            o_ref[rows, cols] = out.astype(BF)
            lse_ref[g, :, rows] = jnp.transpose(stats)[:8]
            return inner

        return lax.fori_loop(0, T // tb, block, carry)

    lax.fori_loop(0, W // G, heads, 0)

    go.relay()
    gk.relay()
    passed = []
    for gather, ref, rows, send, recv in ((gq, xqa_ref, rows_q, fsq, frq), (go, xoa_ref, rows_o, fso, fro)):
        for d in range(1, n):
            gather.wait(d)
            block = ref.at[me ^ d, rows]
            copy = to_dp(block, block, send.at[d - 1], recv.at[d - 1], partner)
            copy.start()
            passed.append(copy)
    for copy in (*own, *kept):
        copy.wait()
    for d in range(1, n):
        gk.wait(d)
    for copy in passed:
        copy.wait_recv()
    for copy in (gq, go, gk):
        copy.finish()
    for copy in passed:
        copy.wait_send()


def front(n, ctx, x, gain, wq, wk, wv, cs, sn, xq, xo, ctx_rows, xk, xv):
    T, D = x.shape
    W = wq.shape[1]
    KP = ctx_rows.shape[0]
    groups = W // lane_group(W)
    link, pair = pltpu.SemaphoreType.DMA((links(n),)), pltpu.SemaphoreType.DMA((n - 1,))
    return pl.pallas_call(
        functools.partial(front_kernel, n, ctx),
        in_specs=[ANYSPEC, VSPEC] + [ANYSPEC] * 3 + [VSPEC] * 5 + [ANYSPEC] * 2,
        out_specs=[ANYSPEC] * 4 + [VSPEC] * 2 + [ANYSPEC] * 2 + [VSPEC],
        out_shape=[sds((T, D), BF)]
        + [sds((T, W), BF)] * 4
        + [sds((groups, 8, T), F32), sds((n, D, W), BF), sds((n, W, D), BF), sds((n, 2 * KP, W), BF)],
        scratch_shapes=[pltpu.VMEM((2 * KP, W), BF)] + [link] * 6 + [pair] * 4 + [pltpu.SemaphoreType.DMA((2,))]
        + held(x, wq, wk, wv, xk, xv)
        + held(sds((T, D), BF), *[sds((T, W), BF)] * 3),
        compiler_params=params(collective_id=4, has_side_effects=True),
        cost_estimate=cost(6 * T * D * W, 4 * T * D + 6 * D * W + 6 * T * W),
        name="front",
    )(x, gain, wq, wk, wv, cs, sn, xq, xo, ctx_rows, xk, xv)


def out_rs_kernel(n, a_ref, w_ref, x_hbm, g_ref, after_ref, h_ref, sbuf, rbuf, ss, rs, x_buf, lsem):
    me = lax.axis_index("tensor")
    C, D = x_buf.shape
    x = Late(rows_of(x_hbm, me, C), x_buf, lsem.at[0])
    greet(n, me)

    def part(t):
        return nn(a_ref[pl.ds(pl.multiple_of(t * C, C), C), :], w_ref[...])

    total, copies = reduce_parts(n, me, part, lambda: None, sbuf, rbuf, ss, rs)
    after = x()[...].astype(F32) + total
    after_ref[...] = after
    u, _ = unit(after)
    h_ref[...] = (u * g_ref[...].reshape(1, D)).astype(BF)
    for copy in copies.values():
        copy.wait_send()


def out_rs(n, a, w, x, gain):
    T, D = x.shape
    C = T // n
    W = a.shape[1]
    return pl.pallas_call(
        functools.partial(out_rs_kernel, n),
        in_specs=[VSPEC, VSPEC, ANYSPEC, VSPEC],
        out_specs=[VSPEC] * 2,
        out_shape=[sds((C, D), F32), sds((C, D), BF)],
        scratch_shapes=reduce_bufs(n, C, D) + held(sds((C, D), BF)),
        compiler_params=params(collective_id=0, has_side_effects=True),
        cost_estimate=cost(2 * T * W * D + 2e10, 8 * C * D),
        name="out_rs",
    )(a, w, x, gain)


def ff_kernel(n, h_in, gb_hbm, wg_hbm, wu_hbm, wd_hbm, h_hbm, hid_hbm, dgu_hbm, dh_ref, gd_hbm,
              gb_ref, wg_ref, wu_ref, wd_ref, sbuf, rbuf, ss, rs, ss2, rs2, ls, h_ref, hid_ref, dgu_ref, osem, gd_ref, gsem):
    me = lax.axis_index("tensor")
    C, D = h_in.shape
    F = wg_ref.shape[1]
    loads = [
        pltpu.make_async_copy(src, dst, ls.at[i])
        for i, (src, dst) in enumerate(((wg_hbm, wg_ref), (wu_hbm, wu_ref), (wd_hbm, wd_ref), (gb_hbm, gb_ref)))
    ]
    for c in loads:
        c.start()
    greet(n, me)
    gather = Gather(n, me, h_in, lambda t: h_ref.at[t], lambda t, i: h_ref.at[t, pl.ds(i * C // 2, C // 2)], ss, rs)
    gather.start()
    h_ref[me] = h_in[...]
    for c in loads:
        c.wait()
    tf = 512

    def chunk(t, store):
        rows = pl.ds(pl.multiple_of(t * C, C), C)
        h = h_ref[t]
        gb = gb_ref[rows, :]

        def tile(j, carry):
            cols = pl.ds(pl.multiple_of(j * tf, tf), tf)
            gate = nn(h, wg_ref[:, cols])
            up = nn(h, wu_ref[:, cols])
            dhid = nt(gb, wd_ref[cols, :])
            sig = 1.0 / (1.0 + jnp.exp(-gate))
            act = gate * sig
            hid_ref[rows, cols] = (act * up).astype(BF)
            dgu_ref[rows, cols] = (dhid * up * (sig * (1.0 + gate * (1.0 - sig)))).astype(BF)
            dgu_ref[rows, pl.ds(pl.multiple_of(F + j * tf, tf), tf)] = (dhid * act).astype(BF)
            return carry

        lax.fori_loop(0, F // tf, tile, 0)

        def back(j, carry):
            out = pl.ds(pl.multiple_of(j * tf, tf), tf)
            store(out, nt(dgu_ref[rows, :F], wg_ref[out, :]) + nt(dgu_ref[rows, F:], wu_ref[out, :]))
            return carry

        lax.fori_loop(0, D // tf, back, 0)

    def store_own(cols, val):
        dh_ref[:, cols] = val

    kept = []

    def keep(i, t):
        pieces = [(h_ref.at[t], h_hbm.at[t])]
        pieces += [(rows_of(a, t, C), rows_of(b, t, C)) for a, b in ((hid_ref, hid_hbm), (dgu_ref, dgu_hbm))]
        for k, (src, dst) in enumerate(pieces):
            kept.append(pltpu.make_async_copy(src, dst, osem.at[i, k]))
            kept[-1].start()

    chunk(me, store_own)
    keep(0, me)
    gather.relay()
    copies = {}
    for d in range(1, n):
        t = me ^ d
        gather.wait(d)

        def store_sent(cols, val):
            sbuf[d - 1, :, cols] = val.astype(BF)

        chunk(t, store_sent)
        keep(d, t)
        copies[d] = remote(sbuf.at[d - 1], rbuf.at[d - 1], ss2.at[d - 1], rs2.at[d - 1], t)
        copies[d].start()
    gather.finish()

    def leave(i):
        return pltpu.make_async_copy(rows_of(gd_ref, i, td), rows_of(gd_hbm, i, td), gsem.at[i])

    td = 512
    tg = 512 if F % 512 == 0 else 256

    def down(i, carry):
        g = gb_ref[:, pl.ds(pl.multiple_of(i * td, td), td)]
        for j in range(F // tg):
            cols = slice(j * tg, (j + 1) * tg)
            gd_ref[pl.ds(pl.multiple_of(i * td, td), td), cols] = tn(g, hid_ref[:, cols]).astype(BF)
        leave(i).start()
        return carry

    lax.fori_loop(0, D // td, down, 0)
    for d in range(1, n):
        copies[d].wait_recv()
        dh_ref[...] += rbuf[d - 1].astype(F32)
    for d in range(1, n):
        copies[d].wait_send()
    for copy in kept:
        copy.wait()
    for i in range(D // td):
        leave(i).wait()


def ff(n, h, gb, wg, wu, wd):
    C, D = h.shape
    T = gb.shape[0]
    F = wg.shape[1]
    return pl.pallas_call(
        functools.partial(ff_kernel, n),
        in_specs=[VSPEC] + [ANYSPEC] * 4,
        out_specs=[ANYSPEC] * 3 + [VSPEC, ANYSPEC],
        out_shape=[sds((n, C, D), BF), sds((T, F), BF), sds((T, 2 * F), BF), sds((C, D), F32), sds((D, F), BF)],
        scratch_shapes=[
            pltpu.VMEM((T, D), BF),
            pltpu.VMEM((D, F), BF),
            pltpu.VMEM((D, F), BF),
            pltpu.VMEM((F, D), BF),
            pltpu.VMEM((n - 1, C, D), BF),
            pltpu.VMEM((n - 1, C, D), BF),
        ]
        + [pltpu.SemaphoreType.DMA((links(n),))] * 2
        + [pltpu.SemaphoreType.DMA((n - 1,))] * 2
        + [pltpu.SemaphoreType.DMA((4,))]
        + [pltpu.VMEM((n, C, D), BF), pltpu.VMEM((T, F), BF), pltpu.VMEM((T, 2 * F), BF)]
        + [pltpu.SemaphoreType.DMA((n, 3))]
        + [pltpu.VMEM((D, F), BF), pltpu.SemaphoreType.DMA((D // 512,))],
        compiler_params=params(collective_id=1, has_side_effects=True),
        cost_estimate=cost(10 * T * D * F + 3e10, 6 * D * F + 8 * T * D),
        name="ff",
    )(h, gb, wg, wu, wd)


def feed_kernel(n, hid_ref, wd_ref, after_hbm, h_hbm, dgu_hbm, out_ref, gr_hbm,
                sbuf, rbuf, ss, rs, h_ref, dgu_ref, after_ref, lsem, gr_ref, osem):
    me = lax.axis_index("tensor")
    h, dgu, after = (
        Late(src, dst, lsem.at[i])
        for i, (src, dst) in enumerate(((h_hbm, h_ref), (dgu_hbm, dgu_ref), (after_hbm, after_ref)))
    )
    C, D = after_ref.shape
    F2 = dgu_ref.shape[1]
    greet(n, me)

    def part(t):
        return nn(hid_ref[pl.ds(pl.multiple_of(t * C, C), C), :], wd_ref[...])

    tb, tf = 512, 512

    def tile(j, carry):
        cols = pl.ds(pl.multiple_of(j * tf, tf), tf)
        for i in range(D // tb):
            rows = slice(i * tb, (i + 1) * tb)
            gr_ref[rows, cols] = tn(h_ref[:, rows], dgu_ref[:, cols]).astype(BF)
        leave(j).start()
        return carry

    def leave(j):
        cols = pl.ds(pl.multiple_of(j * tf, tf), tf)
        return pltpu.make_async_copy(gr_ref.at[:, cols], gr_hbm.at[:, cols], osem.at[j])

    def filler():
        h()
        dgu()
        lax.fori_loop(0, F2 // tf, tile, 0)

    total, copies = reduce_parts(n, me, part, filler, sbuf, rbuf, ss, rs)
    out_ref[...] = (after()[...] + total).astype(BF)
    for copy in copies.values():
        copy.wait_send()
    for j in range(F2 // tf):
        leave(j).wait()


def feed_grads(n, hidden, wd, after, h, dgu):
    C, D = after.shape
    T, F2 = dgu.shape
    return pl.pallas_call(
        functools.partial(feed_kernel, n),
        in_specs=[VSPEC] * 2 + [ANYSPEC] * 3,
        out_specs=[VSPEC, ANYSPEC],
        out_shape=[sds((C, D), BF), sds((D, F2), BF)],
        scratch_shapes=reduce_bufs(n, C, D)
        + held(h, dgu, after)
        + [pltpu.VMEM((D, F2), BF), pltpu.SemaphoreType.DMA((F2 // 512,))],
        compiler_params=params(collective_id=6, has_side_effects=True),
        cost_estimate=cost(3 * T * D * F2, 6 * D * F2),
        name="feed_grads",
    )(hidden, wd, after, h, dgu)


def gather_kernel(n, ndp, x_in, w_ref, h2_ref, dcq_ref, cb_ref, ca_ref, dkv_ref, ctx_ref, at_ref, x_hbm, da_ref, gr_hbm, kv_ref,
                  buf, other, ksend, krecv, ss, rs, ss2, rs2, pair, x_ref, acc, gr_ref, osem, gsem):
    me = lax.axis_index("tensor")
    dp = lax.axis_index("dp")
    core = dp % 2
    partner = dp + 1 - 2 * core
    C, D = x_in.shape
    W = w_ref.shape[0]
    KP = ctx_ref.shape[0]
    R = D // ndp
    greet(n, me, [partner])
    gather = Gather(n, me, x_in, lambda t: x_ref.at[t], lambda t, i: x_ref.at[t, pl.ds(i * C // 2, C // 2)], ss, rs)
    gather.start()
    kv = {}
    for d in range(1, n):
        ksend[d - 1] = dkv_ref[me ^ d].astype(BF)
        kv[d] = remote(ksend.at[d - 1], krecv.at[d - 1], ss2.at[d - 1], rs2.at[d - 1], me ^ d)
        kv[d].start()

    kept = []

    def back(i, t):
        rows = pl.ds(pl.multiple_of(t * C, C), C)
        x = x_ref[t]
        kept.append(pltpu.make_async_copy(x_ref.at[t], x_hbm.at[t], osem.at[i]))
        kept[-1].start()
        da_ref[rows, :] = nt(x, w_ref[...]).astype(BF)
        term = tn(x, at_ref[rows, :])
        if i == 0:
            acc[...] = term
        else:
            acc[...] += term

    x_ref[me] = x_in[...]
    back(0, me)

    for j in range(ndp // 2):
        h2, cb = h2_ref[:, 2 * R * j : 2 * R * (j + 1)], cb_ref[:, 2 * R * j : 2 * R * (j + 1)]

        def weights(t, carry):
            for i, (a, b) in enumerate(((h2, dcq_ref[t]), (cb, ca_ref[t]))):
                res = tn(a, b).astype(BF)
                for c in range(2):
                    buf[c, t, j * R : (j + 1) * R, i * W : (i + 1) * W] = res[c * R : (c + 1) * R]
            return carry

        lax.fori_loop(0, n, weights, 0)
    swap = to_dp(buf.at[1 - core], other, pair.at[0], pair.at[1], partner)
    swap.start()
    gather.relay()
    dkv = dkv_ref[me]
    for d in range(1, n):
        kv[d].wait_recv()
        dkv = dkv + krecv[d - 1].astype(F32)
    for half in range(2):
        kvg = tn(ctx_ref[...], dkv[half * KP : (half + 1) * KP].astype(BF)).astype(BF)
        S = kvg.shape[0] // ndp
        for i in range(ndp):
            kv_ref[(2 * i + half) * S : (2 * i + half + 1) * S, W:] = kvg[i * S : (i + 1) * S]
    for d in range(1, n - 1):
        gather.wait(d)
        back(d, me ^ d)
    swap.wait_recv()

    def leave(t):
        return pltpu.make_async_copy(gr_ref.at[t], gr_hbm.at[t], gsem.at[t])

    def add(t, carry):
        gr_ref[t] = (buf[core, t].astype(F32) + other[t].astype(F32)).astype(BF)
        leave(t).start()
        return carry

    lax.fori_loop(0, n, add, 0)
    gather.wait(n - 1)
    back(n - 1, me ^ (n - 1))
    kv_ref[:, :W] = acc[...].astype(BF)
    gather.finish()
    for copy in kept:
        copy.wait()
    for t in range(n):
        leave(t).wait()
    for d in range(1, n):
        kv[d].wait_send()
    swap.wait_send()


def gather_back(n, ndp, x, w, h2, dcq, cb, ca, dkv, ctx, attn):
    C, D = x.shape
    W = w.shape[0]
    KP = ctx.shape[0]
    half = (n, D // 2, 2 * W)
    return pl.pallas_call(
        functools.partial(gather_kernel, n, ndp),
        in_specs=[VSPEC] * 9,
        out_specs=[ANYSPEC, VSPEC, ANYSPEC, VSPEC],
        out_shape=[sds((n, C, D), BF), sds((n * C, W), BF), sds(half, BF), sds((D, 2 * W), BF)],
        scratch_shapes=[pltpu.VMEM((2, *half), BF), pltpu.VMEM(half, BF)]
        + [pltpu.VMEM((n - 1, 2 * KP, W), BF)] * 2
        + [pltpu.SemaphoreType.DMA((links(n),))] * 2
        + [pltpu.SemaphoreType.DMA((n - 1,))] * 2
        + [pltpu.SemaphoreType.DMA((2,))]
        + [pltpu.VMEM((n, C, D), BF), pltpu.VMEM((D, W), F32), pltpu.VMEM(half, BF)]
        + [pltpu.SemaphoreType.DMA((n,))] * 2,
        compiler_params=params(collective_id=2, has_side_effects=True),
        cost_estimate=cost(2 * n * C * W * D + 2e10, 8 * C * D),
        name="gather_back",
    )(x, w, h2, dcq, cb, ca, dkv, ctx, attn)


def attn_bwd_kernel(n, ndp, q_ref, k_ref, v_ref, o_ref, do_ref, lse_ref, c_ref, s_ref, h_hbm, e_hbm, a_hbm,
                    dq_ref, dk_ref, dv_ref, gr_hbm, dk_acc, dv_acc, kt_ref, sbuf, rbuf, ss, rs,
                    a_ref, h_ref, e_ref, lsem, gr_ref, osem, x_ref):
    me = lax.axis_index("tensor")
    T, W = q_ref.shape
    G = lane_group(W)
    qb = 256
    mult = SCALE * LOG2E
    nh = G // HEAD_DIM
    greet(n, me)
    shards = ShardSum(n, me, a_ref, sbuf, rbuf, ss, rs)
    shards.start(a_hbm)
    a, h_all, early = (
        Late(src, dst, lsem.at[i]) for i, (src, dst) in enumerate(((a_hbm, a_ref), (h_hbm, h_ref), (e_hbm, e_ref)))
    )
    masks = [m.astype(BF) for m in head_masks(1, G)]
    head_rows = jnp.where(
        lax.broadcasted_iota(jnp.int32, (16, G), 0) == lax.broadcasted_iota(jnp.int32, (16, G), 1) // HEAD_DIM, 1.0, 0.0
    ).astype(BF)

    def heads(g, outer):
        cols = pl.ds(pl.multiple_of(g * G, G), G) if G < W else slice(None)
        k, v = k_ref[:, cols], v_ref[:, cols]
        kt_ref[...] = jnp.transpose(k.astype(F32)).astype(BF)
        dk_acc[...] = jnp.zeros_like(dk_acc)
        dv_acc[...] = jnp.zeros_like(dv_acc)

        def block(i, carry):
            rows = pl.ds(pl.multiple_of(i * qb, qb), qb)
            q = q_ref[rows, cols]
            do = do_ref[rows, cols]
            prod = do.astype(F32) * o_ref[rows, cols].astype(F32)
            high = prod.astype(BF)
            delta = nt(head_rows, high) + nt(head_rows, (prod - high.astype(F32)).astype(BF))
            lse = lse_ref[g, :, rows]
            parts = []
            for h in range(nh):
                qm = q * masks[h]
                dom = do * masks[h]
                st = nt(k, qm)
                pt = jnp.exp2(st * mult - lse[h : h + 1, :])
                dpt = nt(v, dom)
                dst = (pt * (dpt - delta[h : h + 1, :])).astype(BF)
                dv_acc[...] += nn(pt.astype(BF), dom)
                dk_acc[...] += nn(dst, qm)
                parts.append(nn(kt_ref[h * HEAD_DIM : (h + 1) * HEAD_DIM, :], dst))
            dq = jnp.transpose(jnp.concatenate(parts, 0)) * SCALE
            dq_ref[rows, cols] = (dq * c_ref[rows, :] - turned(dq) * s_ref[rows, :]).astype(BF)
            return carry

        lax.fori_loop(0, T // qb, block, 0)
        dk = dk_acc[...] * SCALE
        dk_ref[:, cols] = (dk * c_ref[...] - turned(dk) * s_ref[...]).astype(BF)
        dv_ref[:, cols] = dv_acc[...].astype(BF)
        return outer

    lax.fori_loop(0, W // G, heads, 0)
    a()
    shards.middle()
    h_all()
    early()
    tf = 256
    cut = 5 * W if W % 128 == 0 else 0

    def leave(j):
        rows = pl.ds(pl.multiple_of(j * tf, tf), tf)
        return pltpu.make_async_copy(gr_ref.at[rows, :cut], gr_hbm.at[rows, :cut], osem.at[j])

    def weights(j, carry):
        rows = pl.ds(pl.multiple_of(j * tf, tf), tf)
        h = h_ref[:, rows]
        for i, g_ref in enumerate((dq_ref, dk_ref, dv_ref)):
            gr_ref[rows, i * W : (i + 1) * W] = tn(h, g_ref[...]).astype(BF)
        gr_ref[rows, 3 * W : 5 * W] = e_ref[rows, :]
        if cut:
            leave(j).start()
        return carry

    lax.fori_loop(0, gr_ref.shape[0] // tf, weights, 0)
    shards.store(x_ref)
    core = lax.axis_index("dp") % 2
    R = gr_ref.shape[0] // ndp
    for i in range(ndp // 2):
        gr_ref[pl.ds(pl.multiple_of((2 * i + core) * R, 16), R), 5 * W :] = x_ref[i * R : (i + 1) * R]
        gr_ref[pl.ds(pl.multiple_of((2 * i + 1 - core) * R, 16), R), 5 * W :] = jnp.zeros((R, 2 * W), BF)
    final = pltpu.make_async_copy(gr_ref.at[:, cut:], gr_hbm.at[:, cut:], osem.at[gr_ref.shape[0] // tf])
    final.start()
    if cut:
        for j in range(gr_ref.shape[0] // tf):
            leave(j).wait()
    final.wait()


def attn_bwd(n, ndp, q, k, v, o, do, lse, cs, sn, h, early, a):
    T, W = q.shape
    D = h.shape[1]
    G = lane_group(W)
    _, R, N = a.shape
    slots = 6 if n == 4 else n - 1
    H = R // 2 if n == 4 else R
    return pl.pallas_call(
        functools.partial(attn_bwd_kernel, n, ndp),
        in_specs=[VSPEC] * 8 + [ANYSPEC] * 3,
        out_specs=[VSPEC] * 3 + [ANYSPEC],
        out_shape=[sds((T, W), BF)] * 3 + [sds((D, 7 * W), BF)],
        scratch_shapes=[pltpu.VMEM((T, G), F32), pltpu.VMEM((T, G), F32), pltpu.VMEM((G, T), BF)]
        + [pltpu.VMEM((2, H, N), BF), pltpu.VMEM((slots, H, N), BF)]
        + [pltpu.SemaphoreType.DMA((slots,))] * 2
        + held(a, h, early)
        + [pltpu.VMEM((D, 7 * W), BF), pltpu.SemaphoreType.DMA((D // 256 + 1,)), pltpu.VMEM((R, N), BF)],
        compiler_params=params(collective_id=5, has_side_effects=True),
        cost_estimate=cost(40 * T * T * W, 16 * T * W, T * T * W // HEAD_DIM),
        name="attn_bwd",
    )(q, k, v, o, do, lse, cs, sn, h, early, a)


def last_kernel(n, ndp, dq_ref, dk_ref, dv_ref, wq_ref, wk_ref, wv_ref, x_hbm, da_ref, g_ref, gg_in,
                lbuf, gg_ref, sbuf, rbuf, gbuf, gsum, gown, gall, ss, rs, ss2, rs2, ss3, rs3, ss4, rs4, x_buf, lsem):
    me = lax.axis_index("tensor")
    dp = lax.axis_index("dp")
    C, D = x_buf.shape
    x = Late(rows_of(x_hbm, me, C), x_buf, lsem.at[0])
    R = D // ndp
    others = [(dp + i) % ndp for i in range(1, ndp)]
    greet(n, me, others)

    def part(t):
        rows = pl.ds(pl.multiple_of(t * C, C), C)
        return nt(dq_ref[rows, :], wq_ref[...]) + nt(dk_ref[rows, :], wk_ref[...]) + nt(dv_ref[rows, :], wv_ref[...])

    total, copies = reduce_parts(n, me, part, lambda: None, sbuf, rbuf, ss, rs)
    u, inverse = unit(x()[...].astype(F32))
    row = lax.broadcasted_iota(jnp.int32, (8, D), 0)
    gsum[...] = gg_in[...] + jnp.where(row == 2, jnp.sum(total * u, axis=0, keepdims=True), 0.0)
    small = {}
    for d in range(1, n):
        small[d] = remote(gsum, gbuf.at[d - 1], ss3.at[d - 1], rs3.at[d - 1], me ^ d)
        small[d].start()
    lbuf[me] = (da_ref[...] + norm_back(total, u, inverse, g_ref[...].reshape(1, D))).astype(BF)
    gather = Gather(
        n, me, lbuf.at[me], lambda t: lbuf.at[t], lambda t, i: lbuf.at[t, pl.ds(i * C // 2, C // 2)], ss2, rs2
    )
    gather.start()
    gains = gsum[...]
    for d in range(1, n):
        small[d].wait_recv()
        gains = gains + gbuf[d - 1]
    for i in range(ndp):
        gown[i] = gains[:, i * R : (i + 1) * R]
    sums = []
    for i, other in enumerate(others):
        sums.append(to_dp(gown.at[other], gall.at[i], ss4.at[i], rs4.at[i], other))
        sums[i].start()
    gather.relay()
    mine = gown[dp]
    for i in range(ndp - 1):
        sums[i].wait_recv()
        mine = mine + gall[i]
    gg_ref[...] = mine
    for d in range(1, n):
        gather.wait(d)
    gather.finish()
    for copy in (*copies.values(), *small.values(), *sums):
        copy.wait_send()


def last(n, ndp, dq, dk, dv, wq, wk, wv, x, da, gain, gains):
    T, W = dq.shape
    C, D = da.shape
    return pl.pallas_call(
        functools.partial(last_kernel, n, ndp),
        in_specs=[VSPEC] * 6 + [ANYSPEC] + [VSPEC] * 3,
        out_specs=[VSPEC] * 2,
        out_shape=[sds((n, C, D), BF), sds((8, D // ndp), F32)],
        scratch_shapes=reduce_bufs(n, C, D)[:2]
        + [pltpu.VMEM((n - 1, 8, D), F32), pltpu.VMEM((8, D), F32)]
        + [pltpu.VMEM((ndp, 8, D // ndp), F32), pltpu.VMEM((ndp - 1, 8, D // ndp), F32)]
        + reduce_bufs(n, C, D)[2:]
        + [pltpu.SemaphoreType.DMA((links(n),))] * 2
        + [pltpu.SemaphoreType.DMA((n - 1,))] * 2
        + [pltpu.SemaphoreType.DMA((ndp - 1,))] * 2
        + held(sds((C, D), BF)),
        compiler_params=params(collective_id=3, has_side_effects=True),
        cost_estimate=cost(6 * T * W * D + 4e10, 8 * T * D),
        name="last",
    )(dq, dk, dv, wq, wk, wv, x, da, gain, gains)


def cross_fwd_kernel(n, ctx, h_ref, x_ref, wq_ref, kv_ref, wo_hbm, g_ref, q_ref, o_ref, after_ref, h3_ref, wo_ref, lsem):
    wo = Late(wo_hbm, wo_ref, lsem.at[0])
    _, C, W = q_ref.shape
    KP = kv_ref.shape[1] // 2
    mult = SCALE * LOG2E
    G = lane_group(W)
    per = W // G
    masks = [m.astype(BF) for m in head_masks(1, G)]
    lane = lax.broadcasted_iota(jnp.int32, (C, G), 1) // HEAD_DIM
    valid = lax.broadcasted_iota(jnp.int32, (C, KP), 1) < ctx

    def group(t, j):
        cols = slice(j * G, (j + 1) * G)
        q = nn(h_ref[...], wq_ref[t, :, cols]).astype(BF)
        q_ref[t, :, cols] = q
        k, v = kv_ref[t, :KP, cols], kv_ref[t, KP:, cols]
        out = jnp.zeros((C, G), F32)
        for h in range(G // HEAD_DIM):
            s = jnp.where(valid, nt(q * masks[h], k), -1e30)
            p = jnp.exp2((s - jnp.max(s, axis=-1, keepdims=True)) * mult)
            o = nn(p.astype(BF), v) / jnp.sum(p, axis=-1, keepdims=True)
            out = jnp.where(lane == h, o, out)
        o_ref[t, :, cols] = out.astype(BF)

    def shard(t, carry):
        for j in range(per):
            group(t, j)
        return carry

    lax.fori_loop(0, n, shard, 0)
    D = h_ref.shape[1]
    tf = 256
    wo()

    def project(j, carry):
        cols = pl.ds(pl.multiple_of(j * tf, tf), tf)
        total = nn(o_ref[0], wo_ref[0, :, cols])
        for t in range(1, n):
            total = total + nn(o_ref[t], wo_ref[t, :, cols])
        after_ref[:, cols] = x_ref[:, cols] + total
        return carry

    lax.fori_loop(0, D // tf, project, 0)
    u, _ = unit(after_ref[...])
    h3_ref[...] = (u * g_ref[...].reshape(1, D)).astype(BF)


def cross_fwd(ctx, h, x, wq, kv, wo, gain):
    C, D = h.shape
    n, W = wq.shape[0], wq.shape[2]
    return pl.pallas_call(
        functools.partial(cross_fwd_kernel, n, ctx),
        in_specs=[VSPEC] * 4 + [ANYSPEC, VSPEC],
        out_specs=[VSPEC] * 4,
        out_shape=[sds((n, C, W), BF), sds((n, C, W), BF), sds((C, D), F32), sds((C, D), BF)],
        scratch_shapes=held(wo),
        compiler_params=params(),
        cost_estimate=cost(4 * C * D * n * W + 16 * C * 256 * n * W, 8 * D * n * W),
        name="cross_fwd",
    )(h, x, wq, kv, wo, gain)


def cross_bwd_kernel(n, ctx, dh3_ref, after2_ref, cot_hbm, g3_ref, wo_hbm, q_ref, kv_ref, wq_hbm, after1_hbm, g2_ref, bo_in,
                     cb_ref, dq_ref, dkv_ref, da_ref, sb_ref, gg_ref, bo_ref, dh2_ref, ss, rs,
                     cot_buf, wo_ref, wq_ref, after1_buf, lsem):
    me = lax.axis_index("tensor")
    cot, wo, wq, after1 = (
        Late(src, dst, lsem.at[i])
        for i, (src, dst) in enumerate(
            (
                (rows_of(cot_hbm, me, cot_buf.shape[0]), cot_buf),
                (wo_hbm, wo_ref),
                (wq_hbm, wq_ref),
                (after1_hbm, after1_buf),
            )
        )
    )
    _, C, W = q_ref.shape
    KP = kv_ref.shape[1] // 2
    D = da_ref.shape[1]
    mult = SCALE * LOG2E
    G = lane_group(W)
    per = W // G
    masks = [m.astype(BF) for m in head_masks(1, G)]
    lane = lax.broadcasted_iota(jnp.int32, (C, G), 1) // HEAD_DIM
    valid = lax.broadcasted_iota(jnp.int32, (C, KP), 1) < ctx
    greet(n, me)
    gather = Gather(n, me, bo_in, lambda t: bo_ref.at[t], lambda t, i: bo_ref.at[t, pl.ds(i * C // 2, C // 2)], ss, rs)
    gather.start()
    bo_ref[me] = bo_in[...]
    dh3 = dh3_ref[...]
    u3, inv3 = unit(after2_ref[...])
    gain3 = jnp.sum(dh3 * u3, axis=0, keepdims=True)
    da2 = cot()[...].astype(F32) + norm_back(dh3, u3, inv3, g3_ref[...].reshape(1, D))
    da_ref[...] = da2
    cb_ref[...] = da2.astype(BF)
    wo()

    def group(t, j):
        cols = slice(j * G, (j + 1) * G)
        do = nt(cb_ref[...], wo_ref[t, cols, :]).astype(BF)
        q, k, v = q_ref[t, :, cols], kv_ref[t, :KP, cols], kv_ref[t, KP:, cols]
        dq = jnp.zeros((C, G), F32)
        dk = jnp.zeros((KP, G), F32)
        dv = jnp.zeros((KP, G), F32)
        for h in range(G // HEAD_DIM):
            qm = q * masks[h]
            dom = do * masks[h]
            s = jnp.where(valid, nt(qm, k), -1e30)
            p = jnp.exp2((s - jnp.max(s, axis=-1, keepdims=True)) * mult)
            p = p / jnp.sum(p, axis=-1, keepdims=True)
            dp = nt(dom, v)
            ds = (p * (dp - jnp.sum(p * dp, axis=-1, keepdims=True))).astype(BF)
            dq = jnp.where(lane == h, nn(ds, k), dq)
            dk = dk + tn(ds, qm)
            dv = dv + tn(p.astype(BF), dom)
        dq_ref[t, :, cols] = (dq * SCALE).astype(BF)
        dkv_ref[t, :KP, cols] = dk * SCALE
        dkv_ref[t, KP:, cols] = dv

    def shard(t, carry):
        for j in range(per):
            group(t, j)
        return carry

    lax.fori_loop(0, n, shard, 0)
    gather.relay()
    wq()
    tf = 256

    def project(j, carry):
        cols = pl.ds(pl.multiple_of(j * tf, tf), tf)
        total = nt(dq_ref[0], wq_ref[0, cols, :])
        for t in range(1, n):
            total = total + nt(dq_ref[t], wq_ref[t, cols, :])
        dh2_ref[:, cols] = total
        return carry

    lax.fori_loop(0, D // tf, project, 0)
    dh2 = dh2_ref[...]
    u2, inv2 = unit(after1()[...])
    gain2 = jnp.sum(dh2 * u2, axis=0, keepdims=True)
    da1 = da_ref[...] + norm_back(dh2, u2, inv2, g2_ref[...].reshape(1, D))
    da_ref[...] = da1
    sb_ref[...] = da1.astype(BF)
    row = lax.broadcasted_iota(jnp.int32, (8, D), 0)
    gg_ref[...] = jnp.where(row == 0, gain3, 0.0) + jnp.where(row == 1, gain2, 0.0)
    for d in range(1, n):
        gather.wait(d)
    gather.finish()


def cross_bwd(ctx, dh3, after2, cot, g3, wo, q, kv, wq, after1, g2, bo):
    C, D = after2.shape
    n, W = wq.shape[0], wq.shape[2]
    return pl.pallas_call(
        functools.partial(cross_bwd_kernel, n, ctx),
        in_specs=[VSPEC, VSPEC, ANYSPEC, VSPEC, ANYSPEC, VSPEC, VSPEC, ANYSPEC, ANYSPEC, VSPEC, VSPEC],
        out_specs=[VSPEC] * 7,
        out_shape=[
            sds((C, D), BF),
            sds((n, C, W), BF),
            sds(kv.shape, F32),
            sds((C, D), F32),
            sds((C, D), BF),
            sds((8, D), F32),
            sds((n, C, D), BF),
        ],
        scratch_shapes=[pltpu.VMEM((C, D), F32)]
        + [pltpu.SemaphoreType.DMA((links(n),))] * 2
        + held(sds((C, D), BF), wo, wq, after1),
        compiler_params=params(collective_id=7, has_side_effects=True),
        cost_estimate=cost(4 * C * D * n * W + 40 * C * 256 * n * W, 8 * D * n * W),
        name="cross_bwd",
    )(dh3, after2, cot, g3, wo, q, kv, wq, after1, g2, bo)


def body(latents, context, cotangent, g1, wq, wk, wv, wo, g2, xq, xk, xv, xo, g3, wg, wu, wd, n, ndp):
    _, T, D = latents.shape
    ctx = context.shape[1]
    W = wq.shape[1]
    F = wg.shape[1]
    C = T // n
    x = latents.reshape(T, D)
    gb = cotangent.reshape(T, D)
    ctx_rows = context.reshape(ctx, -1)
    KP = -(-ctx // 16) * 16
    cs, sn = tables(T, lane_group(W))

    ctx_pad = jnp.pad(ctx_rows, ((0, KP - ctx), (0, 0)))
    h1, q, k, v, attn, lse, xq_all, xo_all, kv_all = front(n, ctx, x, g1, wq, wk, wv, cs, sn, xq, xo, ctx_pad, xk, xv)
    after1, h2 = out_rs(n, attn, wo, x, g2)
    cq, cattn, after2, h3_own = cross_fwd(ctx, h2, after1, xq_all, kv_all, xo_all, g3)
    h3, hidden, dgu, dh3, down_part = ff(n, h3_own, gb, wg, wu, wd)
    h3 = h3.reshape(T, D)

    def scatter(a, axis):
        return lax.psum_scatter(a, axis, scatter_dimension=0, tiled=True)

    down_grad = scatter(down_part, "dp")
    out_own, gu_part = feed_grads(n, hidden, wd, after2, h3, dgu)
    dh3, gu_part = lax.optimization_barrier((dh3, gu_part))
    gu_grad = scatter(gu_part, "dp")

    cb, dcq, dckv, dafter1, sb_own, gains, block_out = cross_bwd(
        ctx, dh3, after2, gb, g3, xo_all, cq, kv_all, xq_all, after1, g2, out_own
    )
    sb_own, down_grad = lax.optimization_barrier((sb_own, down_grad))
    sb, dattn, cross_part, early_part = gather_back(n, ndp, sb_own, wo, h2, dcq, cb, cattn, dckv, ctx_pad, attn)
    dq, dk, dv, self_part = attn_bwd(n, ndp, q, k, v, attn, dattn, lse, cs, sn, h1, early_part, cross_part)
    self_grads = scatter(self_part, "dp")
    dq, gu_grad = lax.optimization_barrier((dq, gu_grad))
    latent_grad, gains = last(n, ndp, dq, dk, dv, wq, wk, wv, x, dafter1, g1, gains)

    latent_grad = latent_grad.astype(F32)
    gu_grad = gu_grad.astype(F32)
    gate_grad, up_grad, down_grad = gu_grad[:, :F], gu_grad[:, F:], down_grad.astype(F32).T
    block_out = jnp.maximum(block_out, jnp.finfo(BF).min)
    self_grads, gains, latent_grad, gate_grad, up_grad, down_grad, block_out = lax.optimization_barrier(
        (self_grads, gains, latent_grad, gate_grad, up_grad, down_grad, block_out)
    )
    self_grads = self_grads.astype(F32)
    so_grad, kv_grads = self_grads[:, 3 * W : 4 * W].T, self_grads[:, 4 * W : 5 * W].reshape(2, D // ndp // 2, W)
    xq_grad, xo_grad = self_grads[:, 5 * W : 6 * W], self_grads[:, 6 * W :].T
    return (
        block_out.reshape(1, T, D),
        latent_grad.reshape(1, T, D),
        gains[2],
        self_grads[:, :W],
        self_grads[:, W : 2 * W],
        self_grads[:, 2 * W : 3 * W],
        so_grad,
        gains[1],
        xq_grad,
        kv_grads[0],
        kv_grads[1],
        xo_grad,
        gains[0],
        gate_grad,
        up_grad,
        down_grad,
    )


def solution(mesh):
    tokens = P("dp", None, None)
    cols = P(None, "tensor")
    rows = P("tensor", None)
    return jax.shard_map(
        functools.partial(body, n=mesh.shape["tensor"], ndp=mesh.shape["dp"]),
        mesh=mesh,
        in_specs=(tokens, tokens, tokens, P(), cols, cols, cols, rows, P(), cols, cols, cols, rows, P(), cols, cols, rows),
        out_specs=(
            tokens,
            tokens,
            P("dp"),
            P("dp", "tensor"),
            P("dp", "tensor"),
            P("dp", "tensor"),
            P("tensor", "dp"),
            P("dp"),
            P("dp", "tensor"),
            P("dp", "tensor"),
            P("dp", "tensor"),
            P("tensor", "dp"),
            P("dp"),
            P("dp", "tensor"),
            P("dp", "tensor"),
            P("tensor", "dp"),
        ),
        check_vma=False,
    )
```
